32 devices in a mesh: shard: 4 (over y, x), ctx: 4 (over z), tp: 2 (over core).
Axes of the slice: x: 2, y: 2, z: 4, core: 2. Of those that a mesh axis runs over, the one named last changes fastest.
Arguments:
- frames: bfloat16 [4, 2048, 768], P('shard', 'ctx'), may hold values from -6 to 6
- lengths: int32 [4], P('shard'), may hold values from 512 to 2048, as said below
- cotangent: bfloat16 [4, 2048, 768], P('shard', 'ctx'), may hold values from -6 to 6
- ln1_gain: float32 [768], replicated, may hold values from 0.5 to 1.5
- ln1_bias: float32 [768], replicated, may hold values from -1 to 1
- w_query: bfloat16 [768, 768], P(('shard', 'ctx'), 'tp'), may hold values from -0.3125 to 0.3125
- b_query: float32 [768], P('tp'), may hold values from -1 to 1
- w_key: bfloat16 [768, 768], P(('shard', 'ctx'), 'tp'), may hold values from -0.3125 to 0.3125
- w_value: bfloat16 [768, 768], P(('shard', 'ctx'), 'tp'), may hold values from -0.21875 to 0.21875
- b_value: float32 [768], P('tp'), may hold values from -1 to 1
- w_out: bfloat16 [768, 768], P('tp', ('shard', 'ctx')), may hold values from -1.25 to 1.25
- b_out: float32 [768], replicated, may hold values from -1 to 1
- ln2_gain: float32 [768], replicated, may hold values from 0.5 to 1.5
- ln2_bias: float32 [768], replicated, may hold values from -1 to 1
- w_up: bfloat16 [768, 3072], P(('shard', 'ctx'), 'tp'), may hold values from -0.21875 to 0.21875
- b_up: float32 [3072], P('tp'), may hold values from -1 to 1
- w_down: bfloat16 [3072, 768], P('tp', ('shard', 'ctx')), may hold values from -0.109375 to 0.109375
- b_down: float32 [768], replicated, may hold values from -1 to 1
Outputs:
- output: bfloat16 [4, 2048, 768], P('shard', 'ctx')
- grad_input: float32 [4, 2048, 768], P('shard', 'ctx')
- grad_ln1_gain: float32 [768], replicated
- grad_ln1_bias: float32 [768], replicated
- grad_w_query: float32 [768, 768], P(('shard', 'ctx'), 'tp')
- grad_b_query: float32 [768], P('tp')
- grad_w_key: float32 [768, 768], P(('shard', 'ctx'), 'tp')
- grad_w_value: float32 [768, 768], P(('shard', 'ctx'), 'tp')
- grad_b_value: float32 [768], P('tp')
- grad_w_out: float32 [768, 768], P('tp', ('shard', 'ctx'))
- grad_b_out: float32 [768], replicated
- grad_ln2_gain: float32 [768], replicated
- grad_ln2_bias: float32 [768], replicated
- grad_w_up: float32 [768, 3072], P(('shard', 'ctx'), 'tp')
- grad_b_up: float32 [3072], P('tp')
- grad_w_down: float32 [3072, 768], P('tp', ('shard', 'ctx'))
- grad_b_down: float32 [768], replicated
The draws below stay inside these ranges and needn't reach their ends.
Inputs may be any that keep to these rules, and one draw needn't show every extreme that they name: lengths[s] is the number of live frames at the start of slot s, at least 512; at least one slot has exactly 2048.
All inputs are finite; a program needn't handle non-finite values.
Results may differ from the reference program's by a relative error of at most 0.018.
Values may be sent and summed in bfloat16 or wider, within the bound.
A program may use at most 128 MiB of HBM per device.

```python
import math
import jax
import jax.numpy as jnp
from jax import lax

D = 768
H = 12
HD = 64
FF = 3072
LEN = 2048
SLOTS = 4


def draw_lengths(key, part):
    spread_key = jax.random.fold_in(key, 11)
    pick_key = jax.random.fold_in(key, 12)
    sampled = jax.random.randint(spread_key, (SLOTS,), LEN // 4, LEN + 1)
    chosen = jax.random.randint(pick_key, (), 0, SLOTS)
    return jnp.where(jnp.arange(SLOTS) == chosen, LEN, sampled).astype(jnp.int32)


def steps_of(own_key, dims, shards, low, top_value):
    level, own = 1.0, jax.random.fold_in(own_key, 6)
    for position, blocks in shards:
        draws = jnp.exp(jax.random.uniform(jax.random.fold_in(own, position), (blocks,), jnp.float32, low / len(shards), top_value / len(shards)))
        level = level * jnp.repeat(draws, dims[position] // blocks).reshape([-1 if axis == position else 1 for axis in range(len(dims))])
    return level


def gaussian(own_key, shape, width, limit, split=(), held_as=jnp.bfloat16):
    values = width * jax.random.normal(own_key, shape, jnp.float32)
    if split:
        values = values * steps_of(own_key, shape, split, -0.22, 0.18)
    return jnp.clip(values, -limit, limit).astype(held_as)


def setup_inputs(seed: int = 0) -> dict:
    keys = jax.random.split(jax.random.key(seed), 19)
    frames = gaussian(keys[0], (SLOTS, LEN, D), 1.0, 6.0, ((0, 4), (1, 4)))
    lengths = draw_lengths(jax.random.fold_in(keys[18], 71), 0)
    cotangent = gaussian(keys[2], (SLOTS, LEN, D), 1.0, 6.0, ((0, 4), (1, 4)))
    ln1_gain = jnp.clip(1.0 + 0.1 * jax.random.normal(keys[3], (D,), jnp.float32), 0.5, 1.5)
    ln1_bias = gaussian(keys[4], (D,), 0.2, 1.0, (), jnp.float32)
    w_query = gaussian(keys[5], (D, H * HD), (D // 2) ** -0.5, 0.3125, ((0, 16), (1, 2)))
    b_query = gaussian(keys[6], (H * HD,), 0.2, 1.0, ((0, 2),), jnp.float32)
    w_key = gaussian(keys[7], (D, H * HD), (D // 2) ** -0.5, 0.3125, ((0, 16), (1, 2)))
    w_value = gaussian(keys[8], (D, H * HD), D ** -0.5, 0.21875, ((0, 16), (1, 2)))
    b_value = gaussian(keys[9], (H * HD,), 0.2, 1.0, ((0, 2),), jnp.float32)
    w_out = gaussian(keys[10], (H * HD, D), (H * HD // 32) ** -0.5, 1.25, ((0, 2), (1, 16)))
    b_out = gaussian(keys[11], (D,), 0.2, 1.0, (), jnp.float32)
    ln2_gain = jnp.clip(1.0 + 0.1 * jax.random.normal(keys[12], (D,), jnp.float32), 0.5, 1.5)
    ln2_bias = gaussian(keys[13], (D,), 0.2, 1.0, (), jnp.float32)
    w_up = gaussian(keys[14], (D, FF), D ** -0.5, 0.21875, ((0, 16), (1, 2)))
    b_up = gaussian(keys[15], (FF,), 0.2, 1.0, ((0, 2),), jnp.float32)
    w_down = gaussian(keys[16], (FF, D), FF ** -0.5, 0.109375, ((0, 2), (1, 16)))
    b_down = gaussian(keys[17], (D,), 0.2, 1.0, (), jnp.float32)
    return dict(frames=frames, lengths=lengths, cotangent=cotangent, ln1_gain=ln1_gain, ln1_bias=ln1_bias, w_query=w_query, b_query=b_query, w_key=w_key, w_value=w_value, b_value=b_value, w_out=w_out, b_out=b_out, ln2_gain=ln2_gain, ln2_bias=ln2_bias, w_up=w_up, b_up=b_up, w_down=w_down, b_down=b_down)


@jax.custom_vjp
def low(v):
    return lax.optimization_barrier(v.astype(jnp.bfloat16)).astype(jnp.float32)

@jax.custom_vjp
def low_back(v):
    return v

def low_keep(v):
    return (low(v), None)

def low_pass(kept, grad):
    return (grad,)

def back_keep(v):
    return (v, None)

def back_low(kept, grad):
    return (low(grad),)
low.defvjp(low_keep, low_pass)
low_back.defvjp(back_keep, back_low)
HIGHEST = lax.Precision.HIGHEST
EPSILON = 1e-05

def layer_norm(values, gain, shift):
    centred = values - lax.optimization_barrier(jnp.mean(values, axis=-1, keepdims=True))
    inverse = lax.rsqrt(lax.optimization_barrier(jnp.mean(centred * centred, axis=-1, keepdims=True)) + EPSILON)
    return centred * inverse * gain + shift

def slot_layer(params, slot_frames, length):
    gain_one, shift_one, weight_query, bias_query, weight_key, weight_value, bias_value, weight_out, bias_out, gain_two, shift_two, weight_up, bias_up, weight_down, bias_down = params
    positions = jnp.arange(LEN, dtype=jnp.int32)
    live_keys = positions < length
    normed = low(layer_norm(slot_frames, gain_one, shift_one))
    queries = low_back(low(jnp.dot(normed, weight_query, precision=HIGHEST) + bias_query))
    keys_all = low_back(low(jnp.dot(normed, weight_key, precision=HIGHEST)))
    values_all = low_back(low(jnp.dot(normed, weight_value, precision=HIGHEST) + bias_value))
    key_heads = keys_all.reshape(LEN, H, HD)
    value_heads = values_all.reshape(LEN, H, HD)
    block_rows = math.gcd(LEN, 512)

    def attend(query_block):
        scores = low_back(jnp.einsum('qhd,khd->hqk', query_block, key_heads, precision=HIGHEST) * HD ** (-0.5))
        scores = jnp.where(live_keys[None, None, :], scores, -jnp.inf)
        shifted = scores - lax.optimization_barrier(jnp.max(scores, axis=-1, keepdims=True))
        expo_terms = jnp.exp(shifted)
        probabilities = low(expo_terms / lax.optimization_barrier(jnp.sum(expo_terms, axis=-1, keepdims=True)))
        return jnp.einsum('hqk,khd->qhd', probabilities, value_heads, precision=HIGHEST)
    attended = lax.map(jax.checkpoint(attend), queries.reshape(LEN // block_rows, block_rows, H, HD))
    attended = low_back(low(attended.reshape(LEN, H * HD)))
    hidden = slot_frames + low_back(jnp.dot(attended, weight_out, precision=HIGHEST) + bias_out)
    second = low(layer_norm(hidden, gain_two, shift_two))
    upper = low_back(jnp.dot(second, weight_up, precision=HIGHEST) + bias_up)
    activated = low(jax.nn.gelu(upper, approximate=False))
    branch = low_back(jnp.dot(activated, weight_down, precision=HIGHEST) + bias_down)
    return live_keys.astype(jnp.float32)[:, None] * (hidden + branch)

def reference(frames, lengths, cotangent, ln1_gain, ln1_bias, w_query, b_query, w_key, w_value, b_value, w_out, b_out, ln2_gain, ln2_bias, w_up, b_up, w_down, b_down):
    params = tuple((argument.astype(jnp.float32) for argument in (ln1_gain, ln1_bias, w_query, b_query, w_key, w_value, b_value, w_out, b_out, ln2_gain, ln2_bias, w_up, b_up, w_down, b_down)))
    frames_full = frames.astype(jnp.float32)

    def whole_layer(layer_params, layer_frames):

        def per_slot(frames_one, length):
            return slot_layer(layer_params, frames_one, length)
        checked = jax.checkpoint(per_slot)

        def step(carried, scan_item):
            return (carried, checked(scan_item[0], scan_item[1]))
        ignored, outputs = lax.scan(step, jnp.float32(0.0), (layer_frames, lengths))
        return outputs
    outputs, pullback = jax.vjp(whole_layer, params, frames_full)
    grads, grad_frames = pullback(cotangent.astype(jnp.float32))
    return (outputs.astype(jnp.bfloat16), grad_frames, grads[0], grads[1], grads[2], grads[3], grads[4], grads[5], grads[6], grads[7], grads[8], grads[9], grads[10], grads[11], grads[12], grads[13], grads[14])
```

```python
import functools
import math

import jax
import jax.numpy as jnp
from jax import lax
from jax.experimental import pallas as pl
from jax.experimental.pallas import tpu as pltpu
from jax.sharding import PartitionSpec as P

HD = 64


EPSILON = 1e-05
INV_ROOT_TWO = 0.7071067811865476
INV_ROOT_TAU = 0.3989422804014327


def norm_rows(values, gain, shift):
    centred = values - jnp.mean(values, axis=-1, keepdims=True)
    inverse = lax.rsqrt(jnp.mean(centred * centred, axis=-1, keepdims=True) + EPSILON)
    normed = centred * inverse
    return (normed * gain + shift, normed, inverse)


def norm_back(grad_rows, normed, inverse, gain):
    scaled = grad_rows * gain
    inner = (
        scaled
        - jnp.mean(scaled, axis=-1, keepdims=True)
        - normed * jnp.mean(scaled * normed, axis=-1, keepdims=True)
    )
    return (inner * inverse, jnp.sum(grad_rows * normed, axis=0), jnp.sum(grad_rows, axis=0))


def gelu_slope(values):
    return (
        0.5 * (1.0 + lax.erf(values * INV_ROOT_TWO))
        + values * jnp.exp(-0.5 * values * values) * INV_ROOT_TAU
    )


def pair_scores(queries, block_keys, score_scale):
    return (
        jnp.einsum("qhd,khd->hqk", queries, block_keys, preferred_element_type=jnp.float32)
        * score_scale
    )


def live_weights(scores, query_live, key_live, log_totals):
    both_live = query_live[None, :, None] & key_live[None, None, :]
    return jnp.where(both_live, jnp.exp(scores - log_totals[:, :, None]), 0.0)


def in_blocks(array, block_rows):
    return array.reshape((array.shape[0] // block_rows, block_rows) + array.shape[1:])


def slot_forward(queries, slot_keys, slot_values, query_live, key_live, key_block, score_scale):
    seg_rows, head_count, head_dim = queries.shape
    key_starts = jnp.arange(slot_keys.shape[0] // key_block, dtype=jnp.int32) * key_block
    blocks = (
        in_blocks(slot_keys, key_block),
        in_blocks(slot_values, key_block),
        in_blocks(key_live, key_block),
        key_starts,
    )
    start_state = (
        jnp.full((head_count, seg_rows), -jnp.inf, jnp.float32),
        jnp.zeros((head_count, seg_rows), jnp.float32),
    )

    def totals_step(carried, scan_item):
        block_keys, block_values, block_live, block_start = scan_item
        running_max, running_sum = carried
        scores = jnp.where(
            block_live[None, None, :], pair_scores(queries, block_keys, score_scale), -jnp.inf
        )
        new_max = jnp.maximum(running_max, jnp.max(scores, axis=-1))
        new_sum = running_sum * jnp.exp(running_max - new_max) + jnp.sum(
            jnp.exp(scores - new_max[:, :, None]), axis=-1
        )
        return ((new_max, new_sum), None)

    def whole_slot(ignored):
        final_state, unused = lax.scan(totals_step, start_state, blocks)
        log_totals = final_state[0] + jnp.log(final_state[1])

        def output_step(output_sum, scan_item):
            block_keys, block_values, block_live, block_start = scan_item
            weights_here = live_weights(
                pair_scores(queries, block_keys, score_scale), query_live, block_live, log_totals
            ).astype(jnp.bfloat16)
            return (
                output_sum
                + jnp.einsum(
                    "hqk,khd->qhd", weights_here, block_values, preferred_element_type=jnp.float32
                ),
                None,
            )

        attended, unused_too = lax.scan(
            output_step, jnp.zeros((seg_rows, head_count, head_dim), jnp.float32), blocks
        )
        return (log_totals, attended)

    return whole_slot(0)


def slot_back(
    queries,
    grad_att,
    log_totals,
    delta,
    slot_keys,
    slot_values,
    query_live,
    key_live,
    key_block,
    score_scale,
):
    seg_rows, head_count, head_dim = queries.shape
    key_starts = jnp.arange(slot_keys.shape[0] // key_block, dtype=jnp.int32) * key_block
    blocks = (
        in_blocks(slot_keys, key_block),
        in_blocks(slot_values, key_block),
        in_blocks(key_live, key_block),
        key_starts,
    )

    def grad_step(grad_query, scan_item):
        block_keys, block_values, block_live, block_start = scan_item
        partial_value = grad_query
        weights_full = live_weights(
            pair_scores(queries, block_keys, score_scale), query_live, block_live, log_totals
        )
        grad_probs = jnp.einsum(
            "qhd,khd->hqk", grad_att, block_values, preferred_element_type=jnp.float32
        )
        grad_scores = (weights_full * (grad_probs - delta[:, :, None])).astype(jnp.bfloat16)
        partial_value = (
            partial_value
            + jnp.einsum(
                "hqk,khd->qhd", grad_scores, block_keys, preferred_element_type=jnp.float32
            )
            * score_scale
        )
        grad_value = jnp.einsum(
            "hqk,qhd->khd",
            weights_full.astype(jnp.bfloat16),
            grad_att,
            preferred_element_type=jnp.float32,
        )
        grad_key = (
            jnp.einsum("hqk,qhd->khd", grad_scores, queries, preferred_element_type=jnp.float32)
            * score_scale
        )
        return (partial_value, (grad_key, grad_value))

    def whole_slot(ignored):
        grad_query, key_parts = lax.scan(
            grad_step, jnp.zeros((seg_rows, head_count, head_dim), jnp.float32), blocks
        )
        return (
            grad_query,
            key_parts[0].reshape(slot_keys.shape),
            key_parts[1].reshape(slot_keys.shape),
        )

    return whole_slot(0)


def plain_layer(
    frames,
    lengths,
    cotangent,
    ln1_gain,
    ln1_bias,
    w_query,
    b_query,
    w_key,
    w_value,
    b_value,
    w_out,
    b_out,
    ln2_gain,
    ln2_bias,
    w_up,
    b_up,
    w_down,
    b_down,
):
    slot_count, seg_rows, model_width = frames.shape
    row_count = slot_count * seg_rows
    head_cols = w_query.shape[1]
    head_count = head_cols // HD
    seq_length = seg_rows * lax.axis_size("ctx")
    seg_start = lax.axis_index("ctx") * seg_rows
    score_scale = HD ** (-0.5)
    key_block = math.gcd(seq_length, 512)
    positions = seg_start + jnp.arange(seg_rows, dtype=jnp.int32)
    query_live = positions[None, :] < lengths[:, None]
    key_live = jnp.arange(seq_length, dtype=jnp.int32)[None, :] < lengths[:, None]
    live_rows = query_live.astype(jnp.float32).reshape(row_count, 1)
    weight_query, weight_key, weight_value, weight_out = (
        lax.all_gather(w_query, ("shard", "ctx"), axis=0, tiled=True),
        lax.all_gather(w_key, ("shard", "ctx"), axis=0, tiled=True),
        lax.all_gather(w_value, ("shard", "ctx"), axis=0, tiled=True),
        lax.all_gather(w_out, ("shard", "ctx"), axis=1, tiled=True),
    )
    frames_flat = frames.astype(jnp.float32).reshape(row_count, model_width)
    first, normed_one, inverse_one = norm_rows(frames_flat, ln1_gain, ln1_bias)
    first_low = first.astype(jnp.bfloat16)
    queries = (
        jnp.dot(first_low, weight_query, preferred_element_type=jnp.float32) + b_query
    ).astype(jnp.bfloat16)
    keys_local = jnp.dot(first_low, weight_key, preferred_element_type=jnp.float32).astype(
        jnp.bfloat16
    )
    values_local = (
        jnp.dot(first_low, weight_value, preferred_element_type=jnp.float32) + b_value
    ).astype(jnp.bfloat16)
    keys_all, values_all = (
        lax.all_gather(
            keys_local.reshape(slot_count, seg_rows, head_cols), "ctx", axis=1, tiled=True
        ),
        lax.all_gather(
            values_local.reshape(slot_count, seg_rows, head_cols), "ctx", axis=1, tiled=True
        ),
    )
    query_heads = queries.reshape(slot_count, seg_rows, head_count, HD)
    key_heads = keys_all.reshape(slot_count, seq_length, head_count, HD)
    value_heads = values_all.reshape(slot_count, seq_length, head_count, HD)
    slot = 0
    log_totals, attended_slot = slot_forward(
        query_heads[slot],
        key_heads[slot],
        value_heads[slot],
        query_live[slot],
        key_live[slot],
        key_block,
        score_scale,
    )
    totals_list = [log_totals]
    attended_list = [attended_slot]
    attended = jnp.stack(attended_list).reshape(row_count, head_cols)
    attended_low = attended.astype(jnp.bfloat16)
    attn_sum = lax.psum(
        jnp.dot(attended_low, weight_out, preferred_element_type=jnp.float32).astype(jnp.bfloat16),
        "tp",
    ).astype(jnp.float32)
    hidden = frames_flat + attn_sum + b_out
    weight_up, weight_down = (
        lax.all_gather(w_up, ("shard", "ctx"), axis=0, tiled=True),
        lax.all_gather(w_down, ("shard", "ctx"), axis=1, tiled=True),
    )
    second, normed_two, inverse_two = norm_rows(hidden, ln2_gain, ln2_bias)
    second_low = second.astype(jnp.bfloat16)
    upper = jnp.dot(second_low, weight_up, preferred_element_type=jnp.float32) + b_up
    activated = jax.nn.gelu(upper, approximate=False).astype(jnp.bfloat16)
    mlp_sum = lax.psum(
        jnp.dot(activated, weight_down, preferred_element_type=jnp.float32).astype(jnp.bfloat16),
        "tp",
    ).astype(jnp.float32)
    output = (
        (live_rows * (hidden + mlp_sum + b_down))
        .astype(jnp.bfloat16)
        .reshape(slot_count, seg_rows, model_width)
    )
    grad_out = live_rows * cotangent.astype(jnp.float32).reshape(row_count, model_width)
    grad_out_low = grad_out.astype(jnp.bfloat16)
    grad_b_down = jnp.sum(grad_out, axis=0)
    grad_w_down = jnp.einsum(
        "rf,rd->fd", activated, grad_out_low, preferred_element_type=jnp.float32
    )
    grad_act = jnp.einsum(
        "rd,fd->rf", grad_out_low, weight_down, preferred_element_type=jnp.float32
    )
    grad_upper = (grad_act * gelu_slope(upper)).astype(jnp.bfloat16)
    grad_b_up = jnp.sum(grad_upper.astype(jnp.float32), axis=0)
    grad_w_up = jnp.einsum("rd,rf->df", second_low, grad_upper, preferred_element_type=jnp.float32)
    grad_second = lax.psum(
        jnp.einsum("rf,df->rd", grad_upper, weight_up, preferred_element_type=jnp.float32).astype(
            jnp.bfloat16
        ),
        "tp",
    ).astype(jnp.float32)
    grad_norm_two, grad_ln2_gain, grad_ln2_bias = norm_back(
        grad_second, normed_two, inverse_two, ln2_gain
    )
    grad_hidden = grad_out + grad_norm_two
    grad_hidden_low = grad_hidden.astype(jnp.bfloat16)
    grad_b_out = jnp.sum(grad_hidden_low.astype(jnp.float32), axis=0)
    grad_w_out = jnp.einsum(
        "rc,rd->cd", attended_low, grad_hidden_low, preferred_element_type=jnp.float32
    )
    grad_att = jnp.einsum(
        "rd,cd->rc", grad_hidden_low, weight_out, preferred_element_type=jnp.float32
    ).astype(jnp.bfloat16)
    delta = jnp.sum(
        (grad_att.astype(jnp.float32) * attended).reshape(row_count, head_count, HD), axis=-1
    )
    delta_heads = delta.reshape(slot_count, seg_rows, head_count)
    grad_att_heads = grad_att.reshape(slot_count, seg_rows, head_count, HD)
    slot = 0
    grad_query_slot, key_part, value_part = slot_back(
        query_heads[slot],
        grad_att_heads[slot],
        totals_list[slot],
        delta_heads[slot].T,
        key_heads[slot],
        value_heads[slot],
        query_live[slot],
        key_live[slot],
        key_block,
        score_scale,
    )
    grad_query_list = [grad_query_slot]
    key_part_list = [key_part.reshape(seq_length, head_cols)]
    value_part_list = [value_part.reshape(seq_length, head_cols)]
    grad_keys, grad_values = (
        lax.psum_scatter(
            jnp.stack(key_part_list).astype(jnp.bfloat16), "ctx", scatter_dimension=1, tiled=True
        ).astype(jnp.float32),
        lax.psum_scatter(
            jnp.stack(value_part_list).astype(jnp.bfloat16), "ctx", scatter_dimension=1, tiled=True
        ).astype(jnp.float32),
    )
    grad_query_low = jnp.stack(grad_query_list).reshape(row_count, head_cols).astype(jnp.bfloat16)
    grad_key_low = grad_keys.reshape(row_count, head_cols).astype(jnp.bfloat16)
    grad_value_low = grad_values.reshape(row_count, head_cols).astype(jnp.bfloat16)
    grad_b_query = jnp.sum(grad_query_low.astype(jnp.float32), axis=0)
    grad_b_value = jnp.sum(grad_value_low.astype(jnp.float32), axis=0)
    grad_w_query = jnp.einsum(
        "rd,rc->dc", first_low, grad_query_low, preferred_element_type=jnp.float32
    )
    grad_w_key = jnp.einsum(
        "rd,rc->dc", first_low, grad_key_low, preferred_element_type=jnp.float32
    )
    grad_w_value = jnp.einsum(
        "rd,rc->dc", first_low, grad_value_low, preferred_element_type=jnp.float32
    )
    first_terms = jnp.einsum(
        "rc,dc->rd", grad_query_low, weight_query, preferred_element_type=jnp.float32
    )
    first_terms = first_terms + jnp.einsum(
        "rc,dc->rd", grad_key_low, weight_key, preferred_element_type=jnp.float32
    )
    first_terms = first_terms + jnp.einsum(
        "rc,dc->rd", grad_value_low, weight_value, preferred_element_type=jnp.float32
    )
    grad_first = lax.psum(first_terms.astype(jnp.bfloat16), "tp").astype(jnp.float32)
    grad_norm_one, grad_ln1_gain, grad_ln1_bias = norm_back(
        grad_first, normed_one, inverse_one, ln1_gain
    )
    grad_input = (grad_hidden + grad_norm_one).reshape(slot_count, seg_rows, model_width)
    shard_grads = (
        lax.psum_scatter(grad_w_query, ("shard", "ctx"), scatter_dimension=0, tiled=True),
        lax.psum_scatter(grad_w_key, ("shard", "ctx"), scatter_dimension=0, tiled=True),
        lax.psum_scatter(grad_w_value, ("shard", "ctx"), scatter_dimension=0, tiled=True),
        lax.psum_scatter(grad_w_out, ("shard", "ctx"), scatter_dimension=1, tiled=True),
        lax.psum_scatter(grad_w_up, ("shard", "ctx"), scatter_dimension=0, tiled=True),
        lax.psum_scatter(grad_w_down, ("shard", "ctx"), scatter_dimension=1, tiled=True),
    )
    small_sums = lax.psum(
        (
            grad_ln1_gain,
            grad_ln1_bias,
            grad_b_query,
            grad_b_value,
            grad_b_out,
            grad_ln2_gain,
            grad_ln2_bias,
            grad_b_up,
            grad_b_down,
        ),
        ("shard", "ctx"),
    )
    return (
        output,
        grad_input,
        small_sums[0],
        small_sums[1],
        shard_grads[0],
        small_sums[2],
        shard_grads[1],
        shard_grads[2],
        small_sums[3],
        shard_grads[3],
        small_sums[4],
        small_sums[5],
        small_sums[6],
        shard_grads[4],
        small_sums[7],
        shard_grads[5],
        small_sums[8],
    )


MESH = pl.DeviceIdType.MESH
F32 = jnp.float32
BF16 = jnp.bfloat16
NEG = -1e30
LIVE_LANE = 192


def nn(left, right):
    return jnp.dot(left, right, preferred_element_type=F32)


def nt(left, right):
    return lax.dot_general(left, right, (((1,), (1,)), ((), ())), preferred_element_type=F32)


def flip(values):
    return values.astype(F32).T.astype(BF16)


def layer_kernel(
    dims,
    frames,
    cot,
    lengths,
    vecs,
    b_up,
    wqkv_own,
    bias_own,
    wf_own,
    out_o,
    gin_o,
    gf_o,
    go_o,
    gq_o,
    sums_o,
    ss,
    rs,
    ls,
    a_all,
    a_t,
    wqkv,
    bias_all,
    wf,
    wo_sib,
    k_tr,
    v_tr,
    k_n,
    v_n,
    q_n,
    q_t,
    lse,
    att_f,
    att_s,
    att_r,
    hid,
    z_all,
    z_t,
    g_n,
    g_t,
    act,
    gup,
    part_s,
    part_r,
    gz_s,
    gz_r,
    ghl_t,
    gatt_r,
    gatt_t,
    wg,
    wg_r,
    wg_zr,
    og_x,
    og_r,
    og_z,
    og_zr,
    dk_t,
    dv_t,
    dq_f,
    dkv_s,
    dkv_r,
    g_nat,
    ga_s,
    ga_r,
    qg,
    qg_r,
    qg_p,
    qg_z,
    qg_zr,
    sums,
    sum_p,
    sum_z,
    sum_c,
):
    S, C, R, D, GP, HG, FH = dims
    HF = R // 2
    CH = C // 2
    DB = D // (S * C)
    PB = C * DB
    s, z, c = lax.axis_index("shard"), lax.axis_index("ctx"), lax.axis_index("tp")
    o = 1 - c
    sib = (s, z, o)
    owed = []
    next_sem = [0]

    def sems(count):
        base = next_sem[0]
        next_sem[0] = base + count
        return base

    def remote(src, dst, index, device):
        return pltpu.make_async_remote_copy(
            src_ref=src,
            dst_ref=dst,
            send_sem=ss.at[index],
            recv_sem=rs.at[index],
            device_id=device,
            device_id_type=MESH,
        )

    def send(src, dst, index, device, when=None):
        def go():
            remote(src, dst, index, device).start()

        if when is None:
            go()
        else:
            pl.when(when)(go)
        owed.append((src, dst, index, device, when))

    def arrive(dst, index, when=None):
        def go():
            remote(dst, dst, index, sib).wait_recv()

        if when is None:
            go()
        else:
            pl.when(when)(go)

    def plane(k):
        return (lax.rem(s + k, S), z, c)

    def column(k):
        return (s, lax.rem(z + k, C), c)

    def s_from(k):
        return lax.rem(s + S - k, S)

    def z_from(k):
        return lax.rem(z + C - k, C)

    def rows_of(block):
        return pl.ds(pl.multiple_of(block * DB, 16), DB)

    def half_rows(block, half):
        return pl.ds(pl.multiple_of(block * R + half * HF, HF), HF)

    def blk(block):
        return pl.ds(pl.multiple_of(block * HF, HF), HF)

    k_bias = sems(1)
    k_q1 = sems(CH)
    k_q2 = sems(S)
    k_q3 = sems(1)
    k_a = sems(2 * C)
    k_as = sems(2 * C)
    k_f = sems(2 * C)
    k_fp0 = sems(S)
    k_fp = sems(2 * C * S)
    k_wo = sems(1)
    k_att = sems(C)
    k_n2 = sems(1)
    k_part = sems(1)
    k_gz = sems(1)
    k_out = sems(1)
    k_gatt = sems(C)
    k_wg = sems(S)
    k_wgz = sems(C)
    k_ox = sems(1)
    k_og = sems(S)
    k_ogz = sems(C)
    k_dkv = sems(1)
    k_ga = sems(C)
    k_qx = sems(1)
    k_qp = sems(S)
    k_qz = sems(CH)
    k_gin = sems(1)
    k_sp = sems(S)
    k_sz = sems(C)
    k_sc = sems(1)

    barrier = pltpu.get_barrier_semaphore()
    friends = [sib]
    friends += [plane(k) for k in range(1, S)]
    for k in range(1, C):
        friends += [(s, lax.rem(z + k, C), c), (s, lax.rem(z + k, C), o)]
    for friend in friends:
        pl.semaphore_signal(barrier, inc=1, device_id=friend, device_id_type=MESH)

    length = lengths[0]
    lane = lax.broadcasted_iota(jnp.int32, (HF, GP), 1)

    def head_lanes(count, h):
        at = lax.broadcasted_iota(jnp.int32, (count, GP), 1)
        return jnp.logical_and(at >= HD * h, at < HD * (h + 1))

    def only_head(values, h, keep_live=False):
        picked = head_lanes(values.shape[0], h)
        if keep_live:
            at = lax.broadcasted_iota(jnp.int32, values.shape, 1)
            picked = jnp.logical_or(picked, at == LIVE_LANE)
        return jnp.where(picked, values, jnp.zeros_like(values))

    ln1_gain, ln1_bias, b_out, ln2_gain, ln2_bias, b_down = (
        vecs[i : i + 1, :] for i in range(6)
    )

    def norm(values):
        centred = values - jnp.mean(values, axis=-1, keepdims=True)
        inverse = lax.rsqrt(jnp.mean(centred * centred, axis=-1, keepdims=True) + EPSILON)
        return centred * inverse, inverse

    def live_of(first, count):
        at = z * R + first + lax.broadcasted_iota(jnp.int32, (count, 1), 0)
        return (at < length).astype(F32)

    def first_norm(i, carry):
        at = pl.ds(pl.multiple_of(i * 64, 64), 64)
        to = pl.ds(pl.multiple_of(z * R + i * 64, 64), 64)
        normed, unused = norm(frames[at, :].astype(F32))
        a_all[to, :] = (normed * ln1_gain + ln1_bias).astype(BF16)
        g_n[at, :] = (cot[at, :].astype(F32) * live_of(i * 64, 64)).astype(BF16)
        return carry

    lax.fori_loop(0, R // 64, first_norm, 0)
    sums[...] = jnp.zeros_like(sums)
    pl.semaphore_wait(barrier, len(friends))

    c_of_z = z // CH
    for j in range(CH):
        to_z = CH * c + j
        same = jnp.logical_and(to_z == z, c_of_z == c)
        for i in range(CH):
            ok = jnp.logical_and(z - CH * c_of_z == i, jnp.logical_not(same))
            here = wqkv.at[s, c_of_z, pl.ds(i * DB, DB), :]

            def go(i=i, here=here, j=j, to_z=to_z):
                pltpu.make_async_remote_copy(
                    src_ref=wqkv_own.at[j],
                    dst_ref=here,
                    send_sem=ls.at[j],
                    recv_sem=rs.at[k_q1 + i],
                    device_id=(s, to_z, c_of_z),
                    device_id_type=MESH,
                ).start()

            pl.when(ok)(go)

        def keep(j=j):
            wqkv[s, c, pl.ds(pl.multiple_of((z - CH * c) * DB, 16), DB), :] = wqkv_own[j]

        pl.when(same)(keep)
    send(bias_own, bias_all.at[c], k_bias, sib)
    bias_all[c] = bias_own[...]
    mine_rows = rows_of(s * C + z)
    for k in range(1, S):
        send(wf_own, wf.at[mine_rows, :], k_fp0 + k, plane(k))
    can_right, can_left = z + 1 < C, z >= 1

    def a_step(t):
        send(
            a_all.at[half_rows(jnp.maximum(z - t, 0), c), :],
            a_all.at[half_rows(jnp.maximum(z - t, 0), c), :],
            k_a + 2 * t,
            (s, jnp.minimum(z + 1, C - 1), c),
            jnp.logical_and(can_right, z - t >= 0),
        )
        send(
            a_all.at[half_rows(jnp.minimum(z + t, C - 1), c), :],
            a_all.at[half_rows(jnp.minimum(z + t, C - 1), c), :],
            k_a + 2 * t + 1,
            (s, jnp.maximum(z - 1, 0), c),
            jnp.logical_and(can_left, z + t < C),
        )

    a_step(0)
    wf[mine_rows, :] = wf_own[...]
    key_at = lax.broadcasted_iota(jnp.int32, (GP - LIVE_LANE, C * R), 1)
    first_row = lax.broadcasted_iota(jnp.int32, (GP - LIVE_LANE, C * R), 0) == 0
    dead = jnp.where(jnp.logical_and(first_row, key_at >= length), NEG, 0.0)
    k_tr[LIVE_LANE:, :] = dead.astype(BF16)
    v_tr[LIVE_LANE:, :] = jnp.zeros((GP - LIVE_LANE, C * R), BF16)
    for i in range(CH):
        from_z = CH * c + i
        same = jnp.logical_and(from_z == z, c_of_z == c)
        arrive(wqkv.at[s, c, pl.ds(i * DB, DB), :], k_q1 + i, jnp.logical_not(same))
    for k in range(1, S):
        send(wqkv.at[s, c], wqkv.at[s, c], k_q2 + k, plane(k))
    for k in range(1, S):
        arrive(wqkv.at[s_from(k), c], k_q2 + k)
    send(wqkv.at[:, c], wqkv.at[:, c], k_q3, sib)
    arrive(bias_all.at[o], k_bias)
    arrive(wqkv.at[:, o], k_q3)
    bias_z = bias_all[c_of_z, z - CH * c_of_z]

    def project(block, half, own):
        at = half_rows(block, half)
        rows = a_all[at, :]
        width = 3 * GP if own else 2 * GP
        weights = wqkv[:, :, :, :width].reshape(D, width)
        made = nn(rows, weights) + bias_z[0:1, :width]
        keys = made[:, :GP].astype(BF16)
        values = made[:, GP : 2 * GP].astype(BF16)
        k_n[at, :] = keys
        v_n[at, :] = values
        k_tr[:LIVE_LANE, at] = flip(keys)[:LIVE_LANE, :]
        v_tr[:LIVE_LANE, at] = flip(values)[:LIVE_LANE, :]
        if own:
            queries = made[:, 2 * GP :].astype(BF16).astype(F32) * (HD**-0.5)
            queries = jnp.where(lane == LIVE_LANE, 1.0, queries).astype(BF16)
            q_n[blk(block), :] = queries
            q_t[:, blk(block)] = flip(queries)
            a_t[:, blk(block)] = flip(rows)

    project(z, c, True)
    project(z, o, False)
    g_t[:, :HF] = flip(g_n[:HF, :])
    g_t[:, HF:] = flip(g_n[HF:, :])

    def f_step(t):
        send(
            wf.at[rows_of(s * C + jnp.maximum(z - t, 0)), :],
            wf.at[rows_of(s * C + jnp.maximum(z - t, 0)), :],
            k_f + 2 * t,
            (s, jnp.minimum(z + 1, C - 1), c),
            jnp.logical_and(can_right, z - t >= 0),
        )
        send(
            wf.at[rows_of(s * C + jnp.minimum(z + t, C - 1)), :],
            wf.at[rows_of(s * C + jnp.minimum(z + t, C - 1)), :],
            k_f + 2 * t + 1,
            (s, jnp.maximum(z - 1, 0), c),
            jnp.logical_and(can_left, z + t < C),
        )

    def from_left(t):
        return jnp.maximum(z - 1 - t, 0), z - 1 - t >= 0

    def from_right(t):
        return jnp.minimum(z + 1 + t, C - 1), z + 1 + t < C

    def f_arrive(t):
        for side, (block, ok) in enumerate((from_left(t), from_right(t))):
            arrive(wf.at[rows_of(s * C + block), :], k_f + 2 * t + side, ok)
        if t + 1 < C - 1:
            f_step(t + 1)
        for side, (block, ok) in enumerate((from_left(t), from_right(t))):
            for k in range(1, S):
                send(
                    wf.at[rows_of(s * C + block), :],
                    wf.at[rows_of(s * C + block), :],
                    k_fp + (2 * t + side) * S + k,
                    plane(k),
                    ok,
                )

    for t in range(C - 1):
        sides = (from_left(t), from_right(t))
        for side, (block, ok) in enumerate(sides):
            arrive(a_all.at[half_rows(block, c), :], k_a + 2 * t + side, ok)
        if t + 1 < C - 1:
            a_step(t + 1)
        for side, (block, ok) in enumerate(sides):
            send(
                a_all.at[half_rows(block, c), :],
                a_all.at[half_rows(block, c), :],
                k_as + 2 * t + side,
                sib,
                ok,
            )
        if t == C - 3:
            f_step(0)
        for side, (block, ok) in enumerate(sides):

            def come(block=block, t=t, side=side):
                project(block, c, True)
                remote(
                    a_all.at[half_rows(block, o), :],
                    a_all.at[half_rows(block, o), :],
                    k_as + 2 * t + side,
                    sib,
                ).wait_recv()
                project(block, o, False)

            pl.when(ok)(come)

    TQ = 128

    def attend(block):
        def step(i, carry):
            at = pl.ds(pl.multiple_of(block * HF + i * TQ, TQ), TQ)
            queries = q_n[at, :]
            total = jnp.zeros((TQ, GP), F32)
            for h in range(HG):
                scores = nn(only_head(queries, h, True), k_tr[...])
                top = jnp.max(scores, axis=-1, keepdims=True)
                weights = jnp.exp(scores - top)
                norm_sum = jnp.sum(weights, axis=-1, keepdims=True)
                got = nn(weights.astype(BF16), v_n[...]) * (1.0 / norm_sum)
                total = total + only_head(got, h)
                lse[at, h : h + 1] = top + jnp.log(norm_sum)
            att_f[at, :] = total
            att_s[at, :] = total.astype(BF16)
            return carry

        lax.fori_loop(0, HF // TQ, step, 0)

    for k in range(1, C):
        block = lax.rem(z + k, C)
        attend(block)
        remote(att_s.at[blk(block), :], att_r.at[blk(z), :], k_att + k, column(k)).start()
        f_arrive(k - 1)
    attend(z)
    att_r[blk(z), :] = att_s[blk(z), :]

    for k in range(1, S):
        arrive(wf.at[rows_of(s_from(k) * C + z), :], k_fp0 + k)
        for t in range(C - 1):
            for side, (block, ok) in enumerate((from_left(t), from_right(t))):
                arrive(
                    wf.at[rows_of(s_from(k) * C + block), :], k_fp + (2 * t + side) * S + k, ok
                )
    wo_cols = slice(2 * FH, 2 * FH + CH * GP)
    send(wf.at[:, wo_cols], wo_sib, k_wo, sib)
    for k in range(1, C):
        arrive(att_r.at[blk(z_from(k)), :], k_att + k)
        remote(att_s.at[blk(z), :], att_r.at[blk(z), :], k_att + k, column(k)).wait_send()
    arrive(wo_sib, k_wo)

    own_rows = pl.ds(pl.multiple_of(c * HF, HF), HF)
    hidden = frames[own_rows, :].astype(F32) + b_out
    for j in range(CH):
        hidden = hidden + nt(
            att_r[blk(CH * c + j), :], wf[:, 2 * FH + j * GP : 2 * FH + (j + 1) * GP]
        )
        hidden = hidden + nt(att_r[blk(CH * o + j), :], wo_sib[:, j * GP : (j + 1) * GP])
    hid[...] = hidden
    normed, unused = norm(hidden)
    z_all[own_rows, :] = (normed * ln2_gain + ln2_bias).astype(BF16)
    send(z_all.at[own_rows, :], z_all.at[own_rows, :], k_n2, sib)
    other_rows = pl.ds(pl.multiple_of(o * HF, HF), HF)
    z_t[:, own_rows] = flip(z_all[own_rows, :])
    arrive(z_all.at[other_rows, :], k_n2)
    z_t[:, other_rows] = flip(z_all[other_rows, :])

    TF = 256

    def units(i, carry):
        cols = pl.ds(pl.multiple_of(i * TF, TF), TF)
        down = pl.ds(pl.multiple_of(FH + i * TF, TF), TF)
        upper = nn(z_all[...], wf[:, cols]) + b_up[:, cols]
        cumulative = 0.5 * (1.0 + lax.erf(upper * INV_ROOT_TWO))
        act[:, cols] = (upper * cumulative).astype(BF16)
        slope = cumulative + upper * jnp.exp(-0.5 * upper * upper) * INV_ROOT_TAU
        grad_units = (nn(g_n[...], wf[:, down]) * slope).astype(BF16)
        gup[:, cols] = grad_units
        return carry

    lax.fori_loop(0, FH // TF, units, 0)

    def z_grad(i, carry):
        at = pl.ds(pl.multiple_of(i * 256, 256), 256)
        gz_s[:, at] = nt(gup[other_rows, :], wf[at, :FH]).astype(BF16)
        return carry

    lax.fori_loop(0, D // 256, z_grad, 0)
    send(gz_s, gz_r, k_gz, sib)

    def down_part(i, carry):
        at = pl.ds(pl.multiple_of(i * 256, 256), 256)
        part_s[:, at] = nt(act[other_rows, :], wf[at, FH : 2 * FH]).astype(BF16)
        return carry

    lax.fori_loop(0, D // 256, down_part, 0)
    send(part_s, part_r, k_part, sib)

    def unit_grads(k):
        at = pl.ds(pl.multiple_of(lax.rem(s + k, S) * PB, 64), PB)

        def step(i, carry):
            cols = pl.ds(pl.multiple_of(i * TF, TF), TF)
            down = pl.ds(pl.multiple_of(FH + i * TF, TF), TF)
            wg[at, cols] = nn(z_t[at, :], gup[:, cols]).astype(BF16)
            wg[at, down] = nn(g_t[at, :], act[:, cols]).astype(BF16)
            return carry

        lax.fori_loop(0, FH // TF, step, 0)

    for k in range(1, S):
        unit_grads(k)
        at = pl.ds(pl.multiple_of(lax.rem(s + k, S) * PB, 64), PB)
        send(wg.at[at, :], wg_r.at[k - 1], k_wg + k, plane(k))

    gz_rows = jnp.concatenate(
        [nt(gup[own_rows, :], wf[i * 256 : (i + 1) * 256, :FH]) for i in range(D // 256)], axis=1
    )
    down_rows = jnp.concatenate(
        [nt(act[own_rows, :], wf[i * 256 : (i + 1) * 256, FH : 2 * FH]) for i in range(D // 256)],
        axis=1,
    )
    arrive(gz_r, k_gz)
    grad_z = gz_rows + gz_r[...].astype(F32)
    live_own = live_of(c * HF, HF)
    normed, inverse = norm(hid[...])
    scaled = grad_z * ln2_gain
    inner = (
        scaled
        - jnp.mean(scaled, axis=-1, keepdims=True)
        - normed * jnp.mean(scaled * normed, axis=-1, keepdims=True)
    )
    g_own = g_n[own_rows, :].astype(F32)
    grad_hidden = g_own + inner * inverse
    gin_o[own_rows, :] = grad_hidden
    low = grad_hidden.astype(BF16)
    sums[3:4, :] = jnp.sum(grad_z * normed, axis=0, keepdims=True)
    sums[4:5, :] = jnp.sum(grad_z, axis=0, keepdims=True)
    sums[5:6, :] = jnp.sum(g_own, axis=0, keepdims=True)
    sums[2:3, :] = jnp.sum(low.astype(F32), axis=0, keepdims=True)
    for j in range(CH):
        att_s[blk(CH * c + j), :] = nn(
            low, wf[:, 2 * FH + j * GP : 2 * FH + (j + 1) * GP]
        ).astype(BF16)
        att_s[blk(CH * o + j), :] = nn(low, wo_sib[:, j * GP : (j + 1) * GP]).astype(BF16)
    for k in range(1, C):
        send(att_s.at[blk(lax.rem(z + k, C)), :], gatt_r.at[blk(z), :], k_gatt + k, column(k))
    gatt_r[blk(z), :] = att_s[blk(z), :]
    ghl_t[...] = flip(low)
    for j in range(CH):
        og_x[0, :, j * GP : (j + 1) * GP] = nn(ghl_t[...], att_r[blk(CH * o + j), :]).astype(BF16)
    remote(og_x.at[0], og_x.at[1], k_ox, sib).start()
    arrive(part_r, k_part)
    out_rows = live_own * (hid[...] + down_rows + part_r[...].astype(F32) + b_down)
    out_o[own_rows, :] = out_rows.astype(BF16)
    send(out_o.at[own_rows, :], out_o.at[own_rows, :], k_out, sib)
    unit_grads(0)
    for i in range(2):
        sums[pl.ds(6 + 2 * c + i, 1), :] = jnp.sum(
            gup[:, i * D : (i + 1) * D].astype(F32), axis=0, keepdims=True
        )
    arrive(og_x.at[1], k_ox)
    remote(og_x.at[0], og_x.at[1], k_ox, sib).wait_send()
    for j in range(CH):
        cols = slice(j * GP, (j + 1) * GP)
        own_part = nn(ghl_t[...], att_r[blk(CH * c + j), :])
        og_x[0, :, cols] = (own_part + og_x[1, :, cols].astype(F32)).astype(BF16)
    for k in range(1, S):
        at = pl.ds(pl.multiple_of(lax.rem(s + k, S) * PB, 64), PB)
        send(og_x.at[0, at, :], og_r.at[k - 1], k_og + k, plane(k))

    dk_t[...] = jnp.zeros_like(dk_t)
    dv_t[...] = jnp.zeros_like(dv_t)
    TK = 512

    def attend_back(block):
        at = blk(block)
        gatt_t[...] = flip(gatt_r[at, :])
        product = gatt_r[at, :].astype(F32) * att_f[at, :]
        deltas = []
        for h in range(HG):
            deltas.append(jnp.sum(only_head(product, h), axis=-1, keepdims=True))
        dq_f[...] = jnp.zeros_like(dq_f)

        def step(i, carry):
            keys = pl.ds(pl.multiple_of(i * TK, TK), TK)
            for h in range(HG):
                head = slice(HD * h, HD * (h + 1))
                scores = nn(only_head(q_n[at, :], h, True), k_tr[:, keys])
                weights = jnp.exp(scores - lse[at, h : h + 1])
                grads = nn(only_head(gatt_r[at, :], h), v_tr[:, keys])
                grad_scores = (weights * (grads - deltas[h])).astype(BF16)
                dv_t[head, keys] += nn(gatt_t[head, :], weights.astype(BF16))
                dk_t[head, keys] += nn(q_t[head, at], grad_scores)
                dq_f[...] += only_head(nn(grad_scores, k_n[keys, :]), h)
            return carry

        lax.fori_loop(0, C * R // TK, step, 0)
        g_nat[at, 2 * GP :] = (dq_f[...] * (HD**-0.5)).astype(BF16)

    def wg_reduce():
        for k in range(1, S):
            arrive(wg_r.at[k - 1], k_wg + k)
        for j in range(C):
            part = pl.ds(j * DB, DB)
            own = pl.ds(pl.multiple_of(s * PB + j * DB, 16), DB)

            def step(i, carry):
                cols = pl.ds(pl.multiple_of(i * 512, 512), 512)
                total = wg[own, cols].astype(F32)
                for k in range(1, S):
                    total = total + wg_r[k - 1, part, cols].astype(F32)
                wg[own, cols] = total.astype(BF16)
                return carry

            lax.fori_loop(0, 2 * FH // 512, step, 0)
        for k in range(1, C):
            at = pl.ds(pl.multiple_of(s * PB + lax.rem(z + k, C) * DB, 16), DB)
            send(wg.at[at, :], wg_zr.at[k - 1], k_wgz + k, column(k))

    def og_reduce():
        for k in range(1, S):
            arrive(og_r.at[k - 1], k_og + k)
        own = pl.ds(pl.multiple_of(s * PB, 64), PB)
        total = og_x[0, own, :].astype(F32)
        for k in range(1, S):
            total = total + og_r[k - 1].astype(F32)
        og_z[...] = total.astype(BF16)
        for k in range(1, C):
            at = pl.ds(pl.multiple_of(lax.rem(z + k, C) * DB, 16), DB)
            send(og_z.at[at, :], og_zr.at[k - 1], k_ogz + k, column(k))

    attend_back(z)
    for k in range(1, C):
        arrive(gatt_r.at[blk(z_from(k)), :], k_gatt + k)
    attend_back(z_from(1))
    for k in range(2, C):
        attend_back(z_from(k))

    for i in range(C):
        cols = pl.ds(pl.multiple_of(i * R + o * HF, HF), HF)
        dkv_s[i, 0] = dk_t[:, cols].astype(BF16)
        dkv_s[i, 1] = dv_t[:, cols].astype(BF16)
    send(dkv_s, dkv_r, k_dkv, sib)
    wg_reduce()
    arrive(dkv_r, k_dkv)

    def finish(block):
        cols = pl.ds(pl.multiple_of(block * R + c * HF, HF), HF)
        at = blk(block)
        keys_t = dk_t[:, cols] + dkv_r[block, 0].astype(F32)
        values_t = dv_t[:, cols] + dkv_r[block, 1].astype(F32)
        none = jnp.zeros((GP - LIVE_LANE, HF), F32)
        g_nat[at, :GP] = jnp.concatenate([keys_t, none], axis=0).T.astype(BF16)
        g_nat[at, GP : 2 * GP] = jnp.concatenate([values_t, none], axis=0).T.astype(BF16)
        ga_s[at, :] = nt(g_nat[at, :], wqkv[...].reshape(D, 3 * GP)).astype(BF16)

    for k in range(1, C):
        block = lax.rem(z + k, C)
        finish(block)
        send(ga_s.at[blk(block), :], ga_r.at[k - 1], k_ga + k, column(k))
    finish(z)
    og_reduce()

    for i in range(S):
        got = nn(a_t[i * PB : (i + 1) * PB, :], g_nat[...])
        qg[i] = got.reshape(2, CH * DB, 3 * GP).astype(BF16)
    send(qg.at[:, o], qg_r, k_qx, sib)
    sums[pl.ds(10 + z, 1), :] = jnp.sum(g_nat[...].astype(F32), axis=0, keepdims=True)
    arrive(qg_r, k_qx)
    for i in range(S):
        qg_r[i] = (qg_r[i].astype(F32) + qg[i, c].astype(F32)).astype(BF16)
    for k in range(1, S):
        send(qg_r.at[lax.rem(s + k, S)], qg_p.at[k - 1], k_qp + k, plane(k))

    own_block = blk(z)
    for k in range(1, C):
        arrive(ga_r.at[k - 1], k_ga + k)
    grad_a = ga_s[own_block, :].astype(F32)
    for k in range(1, C):
        grad_a = grad_a + ga_r[k - 1].astype(F32)
    normed, inverse = norm(frames[own_rows, :].astype(F32))
    scaled = grad_a * ln1_gain
    inner = (
        scaled
        - jnp.mean(scaled, axis=-1, keepdims=True)
        - normed * jnp.mean(scaled * normed, axis=-1, keepdims=True)
    )
    sums[0:1, :] = jnp.sum(grad_a * normed, axis=0, keepdims=True)
    sums[1:2, :] = jnp.sum(grad_a, axis=0, keepdims=True)
    gin_o[own_rows, :] = gin_o[own_rows, :] + inner * inverse
    send(gin_o.at[own_rows, :], gin_o.at[own_rows, :], k_gin, sib)
    sum_p[s] = sums[...]
    for k in range(1, S):
        send(sum_p.at[s], sum_p.at[s], k_sp + k, plane(k))

    for k in range(1, S):
        arrive(qg_p.at[k - 1], k_qp + k)
    total = qg_r[s].astype(F32)
    for k in range(1, S):
        total = total + qg_p[k - 1].astype(F32)
    qg_z[...] = total.reshape(CH, DB, 3 * GP).astype(BF16)
    for i in range(CH):
        to_z = CH * c + i
        same = jnp.logical_and(to_z == z, c_of_z == c)
        for j in range(CH):
            ok = jnp.logical_and(z - CH * c_of_z == j, jnp.logical_not(same))

            def go(i=i, j=j, to_z=to_z):
                pltpu.make_async_remote_copy(
                    src_ref=qg_z.at[i],
                    dst_ref=qg_zr.at[j],
                    send_sem=ls.at[CH + i],
                    recv_sem=rs.at[k_qz + j],
                    device_id=(s, to_z, c_of_z),
                    device_id_type=MESH,
                ).start()

            pl.when(ok)(go)

        def keep(i=i):
            qg_zr[z - CH * c] = qg_z[i]

        pl.when(same)(keep)

    for k in range(1, S):
        arrive(sum_p.at[s_from(k)], k_sp + k)
    total = sum_p[0]
    for k in range(1, S):
        total = total + sum_p[k]
    sum_z[z] = total
    for k in range(1, C):
        send(sum_z.at[z], sum_z.at[z], k_sz + k, column(k))

    def last(own, got, index, to):
        for k in range(1, C):
            arrive(got.at[k - 1], index + k)
        total = own.astype(F32)
        for k in range(1, C):
            total = total + got[k - 1].astype(F32)
        to[...] = total

    last(wg[rows_of(s * C + z), :], wg_zr, k_wgz, gf_o)
    last(og_z[pl.ds(pl.multiple_of(z * DB, 16), DB), :], og_zr, k_ogz, go_o)
    for k in range(1, C):
        arrive(sum_z.at[z_from(k)], k_sz + k)
    total = sum_z[0]
    for k in range(1, C):
        total = total + sum_z[k]
    sum_c[c] = total
    send(sum_c.at[c], sum_c.at[c], k_sc, sib)
    for j in range(CH):
        same = jnp.logical_and(CH * c + j == z, c_of_z == c)
        arrive(qg_zr.at[j], k_qz + j, jnp.logical_not(same))
    gq_o[...] = qg_zr[...].astype(F32)
    arrive(sum_c.at[o], k_sc)
    sums_o[...] = sum_c[0] + sum_c[1]
    arrive(out_o.at[other_rows, :], k_out)
    arrive(gin_o.at[other_rows, :], k_gin)

    for src, dst, index, device, when in owed:

        def done(src=src, dst=dst, index=index, device=device):
            remote(src, dst, index, device).wait_send()

        if when is None:
            done()
        else:
            pl.when(when)(done)
    for j in range(CH):
        same = jnp.logical_and(CH * c + j == z, c_of_z == c)

        def done_weights(j=j):
            pltpu.make_async_remote_copy(
                src_ref=wqkv_own.at[j],
                dst_ref=wqkv_own.at[j],
                send_sem=ls.at[j],
                recv_sem=rs.at[k_q1],
                device_id=sib,
                device_id_type=MESH,
            ).wait_send()
            pltpu.make_async_remote_copy(
                src_ref=qg_z.at[j],
                dst_ref=qg_z.at[j],
                send_sem=ls.at[CH + j],
                recv_sem=rs.at[k_qz],
                device_id=sib,
                device_id_type=MESH,
            ).wait_send()

        pl.when(jnp.logical_not(same))(done_weights)
    assert next_sem[0] <= SEMS


SEMS = 160


def fits(frames, w_query, w_up):
    shards, ctx, cores = (lax.axis_size(name) for name in ("shard", "ctx", "tp"))
    slot_count, seg_rows, width = frames.shape
    heads = w_query.shape[1] * cores // HD
    return (
        slot_count == 1
        and cores == 2
        and ctx % 2 == 0
        and ctx > 2
        and shards > 1
        and heads == 3 * ctx
        and width % (16 * shards * ctx) == 0
        and width % 256 == 0
        and seg_rows % 512 == 0
        and w_up.shape[1] % 512 == 0
        and w_up.shape[1] == 2 * width
        and ctx * seg_rows <= 2048
        and width <= 768
        and w_up.shape[1] <= 1536
    )


def fast_layer(
    frames,
    lengths,
    cotangent,
    ln1_gain,
    ln1_bias,
    w_query,
    b_query,
    w_key,
    w_value,
    b_value,
    w_out,
    b_out,
    ln2_gain,
    ln2_bias,
    w_up,
    b_up,
    w_down,
    b_down,
):
    S, C = lax.axis_size("shard"), lax.axis_size("ctx")
    unused, R, D = frames.shape
    FH = w_up.shape[1]
    HG, CH = 3, C // 2
    G, GP = HG * HD, 256
    DB = D // (S * C)
    HF = R // 2
    PB = C * DB
    T = C * R

    def grouped(array):
        parts = array.reshape(array.shape[:-1] + (CH, G))
        return jnp.pad(parts, [(0, 0)] * (parts.ndim - 1) + [(0, GP - G)])

    wqkv = jnp.concatenate([grouped(w_key), grouped(w_value), grouped(w_query)], axis=-1)
    wqkv = wqkv.transpose(1, 0, 2)
    bias = jnp.concatenate(
        [jnp.zeros((CH, GP), F32), grouped(b_value), grouped(b_query)], axis=-1
    )
    bias = jnp.broadcast_to(bias[:, None, :], (CH, 8, 3 * GP))
    wf = jnp.concatenate([w_up, w_down.T, grouped(w_out.T).reshape(DB, CH * GP)], axis=1)
    WF = wf.shape[1]
    vecs = jnp.stack([ln1_gain, ln1_bias, b_out, ln2_gain, ln2_bias, b_down, b_down, b_down])
    vmem = pl.BlockSpec(memory_space=pltpu.VMEM)
    V = pltpu.VMEM
    dims = (S, C, R, D, GP, HG, FH)
    scratch = [
        pltpu.SemaphoreType.DMA((SEMS,)),
        pltpu.SemaphoreType.DMA((SEMS,)),
        pltpu.SemaphoreType.DMA((2 * CH,)),
        V((T, D), BF16),
        V((D, C * HF), BF16),
        V((S, 2, CH * DB, 3 * GP), BF16),
        V((2, CH, 8, 3 * GP), F32),
        V((D, WF), BF16),
        V((D, CH * GP), BF16),
        V((GP, T), BF16),
        V((GP, T), BF16),
        V((T, GP), BF16),
        V((T, GP), BF16),
        V((C * HF, GP), BF16),
        V((GP, C * HF), BF16),
        V((C * HF, 8), F32),
        V((C * HF, GP), F32),
        V((C * HF, GP), BF16),
        V((C * HF, GP), BF16),
        V((HF, D), F32),
        V((R, D), BF16),
        V((D, R), BF16),
        V((R, D), BF16),
        V((D, R), BF16),
        V((R, FH), BF16),
        V((R, FH), BF16),
        V((HF, D), BF16),
        V((HF, D), BF16),
        V((HF, D), BF16),
        V((HF, D), BF16),
        V((D, HF), BF16),
        V((C * HF, GP), BF16),
        V((GP, HF), BF16),
        V((D, 2 * FH), BF16),
        V((S - 1, PB, 2 * FH), BF16),
        V((C - 1, DB, 2 * FH), BF16),
        V((2, D, CH * GP), BF16),
        V((S - 1, PB, CH * GP), BF16),
        V((PB, CH * GP), BF16),
        V((C - 1, DB, CH * GP), BF16),
        V((G, T), F32),
        V((G, T), F32),
        V((HF, GP), F32),
        V((C, 2, G, HF), BF16),
        V((C, 2, G, HF), BF16),
        V((C * HF, 3 * GP), BF16),
        V((C * HF, D), BF16),
        V((C - 1, HF, D), BF16),
        V((S, 2, CH * DB, 3 * GP), BF16),
        V((S, CH * DB, 3 * GP), BF16),
        V((S - 1, CH * DB, 3 * GP), BF16),
        V((CH, DB, 3 * GP), BF16),
        V((CH, DB, 3 * GP), BF16),
        V((16, D), F32),
        V((S, 16, D), F32),
        V((C, 16, D), F32),
        V((2, 16, D), F32),
    ]
    outs = (
        jax.ShapeDtypeStruct((R, D), BF16),
        jax.ShapeDtypeStruct((R, D), F32),
        jax.ShapeDtypeStruct((DB, 2 * FH), F32),
        jax.ShapeDtypeStruct((DB, CH * GP), F32),
        jax.ShapeDtypeStruct((CH, DB, 3 * GP), F32),
        jax.ShapeDtypeStruct((16, D), F32),
    )
    output, grad_input, gf, go, gq, sums = pl.pallas_call(
        functools.partial(layer_kernel, dims),
        out_shape=outs,
        in_specs=[vmem, vmem, pl.BlockSpec(memory_space=pltpu.SMEM)] + [vmem] * 5,
        out_specs=[vmem] * 6,
        scratch_shapes=scratch,
        compiler_params=pltpu.CompilerParams(
            collective_id=0, has_side_effects=True, vmem_limit_bytes=63 << 20
        ),
    )(frames[0], cotangent[0], lengths, vecs, b_up.reshape(1, FH), wqkv, bias, wf)
    c = lax.axis_index("tp")

    def ungroup(array, start):
        part = array[..., start : start + G]
        return part

    def heads_of(start):
        return gq[:, :, start : start + G].transpose(1, 0, 2).reshape(DB, CH * G)

    biases = lax.dynamic_slice_in_dim(sums, 10 + CH * c, CH, 0)
    grad_b_up = lax.dynamic_slice_in_dim(sums, 6 + 2 * c, 2, 0).reshape(FH)
    return (
        output[None],
        grad_input[None],
        sums[0],
        sums[1],
        heads_of(2 * GP),
        biases[:, 2 * GP : 2 * GP + G].reshape(CH * G),
        heads_of(0),
        heads_of(GP),
        biases[:, GP : GP + G].reshape(CH * G),
        go.reshape(DB, CH, GP)[:, :, :G].reshape(DB, CH * G).T,
        sums[2],
        sums[3],
        sums[4],
        gf[:, :FH],
        grad_b_up,
        gf[:, FH:].T,
        sums[5],
    )


def per_device(frames, lengths, cotangent, *params):
    if fits(frames, params[2], params[11]):
        return fast_layer(frames, lengths, cotangent, *params)
    return plain_layer(frames, lengths, cotangent, *params)


def solution(mesh):
    in_specs = (
        P("shard", "ctx", None),
        P("shard"),
        P("shard", "ctx", None),
        P(),
        P(),
        P(("shard", "ctx"), "tp"),
        P("tp"),
        P(("shard", "ctx"), "tp"),
        P(("shard", "ctx"), "tp"),
        P("tp"),
        P("tp", ("shard", "ctx")),
        P(),
        P(),
        P(),
        P(("shard", "ctx"), "tp"),
        P("tp"),
        P("tp", ("shard", "ctx")),
        P(),
    )
    out_specs = (
        P("shard", "ctx", None),
        P("shard", "ctx", None),
        P(),
        P(),
        P(("shard", "ctx"), "tp"),
        P("tp"),
        P(("shard", "ctx"), "tp"),
        P(("shard", "ctx"), "tp"),
        P("tp"),
        P("tp", ("shard", "ctx")),
        P(),
        P(),
        P(),
        P(("shard", "ctx"), "tp"),
        P("tp"),
        P("tp", ("shard", "ctx")),
        P(),
    )
    return jax.shard_map(
        per_device, mesh=mesh, in_specs=in_specs, out_specs=out_specs, check_vma=False
    )
```

```python
import functools
import math

import jax
import jax.numpy as jnp
from jax import lax
from jax.experimental import pallas as pl
from jax.experimental.pallas import tpu as pltpu
from jax.sharding import PartitionSpec as P

HD = 64


EPSILON = 1e-05
INV_ROOT_TWO = 0.7071067811865476
INV_ROOT_TAU = 0.3989422804014327


def norm_rows(values, gain, shift):
    centred = values - jnp.mean(values, axis=-1, keepdims=True)
    inverse = lax.rsqrt(jnp.mean(centred * centred, axis=-1, keepdims=True) + EPSILON)
    normed = centred * inverse
    return (normed * gain + shift, normed, inverse)


def norm_back(grad_rows, normed, inverse, gain):
    scaled = grad_rows * gain
    inner = (
        scaled
        - jnp.mean(scaled, axis=-1, keepdims=True)
        - normed * jnp.mean(scaled * normed, axis=-1, keepdims=True)
    )
    return (inner * inverse, jnp.sum(grad_rows * normed, axis=0), jnp.sum(grad_rows, axis=0))


def gelu_slope(values):
    return (
        0.5 * (1.0 + lax.erf(values * INV_ROOT_TWO))
        + values * jnp.exp(-0.5 * values * values) * INV_ROOT_TAU
    )


def pair_scores(queries, block_keys, score_scale):
    return (
        jnp.einsum("qhd,khd->hqk", queries, block_keys, preferred_element_type=jnp.float32)
        * score_scale
    )


def live_weights(scores, query_live, key_live, log_totals):
    both_live = query_live[None, :, None] & key_live[None, None, :]
    return jnp.where(both_live, jnp.exp(scores - log_totals[:, :, None]), 0.0)


def in_blocks(array, block_rows):
    return array.reshape((array.shape[0] // block_rows, block_rows) + array.shape[1:])


def slot_forward(queries, slot_keys, slot_values, query_live, key_live, key_block, score_scale):
    seg_rows, head_count, head_dim = queries.shape
    key_starts = jnp.arange(slot_keys.shape[0] // key_block, dtype=jnp.int32) * key_block
    blocks = (
        in_blocks(slot_keys, key_block),
        in_blocks(slot_values, key_block),
        in_blocks(key_live, key_block),
        key_starts,
    )
    start_state = (
        jnp.full((head_count, seg_rows), -jnp.inf, jnp.float32),
        jnp.zeros((head_count, seg_rows), jnp.float32),
    )

    def totals_step(carried, scan_item):
        block_keys, block_values, block_live, block_start = scan_item
        running_max, running_sum = carried
        scores = jnp.where(
            block_live[None, None, :], pair_scores(queries, block_keys, score_scale), -jnp.inf
        )
        new_max = jnp.maximum(running_max, jnp.max(scores, axis=-1))
        new_sum = running_sum * jnp.exp(running_max - new_max) + jnp.sum(
            jnp.exp(scores - new_max[:, :, None]), axis=-1
        )
        return ((new_max, new_sum), None)

    def whole_slot(ignored):
        final_state, unused = lax.scan(totals_step, start_state, blocks)
        log_totals = final_state[0] + jnp.log(final_state[1])

        def output_step(output_sum, scan_item):
            block_keys, block_values, block_live, block_start = scan_item
            weights_here = live_weights(
                pair_scores(queries, block_keys, score_scale), query_live, block_live, log_totals
            ).astype(jnp.bfloat16)
            return (
                output_sum
                + jnp.einsum(
                    "hqk,khd->qhd", weights_here, block_values, preferred_element_type=jnp.float32
                ),
                None,
            )

        attended, unused_too = lax.scan(
            output_step, jnp.zeros((seg_rows, head_count, head_dim), jnp.float32), blocks
        )
        return (log_totals, attended)

    return whole_slot(0)


def slot_back(
    queries,
    grad_att,
    log_totals,
    delta,
    slot_keys,
    slot_values,
    query_live,
    key_live,
    key_block,
    score_scale,
):
    seg_rows, head_count, head_dim = queries.shape
    key_starts = jnp.arange(slot_keys.shape[0] // key_block, dtype=jnp.int32) * key_block
    blocks = (
        in_blocks(slot_keys, key_block),
        in_blocks(slot_values, key_block),
        in_blocks(key_live, key_block),
        key_starts,
    )

    def grad_step(grad_query, scan_item):
        block_keys, block_values, block_live, block_start = scan_item
        partial_value = grad_query
        weights_full = live_weights(
            pair_scores(queries, block_keys, score_scale), query_live, block_live, log_totals
        )
        grad_probs = jnp.einsum(
            "qhd,khd->hqk", grad_att, block_values, preferred_element_type=jnp.float32
        )
        grad_scores = (weights_full * (grad_probs - delta[:, :, None])).astype(jnp.bfloat16)
        partial_value = (
            partial_value
            + jnp.einsum(
                "hqk,khd->qhd", grad_scores, block_keys, preferred_element_type=jnp.float32
            )
            * score_scale
        )
        grad_value = jnp.einsum(
            "hqk,qhd->khd",
            weights_full.astype(jnp.bfloat16),
            grad_att,
            preferred_element_type=jnp.float32,
        )
        grad_key = (
            jnp.einsum("hqk,qhd->khd", grad_scores, queries, preferred_element_type=jnp.float32)
            * score_scale
        )
        return (partial_value, (grad_key, grad_value))

    def whole_slot(ignored):
        grad_query, key_parts = lax.scan(
            grad_step, jnp.zeros((seg_rows, head_count, head_dim), jnp.float32), blocks
        )
        return (
            grad_query,
            key_parts[0].reshape(slot_keys.shape),
            key_parts[1].reshape(slot_keys.shape),
        )

    return whole_slot(0)


def plain_layer(
    frames,
    lengths,
    cotangent,
    ln1_gain,
    ln1_bias,
    w_query,
    b_query,
    w_key,
    w_value,
    b_value,
    w_out,
    b_out,
    ln2_gain,
    ln2_bias,
    w_up,
    b_up,
    w_down,
    b_down,
):
    slot_count, seg_rows, model_width = frames.shape
    row_count = slot_count * seg_rows
    head_cols = w_query.shape[1]
    head_count = head_cols // HD
    seq_length = seg_rows * lax.axis_size("ctx")
    seg_start = lax.axis_index("ctx") * seg_rows
    score_scale = HD ** (-0.5)
    key_block = math.gcd(seq_length, 512)
    positions = seg_start + jnp.arange(seg_rows, dtype=jnp.int32)
    query_live = positions[None, :] < lengths[:, None]
    key_live = jnp.arange(seq_length, dtype=jnp.int32)[None, :] < lengths[:, None]
    live_rows = query_live.astype(jnp.float32).reshape(row_count, 1)
    weight_query, weight_key, weight_value, weight_out = (
        lax.all_gather(w_query, ("shard", "ctx"), axis=0, tiled=True),
        lax.all_gather(w_key, ("shard", "ctx"), axis=0, tiled=True),
        lax.all_gather(w_value, ("shard", "ctx"), axis=0, tiled=True),
        lax.all_gather(w_out, ("shard", "ctx"), axis=1, tiled=True),
    )
    frames_flat = frames.astype(jnp.float32).reshape(row_count, model_width)
    first, normed_one, inverse_one = norm_rows(frames_flat, ln1_gain, ln1_bias)
    first_low = first.astype(jnp.bfloat16)
    queries = (
        jnp.dot(first_low, weight_query, preferred_element_type=jnp.float32) + b_query
    ).astype(jnp.bfloat16)
    keys_local = jnp.dot(first_low, weight_key, preferred_element_type=jnp.float32).astype(
        jnp.bfloat16
    )
    values_local = (
        jnp.dot(first_low, weight_value, preferred_element_type=jnp.float32) + b_value
    ).astype(jnp.bfloat16)
    keys_all, values_all = (
        lax.all_gather(
            keys_local.reshape(slot_count, seg_rows, head_cols), "ctx", axis=1, tiled=True
        ),
        lax.all_gather(
            values_local.reshape(slot_count, seg_rows, head_cols), "ctx", axis=1, tiled=True
        ),
    )
    query_heads = queries.reshape(slot_count, seg_rows, head_count, HD)
    key_heads = keys_all.reshape(slot_count, seq_length, head_count, HD)
    value_heads = values_all.reshape(slot_count, seq_length, head_count, HD)
    slot = 0
    log_totals, attended_slot = slot_forward(
        query_heads[slot],
        key_heads[slot],
        value_heads[slot],
        query_live[slot],
        key_live[slot],
        key_block,
        score_scale,
    )
    totals_list = [log_totals]
    attended_list = [attended_slot]
    attended = jnp.stack(attended_list).reshape(row_count, head_cols)
    attended_low = attended.astype(jnp.bfloat16)
    attn_sum = lax.psum(
        jnp.dot(attended_low, weight_out, preferred_element_type=jnp.float32).astype(jnp.bfloat16),
        "tp",
    ).astype(jnp.float32)
    hidden = frames_flat + attn_sum + b_out
    weight_up, weight_down = (
        lax.all_gather(w_up, ("shard", "ctx"), axis=0, tiled=True),
        lax.all_gather(w_down, ("shard", "ctx"), axis=1, tiled=True),
    )
    second, normed_two, inverse_two = norm_rows(hidden, ln2_gain, ln2_bias)
    second_low = second.astype(jnp.bfloat16)
    upper = jnp.dot(second_low, weight_up, preferred_element_type=jnp.float32) + b_up
    activated = jax.nn.gelu(upper, approximate=False).astype(jnp.bfloat16)
    mlp_sum = lax.psum(
        jnp.dot(activated, weight_down, preferred_element_type=jnp.float32).astype(jnp.bfloat16),
        "tp",
    ).astype(jnp.float32)
    output = (
        (live_rows * (hidden + mlp_sum + b_down))
        .astype(jnp.bfloat16)
        .reshape(slot_count, seg_rows, model_width)
    )
    grad_out = live_rows * cotangent.astype(jnp.float32).reshape(row_count, model_width)
    grad_out_low = grad_out.astype(jnp.bfloat16)
    grad_b_down = jnp.sum(grad_out, axis=0)
    grad_w_down = jnp.einsum(
        "rf,rd->fd", activated, grad_out_low, preferred_element_type=jnp.float32
    )
    grad_act = jnp.einsum(
        "rd,fd->rf", grad_out_low, weight_down, preferred_element_type=jnp.float32
    )
    grad_upper = (grad_act * gelu_slope(upper)).astype(jnp.bfloat16)
    grad_b_up = jnp.sum(grad_upper.astype(jnp.float32), axis=0)
    grad_w_up = jnp.einsum("rd,rf->df", second_low, grad_upper, preferred_element_type=jnp.float32)
    grad_second = lax.psum(
        jnp.einsum("rf,df->rd", grad_upper, weight_up, preferred_element_type=jnp.float32).astype(
            jnp.bfloat16
        ),
        "tp",
    ).astype(jnp.float32)
    grad_norm_two, grad_ln2_gain, grad_ln2_bias = norm_back(
        grad_second, normed_two, inverse_two, ln2_gain
    )
    grad_hidden = grad_out + grad_norm_two
    grad_hidden_low = grad_hidden.astype(jnp.bfloat16)
    grad_b_out = jnp.sum(grad_hidden_low.astype(jnp.float32), axis=0)
    grad_w_out = jnp.einsum(
        "rc,rd->cd", attended_low, grad_hidden_low, preferred_element_type=jnp.float32
    )
    grad_att = jnp.einsum(
        "rd,cd->rc", grad_hidden_low, weight_out, preferred_element_type=jnp.float32
    ).astype(jnp.bfloat16)
    delta = jnp.sum(
        (grad_att.astype(jnp.float32) * attended).reshape(row_count, head_count, HD), axis=-1
    )
    delta_heads = delta.reshape(slot_count, seg_rows, head_count)
    grad_att_heads = grad_att.reshape(slot_count, seg_rows, head_count, HD)
    slot = 0
    grad_query_slot, key_part, value_part = slot_back(
        query_heads[slot],
        grad_att_heads[slot],
        totals_list[slot],
        delta_heads[slot].T,
        key_heads[slot],
        value_heads[slot],
        query_live[slot],
        key_live[slot],
        key_block,
        score_scale,
    )
    grad_query_list = [grad_query_slot]
    key_part_list = [key_part.reshape(seq_length, head_cols)]
    value_part_list = [value_part.reshape(seq_length, head_cols)]
    grad_keys, grad_values = (
        lax.psum_scatter(
            jnp.stack(key_part_list).astype(jnp.bfloat16), "ctx", scatter_dimension=1, tiled=True
        ).astype(jnp.float32),
        lax.psum_scatter(
            jnp.stack(value_part_list).astype(jnp.bfloat16), "ctx", scatter_dimension=1, tiled=True
        ).astype(jnp.float32),
    )
    grad_query_low = jnp.stack(grad_query_list).reshape(row_count, head_cols).astype(jnp.bfloat16)
    grad_key_low = grad_keys.reshape(row_count, head_cols).astype(jnp.bfloat16)
    grad_value_low = grad_values.reshape(row_count, head_cols).astype(jnp.bfloat16)
    grad_b_query = jnp.sum(grad_query_low.astype(jnp.float32), axis=0)
    grad_b_value = jnp.sum(grad_value_low.astype(jnp.float32), axis=0)
    grad_w_query = jnp.einsum(
        "rd,rc->dc", first_low, grad_query_low, preferred_element_type=jnp.float32
    )
    grad_w_key = jnp.einsum(
        "rd,rc->dc", first_low, grad_key_low, preferred_element_type=jnp.float32
    )
    grad_w_value = jnp.einsum(
        "rd,rc->dc", first_low, grad_value_low, preferred_element_type=jnp.float32
    )
    first_terms = jnp.einsum(
        "rc,dc->rd", grad_query_low, weight_query, preferred_element_type=jnp.float32
    )
    first_terms = first_terms + jnp.einsum(
        "rc,dc->rd", grad_key_low, weight_key, preferred_element_type=jnp.float32
    )
    first_terms = first_terms + jnp.einsum(
        "rc,dc->rd", grad_value_low, weight_value, preferred_element_type=jnp.float32
    )
    grad_first = lax.psum(first_terms.astype(jnp.bfloat16), "tp").astype(jnp.float32)
    grad_norm_one, grad_ln1_gain, grad_ln1_bias = norm_back(
        grad_first, normed_one, inverse_one, ln1_gain
    )
    grad_input = (grad_hidden + grad_norm_one).reshape(slot_count, seg_rows, model_width)
    shard_grads = (
        lax.psum_scatter(grad_w_query, ("shard", "ctx"), scatter_dimension=0, tiled=True),
        lax.psum_scatter(grad_w_key, ("shard", "ctx"), scatter_dimension=0, tiled=True),
        lax.psum_scatter(grad_w_value, ("shard", "ctx"), scatter_dimension=0, tiled=True),
        lax.psum_scatter(grad_w_out, ("shard", "ctx"), scatter_dimension=1, tiled=True),
        lax.psum_scatter(grad_w_up, ("shard", "ctx"), scatter_dimension=0, tiled=True),
        lax.psum_scatter(grad_w_down, ("shard", "ctx"), scatter_dimension=1, tiled=True),
    )
    small_sums = lax.psum(
        (
            grad_ln1_gain,
            grad_ln1_bias,
            grad_b_query,
            grad_b_value,
            grad_b_out,
            grad_ln2_gain,
            grad_ln2_bias,
            grad_b_up,
            grad_b_down,
        ),
        ("shard", "ctx"),
    )
    return (
        output,
        grad_input,
        small_sums[0],
        small_sums[1],
        shard_grads[0],
        small_sums[2],
        shard_grads[1],
        shard_grads[2],
        small_sums[3],
        shard_grads[3],
        small_sums[4],
        small_sums[5],
        small_sums[6],
        shard_grads[4],
        small_sums[7],
        shard_grads[5],
        small_sums[8],
    )


MESH = pl.DeviceIdType.MESH
F32 = jnp.float32
BF16 = jnp.bfloat16
NEG = -1e30
LIVE_LANE = 192


def nn(left, right):
    return jnp.dot(left, right, preferred_element_type=F32)


def nt(left, right):
    return lax.dot_general(left, right, (((1,), (1,)), ((), ())), preferred_element_type=F32)


def flip(values):
    return values.astype(F32).T.astype(BF16)


def layer_kernel(
    dims,
    frames,
    cot,
    lengths,
    vecs,
    b_up,
    wqkv_own,
    bias_own,
    wf_own,
    out_o,
    gin_o,
    gf_o,
    go_o,
    gq_o,
    sums_o,
    ss,
    rs,
    ls,
    a_all,
    a_t,
    wqkv,
    bias_all,
    wf,
    wo_sib,
    k_tr,
    v_tr,
    k_n,
    v_n,
    q_n,
    q_t,
    lse,
    att_f,
    att_s,
    att_r,
    hid,
    z_all,
    z_t,
    g_n,
    g_t,
    act,
    gup,
    part_s,
    part_r,
    gz_s,
    gz_r,
    ghl_t,
    gatt_r,
    gatt_t,
    wg,
    wg_t,
    wg_x,
    wg_y,
    wg_zr,
    og_x,
    og_r,
    og_z,
    og_zr,
    dk_t,
    dv_t,
    dq_f,
    dlt,
    dkv_s,
    dkv_r,
    ga_r,
    ga_f,
    qg,
    qg_r,
    qg_p,
    qg_z,
    qg_zr,
    sums,
    pairs,
    sum_p,
    sum_z,
    sum_c,
):
    S, C, R, D, GP, HG, FH = dims
    ga_s = a_all.at[pl.ds(0, C * R // 2), :]
    g_nat = a_all.at[pl.ds(C * R // 2, C * R // 2), :]
    WF = 2 * FH + C // 2 * GP
    HF = R // 2
    CH = C // 2
    DB = D // (S * C)
    PB = C * DB
    s, z, c = lax.axis_index("shard"), lax.axis_index("ctx"), lax.axis_index("tp")
    o = 1 - c
    sib = (s, z, o)
    owed = []
    next_sem = [0]

    def sems(count):
        base = next_sem[0]
        next_sem[0] = base + count
        return base

    def remote(src, dst, index, device):
        return pltpu.make_async_remote_copy(
            src_ref=src,
            dst_ref=dst,
            send_sem=ss.at[index],
            recv_sem=rs.at[index],
            device_id=device,
            device_id_type=MESH,
        )

    def send(src, dst, index, device, when=None, like=None):
        def go():
            remote(src, dst, index, device).start()

        if when is None:
            go()
        else:
            pl.when(when)(go)
        owed.append((src if like is None else like, index, when))

    def settle(entries):
        for like, index, when in entries:

            def done(like=like, index=index):
                remote(like, like, index, sib).wait_send()

            if when is None:
                done()
            else:
                pl.when(when)(done)

    def arrive(dst, index, when=None):
        def go():
            remote(dst, dst, index, sib).wait_recv()

        if when is None:
            go()
        else:
            pl.when(when)(go)

    def plane(k):
        return (lax.rem(s + k, S), z, c)

    near_x = s + 1 - 2 * lax.rem(s, 2)
    near_y = lax.rem(s + 2, 4)
    far = near_y + 1 - 2 * lax.rem(s, 2)
    to_x, to_y = (near_x, z, c), (near_y, z, c)

    def column(k):
        return (s, lax.rem(z + k, C), c)

    def s_from(k):
        return lax.rem(s + S - k, S)

    def z_from(k):
        return lax.rem(z + C - k, C)

    def rows_of(block):
        return pl.ds(pl.multiple_of(block * DB, 16), DB)

    def half_rows(block, half):
        return pl.ds(pl.multiple_of(block * R + half * HF, HF), HF)

    def blk(block):
        return pl.ds(pl.multiple_of(block * HF, HF), HF)

    k_bias = sems(1)
    k_q1 = sems(CH)
    k_q2 = sems(S)
    k_q3 = sems(1)
    k_a = sems(2 * C)
    k_as = sems(2 * C)
    k_f = sems(2 * C)
    k_fp = sems(4 * 2 * C)
    k_wo = sems(1)
    k_att = sems(C)
    k_n2 = sems(1)
    k_part = sems(1)
    k_gz = sems(1)
    k_out = sems(1)
    k_gatt = sems(C)
    k_wg = sems(6 * C)
    k_wgz = sems(C)
    k_ox = sems(1)
    k_og = sems(S)
    k_ogz = sems(C)
    k_dkv = sems(1)
    k_ga = sems(2 * C)
    k_qx = sems(1)
    k_qp = sems(S)
    k_qz = sems(CH)
    k_gin = sems(1)
    k_sp = sems(S)
    k_sz = sems(C)
    k_sc = sems(1)

    barrier = pltpu.get_barrier_semaphore()
    friends = [sib]
    friends += [plane(k) for k in range(1, S)]
    for k in range(1, C):
        friends += [(s, lax.rem(z + k, C), c), (s, lax.rem(z + k, C), o)]
    for friend in friends:
        pl.semaphore_signal(barrier, inc=1, device_id=friend, device_id_type=MESH)

    length = lengths[0]
    lane = lax.broadcasted_iota(jnp.int32, (HF, GP), 1)

    def head_lanes(count, h):
        at = lax.broadcasted_iota(jnp.int32, (count, GP), 1)
        return jnp.logical_and(at >= HD * h, at < HD * (h + 1))

    def only_head(values, h, keep_live=False):
        picked = head_lanes(values.shape[0], h)
        if keep_live:
            at = lax.broadcasted_iota(jnp.int32, values.shape, 1)
            picked = jnp.logical_or(picked, at == LIVE_LANE)
        return jnp.where(picked, values, jnp.zeros_like(values))

    ln1_gain, ln1_bias, b_out, ln2_gain, ln2_bias, b_down = (
        vecs[i : i + 1, :] for i in range(6)
    )

    def norm(values):
        centred = values - jnp.mean(values, axis=-1, keepdims=True)
        inverse = lax.rsqrt(jnp.mean(centred * centred, axis=-1, keepdims=True) + EPSILON)
        return centred * inverse, inverse

    def live_of(first, count):
        at = z * R + first + lax.broadcasted_iota(jnp.int32, (count, 1), 0)
        return (at < length).astype(F32)

    sums[...] = jnp.zeros_like(sums)
    pl.semaphore_wait(barrier, len(friends))

    c_of_z = z // CH
    for j in range(CH):
        to_z = CH * c + j
        same = jnp.logical_and(to_z == z, c_of_z == c)
        for i in range(CH):
            ok = jnp.logical_and(z - CH * c_of_z == i, jnp.logical_not(same))
            here = wqkv.at[s, c_of_z, pl.ds(i * DB, DB), :]

            def go(i=i, here=here, j=j, to_z=to_z):
                pltpu.make_async_remote_copy(
                    src_ref=wqkv_own.at[j],
                    dst_ref=here,
                    send_sem=ls.at[j],
                    recv_sem=rs.at[k_q1 + i],
                    device_id=(s, to_z, c_of_z),
                    device_id_type=MESH,
                ).start()

            pl.when(ok)(go)

        def keep(j=j):
            wqkv[s, c, pl.ds(pl.multiple_of((z - CH * c) * DB, 16), DB), :] = wqkv_own[j]

        pl.when(same)(keep)
    send(bias_own, bias_all.at[c], k_bias, sib)
    bias_all[c] = bias_own[...]
    mine_rows = rows_of(s * C + z)
    can_right, can_left = z + 1 < C, z >= 1

    def line_step(view, t, index, like):
        send(
            view(jnp.maximum(z - t, 0)),
            view(jnp.maximum(z - t, 0)),
            index + 2 * t,
            (s, jnp.minimum(z + 1, C - 1), c),
            goes_right[t],
            like,
        )
        send(
            view(jnp.minimum(z + t, C - 1)),
            view(jnp.minimum(z + t, C - 1)),
            index + 2 * t + 1,
            (s, jnp.maximum(z - 1, 0), c),
            goes_left[t],
            like,
        )

    goes_right = [jnp.logical_and(can_right, z - t >= 0) for t in range(C - 1)]
    goes_left = [jnp.logical_and(can_left, z + t < C) for t in range(C - 1)]
    like_f = wf.at[pl.ds(0, DB), :]
    like_fh = wf.at[pl.ds(0, DB), pl.ds(0, WF // 2)]
    like_a = a_all.at[pl.ds(0, HF), :]

    def f_step(t):
        line_step(lambda block: wf.at[rows_of(s * C + block), :], t, k_f, like_f)

    def a_step(t):
        line_step(lambda block: a_all.at[half_rows(block, c), :], t, k_a, like_a)

    def from_left(t):
        return jnp.maximum(z - 1 - t, 0), z - 1 - t >= 0

    def from_right(t):
        return jnp.minimum(z + 1 + t, C - 1), z + 1 + t < C

    halves = (slice(0, WF // 2), slice(WF // 2, WF))

    def row_of(shard, block):
        return rows_of(shard * C + block)

    labels_of = [
        ((2 * t + 2,) + from_left(t), (2 * t + 3,) + from_right(t)) for t in range(C - 1)
    ]
    own_label = ((0, z, None),)
    wo_cols = slice(2 * FH, 2 * FH + CH * GP)

    def wo_pass(shard, block, ok, src=None):
        def go():
            at = row_of(shard, block)
            view = wf.at[at, wo_cols] if src is None else src.at[:, wo_cols]
            remote(view, wo_sib.at[at, :], k_wo, sib).start()

        if ok is None:
            go()
        else:
            pl.when(ok)(go)


    def f_plane(labels, src=None):
        for label, block, ok in labels:
            at = wf.at[row_of(s, block), :]
            send(src if src is not None else at, at, k_fp + 4 * label, to_x, ok, like_f)
            send(src if src is not None else at, at, k_fp + 4 * label + 1, to_y, ok, like_f)
            wo_pass(s, block, ok, src)

    def f_relay(labels):
        for label, block, ok in labels:
            at_x, at_y = wf.at[row_of(near_x, block), :], wf.at[row_of(near_y, block), :]
            arrive(at_x, k_fp + 4 * label, ok)
            at = wf.at[row_of(near_x, block), halves[0]]
            send(at, at, k_fp + 4 * label + 2, to_y, ok, like_fh)
            arrive(at_y, k_fp + 4 * label + 1, ok)
            at = wf.at[row_of(near_y, block), halves[1]]
            send(at, at, k_fp + 4 * label + 3, to_x, ok, like_fh)
            wo_pass(near_x, block, ok)
            wo_pass(near_y, block, ok)

    def f_finish(labels):
        for label, block, ok in labels:
            for i in (1, 0):
                arrive(wf.at[row_of(far, block), halves[i]], k_fp + 4 * label + 2 + i, ok)
                if i == 1:
                    wo_pass(far, block, ok)

    def f_arrive(t):
        for side, (label, block, ok) in enumerate(labels_of[t]):
            arrive(wf.at[row_of(s, block), :], k_f + 2 * t + side, ok)
        f_plane(labels_of[t])

    wf[mine_rows, :] = wf_own[...]
    f_step(0)
    def first_norm(i, carry):
        at = pl.ds(pl.multiple_of(i * 64, 64), 64)
        to = pl.ds(pl.multiple_of(z * R + i * 64, 64), 64)
        normed, unused = norm(frames[at, :].astype(F32))
        a_all[to, :] = (normed * ln1_gain + ln1_bias).astype(BF16)
        g_n[at, :] = (cot[at, :].astype(F32) * live_of(i * 64, 64)).astype(BF16)
        return carry

    lax.fori_loop(0, R // 64, first_norm, 0)
    a_step(0)
    for i in range(CH):
        from_z = CH * c + i
        same = jnp.logical_and(from_z == z, c_of_z == c)
        arrive(wqkv.at[s, c, pl.ds(i * DB, DB), :], k_q1 + i, jnp.logical_not(same))
    for k in range(1, S):
        send(wqkv.at[s, c], wqkv.at[s, c], k_q2 + k, plane(k))
    f_plane(own_label, wf_own)
    key_at = lax.broadcasted_iota(jnp.int32, (GP - LIVE_LANE, C * R), 1)
    first_row = lax.broadcasted_iota(jnp.int32, (GP - LIVE_LANE, C * R), 0) == 0
    dead = jnp.where(jnp.logical_and(first_row, key_at >= length), NEG, 0.0)
    k_tr[LIVE_LANE:, :] = dead.astype(BF16)
    v_tr[LIVE_LANE:, :] = jnp.zeros((GP - LIVE_LANE, C * R), BF16)
    g_t[:, :HF] = flip(g_n[:HF, :])
    g_t[:, HF:] = flip(g_n[HF:, :])
    for k in range(1, S):
        arrive(wqkv.at[s_from(k), c], k_q2 + k)
    send(wqkv.at[:, c], wqkv.at[:, c], k_q3, sib)
    arrive(bias_all.at[o], k_bias)
    arrive(wqkv.at[:, o], k_q3)
    bias_z = bias_all[c_of_z, z - CH * c_of_z]

    def project(block, half):
        at = half_rows(block, half)
        rows = a_all[at, :]
        made = nn(rows, wqkv[...].reshape(D, 3 * GP)) + bias_z[0:1, :]
        keys = made[:, :GP].astype(BF16)
        values = made[:, GP : 2 * GP].astype(BF16)
        k_n[at, :] = keys
        v_n[at, :] = values
        k_tr[:LIVE_LANE, at] = flip(keys)[:LIVE_LANE, :]
        v_tr[:LIVE_LANE, at] = flip(values)[:LIVE_LANE, :]

        def own():
            queries = made[:, 2 * GP :].astype(BF16).astype(F32) * (HD**-0.5)
            queries = jnp.where(lane == LIVE_LANE, 1.0, queries).astype(BF16)
            q_n[blk(block), :] = queries
            q_t[:, blk(block)] = flip(queries)
            a_t[:, blk(block)] = flip(rows)

        pl.when(half == c)(own)

    def project_own(i, carry):
        project(z, lax.rem(c + i, 2))
        return carry

    a_given = []

    def remote_when(src, dst, index, device, when):
        def go():
            remote(src, dst, index, device).start()

        pl.when(when)(go)

    lax.fori_loop(0, 2, project_own, 0)
    f_arrive(0)
    f_relay(own_label)
    for t in range(C - 1):
        if t == C - 2:
            f_arrive(1)
            for later in range(2, C - 1):
                f_step(later)
        for side, (label, block, ok) in enumerate(labels_of[t]):
            arrive(a_all.at[half_rows(block, c), :], k_a + 2 * t + side, ok)
        if t == C - 3:
            f_step(1)
        if t + 1 < C - 1:
            a_step(t + 1)
        for side, (label, block, ok) in enumerate(labels_of[t]):
            at = a_all.at[half_rows(block, c), :]
            remote_when(at, at, k_as + 2 * t + side, sib, ok)
            a_given.append((like_a, k_as + 2 * t + side, ok))

        def come(i, carry, t=t):
            side = i // 2
            block = jnp.where(side == 0, from_left(t)[0], from_right(t)[0])
            ok = jnp.where(side == 0, z - 1 - t >= 0, z + 1 + t < C)

            def other_half():
                at = a_all.at[half_rows(block, o), :]
                remote(at, at, k_as + 2 * t + side, sib).wait_recv()

            def both():
                pl.when(lax.rem(i, 2) == 1)(other_half)
                project(block, lax.rem(c + i, 2))

            pl.when(ok)(both)
            return carry

        lax.fori_loop(0, 4, come, 0)
        if t == C - 3:
            f_relay(labels_of[0])
    f_relay(labels_of[1])
    f_finish(own_label)
    f_finish(labels_of[0])

    TQ = 128

    def attend(block):
        def step(i, carry):
            at = pl.ds(pl.multiple_of(block * HF + i * TQ, TQ), TQ)
            queries = q_n[at, :]
            total = jnp.zeros((TQ, GP), F32)
            for h in range(HG):
                scores = nn(only_head(queries, h, True), k_tr[...])
                top = jnp.max(scores, axis=-1, keepdims=True)
                weights = jnp.exp(scores - top)
                norm_sum = jnp.sum(weights, axis=-1, keepdims=True)
                got = nn(weights.astype(BF16), v_n[...]) * (1.0 / norm_sum)
                total = total + only_head(got, h)
                lse[at, h : h + 1] = top + jnp.log(norm_sum)
            att_f[at, :] = total
            att_s[at, :] = total.astype(BF16)
            return carry

        lax.fori_loop(0, HF // TQ, step, 0)

    def attend_all(i, carry):
        block = lax.rem(z + 1 + i, C)
        attend(block)

        def give():
            remote(
                att_s.at[blk(block), :], att_r.at[blk(z), :], k_att + 1 + i, column(1 + i)
            ).start()

        def more_weights():
            for t in range(2, C - 1):
                f_arrive(t)

        pl.when(i < C - 1)(give)
        pl.when(i == 1)(more_weights)
        return carry

    lax.fori_loop(0, C, attend_all, 0)
    att_r[blk(z), :] = att_s[blk(z), :]

    f_finish(labels_of[1])
    for t in range(2, C - 1):
        f_relay(labels_of[t])
    for t in range(2, C - 1):
        f_finish(labels_of[t])
    owed.append((wo_sib, k_wo, None))
    for k in range(1, C):
        arrive(att_r.at[blk(z_from(k)), :], k_att + k)
        remote(att_s.at[blk(z), :], att_r.at[blk(z), :], k_att + k, column(k)).wait_send()
    arrive(wo_sib, k_wo)

    settle([entry for entry in owed if entry[0] is like_a])
    settle(a_given)
    owed[:] = [entry for entry in owed if entry[0] is not like_a]
    own_rows = pl.ds(pl.multiple_of(c * HF, HF), HF)
    hidden = frames[own_rows, :].astype(F32) + b_out
    for j in range(CH):
        hidden = hidden + nt(
            att_r[blk(CH * c + j), :], wf[:, 2 * FH + j * GP : 2 * FH + (j + 1) * GP]
        )
        hidden = hidden + nt(att_r[blk(CH * o + j), :], wo_sib[:, j * GP : (j + 1) * GP])
    hid[...] = hidden
    normed, unused = norm(hidden)
    z_all[own_rows, :] = (normed * ln2_gain + ln2_bias).astype(BF16)
    send(z_all.at[own_rows, :], z_all.at[own_rows, :], k_n2, sib)
    other_rows = pl.ds(pl.multiple_of(o * HF, HF), HF)
    z_t[:, own_rows] = flip(z_all[own_rows, :])
    arrive(z_all.at[other_rows, :], k_n2)
    z_t[:, other_rows] = flip(z_all[other_rows, :])

    TF = 256

    def units(i, carry):
        cols = pl.ds(pl.multiple_of(i * TF, TF), TF)
        down = pl.ds(pl.multiple_of(FH + i * TF, TF), TF)
        upper = nn(z_all[...], wf[:, cols]) + b_up[:, cols]
        cumulative = 0.5 * (1.0 + lax.erf(upper * INV_ROOT_TWO))
        act[:, cols] = (upper * cumulative).astype(BF16)
        slope = cumulative + upper * jnp.exp(-0.5 * upper * upper) * INV_ROOT_TAU
        grad_units = (nn(g_n[...], wf[:, down]) * slope).astype(BF16)
        gup[:, cols] = grad_units
        return carry

    lax.fori_loop(0, FH // TF, units, 0)

    def z_grad(i, carry):
        at = pl.ds(pl.multiple_of(i * 256, 256), 256)
        gz_s[:, at] = nt(gup[other_rows, :], wf[at, :FH]).astype(BF16)
        return carry

    lax.fori_loop(0, D // 256, z_grad, 0)
    send(gz_s, gz_r, k_gz, sib)

    def unit_grads(i, carry):
        cols = pl.ds(pl.multiple_of(i * TF, TF), TF)
        down = pl.ds(pl.multiple_of(FH + i * TF, TF), TF)
        wg[:, cols] = nn(z_t[...], gup[:, cols]).astype(BF16)
        wg[:, down] = nn(g_t[...], act[:, cols]).astype(BF16)
        return carry

    lax.fori_loop(0, FH // TF, unit_grads, 0)

    def part_z(j):
        return lax.rem(z + 1 + j, C)

    def part_rows(j):
        return pl.ds(pl.multiple_of(part_z(j) * DB, 16), DB)

    part_a, part_b = slice(0, FH), slice(FH, 2 * FH)
    like_g = wg.at[pl.ds(0, DB), :]
    like_gh = wg.at[pl.ds(0, DB), pl.ds(0, FH)]

    def wg_first(j):
        index = k_wg + 6 * j
        own_z = part_z(j)
        send(wg.at[row_of(far, own_z), part_a], wg_t.at[j, 0], index, to_x, like=like_gh)
        send(wg.at[row_of(far, own_z), part_b], wg_t.at[j, 1], index + 1, to_y, like=like_gh)
        near = wg.at[row_of(near_x, own_z), part_a]
        send(near, wg_x.at[part_rows(j), part_a], index + 2, to_x, like=like_gh)
        near = wg.at[row_of(near_y, own_z), part_b]
        send(near, wg_y.at[part_rows(j), part_b], index + 3, to_y, like=like_gh)

    def add_into(at, cols, others):
        def step(i, carry):
            here = pl.ds(pl.multiple_of(cols.start + i * 256, 256), 256)
            total = wg[at, here].astype(F32)
            for other, rows, start in others:
                there = pl.ds(pl.multiple_of(start + i * 256, 256), 256)
                total = total + other[rows, there].astype(F32)
            wg[at, here] = total.astype(BF16)
            return carry

        lax.fori_loop(0, (cols.stop - cols.start) // 256, step, 0)

    def wg_second(j):
        index = k_wg + 6 * j
        own_z = part_z(j)
        arrive(wg_t.at[j, 0], index)
        at = row_of(near_y, own_z)
        add_into(at, part_a, [(wg_t.at[j, 0], slice(None), 0)])
        near = wg.at[at, part_a]
        send(near, wg_y.at[part_rows(j), part_a], index + 4, to_y, like=like_gh)
        arrive(wg_t.at[j, 1], index + 1)
        at = row_of(near_x, own_z)
        add_into(at, part_b, [(wg_t.at[j, 1], slice(None), 0)])
        near = wg.at[at, part_b]
        send(near, wg_x.at[part_rows(j), part_b], index + 5, to_x, like=like_gh)

    def wg_third(j):
        index = k_wg + 6 * j
        arrive(wg_x.at[part_rows(j), part_a], index + 2)
        arrive(wg_y.at[part_rows(j), part_b], index + 3)
        arrive(wg_y.at[part_rows(j), part_a], index + 4)
        arrive(wg_x.at[part_rows(j), part_b], index + 5)
        at = row_of(s, part_z(j))
        add_into(
            at, slice(0, 2 * FH), [(wg_x, part_rows(j), 0), (wg_y, part_rows(j), 0)]
        )
        if j < C - 1:
            send(wg.at[at, :], wg_zr.at[j], k_wgz + 1 + j, column(1 + j), like=like_g)

    wg_first(0)
    wg_first(1)

    gz_rows = jnp.concatenate(
        [nt(gup[own_rows, :], wf[i * 256 : (i + 1) * 256, :FH]) for i in range(D // 256)], axis=1
    )
    arrive(gz_r, k_gz)
    grad_z = gz_rows + gz_r[...].astype(F32)
    live_own = live_of(c * HF, HF)
    normed, inverse = norm(hid[...])
    scaled = grad_z * ln2_gain
    inner = (
        scaled
        - jnp.mean(scaled, axis=-1, keepdims=True)
        - normed * jnp.mean(scaled * normed, axis=-1, keepdims=True)
    )
    g_own = g_n[own_rows, :].astype(F32)
    grad_hidden = g_own + inner * inverse
    gin_o[own_rows, :] = grad_hidden
    low = grad_hidden.astype(BF16)
    sums[3:4, :] = jnp.sum(grad_z * normed, axis=0, keepdims=True)
    sums[4:5, :] = jnp.sum(grad_z, axis=0, keepdims=True)
    sums[5:6, :] = jnp.sum(g_own, axis=0, keepdims=True)
    sums[2:3, :] = jnp.sum(low.astype(F32), axis=0, keepdims=True)
    for j in range(CH):
        att_s[blk(CH * c + j), :] = nn(
            low, wf[:, 2 * FH + j * GP : 2 * FH + (j + 1) * GP]
        ).astype(BF16)
        att_s[blk(CH * o + j), :] = nn(low, wo_sib[:, j * GP : (j + 1) * GP]).astype(BF16)
    for k in range(1, C):
        send(att_s.at[blk(lax.rem(z + k, C)), :], gatt_r.at[blk(z), :], k_gatt + k, column(k))
    gatt_r[blk(z), :] = att_s[blk(z), :]
    ghl_t[...] = flip(low)
    def down_part(i, carry):
        at = pl.ds(pl.multiple_of(i * 256, 256), 256)
        part_s[:, at] = nt(act[other_rows, :], wf[at, FH : 2 * FH]).astype(BF16)
        return carry

    lax.fori_loop(0, D // 256, down_part, 0)
    send(part_s, part_r, k_part, sib)

    for j in range(CH):
        og_x[0, :, j * GP : (j + 1) * GP] = nn(ghl_t[...], att_r[blk(CH * o + j), :]).astype(BF16)
    remote(og_x.at[0], og_x.at[1], k_ox, sib).start()
    dk_t[...] = jnp.zeros_like(dk_t)
    dv_t[...] = jnp.zeros_like(dv_t)
    TK = 512

    steps = C * R // TK

    def attend_back(polls):
        def block_step(b, carry):
            block = lax.rem(z + C - b, C)
            at = blk(block)

            def come():
                remote(gatt_r.at[at, :], gatt_r.at[at, :], k_gatt + b, sib).wait_recv()

            pl.when(b > 0)(come)
            gatt_t[...] = flip(gatt_r[at, :])
            product = gatt_r[at, :].astype(F32) * att_f[at, :]
            deltas = [
                jnp.sum(only_head(product, h), axis=-1, keepdims=True) for h in range(HG)
            ]
            for h in range(HG):
                dlt[:, h : h + 1] = deltas[h]
            dq_f[...] = jnp.zeros_like(dq_f)

            def step(i, carry):
                keys = pl.ds(pl.multiple_of(i * TK, TK), TK)
                for h in range(HG):
                    head = slice(HD * h, HD * (h + 1))
                    scores = nn(only_head(q_n[at, :], h, True), k_tr[:, keys])
                    weights = jnp.exp(scores - lse[at, h : h + 1])
                    grads = nn(only_head(gatt_r[at, :], h), v_tr[:, keys])
                    grad_scores = (weights * (grads - dlt[:, h : h + 1])).astype(BF16)
                    dv_t[head, keys] += nn(gatt_t[head, :], weights.astype(BF16))
                    dk_t[head, keys] += nn(q_t[head, at], grad_scores)
                    dq_f[...] += only_head(nn(grad_scores, k_n[keys, :]), h)
                for number, poll in polls:
                    pl.when(b * steps + i == number)(poll)
                return carry

            lax.fori_loop(0, steps, step, 0)
            g_nat[at, 2 * GP :] = (dq_f[...] * (HD**-0.5)).astype(BF16)
            return carry

        lax.fori_loop(0, C, block_step, 0)

    def og_reduce():
        for k in range(1, S):
            arrive(og_r.at[k - 1], k_og + k)
        own = pl.ds(pl.multiple_of(s * PB, 64), PB)
        total = og_x[0, own, :].astype(F32)
        for k in range(1, S):
            total = total + og_r[k - 1].astype(F32)
        og_z[...] = total.astype(BF16)
        for k in range(1, C):
            at = pl.ds(pl.multiple_of(lax.rem(z + k, C) * DB, 16), DB)
            send(og_z.at[at, :], og_zr.at[k - 1], k_ogz + k, column(k))

    def poll_a():
        wg_second(0)
        wg_first(2)

    def poll_b():
        wg_second(1)
        wg_first(3)

    down_rows = jnp.concatenate(
        [nt(act[own_rows, :], wf[i * 256 : (i + 1) * 256, FH : 2 * FH]) for i in range(D // 256)],
        axis=1,
    )
    arrive(part_r, k_part)
    out_rows = live_own * (hid[...] + down_rows + part_r[...].astype(F32) + b_down)
    out_o[own_rows, :] = out_rows.astype(BF16)
    send(out_o.at[own_rows, :], out_o.at[own_rows, :], k_out, sib)
    for i in range(2):
        sums[pl.ds(6 + 2 * c + i, 1), :] = jnp.sum(
            gup[:, i * D : (i + 1) * D].astype(F32), axis=0, keepdims=True
        )
    arrive(og_x.at[1], k_ox)
    remote(og_x.at[0], og_x.at[1], k_ox, sib).wait_send()
    for j in range(CH):
        cols = slice(j * GP, (j + 1) * GP)
        own_part = nn(ghl_t[...], att_r[blk(CH * c + j), :])
        og_x[0, :, cols] = (own_part + og_x[1, :, cols].astype(F32)).astype(BF16)
    attend_back(
        (
            (1, poll_a),
            (5, poll_b),
            (9, lambda: wg_third(0)),
            (11, lambda: wg_second(2)),
            (15, lambda: wg_third(1)),
        )
    )

    for i in range(C):
        cols = pl.ds(pl.multiple_of(i * R + o * HF, HF), HF)
        dkv_s[i, 0] = dk_t[:, cols].astype(BF16)
        dkv_s[i, 1] = dv_t[:, cols].astype(BF16)
    send(dkv_s, dkv_r, k_dkv, sib)
    wg_second(3)
    for k in range(1, S):
        at = pl.ds(pl.multiple_of(lax.rem(s + k, S) * PB, 64), PB)
        send(og_x.at[0, at, :], og_r.at[k - 1], k_og + k, plane(k))

    arrive(dkv_r, k_dkv)

    def finish(block):
        cols = pl.ds(pl.multiple_of(block * R + c * HF, HF), HF)
        at = blk(block)
        keys_t = dk_t[:, cols] + dkv_r[block, 0].astype(F32)
        values_t = dv_t[:, cols] + dkv_r[block, 1].astype(F32)
        none = jnp.zeros((GP - LIVE_LANE, HF), F32)
        g_nat[at, :GP] = jnp.concatenate([keys_t, none], axis=0).T.astype(BF16)
        g_nat[at, GP : 2 * GP] = jnp.concatenate([values_t, none], axis=0).T.astype(BF16)
        ga_s[at, :] = nt(g_nat[at, :], wqkv[...].reshape(D, 3 * GP)).astype(BF16)

    def finish_all(b, carry):
        finish(b)
        return carry

    lax.fori_loop(0, C, finish_all, 0)

    like_ga = ga_s.at[pl.ds(0, HF), :]

    def ga_send(t, side):
        target = C - 1 - t if side == 0 else t
        device = (s, jnp.minimum(z + 1, C - 1), c) if side == 0 else (s, jnp.maximum(z - 1, 0), c)
        remote(ga_s.at[blk(target), :], ga_r.at[t, side], k_ga + 2 * t + side, device).start()

    def ga_ahead(t, side):
        return C - 1 - t > z if side == 0 else t < z

    for t in range(C - 1):
        for side in range(2):
            behind = z >= 1 if side == 0 else z + 1 < C
            first = jnp.logical_and(ga_ahead(t, side), jnp.logical_not(behind))
            pl.when(first)(lambda t=t, side=side: ga_send(t, side))
            owed.append((like_ga, k_ga + 2 * t + side, ga_ahead(t, side)))

    def ga_hop(u):
        for side in range(2):
            t = u - z if side == 0 else u - (C - 1 - z)
            behind = z >= 1 if side == 0 else z + 1 < C
            ok = jnp.logical_and(jnp.logical_and(t >= 0, behind), ga_ahead(t, side))

            def add(t=t, side=side):
                at = blk(C - 1 - t if side == 0 else t)
                arrive(ga_r.at[t, side], k_ga + 2 * t + side)
                ga_s[at, :] = (ga_s[at, :].astype(F32) + ga_r[t, side].astype(F32)).astype(BF16)
                ga_send(t, side)

            pl.when(ok)(add)

    column_sum = jnp.sum(g_nat[...].astype(F32), axis=0, keepdims=True)
    sums[pl.ds(10 + z, 1), :] = column_sum
    pair_lane = lax.broadcasted_iota(jnp.int32, (PB, 128), 1)
    for i in range(S):
        got = nn(a_t[i * PB : (i + 1) * PB, :], g_nat[...])
        qg[i] = got.reshape(2, CH * DB, 3 * GP).astype(BF16)
        weights = wqkv[i].reshape(PB, 3 * GP).astype(F32)
        with_a = jnp.sum(got * weights, axis=-1, keepdims=True)
        alone = jnp.sum(weights * column_sum, axis=-1, keepdims=True)
        pairs[i * PB : (i + 1) * PB, :] = jnp.where(
            pair_lane == 0, with_a, jnp.where(pair_lane == 1, alone, 0.0)
        )
    send(qg.at[:, o], qg_r, k_qx, sib)
    turned = pairs[...].T
    sums[0:1, :] = (turned[0:1, :] - ln1_bias * turned[1:2, :]) / ln1_gain
    sums[1:2, :] = turned[1:2, :]
    arrive(qg_r, k_qx)
    for i in range(S):
        qg_r[i] = (qg_r[i].astype(F32) + qg[i, c].astype(F32)).astype(BF16)
    for k in range(1, S):
        send(qg_r.at[lax.rem(s + k, S)], qg_p.at[k - 1], k_qp + k, plane(k))

    sum_p[s] = sums[...]
    for k in range(1, S):
        send(sum_p.at[s], sum_p.at[s], k_sp + k, plane(k))
    wg_third(2)
    wg_third(3)
    og_reduce()
    ga_hop(1)
    for u in range(2, C - 1):
        ga_hop(u)
    for k in range(1, S):
        arrive(sum_p.at[s_from(k)], k_sp + k)
    total = sum_p[0]
    for k in range(1, S):
        total = total + sum_p[k]
    sum_z[z] = total
    for k in range(1, C):
        send(sum_z.at[z], sum_z.at[z], k_sz + k, column(k))
    for k in range(1, S):
        arrive(qg_p.at[k - 1], k_qp + k)
    total = qg_r[s].astype(F32)
    for k in range(1, S):
        total = total + qg_p[k - 1].astype(F32)
    qg_z[...] = total.reshape(CH, DB, 3 * GP).astype(BF16)
    for i in range(CH):
        to_z = CH * c + i
        same = jnp.logical_and(to_z == z, c_of_z == c)
        for j in range(CH):
            ok = jnp.logical_and(z - CH * c_of_z == j, jnp.logical_not(same))

            def go(i=i, j=j, to_z=to_z):
                pltpu.make_async_remote_copy(
                    src_ref=qg_z.at[i],
                    dst_ref=qg_zr.at[j],
                    send_sem=ls.at[CH + i],
                    recv_sem=rs.at[k_qz + j],
                    device_id=(s, to_z, c_of_z),
                    device_id_type=MESH,
                ).start()

            pl.when(ok)(go)

        def keep(i=i):
            qg_zr[z - CH * c] = qg_z[i]

        pl.when(same)(keep)

    own_block = blk(z)
    ga_f[...] = ga_s[own_block, :].astype(F32)
    for t in range(C - 1):
        for side in range(2):
            target = C - 1 - t if side == 0 else t
            behind = z >= 1 if side == 0 else z + 1 < C

            def add(t=t, side=side):
                arrive(ga_r.at[t, side], k_ga + 2 * t + side)
                ga_f[...] += ga_r[t, side].astype(F32)

            pl.when(jnp.logical_and(target == z, behind))(add)
    grad_a = ga_f[...]
    normed, inverse = norm(frames[own_rows, :].astype(F32))
    scaled = grad_a * ln1_gain
    inner = (
        scaled
        - jnp.mean(scaled, axis=-1, keepdims=True)
        - normed * jnp.mean(scaled * normed, axis=-1, keepdims=True)
    )
    gin_o[own_rows, :] = gin_o[own_rows, :] + inner * inverse
    send(gin_o.at[own_rows, :], gin_o.at[own_rows, :], k_gin, sib)
    def last(own, got, index, to):
        for k in range(1, C):
            arrive(got.at[k - 1], index + k)
        total = own.astype(F32)
        for k in range(1, C):
            total = total + got[k - 1].astype(F32)
        to[...] = total

    last(wg[rows_of(s * C + z), :], wg_zr, k_wgz, gf_o)
    last(og_z[pl.ds(pl.multiple_of(z * DB, 16), DB), :], og_zr, k_ogz, go_o)
    for j in range(CH):
        same = jnp.logical_and(CH * c + j == z, c_of_z == c)
        arrive(qg_zr.at[j], k_qz + j, jnp.logical_not(same))
    gq_o[...] = qg_zr[...].astype(F32)
    for k in range(1, C):
        arrive(sum_z.at[z_from(k)], k_sz + k)
    total = sum_z[0]
    for k in range(1, C):
        total = total + sum_z[k]
    sum_c[c] = total
    send(sum_c.at[c], sum_c.at[c], k_sc, sib)
    arrive(sum_c.at[o], k_sc)
    sums_o[...] = sum_c[0] + sum_c[1]
    arrive(out_o.at[other_rows, :], k_out)
    arrive(gin_o.at[other_rows, :], k_gin)

    settle(owed)
    for j in range(CH):
        same = jnp.logical_and(CH * c + j == z, c_of_z == c)

        def done_weights(j=j):
            pltpu.make_async_remote_copy(
                src_ref=wqkv_own.at[j],
                dst_ref=wqkv_own.at[j],
                send_sem=ls.at[j],
                recv_sem=rs.at[k_q1],
                device_id=sib,
                device_id_type=MESH,
            ).wait_send()
            pltpu.make_async_remote_copy(
                src_ref=qg_z.at[j],
                dst_ref=qg_z.at[j],
                send_sem=ls.at[CH + j],
                recv_sem=rs.at[k_qz],
                device_id=sib,
                device_id_type=MESH,
            ).wait_send()

        pl.when(jnp.logical_not(same))(done_weights)
    assert next_sem[0] <= SEMS


SEMS = 192


def fits(frames, w_query, w_up):
    shards, ctx, cores = (lax.axis_size(name) for name in ("shard", "ctx", "tp"))
    slot_count, seg_rows, width = frames.shape
    heads = w_query.shape[1] * cores // HD
    return (
        slot_count == 1
        and cores == 2
        and ctx % 2 == 0
        and ctx == 4
        and shards == 4
        and heads == 3 * ctx
        and width % (16 * shards * ctx) == 0
        and width % 256 == 0
        and seg_rows % 512 == 0
        and w_up.shape[1] % 512 == 0
        and w_up.shape[1] == 2 * width
        and ctx * seg_rows <= 2048
        and width <= 768
        and w_up.shape[1] <= 1536
    )


def fast_layer(
    frames,
    lengths,
    cotangent,
    ln1_gain,
    ln1_bias,
    w_query,
    b_query,
    w_key,
    w_value,
    b_value,
    w_out,
    b_out,
    ln2_gain,
    ln2_bias,
    w_up,
    b_up,
    w_down,
    b_down,
):
    S, C = lax.axis_size("shard"), lax.axis_size("ctx")
    unused, R, D = frames.shape
    FH = w_up.shape[1]
    HG, CH = 3, C // 2
    G, GP = HG * HD, 256
    DB = D // (S * C)
    HF = R // 2
    PB = C * DB
    T = C * R

    def grouped(array):
        parts = array.reshape(array.shape[:-1] + (CH, G))
        return jnp.pad(parts, [(0, 0)] * (parts.ndim - 1) + [(0, GP - G)])

    wqkv = jnp.concatenate([grouped(w_key), grouped(w_value), grouped(w_query)], axis=-1)
    wqkv = wqkv.transpose(1, 0, 2)
    bias = jnp.concatenate(
        [jnp.zeros((CH, GP), F32), grouped(b_value), grouped(b_query)], axis=-1
    )
    bias = jnp.broadcast_to(bias[:, None, :], (CH, 8, 3 * GP))
    wf = jnp.concatenate([w_up, w_down.T, grouped(w_out.T).reshape(DB, CH * GP)], axis=1)
    WF = wf.shape[1]
    vecs = jnp.stack([ln1_gain, ln1_bias, b_out, ln2_gain, ln2_bias, b_down, b_down, b_down])
    vmem = pl.BlockSpec(memory_space=pltpu.VMEM)
    V = pltpu.VMEM
    dims = (S, C, R, D, GP, HG, FH)
    scratch = [
        pltpu.SemaphoreType.DMA((SEMS,)),
        pltpu.SemaphoreType.DMA((SEMS,)),
        pltpu.SemaphoreType.DMA((2 * CH,)),
        V((T, D), BF16),
        V((D, C * HF), BF16),
        V((S, 2, CH * DB, 3 * GP), BF16),
        V((2, CH, 8, 3 * GP), F32),
        V((D, WF), BF16),
        V((D, CH * GP), BF16),
        V((GP, T), BF16),
        V((GP, T), BF16),
        V((T, GP), BF16),
        V((T, GP), BF16),
        V((C * HF, GP), BF16),
        V((GP, C * HF), BF16),
        V((C * HF, 8), F32),
        V((C * HF, GP), F32),
        V((C * HF, GP), BF16),
        V((C * HF, GP), BF16),
        V((HF, D), F32),
        V((R, D), BF16),
        V((D, R), BF16),
        V((R, D), BF16),
        V((D, R), BF16),
        V((R, FH), BF16),
        V((R, FH), BF16),
        V((HF, D), BF16),
        V((HF, D), BF16),
        V((HF, D), BF16),
        V((HF, D), BF16),
        V((D, HF), BF16),
        V((C * HF, GP), BF16),
        V((GP, HF), BF16),
        V((D, 2 * FH), BF16),
        V((C, 2, DB, FH), BF16),
        V((PB, 2 * FH), BF16),
        V((PB, 2 * FH), BF16),
        V((C - 1, DB, 2 * FH), BF16),
        V((2, D, CH * GP), BF16),
        V((S - 1, PB, CH * GP), BF16),
        V((PB, CH * GP), BF16),
        V((C - 1, DB, CH * GP), BF16),
        V((G, T), F32),
        V((G, T), F32),
        V((HF, GP), F32),
        V((HF, 8), F32),
        V((C, 2, G, HF), BF16),
        V((C, 2, G, HF), BF16),
        V((C - 1, 2, HF, D), BF16),
        V((HF, D), F32),
        V((S, 2, CH * DB, 3 * GP), BF16),
        V((S, CH * DB, 3 * GP), BF16),
        V((S - 1, CH * DB, 3 * GP), BF16),
        V((CH, DB, 3 * GP), BF16),
        V((CH, DB, 3 * GP), BF16),
        V((16, D), F32),
        V((D, 128), F32),
        V((S, 16, D), F32),
        V((C, 16, D), F32),
        V((2, 16, D), F32),
    ]
    outs = (
        jax.ShapeDtypeStruct((R, D), BF16),
        jax.ShapeDtypeStruct((R, D), F32),
        jax.ShapeDtypeStruct((DB, 2 * FH), F32),
        jax.ShapeDtypeStruct((DB, CH * GP), F32),
        jax.ShapeDtypeStruct((CH, DB, 3 * GP), F32),
        jax.ShapeDtypeStruct((16, D), F32),
    )
    output, grad_input, gf, go, gq, sums = pl.pallas_call(
        functools.partial(layer_kernel, dims),
        out_shape=outs,
        in_specs=[vmem, vmem, pl.BlockSpec(memory_space=pltpu.SMEM)] + [vmem] * 5,
        out_specs=[vmem] * 6,
        scratch_shapes=scratch,
        compiler_params=pltpu.CompilerParams(
            collective_id=0, has_side_effects=True, vmem_limit_bytes=63 << 20
        ),
    )(frames[0], cotangent[0], lengths, vecs, b_up.reshape(1, FH), wqkv, bias, wf)
    c = lax.axis_index("tp")

    def ungroup(array, start):
        part = array[..., start : start + G]
        return part

    def heads_of(start):
        return gq[:, :, start : start + G].transpose(1, 0, 2).reshape(DB, CH * G)

    biases = lax.dynamic_slice_in_dim(sums, 10 + CH * c, CH, 0)
    grad_b_up = lax.dynamic_slice_in_dim(sums, 6 + 2 * c, 2, 0).reshape(FH)
    return (
        output[None],
        grad_input[None],
        sums[0],
        sums[1],
        heads_of(2 * GP),
        biases[:, 2 * GP : 2 * GP + G].reshape(CH * G),
        heads_of(0),
        heads_of(GP),
        biases[:, GP : GP + G].reshape(CH * G),
        go.reshape(DB, CH, GP)[:, :, :G].reshape(DB, CH * G).T,
        sums[2],
        sums[3],
        sums[4],
        gf[:, :FH],
        grad_b_up,
        gf[:, FH:].T,
        sums[5],
    )


def per_device(frames, lengths, cotangent, *params):
    if fits(frames, params[2], params[11]):
        return fast_layer(frames, lengths, cotangent, *params)
    return plain_layer(frames, lengths, cotangent, *params)


def solution(mesh):
    in_specs = (
        P("shard", "ctx", None),
        P("shard"),
        P("shard", "ctx", None),
        P(),
        P(),
        P(("shard", "ctx"), "tp"),
        P("tp"),
        P(("shard", "ctx"), "tp"),
        P(("shard", "ctx"), "tp"),
        P("tp"),
        P("tp", ("shard", "ctx")),
        P(),
        P(),
        P(),
        P(("shard", "ctx"), "tp"),
        P("tp"),
        P("tp", ("shard", "ctx")),
        P(),
    )
    out_specs = (
        P("shard", "ctx", None),
        P("shard", "ctx", None),
        P(),
        P(),
        P(("shard", "ctx"), "tp"),
        P("tp"),
        P(("shard", "ctx"), "tp"),
        P(("shard", "ctx"), "tp"),
        P("tp"),
        P("tp", ("shard", "ctx")),
        P(),
        P(),
        P(),
        P(("shard", "ctx"), "tp"),
        P("tp"),
        P("tp", ("shard", "ctx")),
        P(),
    )
    return jax.shard_map(
        per_device, mesh=mesh, in_specs=in_specs, out_specs=out_specs, check_vma=False
    )
```

```python
import functools
import math

import jax
import jax.numpy as jnp
from jax import lax
from jax.experimental import pallas as pl
from jax.experimental.pallas import tpu as pltpu
from jax.sharding import PartitionSpec as P

HD = 64


EPSILON = 1e-05
INV_ROOT_TWO = 0.7071067811865476
INV_ROOT_TAU = 0.3989422804014327


def norm_rows(values, gain, shift):
    centred = values - jnp.mean(values, axis=-1, keepdims=True)
    inverse = lax.rsqrt(jnp.mean(centred * centred, axis=-1, keepdims=True) + EPSILON)
    normed = centred * inverse
    return (normed * gain + shift, normed, inverse)


def norm_back(grad_rows, normed, inverse, gain):
    scaled = grad_rows * gain
    inner = (
        scaled
        - jnp.mean(scaled, axis=-1, keepdims=True)
        - normed * jnp.mean(scaled * normed, axis=-1, keepdims=True)
    )
    return (inner * inverse, jnp.sum(grad_rows * normed, axis=0), jnp.sum(grad_rows, axis=0))


def gelu_slope(values):
    return (
        0.5 * (1.0 + lax.erf(values * INV_ROOT_TWO))
        + values * jnp.exp(-0.5 * values * values) * INV_ROOT_TAU
    )


def pair_scores(queries, block_keys, score_scale):
    return (
        jnp.einsum("qhd,khd->hqk", queries, block_keys, preferred_element_type=jnp.float32)
        * score_scale
    )


def live_weights(scores, query_live, key_live, log_totals):
    both_live = query_live[None, :, None] & key_live[None, None, :]
    return jnp.where(both_live, jnp.exp(scores - log_totals[:, :, None]), 0.0)


def in_blocks(array, block_rows):
    return array.reshape((array.shape[0] // block_rows, block_rows) + array.shape[1:])


def slot_forward(queries, slot_keys, slot_values, query_live, key_live, key_block, score_scale):
    seg_rows, head_count, head_dim = queries.shape
    key_starts = jnp.arange(slot_keys.shape[0] // key_block, dtype=jnp.int32) * key_block
    blocks = (
        in_blocks(slot_keys, key_block),
        in_blocks(slot_values, key_block),
        in_blocks(key_live, key_block),
        key_starts,
    )
    start_state = (
        jnp.full((head_count, seg_rows), -jnp.inf, jnp.float32),
        jnp.zeros((head_count, seg_rows), jnp.float32),
    )

    def totals_step(carried, scan_item):
        block_keys, block_values, block_live, block_start = scan_item
        running_max, running_sum = carried
        scores = jnp.where(
            block_live[None, None, :], pair_scores(queries, block_keys, score_scale), -jnp.inf
        )
        new_max = jnp.maximum(running_max, jnp.max(scores, axis=-1))
        new_sum = running_sum * jnp.exp(running_max - new_max) + jnp.sum(
            jnp.exp(scores - new_max[:, :, None]), axis=-1
        )
        return ((new_max, new_sum), None)

    def whole_slot(ignored):
        final_state, unused = lax.scan(totals_step, start_state, blocks)
        log_totals = final_state[0] + jnp.log(final_state[1])

        def output_step(output_sum, scan_item):
            block_keys, block_values, block_live, block_start = scan_item
            weights_here = live_weights(
                pair_scores(queries, block_keys, score_scale), query_live, block_live, log_totals
            ).astype(jnp.bfloat16)
            return (
                output_sum
                + jnp.einsum(
                    "hqk,khd->qhd", weights_here, block_values, preferred_element_type=jnp.float32
                ),
                None,
            )

        attended, unused_too = lax.scan(
            output_step, jnp.zeros((seg_rows, head_count, head_dim), jnp.float32), blocks
        )
        return (log_totals, attended)

    return whole_slot(0)


def slot_back(
    queries,
    grad_att,
    log_totals,
    delta,
    slot_keys,
    slot_values,
    query_live,
    key_live,
    key_block,
    score_scale,
):
    seg_rows, head_count, head_dim = queries.shape
    key_starts = jnp.arange(slot_keys.shape[0] // key_block, dtype=jnp.int32) * key_block
    blocks = (
        in_blocks(slot_keys, key_block),
        in_blocks(slot_values, key_block),
        in_blocks(key_live, key_block),
        key_starts,
    )

    def grad_step(grad_query, scan_item):
        block_keys, block_values, block_live, block_start = scan_item
        partial_value = grad_query
        weights_full = live_weights(
            pair_scores(queries, block_keys, score_scale), query_live, block_live, log_totals
        )
        grad_probs = jnp.einsum(
            "qhd,khd->hqk", grad_att, block_values, preferred_element_type=jnp.float32
        )
        grad_scores = (weights_full * (grad_probs - delta[:, :, None])).astype(jnp.bfloat16)
        partial_value = (
            partial_value
            + jnp.einsum(
                "hqk,khd->qhd", grad_scores, block_keys, preferred_element_type=jnp.float32
            )
            * score_scale
        )
        grad_value = jnp.einsum(
            "hqk,qhd->khd",
            weights_full.astype(jnp.bfloat16),
            grad_att,
            preferred_element_type=jnp.float32,
        )
        grad_key = (
            jnp.einsum("hqk,qhd->khd", grad_scores, queries, preferred_element_type=jnp.float32)
            * score_scale
        )
        return (partial_value, (grad_key, grad_value))

    def whole_slot(ignored):
        grad_query, key_parts = lax.scan(
            grad_step, jnp.zeros((seg_rows, head_count, head_dim), jnp.float32), blocks
        )
        return (
            grad_query,
            key_parts[0].reshape(slot_keys.shape),
            key_parts[1].reshape(slot_keys.shape),
        )

    return whole_slot(0)


def plain_layer(
    frames,
    lengths,
    cotangent,
    ln1_gain,
    ln1_bias,
    w_query,
    b_query,
    w_key,
    w_value,
    b_value,
    w_out,
    b_out,
    ln2_gain,
    ln2_bias,
    w_up,
    b_up,
    w_down,
    b_down,
):
    slot_count, seg_rows, model_width = frames.shape
    row_count = slot_count * seg_rows
    head_cols = w_query.shape[1]
    head_count = head_cols // HD
    seq_length = seg_rows * lax.axis_size("ctx")
    seg_start = lax.axis_index("ctx") * seg_rows
    score_scale = HD ** (-0.5)
    key_block = math.gcd(seq_length, 512)
    positions = seg_start + jnp.arange(seg_rows, dtype=jnp.int32)
    query_live = positions[None, :] < lengths[:, None]
    key_live = jnp.arange(seq_length, dtype=jnp.int32)[None, :] < lengths[:, None]
    live_rows = query_live.astype(jnp.float32).reshape(row_count, 1)
    weight_query, weight_key, weight_value, weight_out = (
        lax.all_gather(w_query, ("shard", "ctx"), axis=0, tiled=True),
        lax.all_gather(w_key, ("shard", "ctx"), axis=0, tiled=True),
        lax.all_gather(w_value, ("shard", "ctx"), axis=0, tiled=True),
        lax.all_gather(w_out, ("shard", "ctx"), axis=1, tiled=True),
    )
    frames_flat = frames.astype(jnp.float32).reshape(row_count, model_width)
    first, normed_one, inverse_one = norm_rows(frames_flat, ln1_gain, ln1_bias)
    first_low = first.astype(jnp.bfloat16)
    queries = (
        jnp.dot(first_low, weight_query, preferred_element_type=jnp.float32) + b_query
    ).astype(jnp.bfloat16)
    keys_local = jnp.dot(first_low, weight_key, preferred_element_type=jnp.float32).astype(
        jnp.bfloat16
    )
    values_local = (
        jnp.dot(first_low, weight_value, preferred_element_type=jnp.float32) + b_value
    ).astype(jnp.bfloat16)
    keys_all, values_all = (
        lax.all_gather(
            keys_local.reshape(slot_count, seg_rows, head_cols), "ctx", axis=1, tiled=True
        ),
        lax.all_gather(
            values_local.reshape(slot_count, seg_rows, head_cols), "ctx", axis=1, tiled=True
        ),
    )
    query_heads = queries.reshape(slot_count, seg_rows, head_count, HD)
    key_heads = keys_all.reshape(slot_count, seq_length, head_count, HD)
    value_heads = values_all.reshape(slot_count, seq_length, head_count, HD)
    slot = 0
    log_totals, attended_slot = slot_forward(
        query_heads[slot],
        key_heads[slot],
        value_heads[slot],
        query_live[slot],
        key_live[slot],
        key_block,
        score_scale,
    )
    totals_list = [log_totals]
    attended_list = [attended_slot]
    attended = jnp.stack(attended_list).reshape(row_count, head_cols)
    attended_low = attended.astype(jnp.bfloat16)
    attn_sum = lax.psum(
        jnp.dot(attended_low, weight_out, preferred_element_type=jnp.float32).astype(jnp.bfloat16),
        "tp",
    ).astype(jnp.float32)
    hidden = frames_flat + attn_sum + b_out
    weight_up, weight_down = (
        lax.all_gather(w_up, ("shard", "ctx"), axis=0, tiled=True),
        lax.all_gather(w_down, ("shard", "ctx"), axis=1, tiled=True),
    )
    second, normed_two, inverse_two = norm_rows(hidden, ln2_gain, ln2_bias)
    second_low = second.astype(jnp.bfloat16)
    upper = jnp.dot(second_low, weight_up, preferred_element_type=jnp.float32) + b_up
    activated = jax.nn.gelu(upper, approximate=False).astype(jnp.bfloat16)
    mlp_sum = lax.psum(
        jnp.dot(activated, weight_down, preferred_element_type=jnp.float32).astype(jnp.bfloat16),
        "tp",
    ).astype(jnp.float32)
    output = (
        (live_rows * (hidden + mlp_sum + b_down))
        .astype(jnp.bfloat16)
        .reshape(slot_count, seg_rows, model_width)
    )
    grad_out = live_rows * cotangent.astype(jnp.float32).reshape(row_count, model_width)
    grad_out_low = grad_out.astype(jnp.bfloat16)
    grad_b_down = jnp.sum(grad_out, axis=0)
    grad_w_down = jnp.einsum(
        "rf,rd->fd", activated, grad_out_low, preferred_element_type=jnp.float32
    )
    grad_act = jnp.einsum(
        "rd,fd->rf", grad_out_low, weight_down, preferred_element_type=jnp.float32
    )
    grad_upper = (grad_act * gelu_slope(upper)).astype(jnp.bfloat16)
    grad_b_up = jnp.sum(grad_upper.astype(jnp.float32), axis=0)
    grad_w_up = jnp.einsum("rd,rf->df", second_low, grad_upper, preferred_element_type=jnp.float32)
    grad_second = lax.psum(
        jnp.einsum("rf,df->rd", grad_upper, weight_up, preferred_element_type=jnp.float32).astype(
            jnp.bfloat16
        ),
        "tp",
    ).astype(jnp.float32)
    grad_norm_two, grad_ln2_gain, grad_ln2_bias = norm_back(
        grad_second, normed_two, inverse_two, ln2_gain
    )
    grad_hidden = grad_out + grad_norm_two
    grad_hidden_low = grad_hidden.astype(jnp.bfloat16)
    grad_b_out = jnp.sum(grad_hidden_low.astype(jnp.float32), axis=0)
    grad_w_out = jnp.einsum(
        "rc,rd->cd", attended_low, grad_hidden_low, preferred_element_type=jnp.float32
    )
    grad_att = jnp.einsum(
        "rd,cd->rc", grad_hidden_low, weight_out, preferred_element_type=jnp.float32
    ).astype(jnp.bfloat16)
    delta = jnp.sum(
        (grad_att.astype(jnp.float32) * attended).reshape(row_count, head_count, HD), axis=-1
    )
    delta_heads = delta.reshape(slot_count, seg_rows, head_count)
    grad_att_heads = grad_att.reshape(slot_count, seg_rows, head_count, HD)
    slot = 0
    grad_query_slot, key_part, value_part = slot_back(
        query_heads[slot],
        grad_att_heads[slot],
        totals_list[slot],
        delta_heads[slot].T,
        key_heads[slot],
        value_heads[slot],
        query_live[slot],
        key_live[slot],
        key_block,
        score_scale,
    )
    grad_query_list = [grad_query_slot]
    key_part_list = [key_part.reshape(seq_length, head_cols)]
    value_part_list = [value_part.reshape(seq_length, head_cols)]
    grad_keys, grad_values = (
        lax.psum_scatter(
            jnp.stack(key_part_list).astype(jnp.bfloat16), "ctx", scatter_dimension=1, tiled=True
        ).astype(jnp.float32),
        lax.psum_scatter(
            jnp.stack(value_part_list).astype(jnp.bfloat16), "ctx", scatter_dimension=1, tiled=True
        ).astype(jnp.float32),
    )
    grad_query_low = jnp.stack(grad_query_list).reshape(row_count, head_cols).astype(jnp.bfloat16)
    grad_key_low = grad_keys.reshape(row_count, head_cols).astype(jnp.bfloat16)
    grad_value_low = grad_values.reshape(row_count, head_cols).astype(jnp.bfloat16)
    grad_b_query = jnp.sum(grad_query_low.astype(jnp.float32), axis=0)
    grad_b_value = jnp.sum(grad_value_low.astype(jnp.float32), axis=0)
    grad_w_query = jnp.einsum(
        "rd,rc->dc", first_low, grad_query_low, preferred_element_type=jnp.float32
    )
    grad_w_key = jnp.einsum(
        "rd,rc->dc", first_low, grad_key_low, preferred_element_type=jnp.float32
    )
    grad_w_value = jnp.einsum(
        "rd,rc->dc", first_low, grad_value_low, preferred_element_type=jnp.float32
    )
    first_terms = jnp.einsum(
        "rc,dc->rd", grad_query_low, weight_query, preferred_element_type=jnp.float32
    )
    first_terms = first_terms + jnp.einsum(
        "rc,dc->rd", grad_key_low, weight_key, preferred_element_type=jnp.float32
    )
    first_terms = first_terms + jnp.einsum(
        "rc,dc->rd", grad_value_low, weight_value, preferred_element_type=jnp.float32
    )
    grad_first = lax.psum(first_terms.astype(jnp.bfloat16), "tp").astype(jnp.float32)
    grad_norm_one, grad_ln1_gain, grad_ln1_bias = norm_back(
        grad_first, normed_one, inverse_one, ln1_gain
    )
    grad_input = (grad_hidden + grad_norm_one).reshape(slot_count, seg_rows, model_width)
    shard_grads = (
        lax.psum_scatter(grad_w_query, ("shard", "ctx"), scatter_dimension=0, tiled=True),
        lax.psum_scatter(grad_w_key, ("shard", "ctx"), scatter_dimension=0, tiled=True),
        lax.psum_scatter(grad_w_value, ("shard", "ctx"), scatter_dimension=0, tiled=True),
        lax.psum_scatter(grad_w_out, ("shard", "ctx"), scatter_dimension=1, tiled=True),
        lax.psum_scatter(grad_w_up, ("shard", "ctx"), scatter_dimension=0, tiled=True),
        lax.psum_scatter(grad_w_down, ("shard", "ctx"), scatter_dimension=1, tiled=True),
    )
    small_sums = lax.psum(
        (
            grad_ln1_gain,
            grad_ln1_bias,
            grad_b_query,
            grad_b_value,
            grad_b_out,
            grad_ln2_gain,
            grad_ln2_bias,
            grad_b_up,
            grad_b_down,
        ),
        ("shard", "ctx"),
    )
    return (
        output,
        grad_input,
        small_sums[0],
        small_sums[1],
        shard_grads[0],
        small_sums[2],
        shard_grads[1],
        shard_grads[2],
        small_sums[3],
        shard_grads[3],
        small_sums[4],
        small_sums[5],
        small_sums[6],
        shard_grads[4],
        small_sums[7],
        shard_grads[5],
        small_sums[8],
    )


MESH = pl.DeviceIdType.MESH
F32 = jnp.float32
BF16 = jnp.bfloat16
NEG = -1e30
LIVE_LANE = 192


def nn(left, right):
    return jnp.dot(left, right, preferred_element_type=F32)


def nt(left, right):
    return lax.dot_general(left, right, (((1,), (1,)), ((), ())), preferred_element_type=F32)


def group(values, j):
    taken = values[:, :256] if j == 0 else pltpu.roll(values[:, 128:384], 192, 1)
    at = lax.broadcasted_iota(jnp.int32, taken.shape, 1)
    return jnp.where(at < 3 * HD, taken, 0.0)


def ungroup(first, second):
    turned = pltpu.roll(second, 64, 1)
    at = lax.broadcasted_iota(jnp.int32, turned.shape, 1)
    tail = jnp.concatenate([first[:, 128:], first[:, 128:]], axis=1)
    return jnp.concatenate([first[:, :128], jnp.where(at < 64, tail, turned)], axis=1)


def flip(values):
    return values.astype(F32).T.astype(BF16)


def layer_kernel(
    dims,
    frames,
    cot,
    lengths,
    v_gain1,
    v_bias1,
    v_b_out,
    v_gain2,
    v_bias2,
    v_b_down,
    v_b_up,
    v_b_query,
    v_b_value,
    w_query,
    w_key,
    w_value,
    w_up,
    w_down,
    w_out,
    out_h,
    gin_h,
    gf_h,
    go_h,
    gq_h,
    sums_h,
    ss,
    rs,
    ls,
    os,
    out_o,
    gin_o,
    gf_o,
    go_o,
    gq_o,
    sums_o,
    wqkv_own,
    bias_own,
    up_bias,
    a_all,
    a_t,
    wqkv,
    bias_all,
    wf,
    wo_sib,
    k_tr,
    v_tr,
    k_n,
    v_n,
    q_n,
    q_t,
    lse,
    att_f,
    att_s,
    att_r,
    hid,
    z_all,
    z_t,
    g_n,
    g_t,
    act,
    gup,
    part_s,
    part_r,
    gz_s,
    gz_r,
    ghl_t,
    gatt_r,
    gatt_t,
    wg,
    wg_t,
    wg_x,
    wg_y,
    wg_zr,
    og_x,
    og_r,
    og_z,
    og_zr,
    dk_t,
    dv_t,
    dq_f,
    dlt,
    dkv_s,
    dkv_r,
    ga_r,
    ga_f,
    qg,
    qg_r,
    qg_p,
    qg_z,
    qg_zr,
    sums,
    pairs,
    sum_p,
    sum_z,
    sum_c,
):
    S, C, R, D, GP, HG, FH = dims
    ga_s = a_all.at[pl.ds(0, C * R // 2), :]
    g_nat = a_all.at[pl.ds(C * R // 2, C * R // 2), :]
    WF = 2 * FH + C // 2 * GP
    HF = R // 2
    CH = C // 2
    DB = D // (S * C)
    PB = C * DB
    s, z, c = lax.axis_index("shard"), lax.axis_index("ctx"), lax.axis_index("tp")
    o = 1 - c
    sib = (s, z, o)
    owed = []
    next_sem = [0]

    def sems(count):
        base = next_sem[0]
        next_sem[0] = base + count
        return base

    def remote(src, dst, index, device):
        return pltpu.make_async_remote_copy(
            src_ref=src,
            dst_ref=dst,
            send_sem=ss.at[index],
            recv_sem=rs.at[index],
            device_id=device,
            device_id_type=MESH,
        )

    def send(src, dst, index, device, when=None, like=None):
        def go():
            remote(src, dst, index, device).start()

        if when is None:
            go()
        else:
            pl.when(when)(go)
        owed.append((src if like is None else like, index, when))

    def settle(entries):
        for like, index, when in entries:

            def done(like=like, index=index):
                remote(like, like, index, sib).wait_send()

            if when is None:
                done()
            else:
                pl.when(when)(done)

    stored = []

    def store(src, dst):
        copy = pltpu.make_async_copy(src, dst, os.at[len(stored)])
        copy.start()
        stored.append(copy)

    def arrive(dst, index, when=None):
        def go():
            remote(dst, dst, index, sib).wait_recv()

        if when is None:
            go()
        else:
            pl.when(when)(go)

    def plane(k):
        return (lax.rem(s + k, S), z, c)

    near_x = s + 1 - 2 * lax.rem(s, 2)
    near_y = lax.rem(s + 2, 4)
    far = near_y + 1 - 2 * lax.rem(s, 2)
    to_x, to_y = (near_x, z, c), (near_y, z, c)

    def column(k):
        return (s, lax.rem(z + k, C), c)

    def s_from(k):
        return lax.rem(s + S - k, S)

    def z_from(k):
        return lax.rem(z + C - k, C)

    def rows_of(block):
        return pl.ds(pl.multiple_of(block * DB, 16), DB)

    def half_rows(block, half):
        return pl.ds(pl.multiple_of(block * R + half * HF, HF), HF)

    def blk(block):
        return pl.ds(pl.multiple_of(block * HF, HF), HF)

    k_bias = sems(1)
    k_q1 = sems(CH)
    k_q2 = sems(S)
    k_q3 = sems(1)
    k_a = sems(2 * C)
    k_as = sems(2 * C)
    k_f = sems(2 * C)
    k_fp = sems(6 * 2 * C)
    k_wo = sems(1)
    k_att = sems(C)
    k_n2 = sems(1)
    k_part = sems(1)
    k_gz = sems(1)
    k_out = sems(1)
    k_gatt = sems(C)
    k_wg = sems(6 * C)
    k_wgz = sems(C)
    k_ox = sems(1)
    k_og = sems(S)
    k_ogz = sems(C)
    k_dkv = sems(1)
    k_ga = sems(2 * C)
    k_qx = sems(1)
    k_qp = sems(S)
    k_qz = sems(CH)
    k_gin = sems(1)
    k_sp = sems(S)
    k_sz = sems(C)
    k_sc = sems(1)

    barrier = pltpu.get_barrier_semaphore()
    friends = [sib]
    friends += [plane(k) for k in range(1, S)]
    for k in range(1, C):
        friends += [(s, lax.rem(z + k, C), c), (s, lax.rem(z + k, C), o)]
    for friend in friends:
        pl.semaphore_signal(barrier, inc=1, device_id=friend, device_id_type=MESH)

    length = lengths[0]
    lane = lax.broadcasted_iota(jnp.int32, (HF, GP), 1)

    def head_lanes(count, h):
        at = lax.broadcasted_iota(jnp.int32, (count, GP), 1)
        return jnp.logical_and(at >= HD * h, at < HD * (h + 1))

    def only_head(values, h, keep_live=False):
        picked = head_lanes(values.shape[0], h)
        if keep_live:
            at = lax.broadcasted_iota(jnp.int32, values.shape, 1)
            picked = jnp.logical_or(picked, at == LIVE_LANE)
        return jnp.where(picked, values, jnp.zeros_like(values))

    ln1_gain, ln1_bias, b_out, ln2_gain, ln2_bias, b_down = (
        ref[...].reshape(1, D) for ref in (v_gain1, v_bias1, v_b_out, v_gain2, v_bias2, v_b_down)
    )
    for j in range(CH):
        for i, part in enumerate((w_key, w_value, w_query)):
            cols = slice(i * GP, (i + 1) * GP)
            wqkv_own[j, :, cols] = group(part[...].astype(F32), j).astype(BF16)
    mine_rows = rows_of(s * C + z)
    wf[mine_rows, :FH] = w_up[...]
    wf[mine_rows, FH : 2 * FH] = w_down[...]
    out_t = w_out[...].astype(F32)
    for j in range(CH):
        cols = slice(2 * FH + j * GP, 2 * FH + (j + 1) * GP)
        wf[mine_rows, cols] = group(out_t, j).astype(BF16)
    for j in range(CH):
        bias_own[j] = jnp.zeros((8, 3 * GP), F32)
        bias_own[j, 0:1, GP : 2 * GP] = group(v_b_value[...].reshape(1, CH * 3 * HD), j)
        bias_own[j, 0:1, 2 * GP :] = group(v_b_query[...].reshape(1, CH * 3 * HD), j)

    def norm(values):
        centred = values - jnp.mean(values, axis=-1, keepdims=True)
        inverse = lax.rsqrt(jnp.mean(centred * centred, axis=-1, keepdims=True) + EPSILON)
        return centred * inverse, inverse

    def live_of(first, count):
        at = z * R + first + lax.broadcasted_iota(jnp.int32, (count, 1), 0)
        return (at < length).astype(F32)

    sums[...] = jnp.zeros_like(sums)
    pl.semaphore_wait(barrier, len(friends))

    c_of_z = z // CH
    for j in range(CH):
        to_z = CH * c + j
        same = jnp.logical_and(to_z == z, c_of_z == c)
        for i in range(CH):
            ok = jnp.logical_and(z - CH * c_of_z == i, jnp.logical_not(same))
            here = wqkv.at[s, c_of_z, pl.ds(i * DB, DB), :]

            def go(i=i, here=here, j=j, to_z=to_z):
                pltpu.make_async_remote_copy(
                    src_ref=wqkv_own.at[j],
                    dst_ref=here,
                    send_sem=ls.at[j],
                    recv_sem=rs.at[k_q1 + i],
                    device_id=(s, to_z, c_of_z),
                    device_id_type=MESH,
                ).start()

            pl.when(ok)(go)

        def keep(j=j):
            wqkv[s, c, pl.ds(pl.multiple_of((z - CH * c) * DB, 16), DB), :] = wqkv_own[j]

        pl.when(same)(keep)
    send(bias_own, bias_all.at[c], k_bias, sib)
    bias_all[c] = bias_own[...]
    can_right, can_left = z + 1 < C, z >= 1

    def line_step(view, t, index, like):
        send(
            view(jnp.maximum(z - t, 0)),
            view(jnp.maximum(z - t, 0)),
            index + 2 * t,
            (s, jnp.minimum(z + 1, C - 1), c),
            goes_right[t],
            like,
        )
        send(
            view(jnp.minimum(z + t, C - 1)),
            view(jnp.minimum(z + t, C - 1)),
            index + 2 * t + 1,
            (s, jnp.maximum(z - 1, 0), c),
            goes_left[t],
            like,
        )

    goes_right = [jnp.logical_and(can_right, z - t >= 0) for t in range(C - 1)]
    goes_left = [jnp.logical_and(can_left, z + t < C) for t in range(C - 1)]
    like_f = wf.at[pl.ds(0, DB), :]
    like_fh = wf.at[pl.ds(0, DB), pl.ds(0, WF // 2)]
    like_a = a_all.at[pl.ds(0, HF), :]

    def f_step(t):
        line_step(lambda block: wf.at[rows_of(s * C + block), :], t, k_f, like_f)

    def a_step(t):
        line_step(lambda block: a_all.at[half_rows(block, c), :], t, k_a, like_a)

    def from_left(t):
        return jnp.maximum(z - 1 - t, 0), z - 1 - t >= 0

    def from_right(t):
        return jnp.minimum(z + 1 + t, C - 1), z + 1 + t < C

    halves = (slice(0, WF // 2), slice(WF // 2, WF))

    def row_of(shard, block):
        return rows_of(shard * C + block)

    labels_of = [
        ((2 * t + 2,) + from_left(t), (2 * t + 3,) + from_right(t)) for t in range(C - 1)
    ]
    own_label = ((0, z, None),)
    wo_cols = slice(2 * FH, 2 * FH + CH * GP)

    def wo_pass(shard, block, ok):
        def go():
            at = row_of(shard, block)
            remote(wf.at[at, wo_cols], wo_sib.at[at, :], k_wo, sib).start()

        if ok is None:
            go()
        else:
            pl.when(ok)(go)


    def f_plane(labels):
        for label, block, ok in labels:
            index = k_fp + 6 * label
            for half in range(2):
                at = wf.at[row_of(s, block), halves[half]]
                send(at, at, index + half, to_x, ok, like_fh)
                at = wf.at[row_of(s, block), halves[1 - half]]
                send(at, at, index + 2 + half, to_y, ok, like_fh)
            wo_pass(s, block, ok)

    def f_relay(labels):
        for label, block, ok in labels:
            index = k_fp + 6 * label
            at = wf.at[row_of(near_x, block), halves[0]]
            arrive(at, index, ok)
            send(at, at, index + 4, to_y, ok, like_fh)
            at = wf.at[row_of(near_y, block), halves[1]]
            arrive(at, index + 2, ok)
            send(at, at, index + 5, to_x, ok, like_fh)
            wo_pass(near_y, block, ok)

    def f_finish(labels):
        for label, block, ok in labels:
            index = k_fp + 6 * label
            arrive(wf.at[row_of(near_x, block), halves[1]], index + 1, ok)
            wo_pass(near_x, block, ok)
            arrive(wf.at[row_of(near_y, block), halves[0]], index + 3, ok)
            arrive(wf.at[row_of(far, block), halves[1]], index + 5, ok)
            wo_pass(far, block, ok)
            arrive(wf.at[row_of(far, block), halves[0]], index + 4, ok)

    def f_arrive(t):
        for side, (label, block, ok) in enumerate(labels_of[t]):
            arrive(wf.at[row_of(s, block), :], k_f + 2 * t + side, ok)
        f_plane(labels_of[t])

    f_step(0)
    def first_norm(i, carry):
        at = pl.ds(pl.multiple_of(i * 64, 64), 64)
        to = pl.ds(pl.multiple_of(z * R + i * 64, 64), 64)
        normed, unused = norm(frames[at, :].astype(F32))
        a_all[to, :] = (normed * ln1_gain + ln1_bias).astype(BF16)
        g_n[at, :] = (cot[at, :].astype(F32) * live_of(i * 64, 64)).astype(BF16)
        return carry

    lax.fori_loop(0, R // 64, first_norm, 0)
    a_step(0)
    for i in range(CH):
        from_z = CH * c + i
        same = jnp.logical_and(from_z == z, c_of_z == c)
        arrive(wqkv.at[s, c, pl.ds(i * DB, DB), :], k_q1 + i, jnp.logical_not(same))
    for k in range(1, S):
        send(wqkv.at[s, c], wqkv.at[s, c], k_q2 + k, plane(k))
    f_plane(own_label)
    key_at = lax.broadcasted_iota(jnp.int32, (GP - LIVE_LANE, C * R), 1)
    first_row = lax.broadcasted_iota(jnp.int32, (GP - LIVE_LANE, C * R), 0) == 0
    dead = jnp.where(jnp.logical_and(first_row, key_at >= length), NEG, 0.0)
    k_tr[LIVE_LANE:, :] = dead.astype(BF16)
    v_tr[LIVE_LANE:, :] = jnp.zeros((GP - LIVE_LANE, C * R), BF16)
    g_t[:, :HF] = flip(g_n[:HF, :])
    g_t[:, HF:] = flip(g_n[HF:, :])
    for k in range(1, S):
        arrive(wqkv.at[s_from(k), c], k_q2 + k)
    send(wqkv.at[:, c], wqkv.at[:, c], k_q3, sib)
    arrive(bias_all.at[o], k_bias)
    arrive(wqkv.at[:, o], k_q3)
    bias_z = bias_all[c_of_z, z - CH * c_of_z]

    def project(block, half):
        at = half_rows(block, half)
        rows = a_all[at, :]
        made = nn(rows, wqkv[...].reshape(D, 3 * GP)) + bias_z[0:1, :]
        keys = made[:, :GP].astype(BF16)
        values = made[:, GP : 2 * GP].astype(BF16)
        k_n[at, :] = keys
        v_n[at, :] = values
        k_tr[:LIVE_LANE, at] = flip(keys)[:LIVE_LANE, :]
        v_tr[:LIVE_LANE, at] = flip(values)[:LIVE_LANE, :]

        def own():
            queries = made[:, 2 * GP :].astype(BF16).astype(F32) * (HD**-0.5)
            queries = jnp.where(lane == LIVE_LANE, 1.0, queries).astype(BF16)
            q_n[blk(block), :] = queries
            q_t[:, blk(block)] = flip(queries)
            a_t[:, blk(block)] = flip(rows)

        pl.when(half == c)(own)

    def project_own(i, carry):
        project(z, lax.rem(c + i, 2))
        return carry

    a_given = []

    def remote_when(src, dst, index, device, when):
        def go():
            remote(src, dst, index, device).start()

        pl.when(when)(go)

    lax.fori_loop(0, 2, project_own, 0)
    f_arrive(0)
    f_relay(own_label)
    for t in range(C - 1):
        if t == C - 2:
            f_arrive(1)
            for later in range(2, C - 1):
                f_step(later)
        for side, (label, block, ok) in enumerate(labels_of[t]):
            arrive(a_all.at[half_rows(block, c), :], k_a + 2 * t + side, ok)
        if t == C - 3:
            f_step(1)
        if t + 1 < C - 1:
            a_step(t + 1)
        for side, (label, block, ok) in enumerate(labels_of[t]):
            at = a_all.at[half_rows(block, c), :]
            remote_when(at, at, k_as + 2 * t + side, sib, ok)
            a_given.append((like_a, k_as + 2 * t + side, ok))

        def come(i, carry, t=t):
            side = i // 2
            block = jnp.where(side == 0, from_left(t)[0], from_right(t)[0])
            ok = jnp.where(side == 0, z - 1 - t >= 0, z + 1 + t < C)

            def other_half():
                at = a_all.at[half_rows(block, o), :]
                remote(at, at, k_as + 2 * t + side, sib).wait_recv()

            def both():
                pl.when(lax.rem(i, 2) == 1)(other_half)
                project(block, lax.rem(c + i, 2))

            pl.when(ok)(both)
            return carry

        lax.fori_loop(0, 4, come, 0)
        if t == C - 3:
            f_relay(labels_of[0])
    f_relay(labels_of[1])
    f_finish(own_label)
    f_finish(labels_of[0])

    TQ = 128

    def attend(block):
        def step(i, carry):
            at = pl.ds(pl.multiple_of(block * HF + i * TQ, TQ), TQ)
            queries = q_n[at, :]
            total = jnp.zeros((TQ, GP), F32)
            for h in range(HG):
                scores = nn(only_head(queries, h, True), k_tr[...])
                top = jnp.max(scores, axis=-1, keepdims=True)
                weights = jnp.exp(scores - top)
                norm_sum = jnp.sum(weights, axis=-1, keepdims=True)
                got = nn(weights.astype(BF16), v_n[...]) * (1.0 / norm_sum)
                total = total + only_head(got, h)
                lse[at, h : h + 1] = top + jnp.log(norm_sum)
            att_f[at, :] = total
            att_s[at, :] = total.astype(BF16)
            return carry

        lax.fori_loop(0, HF // TQ, step, 0)

    def attend_all(i, carry):
        block = lax.rem(z + 1 + i, C)
        attend(block)

        def give():
            remote(
                att_s.at[blk(block), :], att_r.at[blk(z), :], k_att + 1 + i, column(1 + i)
            ).start()

        def more_weights():
            for t in range(2, C - 1):
                f_arrive(t)

        pl.when(i < C - 1)(give)
        pl.when(i == 1)(more_weights)
        return carry

    lax.fori_loop(0, C, attend_all, 0)
    att_r[blk(z), :] = att_s[blk(z), :]

    f_finish(labels_of[1])
    for t in range(2, C - 1):
        f_relay(labels_of[t])
    for t in range(2, C - 1):
        f_finish(labels_of[t])
    owed.append((wo_sib, k_wo, None))
    for k in range(1, C):
        arrive(att_r.at[blk(z_from(k)), :], k_att + k)
        remote(att_s.at[blk(z), :], att_r.at[blk(z), :], k_att + k, column(k)).wait_send()
    arrive(wo_sib, k_wo)

    settle([entry for entry in owed if entry[0] is like_a])
    settle(a_given)
    owed[:] = [entry for entry in owed if entry[0] is not like_a]
    own_rows = pl.ds(pl.multiple_of(c * HF, HF), HF)
    hidden = frames[own_rows, :].astype(F32) + b_out
    for j in range(CH):
        hidden = hidden + nt(
            att_r[blk(CH * c + j), :], wf[:, 2 * FH + j * GP : 2 * FH + (j + 1) * GP]
        )
        hidden = hidden + nt(att_r[blk(CH * o + j), :], wo_sib[:, j * GP : (j + 1) * GP])
    hid[...] = hidden
    normed, unused = norm(hidden)
    z_all[own_rows, :] = (normed * ln2_gain + ln2_bias).astype(BF16)
    send(z_all.at[own_rows, :], z_all.at[own_rows, :], k_n2, sib)
    other_rows = pl.ds(pl.multiple_of(o * HF, HF), HF)
    z_t[:, own_rows] = flip(z_all[own_rows, :])
    arrive(z_all.at[other_rows, :], k_n2)
    z_t[:, other_rows] = flip(z_all[other_rows, :])

    TF = 256

    up_bias[...] = v_b_up[...].reshape(1, FH)

    def units(i, carry):
        cols = pl.ds(pl.multiple_of(i * TF, TF), TF)
        down = pl.ds(pl.multiple_of(FH + i * TF, TF), TF)
        upper = nn(z_all[...], wf[:, cols]) + up_bias[:, cols]
        cumulative = 0.5 * (1.0 + lax.erf(upper * INV_ROOT_TWO))
        act[:, cols] = (upper * cumulative).astype(BF16)
        slope = cumulative + upper * jnp.exp(-0.5 * upper * upper) * INV_ROOT_TAU
        grad_units = (nn(g_n[...], wf[:, down]) * slope).astype(BF16)
        gup[:, cols] = grad_units
        return carry

    lax.fori_loop(0, FH // TF, units, 0)

    def z_grad(i, carry):
        at = pl.ds(pl.multiple_of(i * 256, 256), 256)
        gz_s[:, at] = nt(gup[other_rows, :], wf[at, :FH]).astype(BF16)
        return carry

    lax.fori_loop(0, D // 256, z_grad, 0)
    send(gz_s, gz_r, k_gz, sib)

    def unit_grads(i, carry):
        cols = pl.ds(pl.multiple_of(i * TF, TF), TF)
        down = pl.ds(pl.multiple_of(FH + i * TF, TF), TF)
        wg[:, cols] = nn(z_t[...], gup[:, cols]).astype(BF16)
        wg[:, down] = nn(g_t[...], act[:, cols]).astype(BF16)
        return carry

    lax.fori_loop(0, FH // TF, unit_grads, 0)

    near_end = jnp.minimum(z, C - 1 - z)
    part_order = ((3, 3), (2, 0), (1, 2), (0, 1))

    def part_z(j):
        chosen = jnp.where(near_end == 0, part_order[j][0], part_order[j][1])
        return jnp.where(2 * z < C, chosen, C - 1 - chosen)

    def part_rows(j):
        return pl.ds(pl.multiple_of(part_z(j) * DB, 16), DB)

    part_a, part_b = slice(0, FH), slice(FH, 2 * FH)
    like_g = wg.at[pl.ds(0, DB), :]
    like_gh = wg.at[pl.ds(0, DB), pl.ds(0, FH)]

    def wg_far(j):
        index = k_wg + 6 * j
        own_z = part_z(j)
        send(wg.at[row_of(far, own_z), part_a], wg_t.at[j, 0], index, to_x, like=like_gh)
        send(wg.at[row_of(far, own_z), part_b], wg_t.at[j, 1], index + 1, to_y, like=like_gh)

    def wg_near(j):
        index = k_wg + 6 * j
        own_z = part_z(j)
        near = wg.at[row_of(near_x, own_z), part_a]
        send(near, wg_x.at[part_rows(j), part_a], index + 2, to_x, like=like_gh)
        near = wg.at[row_of(near_y, own_z), part_b]
        send(near, wg_y.at[part_rows(j), part_b], index + 3, to_y, like=like_gh)

    def add_into(at, cols, others):
        def step(i, carry):
            here = pl.ds(pl.multiple_of(cols.start + i * 256, 256), 256)
            total = wg[at, here].astype(F32)
            for other, rows, start in others:
                there = pl.ds(pl.multiple_of(start + i * 256, 256), 256)
                total = total + other[rows, there].astype(F32)
            wg[at, here] = total.astype(BF16)
            return carry

        lax.fori_loop(0, (cols.stop - cols.start) // 256, step, 0)

    def wg_second(j):
        index = k_wg + 6 * j
        own_z = part_z(j)
        arrive(wg_t.at[j, 0], index)
        at = row_of(near_y, own_z)
        add_into(at, part_a, [(wg_t.at[j, 0], slice(None), 0)])
        near = wg.at[at, part_a]
        send(near, wg_y.at[part_rows(j), part_a], index + 4, to_y, like=like_gh)
        arrive(wg_t.at[j, 1], index + 1)
        at = row_of(near_x, own_z)
        add_into(at, part_b, [(wg_t.at[j, 1], slice(None), 0)])
        near = wg.at[at, part_b]
        send(near, wg_x.at[part_rows(j), part_b], index + 5, to_x, like=like_gh)

    def wg_third(j):
        index = k_wg + 6 * j
        arrive(wg_x.at[part_rows(j), part_a], index + 2)
        arrive(wg_y.at[part_rows(j), part_b], index + 3)
        arrive(wg_y.at[part_rows(j), part_a], index + 4)
        arrive(wg_x.at[part_rows(j), part_b], index + 5)
        at = row_of(s, part_z(j))
        add_into(
            at, slice(0, 2 * FH), [(wg_x, part_rows(j), 0), (wg_y, part_rows(j), 0)]
        )
        if j < C - 1:
            hop = lax.rem(part_z(j) + C - z, C)
            remote(wg.at[at, :], wg_zr.at[hop - 1], k_wgz + hop, (s, part_z(j), c)).start()

    wg_far(0)
    wg_near(0)
    wg_far(1)

    gz_rows = jnp.concatenate(
        [nt(gup[own_rows, :], wf[i * 256 : (i + 1) * 256, :FH]) for i in range(D // 256)], axis=1
    )
    arrive(gz_r, k_gz)
    grad_z = gz_rows + gz_r[...].astype(F32)
    live_own = live_of(c * HF, HF)
    normed, inverse = norm(hid[...])
    scaled = grad_z * ln2_gain
    inner = (
        scaled
        - jnp.mean(scaled, axis=-1, keepdims=True)
        - normed * jnp.mean(scaled * normed, axis=-1, keepdims=True)
    )
    g_own = g_n[own_rows, :].astype(F32)
    grad_hidden = g_own + inner * inverse
    gin_o[own_rows, :] = grad_hidden
    low = grad_hidden.astype(BF16)
    sums[3:4, :] = jnp.sum(grad_z * normed, axis=0, keepdims=True)
    sums[4:5, :] = jnp.sum(grad_z, axis=0, keepdims=True)
    sums[5:6, :] = jnp.sum(g_own, axis=0, keepdims=True)
    sums[2:3, :] = jnp.sum(low.astype(F32), axis=0, keepdims=True)
    for j in range(CH):
        att_s[blk(CH * c + j), :] = nn(
            low, wf[:, 2 * FH + j * GP : 2 * FH + (j + 1) * GP]
        ).astype(BF16)
        att_s[blk(CH * o + j), :] = nn(low, wo_sib[:, j * GP : (j + 1) * GP]).astype(BF16)
    for k in range(1, C):
        send(att_s.at[blk(lax.rem(z + k, C)), :], gatt_r.at[blk(z), :], k_gatt + k, column(k))
    gatt_r[blk(z), :] = att_s[blk(z), :]
    ghl_t[...] = flip(low)
    def down_part(i, carry):
        at = pl.ds(pl.multiple_of(i * 256, 256), 256)
        part_s[:, at] = nt(act[other_rows, :], wf[at, FH : 2 * FH]).astype(BF16)
        return carry

    lax.fori_loop(0, D // 256, down_part, 0)
    send(part_s, part_r, k_part, sib)

    for j in range(CH):
        og_x[0, :, j * GP : (j + 1) * GP] = nn(ghl_t[...], att_r[blk(CH * o + j), :]).astype(BF16)
    remote(og_x.at[0], og_x.at[1], k_ox, sib).start()
    old = list(owed)
    owed.clear()
    dk_t[...] = jnp.zeros_like(dk_t)
    dv_t[...] = jnp.zeros_like(dv_t)
    TK = 512

    steps = C * R // TK

    def attend_back(polls):
        def block_step(b, carry):
            block = lax.rem(z + C - b, C)
            at = blk(block)

            def come():
                remote(gatt_r.at[at, :], gatt_r.at[at, :], k_gatt + b, sib).wait_recv()

            pl.when(b > 0)(come)
            gatt_t[...] = flip(gatt_r[at, :])
            product = gatt_r[at, :].astype(F32) * att_f[at, :]
            deltas = [
                jnp.sum(only_head(product, h), axis=-1, keepdims=True) for h in range(HG)
            ]
            for h in range(HG):
                dlt[:, h : h + 1] = deltas[h]
            dq_f[...] = jnp.zeros_like(dq_f)

            def step(i, carry):
                keys = pl.ds(pl.multiple_of(i * TK, TK), TK)
                for h in range(HG):
                    head = slice(HD * h, HD * (h + 1))
                    scores = nn(only_head(q_n[at, :], h, True), k_tr[:, keys])
                    weights = jnp.exp(scores - lse[at, h : h + 1])
                    grads = nn(only_head(gatt_r[at, :], h), v_tr[:, keys])
                    grad_scores = (weights * (grads - dlt[:, h : h + 1])).astype(BF16)
                    dv_t[head, keys] += nn(gatt_t[head, :], weights.astype(BF16))
                    dk_t[head, keys] += nn(q_t[head, at], grad_scores)
                    dq_f[...] += only_head(nn(grad_scores, k_n[keys, :]), h)
                for number, poll in polls:
                    pl.when(b * steps + i == number)(poll)
                return carry

            lax.fori_loop(0, steps, step, 0)
            g_nat[at, 2 * GP :] = (dq_f[...] * (HD**-0.5)).astype(BF16)
            return carry

        lax.fori_loop(0, C, block_step, 0)

    def og_reduce():
        for k in range(1, S):
            arrive(og_r.at[k - 1], k_og + k)
        own = pl.ds(pl.multiple_of(s * PB, 64), PB)
        total = og_x[0, own, :].astype(F32)
        for k in range(1, S):
            total = total + og_r[k - 1].astype(F32)
        og_z[...] = total.astype(BF16)
        for k in range(1, C):
            at = pl.ds(pl.multiple_of(lax.rem(z + k, C) * DB, 16), DB)
            send(og_z.at[at, :], og_zr.at[k - 1], k_ogz + k, column(k))

    def poll_a():
        wg_second(0)
        wg_near(1)

    def poll_b():
        wg_second(1)
        wg_far(2)
        wg_near(2)

    def poll_c():
        wg_second(2)
        wg_far(3)
        wg_near(3)

    down_rows = jnp.concatenate(
        [nt(act[own_rows, :], wf[i * 256 : (i + 1) * 256, FH : 2 * FH]) for i in range(D // 256)],
        axis=1,
    )
    arrive(part_r, k_part)
    out_rows = live_own * (hid[...] + down_rows + part_r[...].astype(F32) + b_down)
    out_o[own_rows, :] = out_rows.astype(BF16)
    send(out_o.at[own_rows, :], out_o.at[own_rows, :], k_out, sib)
    for i in range(2):
        sums[pl.ds(6 + 2 * c + i, 1), :] = jnp.sum(
            gup[:, i * D : (i + 1) * D].astype(F32), axis=0, keepdims=True
        )
    arrive(og_x.at[1], k_ox)
    remote(og_x.at[0], og_x.at[1], k_ox, sib).wait_send()
    for j in range(CH):
        cols = slice(j * GP, (j + 1) * GP)
        own_part = nn(ghl_t[...], att_r[blk(CH * c + j), :])
        og_x[0, :, cols] = (own_part + og_x[1, :, cols].astype(F32)).astype(BF16)
    attend_back(
        (
            (0, poll_a),
            (3, poll_b),
            (6, lambda: wg_third(0)),
            (10, lambda: wg_third(1)),
            (11, poll_c),
        )
    )

    for i in range(C):
        cols = pl.ds(pl.multiple_of(i * R + o * HF, HF), HF)
        dkv_s[i, 0] = dk_t[:, cols].astype(BF16)
        dkv_s[i, 1] = dv_t[:, cols].astype(BF16)
    send(dkv_s, dkv_r, k_dkv, sib)
    wg_third(2)
    arrive(dkv_r, k_dkv)

    def finish(block):
        cols = pl.ds(pl.multiple_of(block * R + c * HF, HF), HF)
        at = blk(block)
        keys_t = dk_t[:, cols] + dkv_r[block, 0].astype(F32)
        values_t = dv_t[:, cols] + dkv_r[block, 1].astype(F32)
        none = jnp.zeros((GP - LIVE_LANE, HF), F32)
        g_nat[at, :GP] = jnp.concatenate([keys_t, none], axis=0).T.astype(BF16)
        g_nat[at, GP : 2 * GP] = jnp.concatenate([values_t, none], axis=0).T.astype(BF16)
        ga_s[at, :] = nt(g_nat[at, :], wqkv[...].reshape(D, 3 * GP)).astype(BF16)

    def finish_all(b, carry):
        finish(b)
        return carry

    lax.fori_loop(0, C, finish_all, 0)

    like_ga = ga_s.at[pl.ds(0, HF), :]

    def ga_send(t, side):
        target = jnp.where(side == 0, C - 1 - t, t)
        device = (s, jnp.clip(z + 1 - 2 * side, 0, C - 1), c)
        remote(ga_s.at[blk(target), :], ga_r.at[t, side], k_ga + 2 * t + side, device).start()

    def ga_ahead(t, side):
        return C - 1 - t > z if side == 0 else t < z

    for t in range(C - 1):
        for side in range(2):
            behind = z >= 1 if side == 0 else z + 1 < C
            first = jnp.logical_and(ga_ahead(t, side), jnp.logical_not(behind))
            pl.when(first)(lambda t=t, side=side: ga_send(t, side))
            owed.append((like_ga, k_ga + 2 * t + side, ga_ahead(t, side)))

    def ga_hop(u):
        for i in range(2):
            side = jnp.where(2 * z < C, i, 1 - i)
            t = jnp.where(side == 0, u - z, u - (C - 1 - z))
            target = jnp.where(side == 0, C - 1 - t, t)
            inner = jnp.logical_and(z >= 1, z + 1 < C)
            ahead = jnp.where(side == 0, target > z, target < z)
            ok = jnp.logical_and(jnp.logical_and(t >= 0, inner), ahead)

            def add(t=t, side=side, target=target):
                at = blk(target)
                arrive(ga_r.at[t, side], k_ga + 2 * t + side)
                ga_s[at, :] = (ga_s[at, :].astype(F32) + ga_r[t, side].astype(F32)).astype(BF16)
                ga_send(t, side)

            pl.when(ok)(add)

    wg_second(3)
    for k in range(1, S):
        at = pl.ds(pl.multiple_of(lax.rem(s + k, S) * PB, 64), PB)
        send(og_x.at[0, at, :], og_r.at[k - 1], k_og + k, plane(k))
    column_sum = jnp.sum(g_nat[...].astype(F32), axis=0, keepdims=True)
    sums[pl.ds(10 + z, 1), :] = column_sum
    pair_lane = lax.broadcasted_iota(jnp.int32, (PB, 128), 1)
    for i in range(S):
        got = nn(a_t[i * PB : (i + 1) * PB, :], g_nat[...])
        qg[i] = got.reshape(2, CH * DB, 3 * GP).astype(BF16)
        weights = wqkv[i].reshape(PB, 3 * GP).astype(F32)
        with_a = jnp.sum(got * weights, axis=-1, keepdims=True)
        alone = jnp.sum(weights * column_sum, axis=-1, keepdims=True)
        pairs[i * PB : (i + 1) * PB, :] = jnp.where(
            pair_lane == 0, with_a, jnp.where(pair_lane == 1, alone, 0.0)
        )
    send(qg.at[:, o], qg_r, k_qx, sib)
    turned = pairs[...].T
    sums[0:1, :] = (turned[0:1, :] - ln1_bias * turned[1:2, :]) / ln1_gain
    sums[1:2, :] = turned[1:2, :]
    arrive(qg_r, k_qx)
    for i in range(S):
        qg_r[i] = (qg_r[i].astype(F32) + qg[i, c].astype(F32)).astype(BF16)
    for k in range(1, S):
        send(qg_r.at[lax.rem(s + k, S)], qg_p.at[k - 1], k_qp + k, plane(k))

    sum_p[s] = sums[...]
    for k in range(1, S):
        send(sum_p.at[s], sum_p.at[s], k_sp + k, plane(k))
    settle(old)
    arrive(out_o.at[other_rows, :], k_out)
    store(out_o, out_h)
    wg_third(3)
    for hop in range(1, C):
        owed.append((like_g, k_wgz + hop, None))
    og_reduce()
    ga_hop(1)
    for u in range(2, C - 1):
        ga_hop(u)
    for k in range(1, S):
        arrive(sum_p.at[s_from(k)], k_sp + k)
    total = sum_p[0]
    for k in range(1, S):
        total = total + sum_p[k]
    sum_z[z] = total
    for k in range(1, C):
        send(sum_z.at[z], sum_z.at[z], k_sz + k, column(k))
    for k in range(1, S):
        arrive(qg_p.at[k - 1], k_qp + k)
    total = qg_r[s].astype(F32)
    for k in range(1, S):
        total = total + qg_p[k - 1].astype(F32)
    qg_z[...] = total.reshape(CH, DB, 3 * GP).astype(BF16)
    for i in range(CH):
        to_z = CH * c + i
        same = jnp.logical_and(to_z == z, c_of_z == c)
        for j in range(CH):
            ok = jnp.logical_and(z - CH * c_of_z == j, jnp.logical_not(same))

            def go(i=i, j=j, to_z=to_z):
                pltpu.make_async_remote_copy(
                    src_ref=qg_z.at[i],
                    dst_ref=qg_zr.at[j],
                    send_sem=ls.at[CH + i],
                    recv_sem=rs.at[k_qz + j],
                    device_id=(s, to_z, c_of_z),
                    device_id_type=MESH,
                ).start()

            pl.when(ok)(go)

        def keep(i=i):
            qg_zr[z - CH * c] = qg_z[i]

        pl.when(same)(keep)

    own_block = blk(z)
    ga_f[...] = ga_s[own_block, :].astype(F32)
    for t in range(C - 1):
        for side in range(2):
            target = C - 1 - t if side == 0 else t
            behind = z >= 1 if side == 0 else z + 1 < C

            def add(t=t, side=side):
                arrive(ga_r.at[t, side], k_ga + 2 * t + side)
                ga_f[...] += ga_r[t, side].astype(F32)

            pl.when(jnp.logical_and(target == z, behind))(add)
    grad_a = ga_f[...]
    normed, inverse = norm(frames[own_rows, :].astype(F32))
    scaled = grad_a * ln1_gain
    inner = (
        scaled
        - jnp.mean(scaled, axis=-1, keepdims=True)
        - normed * jnp.mean(scaled * normed, axis=-1, keepdims=True)
    )
    gin_o[own_rows, :] = gin_o[own_rows, :] + inner * inverse
    send(gin_o.at[own_rows, :], gin_o.at[own_rows, :], k_gin, sib)
    store(gin_o.at[own_rows, :], gin_h.at[own_rows, :])
    def last(own, got, index, to):
        for k in range(1, C):
            arrive(got.at[k - 1], index + k)
        total = own.astype(F32)
        for k in range(1, C):
            total = total + got[k - 1].astype(F32)
        to[...] = total

    last(wg[rows_of(s * C + z), :], wg_zr, k_wgz, gf_o)
    last(og_z[pl.ds(pl.multiple_of(z * DB, 16), DB), :], og_zr, k_ogz, go_o)
    store(gf_o, gf_h)
    store(go_o, go_h)
    for j in range(CH):
        same = jnp.logical_and(CH * c + j == z, c_of_z == c)
        arrive(qg_zr.at[j], k_qz + j, jnp.logical_not(same))
    gq_o[...] = qg_zr[...].astype(F32)
    store(gq_o, gq_h)
    for k in range(1, C):
        arrive(sum_z.at[z_from(k)], k_sz + k)
    total = sum_z[0]
    for k in range(1, C):
        total = total + sum_z[k]
    sum_c[c] = total
    send(sum_c.at[c], sum_c.at[c], k_sc, sib)
    arrive(sum_c.at[o], k_sc)
    sums_o[...] = sum_c[0] + sum_c[1]
    store(sums_o, sums_h)
    arrive(gin_o.at[other_rows, :], k_gin)
    store(gin_o.at[other_rows, :], gin_h.at[other_rows, :])

    settle(owed)
    for copy in stored:
        copy.wait()
    for j in range(CH):
        same = jnp.logical_and(CH * c + j == z, c_of_z == c)

        def done_weights(j=j):
            pltpu.make_async_remote_copy(
                src_ref=wqkv_own.at[j],
                dst_ref=wqkv_own.at[j],
                send_sem=ls.at[j],
                recv_sem=rs.at[k_q1],
                device_id=sib,
                device_id_type=MESH,
            ).wait_send()
            pltpu.make_async_remote_copy(
                src_ref=qg_z.at[j],
                dst_ref=qg_z.at[j],
                send_sem=ls.at[CH + j],
                recv_sem=rs.at[k_qz],
                device_id=sib,
                device_id_type=MESH,
            ).wait_send()

        pl.when(jnp.logical_not(same))(done_weights)
    assert next_sem[0] <= SEMS


def unpack_kernel(
    CH,
    output,
    grad_input,
    gf_h,
    go_h,
    gq_h,
    sums_h,
    output_o,
    grad_input_o,
    query_o,
    key_o,
    value_o,
    out_o,
    up_o,
    down_o,
    gain1_o,
    bias1_o,
    b_query_o,
    b_value_o,
    b_out_o,
    gain2_o,
    bias2_o,
    b_up_o,
    b_down_o,
    gf,
    go,
    gq,
    sums,
    sem,
):
    c = lax.axis_index("tp")
    FH = up_o.shape[1]
    D = sums.shape[1]
    GP = 256
    pairs = ((output, output_o), (grad_input, grad_input_o))
    pairs += ((gf_h, gf), (go_h, go), (gq_h, gq), (sums_h, sums))
    copies = [
        pltpu.make_async_copy(src, dst, sem.at[i]) for i, (src, dst) in enumerate(pairs)
    ]
    for copy in copies:
        copy.start()
    for copy in copies[2:]:
        copy.wait()
    for i, to in enumerate((key_o, value_o, query_o)):
        cols = slice(i * GP, (i + 1) * GP)
        to[...] = ungroup(gq[0, :, cols], gq[1, :, cols])
    out_o[...] = ungroup(go[:, :GP], go[:, GP : 2 * GP])
    up_o[...] = gf[:, :FH]
    down_o[...] = gf[:, FH:]
    for i, to in enumerate((gain1_o, bias1_o, b_out_o, gain2_o, bias2_o, b_down_o)):
        to[...] = sums[i, :]
    for i in range(FH // D):
        b_up_o[i * D : (i + 1) * D] = sums[6 + 2 * c + i, :]
    for to, start in ((b_value_o, GP), (b_query_o, 2 * GP)):
        row = [sums[pl.ds(10 + CH * c + j, 1), start : start + GP] for j in range(CH)]
        to[...] = ungroup(row[0], row[1])[0, :]
    for copy in copies[:2]:
        copy.wait()


SEMS = 224


def fits(frames, w_query, w_up):
    shards, ctx, cores = (lax.axis_size(name) for name in ("shard", "ctx", "tp"))
    slot_count, seg_rows, width = frames.shape
    heads = w_query.shape[1] * cores // HD
    return (
        slot_count == 1
        and cores == 2
        and ctx % 2 == 0
        and ctx == 4
        and shards == 4
        and heads == 3 * ctx
        and width % (16 * shards * ctx) == 0
        and width % 256 == 0
        and seg_rows % 512 == 0
        and w_up.shape[1] % 512 == 0
        and w_up.shape[1] == 2 * width
        and ctx * seg_rows <= 2048
        and width <= 768
        and w_up.shape[1] <= 1536
    )


def fast_layer(
    frames,
    lengths,
    cotangent,
    ln1_gain,
    ln1_bias,
    w_query,
    b_query,
    w_key,
    w_value,
    b_value,
    w_out,
    b_out,
    ln2_gain,
    ln2_bias,
    w_up,
    b_up,
    w_down,
    b_down,
):
    S, C = lax.axis_size("shard"), lax.axis_size("ctx")
    unused, R, D = frames.shape
    FH = w_up.shape[1]
    HG, CH = 3, C // 2
    G, GP = HG * HD, 256
    DB = D // (S * C)
    HF = R // 2
    PB = C * DB
    T = C * R

    WF = 2 * FH + CH * GP
    vmem = pl.BlockSpec(memory_space=pltpu.VMEM)
    V = pltpu.VMEM
    dims = (S, C, R, D, GP, HG, FH)
    scratch = [
        pltpu.SemaphoreType.DMA((SEMS,)),
        pltpu.SemaphoreType.DMA((SEMS,)),
        pltpu.SemaphoreType.DMA((2 * CH,)),
        pltpu.SemaphoreType.DMA((7,)),
        V((R, D), BF16),
        V((R, D), F32),
        V((DB, 2 * FH), F32),
        V((DB, CH * GP), F32),
        V((CH, DB, 3 * GP), F32),
        V((16, D), F32),
        V((CH, DB, 3 * GP), BF16),
        V((CH, 8, 3 * GP), F32),
        V((1, FH), F32),
        V((T, D), BF16),
        V((D, C * HF), BF16),
        V((S, 2, CH * DB, 3 * GP), BF16),
        V((2, CH, 8, 3 * GP), F32),
        V((D, WF), BF16),
        V((D, CH * GP), BF16),
        V((GP, T), BF16),
        V((GP, T), BF16),
        V((T, GP), BF16),
        V((T, GP), BF16),
        V((C * HF, GP), BF16),
        V((GP, C * HF), BF16),
        V((C * HF, 8), F32),
        V((C * HF, GP), F32),
        V((C * HF, GP), BF16),
        V((C * HF, GP), BF16),
        V((HF, D), F32),
        V((R, D), BF16),
        V((D, R), BF16),
        V((R, D), BF16),
        V((D, R), BF16),
        V((R, FH), BF16),
        V((R, FH), BF16),
        V((HF, D), BF16),
        V((HF, D), BF16),
        V((HF, D), BF16),
        V((HF, D), BF16),
        V((D, HF), BF16),
        V((C * HF, GP), BF16),
        V((GP, HF), BF16),
        V((D, 2 * FH), BF16),
        V((C, 2, DB, FH), BF16),
        V((PB, 2 * FH), BF16),
        V((PB, 2 * FH), BF16),
        V((C - 1, DB, 2 * FH), BF16),
        V((2, D, CH * GP), BF16),
        V((S - 1, PB, CH * GP), BF16),
        V((PB, CH * GP), BF16),
        V((C - 1, DB, CH * GP), BF16),
        V((G, T), F32),
        V((G, T), F32),
        V((HF, GP), F32),
        V((HF, 8), F32),
        V((C, 2, G, HF), BF16),
        V((C, 2, G, HF), BF16),
        V((C - 1, 2, HF, D), BF16),
        V((HF, D), F32),
        V((S, 2, CH * DB, 3 * GP), BF16),
        V((S, CH * DB, 3 * GP), BF16),
        V((S - 1, CH * DB, 3 * GP), BF16),
        V((CH, DB, 3 * GP), BF16),
        V((CH, DB, 3 * GP), BF16),
        V((16, D), F32),
        V((D, 128), F32),
        V((S, 16, D), F32),
        V((C, 16, D), F32),
        V((2, 16, D), F32),
    ]
    outs = (
        jax.ShapeDtypeStruct((R, D), BF16),
        jax.ShapeDtypeStruct((R, D), F32),
        jax.ShapeDtypeStruct((DB, 2 * FH), F32),
        jax.ShapeDtypeStruct((DB, CH * GP), F32),
        jax.ShapeDtypeStruct((CH, DB, 3 * GP), F32),
        jax.ShapeDtypeStruct((16, D), F32),
    )
    output, grad_input, gf, go, gq, sums = pl.pallas_call(
        functools.partial(layer_kernel, dims),
        out_shape=outs,
        in_specs=[vmem, vmem, pl.BlockSpec(memory_space=pltpu.SMEM)] + [vmem] * 15,
        out_specs=[pl.BlockSpec(memory_space=pltpu.HBM)] * 6,
        scratch_shapes=scratch,
        compiler_params=pltpu.CompilerParams(
            collective_id=0, has_side_effects=True, vmem_limit_bytes=63 << 20
        ),
    )(
        frames[0],
        cotangent[0],
        lengths,
        ln1_gain,
        ln1_bias,
        b_out,
        ln2_gain,
        ln2_bias,
        b_down,
        b_up,
        b_query,
        b_value,
        w_query,
        w_key,
        w_value,
        w_up,
        w_down.T,
        w_out.T,
    )
    flat = [D, D, CH * G, CH * G, D, D, D, FH, D]
    results = pl.pallas_call(
        functools.partial(unpack_kernel, CH),
        out_shape=[
            jax.ShapeDtypeStruct((R, D), BF16),
            jax.ShapeDtypeStruct((R, D), F32),
            jax.ShapeDtypeStruct((DB, CH * G), F32),
            jax.ShapeDtypeStruct((DB, CH * G), F32),
            jax.ShapeDtypeStruct((DB, CH * G), F32),
            jax.ShapeDtypeStruct((DB, CH * G), F32),
            jax.ShapeDtypeStruct((DB, FH), F32),
            jax.ShapeDtypeStruct((DB, FH), F32),
        ]
        + [jax.ShapeDtypeStruct((length,), F32) for length in flat],
        in_specs=[pl.BlockSpec(memory_space=pltpu.HBM)] * 6,
        out_specs=[vmem] * 17,
        scratch_shapes=[
            V((DB, 2 * FH), F32),
            V((DB, CH * GP), F32),
            V((CH, DB, 3 * GP), F32),
            V((16, D), F32),
            pltpu.SemaphoreType.DMA((6,)),
        ],
        compiler_params=pltpu.CompilerParams(vmem_limit_bytes=63 << 20),
    )(output, grad_input, gf, go, gq, sums)
    output, grad_input, g_query, g_key, g_value, g_out, g_up, g_down = results[:8]
    g1, s1, bq, bv, bo, g2, s2, bu, bd = results[8:]
    return (
        output[None],
        grad_input[None],
        g1,
        s1,
        g_query,
        bq,
        g_key,
        g_value,
        bv,
        g_out.T,
        bo,
        g2,
        s2,
        g_up,
        bu,
        g_down.T,
        bd,
    )


def per_device(frames, lengths, cotangent, *params):
    if fits(frames, params[2], params[11]):
        return fast_layer(frames, lengths, cotangent, *params)
    return plain_layer(frames, lengths, cotangent, *params)


def solution(mesh):
    in_specs = (
        P("shard", "ctx", None),
        P("shard"),
        P("shard", "ctx", None),
        P(),
        P(),
        P(("shard", "ctx"), "tp"),
        P("tp"),
        P(("shard", "ctx"), "tp"),
        P(("shard", "ctx"), "tp"),
        P("tp"),
        P("tp", ("shard", "ctx")),
        P(),
        P(),
        P(),
        P(("shard", "ctx"), "tp"),
        P("tp"),
        P("tp", ("shard", "ctx")),
        P(),
    )
    out_specs = (
        P("shard", "ctx", None),
        P("shard", "ctx", None),
        P(),
        P(),
        P(("shard", "ctx"), "tp"),
        P("tp"),
        P(("shard", "ctx"), "tp"),
        P(("shard", "ctx"), "tp"),
        P("tp"),
        P("tp", ("shard", "ctx")),
        P(),
        P(),
        P(),
        P(("shard", "ctx"), "tp"),
        P("tp"),
        P("tp", ("shard", "ctx")),
        P(),
    )
    return jax.shard_map(
        per_device, mesh=mesh, in_specs=in_specs, out_specs=out_specs, check_vma=False
    )
```

```python
import functools
import math

import jax
import jax.numpy as jnp
from jax import lax
from jax.experimental import pallas as pl
from jax.experimental.pallas import tpu as pltpu
from jax.sharding import PartitionSpec as P

HD = 64


EPSILON = 1e-05
INV_ROOT_TWO = 0.7071067811865476
INV_ROOT_TAU = 0.3989422804014327


def norm_rows(values, gain, shift):
    centred = values - jnp.mean(values, axis=-1, keepdims=True)
    inverse = lax.rsqrt(jnp.mean(centred * centred, axis=-1, keepdims=True) + EPSILON)
    normed = centred * inverse
    return (normed * gain + shift, normed, inverse)


def norm_back(grad_rows, normed, inverse, gain):
    scaled = grad_rows * gain
    inner = (
        scaled
        - jnp.mean(scaled, axis=-1, keepdims=True)
        - normed * jnp.mean(scaled * normed, axis=-1, keepdims=True)
    )
    return (inner * inverse, jnp.sum(grad_rows * normed, axis=0), jnp.sum(grad_rows, axis=0))


def gelu_slope(values):
    return (
        0.5 * (1.0 + lax.erf(values * INV_ROOT_TWO))
        + values * jnp.exp(-0.5 * values * values) * INV_ROOT_TAU
    )


def pair_scores(queries, block_keys, score_scale):
    return (
        jnp.einsum("qhd,khd->hqk", queries, block_keys, preferred_element_type=jnp.float32)
        * score_scale
    )


def live_weights(scores, query_live, key_live, log_totals):
    both_live = query_live[None, :, None] & key_live[None, None, :]
    return jnp.where(both_live, jnp.exp(scores - log_totals[:, :, None]), 0.0)


def in_blocks(array, block_rows):
    return array.reshape((array.shape[0] // block_rows, block_rows) + array.shape[1:])


def slot_forward(queries, slot_keys, slot_values, query_live, key_live, key_block, score_scale):
    seg_rows, head_count, head_dim = queries.shape
    key_starts = jnp.arange(slot_keys.shape[0] // key_block, dtype=jnp.int32) * key_block
    blocks = (
        in_blocks(slot_keys, key_block),
        in_blocks(slot_values, key_block),
        in_blocks(key_live, key_block),
        key_starts,
    )
    start_state = (
        jnp.full((head_count, seg_rows), -jnp.inf, jnp.float32),
        jnp.zeros((head_count, seg_rows), jnp.float32),
    )

    def totals_step(carried, scan_item):
        block_keys, block_values, block_live, block_start = scan_item
        running_max, running_sum = carried
        scores = jnp.where(
            block_live[None, None, :], pair_scores(queries, block_keys, score_scale), -jnp.inf
        )
        new_max = jnp.maximum(running_max, jnp.max(scores, axis=-1))
        new_sum = running_sum * jnp.exp(running_max - new_max) + jnp.sum(
            jnp.exp(scores - new_max[:, :, None]), axis=-1
        )
        return ((new_max, new_sum), None)

    def whole_slot(ignored):
        final_state, unused = lax.scan(totals_step, start_state, blocks)
        log_totals = final_state[0] + jnp.log(final_state[1])

        def output_step(output_sum, scan_item):
            block_keys, block_values, block_live, block_start = scan_item
            weights_here = live_weights(
                pair_scores(queries, block_keys, score_scale), query_live, block_live, log_totals
            ).astype(jnp.bfloat16)
            return (
                output_sum
                + jnp.einsum(
                    "hqk,khd->qhd", weights_here, block_values, preferred_element_type=jnp.float32
                ),
                None,
            )

        attended, unused_too = lax.scan(
            output_step, jnp.zeros((seg_rows, head_count, head_dim), jnp.float32), blocks
        )
        return (log_totals, attended)

    return whole_slot(0)


def slot_back(
    queries,
    grad_att,
    log_totals,
    delta,
    slot_keys,
    slot_values,
    query_live,
    key_live,
    key_block,
    score_scale,
):
    seg_rows, head_count, head_dim = queries.shape
    key_starts = jnp.arange(slot_keys.shape[0] // key_block, dtype=jnp.int32) * key_block
    blocks = (
        in_blocks(slot_keys, key_block),
        in_blocks(slot_values, key_block),
        in_blocks(key_live, key_block),
        key_starts,
    )

    def grad_step(grad_query, scan_item):
        block_keys, block_values, block_live, block_start = scan_item
        partial_value = grad_query
        weights_full = live_weights(
            pair_scores(queries, block_keys, score_scale), query_live, block_live, log_totals
        )
        grad_probs = jnp.einsum(
            "qhd,khd->hqk", grad_att, block_values, preferred_element_type=jnp.float32
        )
        grad_scores = (weights_full * (grad_probs - delta[:, :, None])).astype(jnp.bfloat16)
        partial_value = (
            partial_value
            + jnp.einsum(
                "hqk,khd->qhd", grad_scores, block_keys, preferred_element_type=jnp.float32
            )
            * score_scale
        )
        grad_value = jnp.einsum(
            "hqk,qhd->khd",
            weights_full.astype(jnp.bfloat16),
            grad_att,
            preferred_element_type=jnp.float32,
        )
        grad_key = (
            jnp.einsum("hqk,qhd->khd", grad_scores, queries, preferred_element_type=jnp.float32)
            * score_scale
        )
        return (partial_value, (grad_key, grad_value))

    def whole_slot(ignored):
        grad_query, key_parts = lax.scan(
            grad_step, jnp.zeros((seg_rows, head_count, head_dim), jnp.float32), blocks
        )
        return (
            grad_query,
            key_parts[0].reshape(slot_keys.shape),
            key_parts[1].reshape(slot_keys.shape),
        )

    return whole_slot(0)


def plain_layer(
    frames,
    lengths,
    cotangent,
    ln1_gain,
    ln1_bias,
    w_query,
    b_query,
    w_key,
    w_value,
    b_value,
    w_out,
    b_out,
    ln2_gain,
    ln2_bias,
    w_up,
    b_up,
    w_down,
    b_down,
):
    slot_count, seg_rows, model_width = frames.shape
    row_count = slot_count * seg_rows
    head_cols = w_query.shape[1]
    head_count = head_cols // HD
    seq_length = seg_rows * lax.axis_size("ctx")
    seg_start = lax.axis_index("ctx") * seg_rows
    score_scale = HD ** (-0.5)
    key_block = math.gcd(seq_length, 512)
    positions = seg_start + jnp.arange(seg_rows, dtype=jnp.int32)
    query_live = positions[None, :] < lengths[:, None]
    key_live = jnp.arange(seq_length, dtype=jnp.int32)[None, :] < lengths[:, None]
    live_rows = query_live.astype(jnp.float32).reshape(row_count, 1)
    weight_query, weight_key, weight_value, weight_out = (
        lax.all_gather(w_query, ("shard", "ctx"), axis=0, tiled=True),
        lax.all_gather(w_key, ("shard", "ctx"), axis=0, tiled=True),
        lax.all_gather(w_value, ("shard", "ctx"), axis=0, tiled=True),
        lax.all_gather(w_out, ("shard", "ctx"), axis=1, tiled=True),
    )
    frames_flat = frames.astype(jnp.float32).reshape(row_count, model_width)
    first, normed_one, inverse_one = norm_rows(frames_flat, ln1_gain, ln1_bias)
    first_low = first.astype(jnp.bfloat16)
    queries = (
        jnp.dot(first_low, weight_query, preferred_element_type=jnp.float32) + b_query
    ).astype(jnp.bfloat16)
    keys_local = jnp.dot(first_low, weight_key, preferred_element_type=jnp.float32).astype(
        jnp.bfloat16
    )
    values_local = (
        jnp.dot(first_low, weight_value, preferred_element_type=jnp.float32) + b_value
    ).astype(jnp.bfloat16)
    keys_all, values_all = (
        lax.all_gather(
            keys_local.reshape(slot_count, seg_rows, head_cols), "ctx", axis=1, tiled=True
        ),
        lax.all_gather(
            values_local.reshape(slot_count, seg_rows, head_cols), "ctx", axis=1, tiled=True
        ),
    )
    query_heads = queries.reshape(slot_count, seg_rows, head_count, HD)
    key_heads = keys_all.reshape(slot_count, seq_length, head_count, HD)
    value_heads = values_all.reshape(slot_count, seq_length, head_count, HD)
    slot = 0
    log_totals, attended_slot = slot_forward(
        query_heads[slot],
        key_heads[slot],
        value_heads[slot],
        query_live[slot],
        key_live[slot],
        key_block,
        score_scale,
    )
    totals_list = [log_totals]
    attended_list = [attended_slot]
    attended = jnp.stack(attended_list).reshape(row_count, head_cols)
    attended_low = attended.astype(jnp.bfloat16)
    attn_sum = lax.psum(
        jnp.dot(attended_low, weight_out, preferred_element_type=jnp.float32).astype(jnp.bfloat16),
        "tp",
    ).astype(jnp.float32)
    hidden = frames_flat + attn_sum + b_out
    weight_up, weight_down = (
        lax.all_gather(w_up, ("shard", "ctx"), axis=0, tiled=True),
        lax.all_gather(w_down, ("shard", "ctx"), axis=1, tiled=True),
    )
    second, normed_two, inverse_two = norm_rows(hidden, ln2_gain, ln2_bias)
    second_low = second.astype(jnp.bfloat16)
    upper = jnp.dot(second_low, weight_up, preferred_element_type=jnp.float32) + b_up
    activated = jax.nn.gelu(upper, approximate=False).astype(jnp.bfloat16)
    mlp_sum = lax.psum(
        jnp.dot(activated, weight_down, preferred_element_type=jnp.float32).astype(jnp.bfloat16),
        "tp",
    ).astype(jnp.float32)
    output = (
        (live_rows * (hidden + mlp_sum + b_down))
        .astype(jnp.bfloat16)
        .reshape(slot_count, seg_rows, model_width)
    )
    grad_out = live_rows * cotangent.astype(jnp.float32).reshape(row_count, model_width)
    grad_out_low = grad_out.astype(jnp.bfloat16)
    grad_b_down = jnp.sum(grad_out, axis=0)
    grad_w_down = jnp.einsum(
        "rf,rd->fd", activated, grad_out_low, preferred_element_type=jnp.float32
    )
    grad_act = jnp.einsum(
        "rd,fd->rf", grad_out_low, weight_down, preferred_element_type=jnp.float32
    )
    grad_upper = (grad_act * gelu_slope(upper)).astype(jnp.bfloat16)
    grad_b_up = jnp.sum(grad_upper.astype(jnp.float32), axis=0)
    grad_w_up = jnp.einsum("rd,rf->df", second_low, grad_upper, preferred_element_type=jnp.float32)
    grad_second = lax.psum(
        jnp.einsum("rf,df->rd", grad_upper, weight_up, preferred_element_type=jnp.float32).astype(
            jnp.bfloat16
        ),
        "tp",
    ).astype(jnp.float32)
    grad_norm_two, grad_ln2_gain, grad_ln2_bias = norm_back(
        grad_second, normed_two, inverse_two, ln2_gain
    )
    grad_hidden = grad_out + grad_norm_two
    grad_hidden_low = grad_hidden.astype(jnp.bfloat16)
    grad_b_out = jnp.sum(grad_hidden_low.astype(jnp.float32), axis=0)
    grad_w_out = jnp.einsum(
        "rc,rd->cd", attended_low, grad_hidden_low, preferred_element_type=jnp.float32
    )
    grad_att = jnp.einsum(
        "rd,cd->rc", grad_hidden_low, weight_out, preferred_element_type=jnp.float32
    ).astype(jnp.bfloat16)
    delta = jnp.sum(
        (grad_att.astype(jnp.float32) * attended).reshape(row_count, head_count, HD), axis=-1
    )
    delta_heads = delta.reshape(slot_count, seg_rows, head_count)
    grad_att_heads = grad_att.reshape(slot_count, seg_rows, head_count, HD)
    slot = 0
    grad_query_slot, key_part, value_part = slot_back(
        query_heads[slot],
        grad_att_heads[slot],
        totals_list[slot],
        delta_heads[slot].T,
        key_heads[slot],
        value_heads[slot],
        query_live[slot],
        key_live[slot],
        key_block,
        score_scale,
    )
    grad_query_list = [grad_query_slot]
    key_part_list = [key_part.reshape(seq_length, head_cols)]
    value_part_list = [value_part.reshape(seq_length, head_cols)]
    grad_keys, grad_values = (
        lax.psum_scatter(
            jnp.stack(key_part_list).astype(jnp.bfloat16), "ctx", scatter_dimension=1, tiled=True
        ).astype(jnp.float32),
        lax.psum_scatter(
            jnp.stack(value_part_list).astype(jnp.bfloat16), "ctx", scatter_dimension=1, tiled=True
        ).astype(jnp.float32),
    )
    grad_query_low = jnp.stack(grad_query_list).reshape(row_count, head_cols).astype(jnp.bfloat16)
    grad_key_low = grad_keys.reshape(row_count, head_cols).astype(jnp.bfloat16)
    grad_value_low = grad_values.reshape(row_count, head_cols).astype(jnp.bfloat16)
    grad_b_query = jnp.sum(grad_query_low.astype(jnp.float32), axis=0)
    grad_b_value = jnp.sum(grad_value_low.astype(jnp.float32), axis=0)
    grad_w_query = jnp.einsum(
        "rd,rc->dc", first_low, grad_query_low, preferred_element_type=jnp.float32
    )
    grad_w_key = jnp.einsum(
        "rd,rc->dc", first_low, grad_key_low, preferred_element_type=jnp.float32
    )
    grad_w_value = jnp.einsum(
        "rd,rc->dc", first_low, grad_value_low, preferred_element_type=jnp.float32
    )
    first_terms = jnp.einsum(
        "rc,dc->rd", grad_query_low, weight_query, preferred_element_type=jnp.float32
    )
    first_terms = first_terms + jnp.einsum(
        "rc,dc->rd", grad_key_low, weight_key, preferred_element_type=jnp.float32
    )
    first_terms = first_terms + jnp.einsum(
        "rc,dc->rd", grad_value_low, weight_value, preferred_element_type=jnp.float32
    )
    grad_first = lax.psum(first_terms.astype(jnp.bfloat16), "tp").astype(jnp.float32)
    grad_norm_one, grad_ln1_gain, grad_ln1_bias = norm_back(
        grad_first, normed_one, inverse_one, ln1_gain
    )
    grad_input = (grad_hidden + grad_norm_one).reshape(slot_count, seg_rows, model_width)
    shard_grads = (
        lax.psum_scatter(grad_w_query, ("shard", "ctx"), scatter_dimension=0, tiled=True),
        lax.psum_scatter(grad_w_key, ("shard", "ctx"), scatter_dimension=0, tiled=True),
        lax.psum_scatter(grad_w_value, ("shard", "ctx"), scatter_dimension=0, tiled=True),
        lax.psum_scatter(grad_w_out, ("shard", "ctx"), scatter_dimension=1, tiled=True),
        lax.psum_scatter(grad_w_up, ("shard", "ctx"), scatter_dimension=0, tiled=True),
        lax.psum_scatter(grad_w_down, ("shard", "ctx"), scatter_dimension=1, tiled=True),
    )
    small_sums = lax.psum(
        (
            grad_ln1_gain,
            grad_ln1_bias,
            grad_b_query,
            grad_b_value,
            grad_b_out,
            grad_ln2_gain,
            grad_ln2_bias,
            grad_b_up,
            grad_b_down,
        ),
        ("shard", "ctx"),
    )
    return (
        output,
        grad_input,
        small_sums[0],
        small_sums[1],
        shard_grads[0],
        small_sums[2],
        shard_grads[1],
        shard_grads[2],
        small_sums[3],
        shard_grads[3],
        small_sums[4],
        small_sums[5],
        small_sums[6],
        shard_grads[4],
        small_sums[7],
        shard_grads[5],
        small_sums[8],
    )


MESH = pl.DeviceIdType.MESH
F32 = jnp.float32
BF16 = jnp.bfloat16
NEG = -1e30
LIVE_LANE = 192


def nn(left, right):
    return jnp.dot(left, right, preferred_element_type=F32)


def nt(left, right):
    return lax.dot_general(left, right, (((1,), (1,)), ((), ())), preferred_element_type=F32)


def group(values, j):
    taken = values[:, :256] if j == 0 else pltpu.roll(values[:, 128:384], 192, 1)
    at = lax.broadcasted_iota(jnp.int32, taken.shape, 1)
    return jnp.where(at < 3 * HD, taken, 0.0)


def ungroup(first, second):
    turned = pltpu.roll(second, 64, 1)
    at = lax.broadcasted_iota(jnp.int32, turned.shape, 1)
    tail = jnp.concatenate([first[:, 128:], first[:, 128:]], axis=1)
    return jnp.concatenate([first[:, :128], jnp.where(at < 64, tail, turned)], axis=1)


def flip(values):
    return values.astype(F32).T.astype(BF16)


def layer_kernel(
    dims,
    frames,
    cot,
    lengths,
    v_gain1,
    v_bias1,
    v_b_out,
    v_gain2,
    v_bias2,
    v_b_down,
    v_b_up,
    v_b_query,
    v_b_value,
    w_query,
    w_key,
    w_value,
    w_up,
    w_down,
    w_out,
    out_h,
    gin_h,
    gf_h,
    go_h,
    gq_h,
    sums_h,
    ss,
    rs,
    ls,
    os,
    out_o,
    gin_o,
    gf_o,
    go_o,
    gq_o,
    sums_o,
    wqkv_own,
    bias_own,
    up_bias,
    a_all,
    a_t,
    wqkv,
    bias_all,
    wf,
    wo_sib,
    k_tr,
    v_tr,
    k_n,
    v_n,
    q_n,
    q_t,
    att_f,
    att_s,
    att_r,
    hid,
    z_all,
    z_t,
    g_n,
    g_t,
    act,
    gup,
    part_s,
    part_r,
    gz_s,
    gz_r,
    ghl_t,
    gatt_r,
    gatt_t,
    wg,
    wg_t,
    wg_x,
    wg_y,
    wg_zr,
    og_x,
    og_r,
    og_z,
    og_zr,
    dk_t,
    dv_t,
    dq_f,
    dlt,
    q_s,
    d_s,
    dkv_s,
    dkv_r,
    ga_r,
    qg,
    qg_r,
    qg_p,
    qg_z,
    qg_zr,
    sums,
    pairs,
    sum_p,
    sum_z,
    sum_c,
):
    S, C, R, D, GP, HG, FH = dims
    ga_s = a_all.at[pl.ds(0, C * R // 2), :]
    g_nat = a_all.at[pl.ds(C * R // 2, C * R // 2), :]
    OC = C // 2 * GP
    WF = OC + 2 * FH
    pieces = (slice(0, OC + FH), slice(OC + FH, WF))
    HF = R // 2
    CH = C // 2
    DB = D // (S * C)
    PB = C * DB
    s, z, c = lax.axis_index("shard"), lax.axis_index("ctx"), lax.axis_index("tp")
    o = 1 - c
    sib = (s, z, o)
    owed = []
    next_sem = [0]

    def sems(count):
        base = next_sem[0]
        next_sem[0] = base + count
        return base

    def remote(src, dst, index, device):
        return pltpu.make_async_remote_copy(
            src_ref=src,
            dst_ref=dst,
            send_sem=ss.at[index],
            recv_sem=rs.at[index],
            device_id=device,
            device_id_type=MESH,
        )

    def send(src, dst, index, device, when=None, like=None, owe=None):
        def go():
            remote(src, dst, index, device).start()

        if when is None:
            go()
        else:
            pl.when(when)(go)
        if owe is not False:
            owed.append((src if like is None else like, index, when if owe is None else owe))

    def settle(entries):
        for like, index, when in entries:

            def done(like=like, index=index):
                remote(like, like, index, sib).wait_send()

            if when is None:
                done()
            else:
                pl.when(when)(done)

    stored = []

    def store(src, dst):
        copy = pltpu.make_async_copy(src, dst, os.at[len(stored)])
        copy.start()
        stored.append(copy)

    def arrive(dst, index, when=None):
        def go():
            remote(dst, dst, index, sib).wait_recv()

        if when is None:
            go()
        else:
            pl.when(when)(go)

    def plane(k):
        return (lax.rem(s + k, S), z, c)

    near_x = s + 1 - 2 * lax.rem(s, 2)
    near_y = lax.rem(s + 2, 4)
    far = near_y + 1 - 2 * lax.rem(s, 2)
    to_x, to_y = (near_x, z, c), (near_y, z, c)

    def column(k):
        return (s, lax.rem(z + k, C), c)

    def s_from(k):
        return lax.rem(s + S - k, S)

    def z_from(k):
        return lax.rem(z + C - k, C)

    def rows_of(block):
        return pl.ds(pl.multiple_of(block * DB, 16), DB)

    def half_rows(block, half):
        return pl.ds(pl.multiple_of(block * R + half * HF, HF), HF)

    def blk(block):
        return pl.ds(pl.multiple_of(block * HF, HF), HF)

    k_bias = sems(1)
    k_q1 = sems(CH)
    k_q2 = sems(S)
    k_q3 = sems(1)
    k_a = sems(2 * C)
    k_as = sems(2 * C)
    k_f = sems(4 * C)
    k_fp = sems(8 * 2 * C)
    k_wo = sems(1)
    k_att = sems(C)
    k_n2 = sems(1)
    k_part = sems(1)
    k_gz = sems(1)
    k_out = sems(1)
    k_gatt = sems(C)
    k_wg = sems(6 * C)
    k_wgz = sems(C)
    k_ox = sems(1)
    k_og = sems(S)
    k_ogz = sems(C)
    k_dkv = sems(1)
    k_ga = sems(2 * C)
    k_qx = sems(1)
    k_qp = sems(S)
    k_qz = sems(CH)
    k_gin = sems(1)
    k_sp = sems(S)
    k_sz = sems(C)
    k_sc = sems(1)

    barrier = pltpu.get_barrier_semaphore()
    friends = [sib]
    friends += [plane(k) for k in range(1, S)]
    for k in range(1, C):
        friends += [(s, lax.rem(z + k, C), c), (s, lax.rem(z + k, C), o)]
    for friend in friends:
        pl.semaphore_signal(barrier, inc=1, device_id=friend, device_id_type=MESH)

    length = lengths[0]
    lane = lax.broadcasted_iota(jnp.int32, (HF, GP), 1)

    def head_lanes(count, h):
        at = lax.broadcasted_iota(jnp.int32, (count, GP), 1)
        return jnp.logical_and(at >= HD * h, at < HD * (h + 1))

    def only_head(values, h, keep_live=False):
        picked = head_lanes(values.shape[0], h)
        if keep_live:
            at = lax.broadcasted_iota(jnp.int32, values.shape, 1)
            picked = jnp.logical_or(picked, at == LIVE_LANE)
        return jnp.where(picked, values, jnp.zeros_like(values))

    ln1_gain, ln1_bias, b_out, ln2_gain, ln2_bias, b_down = (
        ref[...].reshape(1, D) for ref in (v_gain1, v_bias1, v_b_out, v_gain2, v_bias2, v_b_down)
    )
    for j in range(CH):
        for i, part in enumerate((w_key, w_value, w_query)):
            cols = slice(i * GP, (i + 1) * GP)
            wqkv_own[j, :, cols] = group(part[...].astype(F32), j).astype(BF16)
    mine_rows = rows_of(s * C + z)
    wf[mine_rows, OC : OC + FH] = w_up[...]
    wf[mine_rows, OC + FH :] = w_down[...]
    out_t = w_out[...].astype(F32)
    for j in range(CH):
        wf[mine_rows, j * GP : (j + 1) * GP] = group(out_t, j).astype(BF16)
    for j in range(CH):
        bias_own[j] = jnp.zeros((8, 3 * GP), F32)
        bias_own[j, 0:1, GP : 2 * GP] = group(v_b_value[...].reshape(1, CH * 3 * HD), j)
        bias_own[j, 0:1, 2 * GP :] = group(v_b_query[...].reshape(1, CH * 3 * HD), j)

    def norm(values):
        centred = values - jnp.mean(values, axis=-1, keepdims=True)
        inverse = lax.rsqrt(jnp.mean(centred * centred, axis=-1, keepdims=True) + EPSILON)
        return centred * inverse, inverse

    def live_of(first, count):
        at = z * R + first + lax.broadcasted_iota(jnp.int32, (count, 1), 0)
        return (at < length).astype(F32)

    sums[...] = jnp.zeros_like(sums)
    pl.semaphore_wait(barrier, len(friends))

    c_of_z = z // CH
    for j in range(CH):
        to_z = CH * c + j
        same = jnp.logical_and(to_z == z, c_of_z == c)
        for i in range(CH):
            ok = jnp.logical_and(z - CH * c_of_z == i, jnp.logical_not(same))
            here = wqkv.at[s, c_of_z, pl.ds(i * DB, DB), :]

            def go(i=i, here=here, j=j, to_z=to_z):
                pltpu.make_async_remote_copy(
                    src_ref=wqkv_own.at[j],
                    dst_ref=here,
                    send_sem=ls.at[j],
                    recv_sem=rs.at[k_q1 + i],
                    device_id=(s, to_z, c_of_z),
                    device_id_type=MESH,
                ).start()

            pl.when(ok)(go)

        def keep(j=j):
            wqkv[s, c, pl.ds(pl.multiple_of((z - CH * c) * DB, 16), DB), :] = wqkv_own[j]

        pl.when(same)(keep)
    send(bias_own, bias_all.at[c], k_bias, sib)
    bias_all[c] = bias_own[...]
    can_right, can_left = z + 1 < C, z >= 1

    def line_step(view, t, index, like):
        send(
            view(jnp.maximum(z - t, 0)),
            view(jnp.maximum(z - t, 0)),
            index + 2 * t,
            (s, jnp.minimum(z + 1, C - 1), c),
            goes_right[t],
            like,
        )
        send(
            view(jnp.minimum(z + t, C - 1)),
            view(jnp.minimum(z + t, C - 1)),
            index + 2 * t + 1,
            (s, jnp.maximum(z - 1, 0), c),
            goes_left[t],
            like,
        )

    goes_right = [jnp.logical_and(can_right, z - t >= 0) for t in range(C - 1)]
    goes_left = [jnp.logical_and(can_left, z + t < C) for t in range(C - 1)]
    like_f = [wf.at[pl.ds(0, DB), piece] for piece in pieces]
    like_a = a_all.at[pl.ds(0, HF), :]

    def f_step(t, p):
        view = lambda block: wf.at[rows_of(s * C + block), pieces[p]]
        line_step(view, t, k_f + 2 * C * p, like_f[p])

    def a_step(t):
        line_step(lambda block: a_all.at[half_rows(block, c), :], t, k_a, like_a)

    def from_left(t):
        return jnp.maximum(z - 1 - t, 0), z - 1 - t >= 0

    def from_right(t):
        return jnp.minimum(z + 1 + t, C - 1), z + 1 + t < C

    halves = []
    for piece in pieces:
        middle = (piece.start + piece.stop) // 2
        halves.append((slice(piece.start, middle), slice(middle, piece.stop)))
    like_fh = [wf.at[pl.ds(0, DB), half[0]] for half in halves]

    def row_of(shard, block):
        return rows_of(shard * C + block)

    labels_of = [
        ((2 * t + 2,) + from_left(t), (2 * t + 3,) + from_right(t)) for t in range(C - 1)
    ]
    own_label = ((0, z, None),)
    at_end = jnp.logical_or(z == 0, z == C - 1)
    near_end = jnp.minimum(z, C - 1 - z)
    inside = jnp.logical_not(at_end)
    wo_cols = slice(0, OC)

    def wo_pass(shard, block, ok):
        def go():
            at = row_of(shard, block)
            remote(wf.at[at, wo_cols], wo_sib.at[at, :], k_wo, sib).start()

        if ok is None:
            go()
        else:
            pl.when(ok)(go)


    def f_plane(labels, p):
        for label, block, ok in labels:
            index = k_fp + 8 * label + 4 * p
            at = wf.at[row_of(s, block), pieces[p]]
            send(at, at, index, to_x, ok, like_f[p])
            send(at, at, index + 1, to_y, ok, like_f[p])
            if p == 0:
                wo_pass(s, block, ok)

    def f_relay(labels, p, gate=None, owe=True):
        for label, block, ok in labels:
            index = k_fp + 8 * label + 4 * p
            now = ok if gate is None else jnp.logical_and(ok, gate)
            arrive(wf.at[row_of(near_x, block), pieces[p]], index, now)
            at = wf.at[row_of(near_x, block), halves[p][0]]
            send(at, at, index + 2, to_y, now, like_fh[p], ok if owe else False)
            arrive(wf.at[row_of(near_y, block), pieces[p]], index + 1, now)
            at = wf.at[row_of(near_y, block), halves[p][1]]
            send(at, at, index + 3, to_x, now, like_fh[p], ok if owe else False)
            if p == 0:
                wo_pass(near_x, block, now)
                wo_pass(near_y, block, now)

    def f_finish(labels, p):
        for label, block, ok in labels:
            index = k_fp + 8 * label + 4 * p
            for i in range(2):
                arrive(wf.at[row_of(far, block), halves[p][i]], index + 2 + i, ok)
            if p == 0:
                wo_pass(far, block, ok)

    def f_arrive(t, p):
        for side, (label, block, ok) in enumerate(labels_of[t]):
            arrive(wf.at[row_of(s, block), pieces[p]], k_f + 2 * C * p + 2 * t + side, ok)
        f_plane(labels_of[t], p)

    f_step(0, 0)
    f_step(0, 1)

    def first_norm(i, carry):
        at = pl.ds(pl.multiple_of(i * 64, 64), 64)
        to = pl.ds(pl.multiple_of(z * R + i * 64, 64), 64)
        normed, unused = norm(frames[at, :].astype(F32))
        a_all[to, :] = (normed * ln1_gain + ln1_bias).astype(BF16)
        g_n[at, :] = (cot[at, :].astype(F32) * live_of(i * 64, 64)).astype(BF16)
        return carry

    lax.fori_loop(0, R // 64, first_norm, 0)
    a_step(0)
    for i in range(CH):
        from_z = CH * c + i
        same = jnp.logical_and(from_z == z, c_of_z == c)
        arrive(wqkv.at[s, c, pl.ds(i * DB, DB), :], k_q1 + i, jnp.logical_not(same))
    for k in range(1, S):
        send(wqkv.at[s, c], wqkv.at[s, c], k_q2 + k, plane(k))
    f_plane(own_label, 0)
    f_plane(own_label, 1)
    key_at = lax.broadcasted_iota(jnp.int32, (GP - LIVE_LANE, C * R), 1)
    first_row = lax.broadcasted_iota(jnp.int32, (GP - LIVE_LANE, C * R), 0) == 0
    dead = jnp.where(jnp.logical_and(first_row, key_at >= length), NEG, 0.0)
    k_tr[LIVE_LANE:, :] = dead.astype(BF16)
    v_tr[LIVE_LANE:, :] = jnp.zeros((GP - LIVE_LANE, C * R), BF16)
    g_t[:, :HF] = flip(g_n[:HF, :])
    g_t[:, HF:] = flip(g_n[HF:, :])
    for k in range(1, S):
        arrive(wqkv.at[s_from(k), c], k_q2 + k)
    send(wqkv.at[:, c], wqkv.at[:, c], k_q3, sib)
    arrive(bias_all.at[o], k_bias)
    arrive(wqkv.at[:, o], k_q3)
    bias_z = bias_all[c_of_z, z - CH * c_of_z]

    def project(block, half):
        at = half_rows(block, half)
        rows = a_all[at, :]
        made = nn(rows, wqkv[...].reshape(D, 3 * GP)) + bias_z[0:1, :]
        keys = made[:, :GP].astype(BF16)
        values = made[:, GP : 2 * GP].astype(BF16)
        k_n[at, :] = keys
        v_n[at, :] = values
        k_tr[:LIVE_LANE, at] = flip(keys)[:LIVE_LANE, :]
        v_tr[:LIVE_LANE, at] = flip(values)[:LIVE_LANE, :]

        def own():
            queries = made[:, 2 * GP :].astype(BF16).astype(F32) * (HD**-0.5)
            queries = jnp.where(lane == LIVE_LANE, 1.0, queries).astype(BF16)
            q_n[blk(block), :] = queries
            q_t[:, blk(block)] = flip(queries)
            a_t[:, blk(block)] = flip(rows)

        pl.when(half == c)(own)

    def project_own(i, carry):
        project(z, lax.rem(c + i, 2))
        return carry

    a_given = []

    def remote_when(src, dst, index, device, when):
        def go():
            remote(src, dst, index, device).start()

        pl.when(when)(go)

    lax.fori_loop(0, 2, project_own, 0)
    f_arrive(0, 0)
    f_arrive(0, 1)
    f_relay(own_label, 0)
    f_relay(own_label, 1)
    for t in range(C - 1):
        if t == C - 2:
            for p in range(2):
                f_arrive(1, p)
                f_step(2, p)
        for side, (label, block, ok) in enumerate(labels_of[t]):
            arrive(a_all.at[half_rows(block, c), :], k_a + 2 * t + side, ok)
        if t == C - 3:
            f_step(1, 0)
            f_step(1, 1)
        if t + 1 < C - 1:
            a_step(t + 1)
        for side, (label, block, ok) in enumerate(labels_of[t]):
            at = a_all.at[half_rows(block, c), :]
            remote_when(at, at, k_as + 2 * t + side, sib, ok)
            a_given.append((like_a, k_as + 2 * t + side, ok))

        def come(i, carry, t=t):
            side = i // 2
            block = jnp.where(side == 0, from_left(t)[0], from_right(t)[0])
            ok = jnp.where(side == 0, z - 1 - t >= 0, z + 1 + t < C)

            def other_half():
                at = a_all.at[half_rows(block, o), :]
                remote(at, at, k_as + 2 * t + side, sib).wait_recv()

            def both():
                pl.when(lax.rem(i, 2) == 1)(other_half)
                project(block, lax.rem(c + i, 2))

            pl.when(ok)(both)
            return carry

        lax.fori_loop(0, 4, come, 0)
        if t == C - 3:
            f_relay(labels_of[0], 0)
            f_relay(labels_of[0], 1)
    for p in range(2):
        f_relay(labels_of[1], p, at_end)
    for p in range(2):
        f_finish(own_label, p)
        f_finish(labels_of[0], p)

    TQ = 128

    def attend(block):
        def step(i, carry):
            at = pl.ds(pl.multiple_of(block * HF + i * TQ, TQ), TQ)
            queries = q_n[at, :]
            total = jnp.zeros((TQ, GP), F32)
            log_sums = []
            for h in range(HG):
                scores = nn(only_head(queries, h, True), k_tr[...])
                top = jnp.max(scores, axis=-1, keepdims=True)
                weights = jnp.exp(scores - top)
                norm_sum = jnp.sum(weights, axis=-1, keepdims=True)
                got = nn(weights.astype(BF16), v_n[...]) * (1.0 / norm_sum)
                total = total + only_head(got, h)
                log_sums.append(top + jnp.log(norm_sum))
            att_f[at, :] = total
            for h in range(HG):
                att_f[at, LIVE_LANE + h : LIVE_LANE + h + 1] = log_sums[h]
            att_s[at, :] = total.astype(BF16)
            return carry

        lax.fori_loop(0, HF // TQ, step, 0)

    def attend_all(i, carry):
        inner = jnp.where(i == 0, 2, jnp.where(i == 1, 1, jnp.where(i == 2, 3, 0)))
        block = jnp.where(near_end == 0, lax.rem(i + 1, C), inner)
        block = jnp.where(2 * z < C, block, C - 1 - block)
        attend(block)

        def give():
            hop = lax.rem(block + C - z, C)
            device = (s, block, c)
            remote(att_s.at[blk(block), :], att_r.at[blk(z), :], k_att + hop, device).start()

        def poll_0():
            f_arrive(2, 0)

        def poll_1():
            f_relay(labels_of[1], 0, inside, False)

        def poll_2():
            f_relay(labels_of[1], 1, inside, False)
            f_relay(labels_of[2], 0)
            f_arrive(2, 1)

        pl.when(block != z)(give)
        pl.when(i == 0)(poll_0)
        pl.when(i == 1)(poll_1)
        pl.when(i == 2)(poll_2)
        return carry

    lax.fori_loop(0, C, attend_all, 0)
    att_r[blk(z), :] = att_s[blk(z), :]

    f_finish(labels_of[1], 0)
    f_finish(labels_of[2], 0)
    owed.append((wo_sib, k_wo, None))
    for k in range(1, C):
        arrive(att_r.at[blk(z_from(k)), :], k_att + k)
        remote(att_s.at[blk(z), :], att_r.at[blk(z), :], k_att + k, column(k)).wait_send()
    f_relay(labels_of[2], 1)
    arrive(wo_sib, k_wo)

    settle([entry for entry in owed if entry[0] is like_a])
    settle(a_given)
    owed[:] = [entry for entry in owed if entry[0] is not like_a]
    own_rows = pl.ds(pl.multiple_of(c * HF, HF), HF)
    hidden = frames[own_rows, :].astype(F32) + b_out
    for j in range(CH):
        hidden = hidden + nt(
            att_r[blk(CH * c + j), :], wf[:, j * GP : (j + 1) * GP]
        )
        hidden = hidden + nt(att_r[blk(CH * o + j), :], wo_sib[:, j * GP : (j + 1) * GP])
    hid[...] = hidden
    normed, unused = norm(hidden)
    z_all[own_rows, :] = (normed * ln2_gain + ln2_bias).astype(BF16)
    send(z_all.at[own_rows, :], z_all.at[own_rows, :], k_n2, sib)
    other_rows = pl.ds(pl.multiple_of(o * HF, HF), HF)
    z_t[:, own_rows] = flip(z_all[own_rows, :])
    arrive(z_all.at[other_rows, :], k_n2)
    z_t[:, other_rows] = flip(z_all[other_rows, :])

    f_finish(labels_of[1], 1)
    f_finish(labels_of[2], 1)
    TF = 256

    up_bias[...] = v_b_up[...].reshape(1, FH)

    def units(i, carry):
        cols = pl.ds(pl.multiple_of(i * TF, TF), TF)
        down = pl.ds(pl.multiple_of(OC + FH + i * TF, TF), TF)
        ups = pl.ds(pl.multiple_of(OC + i * TF, TF), TF)
        upper = nn(z_all[...], wf[:, ups]) + up_bias[:, cols]
        cumulative = 0.5 * (1.0 + lax.erf(upper * INV_ROOT_TWO))
        act[:, cols] = (upper * cumulative).astype(BF16)
        slope = cumulative + upper * jnp.exp(-0.5 * upper * upper) * INV_ROOT_TAU
        grad_units = (nn(g_n[...], wf[:, down]) * slope).astype(BF16)
        gup[:, cols] = grad_units
        return carry

    lax.fori_loop(0, FH // TF, units, 0)

    def z_grad(i, carry):
        at = pl.ds(pl.multiple_of(i * 256, 256), 256)
        gz_s[:, at] = nt(gup[other_rows, :], wf[at, OC : OC + FH]).astype(BF16)
        return carry

    lax.fori_loop(0, D // 256, z_grad, 0)
    send(gz_s, gz_r, k_gz, sib)

    def unit_grads(i, carry):
        cols = pl.ds(pl.multiple_of(i * TF, TF), TF)
        down = pl.ds(pl.multiple_of(FH + i * TF, TF), TF)
        wg[:, cols] = nn(z_t[...], gup[:, cols]).astype(BF16)
        wg[:, down] = nn(g_t[...], act[:, cols]).astype(BF16)
        return carry

    lax.fori_loop(0, FH // TF, unit_grads, 0)

    part_order = ((3, 3), (2, 0), (1, 2), (0, 1))

    def part_z(j):
        chosen = jnp.where(near_end == 0, part_order[j][0], part_order[j][1])
        return jnp.where(2 * z < C, chosen, C - 1 - chosen)

    def part_rows(j):
        return pl.ds(pl.multiple_of(part_z(j) * DB, 16), DB)

    part_a, part_b = slice(0, FH), slice(FH, 2 * FH)
    like_g = wg.at[pl.ds(0, DB), :]
    like_gh = wg.at[pl.ds(0, DB), pl.ds(0, FH)]

    def wg_far(j):
        index = k_wg + 6 * j
        own_z = part_z(j)
        send(wg.at[row_of(far, own_z), part_a], wg_t.at[j, 0], index, to_x, like=like_gh)
        send(wg.at[row_of(far, own_z), part_b], wg_t.at[j, 1], index + 1, to_y, like=like_gh)

    def wg_near(j):
        index = k_wg + 6 * j
        own_z = part_z(j)
        near = wg.at[row_of(near_x, own_z), part_a]
        send(near, wg_x.at[part_rows(j), part_a], index + 2, to_x, like=like_gh)
        near = wg.at[row_of(near_y, own_z), part_b]
        send(near, wg_y.at[part_rows(j), part_b], index + 3, to_y, like=like_gh)

    def add_into(at, cols, others):
        def step(i, carry):
            here = pl.ds(pl.multiple_of(cols.start + i * 256, 256), 256)
            total = wg[at, here].astype(F32)
            for other, rows, start in others:
                there = pl.ds(pl.multiple_of(start + i * 256, 256), 256)
                total = total + other[rows, there].astype(F32)
            wg[at, here] = total.astype(BF16)
            return carry

        lax.fori_loop(0, (cols.stop - cols.start) // 256, step, 0)

    def wg_second(j):
        index = k_wg + 6 * j
        own_z = part_z(j)
        arrive(wg_t.at[j, 0], index)
        at = row_of(near_y, own_z)
        add_into(at, part_a, [(wg_t.at[j, 0], slice(None), 0)])
        near = wg.at[at, part_a]
        send(near, wg_y.at[part_rows(j), part_a], index + 4, to_y, like=like_gh)
        arrive(wg_t.at[j, 1], index + 1)
        at = row_of(near_x, own_z)
        add_into(at, part_b, [(wg_t.at[j, 1], slice(None), 0)])
        near = wg.at[at, part_b]
        send(near, wg_x.at[part_rows(j), part_b], index + 5, to_x, like=like_gh)

    def wg_third(j):
        index = k_wg + 6 * j
        arrive(wg_x.at[part_rows(j), part_a], index + 2)
        arrive(wg_y.at[part_rows(j), part_b], index + 3)
        arrive(wg_y.at[part_rows(j), part_a], index + 4)
        arrive(wg_x.at[part_rows(j), part_b], index + 5)
        at = row_of(s, part_z(j))
        add_into(
            at, slice(0, 2 * FH), [(wg_x, part_rows(j), 0), (wg_y, part_rows(j), 0)]
        )
        if j < C - 1:
            hop = lax.rem(part_z(j) + C - z, C)
            remote(wg.at[at, :], wg_zr.at[hop - 1], k_wgz + hop, (s, part_z(j), c)).start()

    wg_far(0)
    wg_near(0)
    wg_far(1)

    gz_rows = jnp.concatenate(
        [nt(gup[own_rows, :], wf[i * 256 : (i + 1) * 256, OC : OC + FH]) for i in range(D // 256)], axis=1
    )
    arrive(gz_r, k_gz)
    grad_z = gz_rows + gz_r[...].astype(F32)
    live_own = live_of(c * HF, HF)
    normed, inverse = norm(hid[...])
    scaled = grad_z * ln2_gain
    inner = (
        scaled
        - jnp.mean(scaled, axis=-1, keepdims=True)
        - normed * jnp.mean(scaled * normed, axis=-1, keepdims=True)
    )
    g_own = g_n[own_rows, :].astype(F32)
    grad_hidden = g_own + inner * inverse
    gin_o[own_rows, :] = grad_hidden
    low = grad_hidden.astype(BF16)
    sums[3:4, :] = jnp.sum(grad_z * normed, axis=0, keepdims=True)
    sums[4:5, :] = jnp.sum(grad_z, axis=0, keepdims=True)
    sums[5:6, :] = jnp.sum(g_own, axis=0, keepdims=True)
    sums[2:3, :] = jnp.sum(low.astype(F32), axis=0, keepdims=True)
    for j in range(CH):
        att_s[blk(CH * c + j), :] = nn(
            low, wf[:, j * GP : (j + 1) * GP]
        ).astype(BF16)
        att_s[blk(CH * o + j), :] = nn(low, wo_sib[:, j * GP : (j + 1) * GP]).astype(BF16)
    for k in range(1, C):
        send(att_s.at[blk(lax.rem(z + k, C)), :], gatt_r.at[blk(z), :], k_gatt + k, column(k))
    gatt_r[blk(z), :] = att_s[blk(z), :]
    ghl_t[...] = flip(low)
    def down_part(i, carry):
        at = pl.ds(pl.multiple_of(i * 256, 256), 256)
        part_s[:, at] = nt(act[other_rows, :], wf[at, OC + FH :]).astype(BF16)
        return carry

    lax.fori_loop(0, D // 256, down_part, 0)
    send(part_s, part_r, k_part, sib)

    for j in range(CH):
        og_x[0, :, j * GP : (j + 1) * GP] = nn(ghl_t[...], att_r[blk(CH * o + j), :]).astype(BF16)
    remote(og_x.at[0], og_x.at[1], k_ox, sib).start()
    old = list(owed)
    owed.clear()
    dk_t[...] = jnp.zeros_like(dk_t)
    dv_t[...] = jnp.zeros_like(dv_t)
    TK = 512

    steps = C * R // TK

    def attend_back(polls):
        def block_step(b, carry):
            block = lax.rem(z + C - b, C)
            at = blk(block)

            def come():
                remote(gatt_r.at[at, :], gatt_r.at[at, :], k_gatt + b, sib).wait_recv()

            pl.when(b > 0)(come)
            gatt_t[...] = flip(gatt_r[at, :])
            product = gatt_r[at, :].astype(F32) * att_f[at, :]
            for h in range(HG):
                rows = slice(h * HF, (h + 1) * HF)
                dlt[rows, 0:1] = jnp.sum(only_head(product, h), axis=-1, keepdims=True)
                dlt[rows, 1:2] = att_f[at, LIVE_LANE + h : LIVE_LANE + h + 1]
                q_s[rows, :] = only_head(q_n[at, :], h, True)
                d_s[rows, :] = only_head(gatt_r[at, :], h)
            dq_f[...] = jnp.zeros_like(dq_f)

            def step(i, carry):
                keys = pl.ds(pl.multiple_of(i * TK, TK), TK)
                weights = jnp.exp(nn(q_s[...], k_tr[:, keys]) - dlt[:, 1:2])
                grads = nn(d_s[...], v_tr[:, keys])
                grad_scores = (weights * (grads - dlt[:, 0:1])).astype(BF16)
                weights = weights.astype(BF16)
                for h in range(HG):
                    head = slice(HD * h, HD * (h + 1))
                    rows = slice(h * HF, (h + 1) * HF)
                    dv_t[head, keys] += nn(gatt_t[head, :], weights[rows, :])
                    dk_t[head, keys] += nn(q_t[head, at], grad_scores[rows, :])
                dq_f[...] += nn(grad_scores, k_n[keys, :])
                for number, poll in polls:
                    pl.when(b * steps + i == number)(poll)
                return carry

            lax.fori_loop(0, steps, step, 0)
            for h in range(HG):
                rows = slice(h * HF, (h + 1) * HF)
                part = only_head(dq_f[rows, :], h)
                total = part if h == 0 else total + part
            g_nat[at, 2 * GP :] = (total * (HD**-0.5)).astype(BF16)
            return carry

        lax.fori_loop(0, C, block_step, 0)

    def og_reduce():
        for k in range(1, S):
            arrive(og_r.at[k - 1], k_og + k)
        own = pl.ds(pl.multiple_of(s * PB, 64), PB)
        total = og_x[0, own, :].astype(F32)
        for k in range(1, S):
            total = total + og_r[k - 1].astype(F32)
        og_z[...] = total.astype(BF16)
        for k in range(1, C):
            at = pl.ds(pl.multiple_of(lax.rem(z + k, C) * DB, 16), DB)
            send(og_z.at[at, :], og_zr.at[k - 1], k_ogz + k, column(k))

    def poll_a():
        wg_second(0)
        wg_near(1)

    def poll_b():
        wg_second(1)
        wg_far(2)
        wg_near(2)

    def poll_c():
        wg_second(2)
        wg_far(3)
        wg_near(3)

    down_rows = jnp.concatenate(
        [nt(act[own_rows, :], wf[i * 256 : (i + 1) * 256, OC + FH :]) for i in range(D // 256)],
        axis=1,
    )
    arrive(part_r, k_part)
    out_rows = live_own * (hid[...] + down_rows + part_r[...].astype(F32) + b_down)
    out_o[own_rows, :] = out_rows.astype(BF16)
    send(out_o.at[own_rows, :], out_o.at[own_rows, :], k_out, sib)
    for i in range(2):
        sums[pl.ds(6 + 2 * c + i, 1), :] = jnp.sum(
            gup[:, i * D : (i + 1) * D].astype(F32), axis=0, keepdims=True
        )
    arrive(og_x.at[1], k_ox)
    remote(og_x.at[0], og_x.at[1], k_ox, sib).wait_send()
    for j in range(CH):
        cols = slice(j * GP, (j + 1) * GP)
        own_part = nn(ghl_t[...], att_r[blk(CH * c + j), :])
        og_x[0, :, cols] = (own_part + og_x[1, :, cols].astype(F32)).astype(BF16)
    attend_back(
        (
            (0, poll_a),
            (3, poll_b),
            (6, lambda: wg_third(0)),
            (10, lambda: wg_third(1)),
            (11, poll_c),
        )
    )

    for i in range(C):
        cols = pl.ds(pl.multiple_of(i * R + o * HF, HF), HF)
        dkv_s[i, 0] = dk_t[:, cols].astype(BF16)
        dkv_s[i, 1] = dv_t[:, cols].astype(BF16)
    send(dkv_s, dkv_r, k_dkv, sib)
    wg_third(2)
    arrive(dkv_r, k_dkv)

    def finish(block):
        cols = pl.ds(pl.multiple_of(block * R + c * HF, HF), HF)
        at = blk(block)
        keys_t = dk_t[:, cols] + dkv_r[block, 0].astype(F32)
        values_t = dv_t[:, cols] + dkv_r[block, 1].astype(F32)
        none = jnp.zeros((GP - LIVE_LANE, HF), F32)
        g_nat[at, :GP] = jnp.concatenate([keys_t, none], axis=0).T.astype(BF16)
        g_nat[at, GP : 2 * GP] = jnp.concatenate([values_t, none], axis=0).T.astype(BF16)
        ga_s[at, :] = nt(g_nat[at, :], wqkv[...].reshape(D, 3 * GP)).astype(BF16)

    def finish_all(b, carry):
        finish(b)
        return carry

    lax.fori_loop(0, C, finish_all, 0)

    like_ga = ga_s.at[pl.ds(0, HF), :]

    def ga_send(t, side):
        target = jnp.where(side == 0, C - 1 - t, t)
        device = (s, jnp.clip(z + 1 - 2 * side, 0, C - 1), c)
        remote(ga_s.at[blk(target), :], ga_r.at[t, side], k_ga + 2 * t + side, device).start()

    def ga_ahead(t, side):
        return C - 1 - t > z if side == 0 else t < z

    for t in range(C - 1):
        for side in range(2):
            behind = z >= 1 if side == 0 else z + 1 < C
            first = jnp.logical_and(ga_ahead(t, side), jnp.logical_not(behind))
            pl.when(first)(lambda t=t, side=side: ga_send(t, side))
            owed.append((like_ga, k_ga + 2 * t + side, ga_ahead(t, side)))

    def ga_hop(u):
        for i in range(2):
            side = jnp.where(2 * z < C, i, 1 - i)
            t = jnp.where(side == 0, u - z, u - (C - 1 - z))
            target = jnp.where(side == 0, C - 1 - t, t)
            inner = jnp.logical_and(z >= 1, z + 1 < C)
            ahead = jnp.where(side == 0, target > z, target < z)
            ok = jnp.logical_and(jnp.logical_and(t >= 0, inner), ahead)

            def add(t=t, side=side, target=target):
                at = blk(target)
                arrive(ga_r.at[t, side], k_ga + 2 * t + side)
                ga_s[at, :] = (ga_s[at, :].astype(F32) + ga_r[t, side].astype(F32)).astype(BF16)
                ga_send(t, side)

            pl.when(ok)(add)

    wg_second(3)
    column_sum = jnp.sum(g_nat[...].astype(F32), axis=0, keepdims=True)
    sums[pl.ds(10 + z, 1), :] = column_sum
    pair_lane = lax.broadcasted_iota(jnp.int32, (PB, 128), 1)
    for i in range(S):
        got = nn(a_t[i * PB : (i + 1) * PB, :], g_nat[...])
        qg[i] = got.reshape(2, CH * DB, 3 * GP).astype(BF16)
        weights = wqkv[i].reshape(PB, 3 * GP).astype(F32)
        with_a = jnp.sum(got * weights, axis=-1, keepdims=True)
        alone = jnp.sum(weights * column_sum, axis=-1, keepdims=True)
        pairs[i * PB : (i + 1) * PB, :] = jnp.where(
            pair_lane == 0, with_a, jnp.where(pair_lane == 1, alone, 0.0)
        )
    send(qg.at[:, o], qg_r, k_qx, sib)
    turned = pairs[...].T
    sums[0:1, :] = (turned[0:1, :] - ln1_bias * turned[1:2, :]) / ln1_gain
    sums[1:2, :] = turned[1:2, :]
    sum_p[s] = sums[...]
    for k in range(1, S):
        send(sum_p.at[s], sum_p.at[s], k_sp + k, plane(k))
    for k in range(1, S):
        at = pl.ds(pl.multiple_of(lax.rem(s + k, S) * PB, 64), PB)
        send(og_x.at[0, at, :], og_r.at[k - 1], k_og + k, plane(k))
    arrive(qg_r, k_qx)
    for i in range(S):
        qg_r[i] = (qg_r[i].astype(F32) + qg[i, c].astype(F32)).astype(BF16)
    for k in range(1, S):
        send(qg_r.at[lax.rem(s + k, S)], qg_p.at[k - 1], k_qp + k, plane(k))
    settle(old)
    arrive(out_o.at[other_rows, :], k_out)
    store(out_o, out_h)
    for k in range(1, S):
        arrive(sum_p.at[s_from(k)], k_sp + k)
    total = sum_p[0]
    for k in range(1, S):
        total = total + sum_p[k]
    sum_z[z] = total
    for k in range(1, C):
        send(sum_z.at[z], sum_z.at[z], k_sz + k, column(k))
    wg_third(3)
    for hop in range(1, C):
        owed.append((like_g, k_wgz + hop, None))
    ga_hop(1)
    og_reduce()
    for u in range(2, C - 1):
        ga_hop(u)
    for k in range(1, S):
        arrive(qg_p.at[k - 1], k_qp + k)
    total = qg_r[s].astype(F32)
    for k in range(1, S):
        total = total + qg_p[k - 1].astype(F32)
    qg_z[...] = total.reshape(CH, DB, 3 * GP).astype(BF16)
    for i in range(CH):
        to_z = CH * c + i
        same = jnp.logical_and(to_z == z, c_of_z == c)
        for j in range(CH):
            ok = jnp.logical_and(z - CH * c_of_z == j, jnp.logical_not(same))

            def go(i=i, j=j, to_z=to_z):
                pltpu.make_async_remote_copy(
                    src_ref=qg_z.at[i],
                    dst_ref=qg_zr.at[j],
                    send_sem=ls.at[CH + i],
                    recv_sem=rs.at[k_qz + j],
                    device_id=(s, to_z, c_of_z),
                    device_id_type=MESH,
                ).start()

            pl.when(ok)(go)

        def keep(i=i):
            qg_zr[z - CH * c] = qg_z[i]

        pl.when(same)(keep)

    for k in range(1, C):
        arrive(sum_z.at[z_from(k)], k_sz + k)
    total = sum_z[0]
    for k in range(1, C):
        total = total + sum_z[k]
    sum_c[c] = total
    send(sum_c.at[c], sum_c.at[c], k_sc, sib)
    own_block = blk(z)
    hid[...] = ga_s[own_block, :].astype(F32)
    for t in range(C - 1):
        for side in range(2):
            target = C - 1 - t if side == 0 else t
            behind = z >= 1 if side == 0 else z + 1 < C

            def add(t=t, side=side):
                arrive(ga_r.at[t, side], k_ga + 2 * t + side)
                hid[...] += ga_r[t, side].astype(F32)

            pl.when(jnp.logical_and(target == z, behind))(add)
    grad_a = hid[...]
    normed, inverse = norm(frames[own_rows, :].astype(F32))
    scaled = grad_a * ln1_gain
    inner = (
        scaled
        - jnp.mean(scaled, axis=-1, keepdims=True)
        - normed * jnp.mean(scaled * normed, axis=-1, keepdims=True)
    )
    gin_o[own_rows, :] = gin_o[own_rows, :] + inner * inverse
    send(gin_o.at[own_rows, :], gin_o.at[own_rows, :], k_gin, sib)
    store(gin_o.at[own_rows, :], gin_h.at[own_rows, :])
    def last(own, got, index, to):
        for k in range(1, C):
            arrive(got.at[k - 1], index + k)
        total = own.astype(F32)
        for k in range(1, C):
            total = total + got[k - 1].astype(F32)
        to[...] = total

    last(wg[rows_of(s * C + z), :], wg_zr, k_wgz, gf_o)
    last(og_z[pl.ds(pl.multiple_of(z * DB, 16), DB), :], og_zr, k_ogz, go_o)
    store(gf_o, gf_h)
    store(go_o, go_h)
    for j in range(CH):
        same = jnp.logical_and(CH * c + j == z, c_of_z == c)
        arrive(qg_zr.at[j], k_qz + j, jnp.logical_not(same))
    gq_o[...] = qg_zr[...].astype(F32)
    store(gq_o, gq_h)
    arrive(sum_c.at[o], k_sc)
    sums_o[...] = sum_c[0] + sum_c[1]
    store(sums_o, sums_h)
    arrive(gin_o.at[other_rows, :], k_gin)
    store(gin_o.at[other_rows, :], gin_h.at[other_rows, :])

    settle(owed)
    for copy in stored:
        copy.wait()
    for j in range(CH):
        same = jnp.logical_and(CH * c + j == z, c_of_z == c)

        def done_weights(j=j):
            pltpu.make_async_remote_copy(
                src_ref=wqkv_own.at[j],
                dst_ref=wqkv_own.at[j],
                send_sem=ls.at[j],
                recv_sem=rs.at[k_q1],
                device_id=sib,
                device_id_type=MESH,
            ).wait_send()
            pltpu.make_async_remote_copy(
                src_ref=qg_z.at[j],
                dst_ref=qg_z.at[j],
                send_sem=ls.at[CH + j],
                recv_sem=rs.at[k_qz],
                device_id=sib,
                device_id_type=MESH,
            ).wait_send()

        pl.when(jnp.logical_not(same))(done_weights)
    assert next_sem[0] <= SEMS


def unpack_kernel(
    CH,
    output,
    grad_input,
    gf_h,
    go_h,
    gq_h,
    sums_h,
    output_o,
    grad_input_o,
    query_o,
    key_o,
    value_o,
    out_o,
    up_o,
    down_o,
    gain1_o,
    bias1_o,
    b_query_o,
    b_value_o,
    b_out_o,
    gain2_o,
    bias2_o,
    b_up_o,
    b_down_o,
    gf,
    go,
    gq,
    sums,
    sem,
):
    c = lax.axis_index("tp")
    FH = up_o.shape[1]
    D = sums.shape[1]
    GP = 256
    pairs = ((output, output_o), (grad_input, grad_input_o))
    pairs += ((gf_h, gf), (go_h, go), (gq_h, gq), (sums_h, sums))
    copies = [
        pltpu.make_async_copy(src, dst, sem.at[i]) for i, (src, dst) in enumerate(pairs)
    ]
    for copy in copies:
        copy.start()
    for copy in copies[2:]:
        copy.wait()
    for i, to in enumerate((key_o, value_o, query_o)):
        cols = slice(i * GP, (i + 1) * GP)
        to[...] = ungroup(gq[0, :, cols], gq[1, :, cols])
    out_o[...] = ungroup(go[:, :GP], go[:, GP : 2 * GP])
    up_o[...] = gf[:, :FH]
    down_o[...] = gf[:, FH:]
    for i, to in enumerate((gain1_o, bias1_o, b_out_o, gain2_o, bias2_o, b_down_o)):
        to[...] = sums[i, :]
    for i in range(FH // D):
        b_up_o[i * D : (i + 1) * D] = sums[6 + 2 * c + i, :]
    for to, start in ((b_value_o, GP), (b_query_o, 2 * GP)):
        row = [sums[pl.ds(10 + CH * c + j, 1), start : start + GP] for j in range(CH)]
        to[...] = ungroup(row[0], row[1])[0, :]
    for copy in copies[:2]:
        copy.wait()


SEMS = 256


def fits(frames, w_query, w_up):
    shards, ctx, cores = (lax.axis_size(name) for name in ("shard", "ctx", "tp"))
    slot_count, seg_rows, width = frames.shape
    heads = w_query.shape[1] * cores // HD
    return (
        slot_count == 1
        and cores == 2
        and ctx % 2 == 0
        and ctx == 4
        and shards == 4
        and heads == 3 * ctx
        and width % (16 * shards * ctx) == 0
        and width % 256 == 0
        and seg_rows % 512 == 0
        and w_up.shape[1] % 512 == 0
        and w_up.shape[1] == 2 * width
        and ctx * seg_rows <= 2048
        and width <= 768
        and w_up.shape[1] <= 1536
    )


def fast_layer(
    frames,
    lengths,
    cotangent,
    ln1_gain,
    ln1_bias,
    w_query,
    b_query,
    w_key,
    w_value,
    b_value,
    w_out,
    b_out,
    ln2_gain,
    ln2_bias,
    w_up,
    b_up,
    w_down,
    b_down,
):
    S, C = lax.axis_size("shard"), lax.axis_size("ctx")
    unused, R, D = frames.shape
    FH = w_up.shape[1]
    HG, CH = 3, C // 2
    G, GP = HG * HD, 256
    DB = D // (S * C)
    HF = R // 2
    PB = C * DB
    T = C * R

    WF = 2 * FH + CH * GP
    vmem = pl.BlockSpec(memory_space=pltpu.VMEM)
    V = pltpu.VMEM
    dims = (S, C, R, D, GP, HG, FH)
    scratch = [
        pltpu.SemaphoreType.DMA((SEMS,)),
        pltpu.SemaphoreType.DMA((SEMS,)),
        pltpu.SemaphoreType.DMA((2 * CH,)),
        pltpu.SemaphoreType.DMA((7,)),
        V((R, D), BF16),
        V((R, D), F32),
        V((DB, 2 * FH), F32),
        V((DB, CH * GP), F32),
        V((CH, DB, 3 * GP), F32),
        V((16, D), F32),
        V((CH, DB, 3 * GP), BF16),
        V((CH, 8, 3 * GP), F32),
        V((1, FH), F32),
        V((T, D), BF16),
        V((D, C * HF), BF16),
        V((S, 2, CH * DB, 3 * GP), BF16),
        V((2, CH, 8, 3 * GP), F32),
        V((D, WF), BF16),
        V((D, CH * GP), BF16),
        V((GP, T), BF16),
        V((GP, T), BF16),
        V((T, GP), BF16),
        V((T, GP), BF16),
        V((C * HF, GP), BF16),
        V((GP, C * HF), BF16),
        V((C * HF, GP), F32),
        V((C * HF, GP), BF16),
        V((C * HF, GP), BF16),
        V((HF, D), F32),
        V((R, D), BF16),
        V((D, R), BF16),
        V((R, D), BF16),
        V((D, R), BF16),
        V((R, FH), BF16),
        V((R, FH), BF16),
        V((HF, D), BF16),
        V((HF, D), BF16),
        V((HF, D), BF16),
        V((HF, D), BF16),
        V((D, HF), BF16),
        V((C * HF, GP), BF16),
        V((GP, HF), BF16),
        V((D, 2 * FH), BF16),
        V((C, 2, DB, FH), BF16),
        V((PB, 2 * FH), BF16),
        V((PB, 2 * FH), BF16),
        V((C - 1, DB, 2 * FH), BF16),
        V((2, D, CH * GP), BF16),
        V((S - 1, PB, CH * GP), BF16),
        V((PB, CH * GP), BF16),
        V((C - 1, DB, CH * GP), BF16),
        V((G, T), F32),
        V((G, T), F32),
        V((3 * HF, GP), F32),
        V((3 * HF, 8), F32),
        V((3 * HF, GP), BF16),
        V((3 * HF, GP), BF16),
        V((C, 2, G, HF), BF16),
        V((C, 2, G, HF), BF16),
        V((C - 1, 2, HF, D), BF16),
        V((S, 2, CH * DB, 3 * GP), BF16),
        V((S, CH * DB, 3 * GP), BF16),
        V((S - 1, CH * DB, 3 * GP), BF16),
        V((CH, DB, 3 * GP), BF16),
        V((CH, DB, 3 * GP), BF16),
        V((16, D), F32),
        V((D, 128), F32),
        V((S, 16, D), F32),
        V((C, 16, D), F32),
        V((2, 16, D), F32),
    ]
    outs = (
        jax.ShapeDtypeStruct((R, D), BF16),
        jax.ShapeDtypeStruct((R, D), F32),
        jax.ShapeDtypeStruct((DB, 2 * FH), F32),
        jax.ShapeDtypeStruct((DB, CH * GP), F32),
        jax.ShapeDtypeStruct((CH, DB, 3 * GP), F32),
        jax.ShapeDtypeStruct((16, D), F32),
    )
    output, grad_input, gf, go, gq, sums = pl.pallas_call(
        functools.partial(layer_kernel, dims),
        out_shape=outs,
        in_specs=[vmem, vmem, pl.BlockSpec(memory_space=pltpu.SMEM)] + [vmem] * 15,
        out_specs=[pl.BlockSpec(memory_space=pltpu.HBM)] * 6,
        scratch_shapes=scratch,
        compiler_params=pltpu.CompilerParams(
            collective_id=0, has_side_effects=True, vmem_limit_bytes=63 << 20
        ),
    )(
        frames[0],
        cotangent[0],
        lengths,
        ln1_gain,
        ln1_bias,
        b_out,
        ln2_gain,
        ln2_bias,
        b_down,
        b_up,
        b_query,
        b_value,
        w_query,
        w_key,
        w_value,
        w_up,
        w_down.T,
        w_out.T,
    )
    flat = [D, D, CH * G, CH * G, D, D, D, FH, D]
    results = pl.pallas_call(
        functools.partial(unpack_kernel, CH),
        out_shape=[
            jax.ShapeDtypeStruct((R, D), BF16),
            jax.ShapeDtypeStruct((R, D), F32),
            jax.ShapeDtypeStruct((DB, CH * G), F32),
            jax.ShapeDtypeStruct((DB, CH * G), F32),
            jax.ShapeDtypeStruct((DB, CH * G), F32),
            jax.ShapeDtypeStruct((DB, CH * G), F32),
            jax.ShapeDtypeStruct((DB, FH), F32),
            jax.ShapeDtypeStruct((DB, FH), F32),
        ]
        + [jax.ShapeDtypeStruct((length,), F32) for length in flat],
        in_specs=[pl.BlockSpec(memory_space=pltpu.HBM)] * 6,
        out_specs=[vmem] * 17,
        scratch_shapes=[
            V((DB, 2 * FH), F32),
            V((DB, CH * GP), F32),
            V((CH, DB, 3 * GP), F32),
            V((16, D), F32),
            pltpu.SemaphoreType.DMA((6,)),
        ],
        compiler_params=pltpu.CompilerParams(vmem_limit_bytes=63 << 20),
    )(output, grad_input, gf, go, gq, sums)
    output, grad_input, g_query, g_key, g_value, g_out, g_up, g_down = results[:8]
    g1, s1, bq, bv, bo, g2, s2, bu, bd = results[8:]
    return (
        output[None],
        grad_input[None],
        g1,
        s1,
        g_query,
        bq,
        g_key,
        g_value,
        bv,
        g_out.T,
        bo,
        g2,
        s2,
        g_up,
        bu,
        g_down.T,
        bd,
    )


def per_device(frames, lengths, cotangent, *params):
    if fits(frames, params[2], params[11]):
        return fast_layer(frames, lengths, cotangent, *params)
    return plain_layer(frames, lengths, cotangent, *params)


def solution(mesh):
    in_specs = (
        P("shard", "ctx", None),
        P("shard"),
        P("shard", "ctx", None),
        P(),
        P(),
        P(("shard", "ctx"), "tp"),
        P("tp"),
        P(("shard", "ctx"), "tp"),
        P(("shard", "ctx"), "tp"),
        P("tp"),
        P("tp", ("shard", "ctx")),
        P(),
        P(),
        P(),
        P(("shard", "ctx"), "tp"),
        P("tp"),
        P("tp", ("shard", "ctx")),
        P(),
    )
    out_specs = (
        P("shard", "ctx", None),
        P("shard", "ctx", None),
        P(),
        P(),
        P(("shard", "ctx"), "tp"),
        P("tp"),
        P(("shard", "ctx"), "tp"),
        P(("shard", "ctx"), "tp"),
        P("tp"),
        P("tp", ("shard", "ctx")),
        P(),
        P(),
        P(),
        P(("shard", "ctx"), "tp"),
        P("tp"),
        P("tp", ("shard", "ctx")),
        P(),
    )
    return jax.shard_map(
        per_device, mesh=mesh, in_specs=in_specs, out_specs=out_specs, check_vma=False
    )
```

```python
import functools
import math

import jax
import jax.numpy as jnp
from jax import lax
from jax.experimental import pallas as pl
from jax.experimental.pallas import tpu as pltpu
from jax.sharding import PartitionSpec as P

HD = 64


EPSILON = 1e-05
INV_ROOT_TWO = 0.7071067811865476
INV_ROOT_TAU = 0.3989422804014327


def norm_rows(values, gain, shift):
    centred = values - jnp.mean(values, axis=-1, keepdims=True)
    inverse = lax.rsqrt(jnp.mean(centred * centred, axis=-1, keepdims=True) + EPSILON)
    normed = centred * inverse
    return (normed * gain + shift, normed, inverse)


def norm_back(grad_rows, normed, inverse, gain):
    scaled = grad_rows * gain
    inner = (
        scaled
        - jnp.mean(scaled, axis=-1, keepdims=True)
        - normed * jnp.mean(scaled * normed, axis=-1, keepdims=True)
    )
    return (inner * inverse, jnp.sum(grad_rows * normed, axis=0), jnp.sum(grad_rows, axis=0))


def gelu_slope(values):
    return (
        0.5 * (1.0 + lax.erf(values * INV_ROOT_TWO))
        + values * jnp.exp(-0.5 * values * values) * INV_ROOT_TAU
    )


def pair_scores(queries, block_keys, score_scale):
    return (
        jnp.einsum("qhd,khd->hqk", queries, block_keys, preferred_element_type=jnp.float32)
        * score_scale
    )


def live_weights(scores, query_live, key_live, log_totals):
    both_live = query_live[None, :, None] & key_live[None, None, :]
    return jnp.where(both_live, jnp.exp(scores - log_totals[:, :, None]), 0.0)


def in_blocks(array, block_rows):
    return array.reshape((array.shape[0] // block_rows, block_rows) + array.shape[1:])


def slot_forward(queries, slot_keys, slot_values, query_live, key_live, key_block, score_scale):
    seg_rows, head_count, head_dim = queries.shape
    key_starts = jnp.arange(slot_keys.shape[0] // key_block, dtype=jnp.int32) * key_block
    blocks = (
        in_blocks(slot_keys, key_block),
        in_blocks(slot_values, key_block),
        in_blocks(key_live, key_block),
        key_starts,
    )
    start_state = (
        jnp.full((head_count, seg_rows), -jnp.inf, jnp.float32),
        jnp.zeros((head_count, seg_rows), jnp.float32),
    )

    def totals_step(carried, scan_item):
        block_keys, block_values, block_live, block_start = scan_item
        running_max, running_sum = carried
        scores = jnp.where(
            block_live[None, None, :], pair_scores(queries, block_keys, score_scale), -jnp.inf
        )
        new_max = jnp.maximum(running_max, jnp.max(scores, axis=-1))
        new_sum = running_sum * jnp.exp(running_max - new_max) + jnp.sum(
            jnp.exp(scores - new_max[:, :, None]), axis=-1
        )
        return ((new_max, new_sum), None)

    def whole_slot(ignored):
        final_state, unused = lax.scan(totals_step, start_state, blocks)
        log_totals = final_state[0] + jnp.log(final_state[1])

        def output_step(output_sum, scan_item):
            block_keys, block_values, block_live, block_start = scan_item
            weights_here = live_weights(
                pair_scores(queries, block_keys, score_scale), query_live, block_live, log_totals
            ).astype(jnp.bfloat16)
            return (
                output_sum
                + jnp.einsum(
                    "hqk,khd->qhd", weights_here, block_values, preferred_element_type=jnp.float32
                ),
                None,
            )

        attended, unused_too = lax.scan(
            output_step, jnp.zeros((seg_rows, head_count, head_dim), jnp.float32), blocks
        )
        return (log_totals, attended)

    return whole_slot(0)


def slot_back(
    queries,
    grad_att,
    log_totals,
    delta,
    slot_keys,
    slot_values,
    query_live,
    key_live,
    key_block,
    score_scale,
):
    seg_rows, head_count, head_dim = queries.shape
    key_starts = jnp.arange(slot_keys.shape[0] // key_block, dtype=jnp.int32) * key_block
    blocks = (
        in_blocks(slot_keys, key_block),
        in_blocks(slot_values, key_block),
        in_blocks(key_live, key_block),
        key_starts,
    )

    def grad_step(grad_query, scan_item):
        block_keys, block_values, block_live, block_start = scan_item
        partial_value = grad_query
        weights_full = live_weights(
            pair_scores(queries, block_keys, score_scale), query_live, block_live, log_totals
        )
        grad_probs = jnp.einsum(
            "qhd,khd->hqk", grad_att, block_values, preferred_element_type=jnp.float32
        )
        grad_scores = (weights_full * (grad_probs - delta[:, :, None])).astype(jnp.bfloat16)
        partial_value = (
            partial_value
            + jnp.einsum(
                "hqk,khd->qhd", grad_scores, block_keys, preferred_element_type=jnp.float32
            )
            * score_scale
        )
        grad_value = jnp.einsum(
            "hqk,qhd->khd",
            weights_full.astype(jnp.bfloat16),
            grad_att,
            preferred_element_type=jnp.float32,
        )
        grad_key = (
            jnp.einsum("hqk,qhd->khd", grad_scores, queries, preferred_element_type=jnp.float32)
            * score_scale
        )
        return (partial_value, (grad_key, grad_value))

    def whole_slot(ignored):
        grad_query, key_parts = lax.scan(
            grad_step, jnp.zeros((seg_rows, head_count, head_dim), jnp.float32), blocks
        )
        return (
            grad_query,
            key_parts[0].reshape(slot_keys.shape),
            key_parts[1].reshape(slot_keys.shape),
        )

    return whole_slot(0)


def plain_layer(
    frames,
    lengths,
    cotangent,
    ln1_gain,
    ln1_bias,
    w_query,
    b_query,
    w_key,
    w_value,
    b_value,
    w_out,
    b_out,
    ln2_gain,
    ln2_bias,
    w_up,
    b_up,
    w_down,
    b_down,
):
    slot_count, seg_rows, model_width = frames.shape
    row_count = slot_count * seg_rows
    head_cols = w_query.shape[1]
    head_count = head_cols // HD
    seq_length = seg_rows * lax.axis_size("ctx")
    seg_start = lax.axis_index("ctx") * seg_rows
    score_scale = HD ** (-0.5)
    key_block = math.gcd(seq_length, 512)
    positions = seg_start + jnp.arange(seg_rows, dtype=jnp.int32)
    query_live = positions[None, :] < lengths[:, None]
    key_live = jnp.arange(seq_length, dtype=jnp.int32)[None, :] < lengths[:, None]
    live_rows = query_live.astype(jnp.float32).reshape(row_count, 1)
    weight_query, weight_key, weight_value, weight_out = (
        lax.all_gather(w_query, ("shard", "ctx"), axis=0, tiled=True),
        lax.all_gather(w_key, ("shard", "ctx"), axis=0, tiled=True),
        lax.all_gather(w_value, ("shard", "ctx"), axis=0, tiled=True),
        lax.all_gather(w_out, ("shard", "ctx"), axis=1, tiled=True),
    )
    frames_flat = frames.astype(jnp.float32).reshape(row_count, model_width)
    first, normed_one, inverse_one = norm_rows(frames_flat, ln1_gain, ln1_bias)
    first_low = first.astype(jnp.bfloat16)
    queries = (
        jnp.dot(first_low, weight_query, preferred_element_type=jnp.float32) + b_query
    ).astype(jnp.bfloat16)
    keys_local = jnp.dot(first_low, weight_key, preferred_element_type=jnp.float32).astype(
        jnp.bfloat16
    )
    values_local = (
        jnp.dot(first_low, weight_value, preferred_element_type=jnp.float32) + b_value
    ).astype(jnp.bfloat16)
    keys_all, values_all = (
        lax.all_gather(
            keys_local.reshape(slot_count, seg_rows, head_cols), "ctx", axis=1, tiled=True
        ),
        lax.all_gather(
            values_local.reshape(slot_count, seg_rows, head_cols), "ctx", axis=1, tiled=True
        ),
    )
    query_heads = queries.reshape(slot_count, seg_rows, head_count, HD)
    key_heads = keys_all.reshape(slot_count, seq_length, head_count, HD)
    value_heads = values_all.reshape(slot_count, seq_length, head_count, HD)
    slot = 0
    log_totals, attended_slot = slot_forward(
        query_heads[slot],
        key_heads[slot],
        value_heads[slot],
        query_live[slot],
        key_live[slot],
        key_block,
        score_scale,
    )
    totals_list = [log_totals]
    attended_list = [attended_slot]
    attended = jnp.stack(attended_list).reshape(row_count, head_cols)
    attended_low = attended.astype(jnp.bfloat16)
    attn_sum = lax.psum(
        jnp.dot(attended_low, weight_out, preferred_element_type=jnp.float32).astype(jnp.bfloat16),
        "tp",
    ).astype(jnp.float32)
    hidden = frames_flat + attn_sum + b_out
    weight_up, weight_down = (
        lax.all_gather(w_up, ("shard", "ctx"), axis=0, tiled=True),
        lax.all_gather(w_down, ("shard", "ctx"), axis=1, tiled=True),
    )
    second, normed_two, inverse_two = norm_rows(hidden, ln2_gain, ln2_bias)
    second_low = second.astype(jnp.bfloat16)
    upper = jnp.dot(second_low, weight_up, preferred_element_type=jnp.float32) + b_up
    activated = jax.nn.gelu(upper, approximate=False).astype(jnp.bfloat16)
    mlp_sum = lax.psum(
        jnp.dot(activated, weight_down, preferred_element_type=jnp.float32).astype(jnp.bfloat16),
        "tp",
    ).astype(jnp.float32)
    output = (
        (live_rows * (hidden + mlp_sum + b_down))
        .astype(jnp.bfloat16)
        .reshape(slot_count, seg_rows, model_width)
    )
    grad_out = live_rows * cotangent.astype(jnp.float32).reshape(row_count, model_width)
    grad_out_low = grad_out.astype(jnp.bfloat16)
    grad_b_down = jnp.sum(grad_out, axis=0)
    grad_w_down = jnp.einsum(
        "rf,rd->fd", activated, grad_out_low, preferred_element_type=jnp.float32
    )
    grad_act = jnp.einsum(
        "rd,fd->rf", grad_out_low, weight_down, preferred_element_type=jnp.float32
    )
    grad_upper = (grad_act * gelu_slope(upper)).astype(jnp.bfloat16)
    grad_b_up = jnp.sum(grad_upper.astype(jnp.float32), axis=0)
    grad_w_up = jnp.einsum("rd,rf->df", second_low, grad_upper, preferred_element_type=jnp.float32)
    grad_second = lax.psum(
        jnp.einsum("rf,df->rd", grad_upper, weight_up, preferred_element_type=jnp.float32).astype(
            jnp.bfloat16
        ),
        "tp",
    ).astype(jnp.float32)
    grad_norm_two, grad_ln2_gain, grad_ln2_bias = norm_back(
        grad_second, normed_two, inverse_two, ln2_gain
    )
    grad_hidden = grad_out + grad_norm_two
    grad_hidden_low = grad_hidden.astype(jnp.bfloat16)
    grad_b_out = jnp.sum(grad_hidden_low.astype(jnp.float32), axis=0)
    grad_w_out = jnp.einsum(
        "rc,rd->cd", attended_low, grad_hidden_low, preferred_element_type=jnp.float32
    )
    grad_att = jnp.einsum(
        "rd,cd->rc", grad_hidden_low, weight_out, preferred_element_type=jnp.float32
    ).astype(jnp.bfloat16)
    delta = jnp.sum(
        (grad_att.astype(jnp.float32) * attended).reshape(row_count, head_count, HD), axis=-1
    )
    delta_heads = delta.reshape(slot_count, seg_rows, head_count)
    grad_att_heads = grad_att.reshape(slot_count, seg_rows, head_count, HD)
    slot = 0
    grad_query_slot, key_part, value_part = slot_back(
        query_heads[slot],
        grad_att_heads[slot],
        totals_list[slot],
        delta_heads[slot].T,
        key_heads[slot],
        value_heads[slot],
        query_live[slot],
        key_live[slot],
        key_block,
        score_scale,
    )
    grad_query_list = [grad_query_slot]
    key_part_list = [key_part.reshape(seq_length, head_cols)]
    value_part_list = [value_part.reshape(seq_length, head_cols)]
    grad_keys, grad_values = (
        lax.psum_scatter(
            jnp.stack(key_part_list).astype(jnp.bfloat16), "ctx", scatter_dimension=1, tiled=True
        ).astype(jnp.float32),
        lax.psum_scatter(
            jnp.stack(value_part_list).astype(jnp.bfloat16), "ctx", scatter_dimension=1, tiled=True
        ).astype(jnp.float32),
    )
    grad_query_low = jnp.stack(grad_query_list).reshape(row_count, head_cols).astype(jnp.bfloat16)
    grad_key_low = grad_keys.reshape(row_count, head_cols).astype(jnp.bfloat16)
    grad_value_low = grad_values.reshape(row_count, head_cols).astype(jnp.bfloat16)
    grad_b_query = jnp.sum(grad_query_low.astype(jnp.float32), axis=0)
    grad_b_value = jnp.sum(grad_value_low.astype(jnp.float32), axis=0)
    grad_w_query = jnp.einsum(
        "rd,rc->dc", first_low, grad_query_low, preferred_element_type=jnp.float32
    )
    grad_w_key = jnp.einsum(
        "rd,rc->dc", first_low, grad_key_low, preferred_element_type=jnp.float32
    )
    grad_w_value = jnp.einsum(
        "rd,rc->dc", first_low, grad_value_low, preferred_element_type=jnp.float32
    )
    first_terms = jnp.einsum(
        "rc,dc->rd", grad_query_low, weight_query, preferred_element_type=jnp.float32
    )
    first_terms = first_terms + jnp.einsum(
        "rc,dc->rd", grad_key_low, weight_key, preferred_element_type=jnp.float32
    )
    first_terms = first_terms + jnp.einsum(
        "rc,dc->rd", grad_value_low, weight_value, preferred_element_type=jnp.float32
    )
    grad_first = lax.psum(first_terms.astype(jnp.bfloat16), "tp").astype(jnp.float32)
    grad_norm_one, grad_ln1_gain, grad_ln1_bias = norm_back(
        grad_first, normed_one, inverse_one, ln1_gain
    )
    grad_input = (grad_hidden + grad_norm_one).reshape(slot_count, seg_rows, model_width)
    shard_grads = (
        lax.psum_scatter(grad_w_query, ("shard", "ctx"), scatter_dimension=0, tiled=True),
        lax.psum_scatter(grad_w_key, ("shard", "ctx"), scatter_dimension=0, tiled=True),
        lax.psum_scatter(grad_w_value, ("shard", "ctx"), scatter_dimension=0, tiled=True),
        lax.psum_scatter(grad_w_out, ("shard", "ctx"), scatter_dimension=1, tiled=True),
        lax.psum_scatter(grad_w_up, ("shard", "ctx"), scatter_dimension=0, tiled=True),
        lax.psum_scatter(grad_w_down, ("shard", "ctx"), scatter_dimension=1, tiled=True),
    )
    small_sums = lax.psum(
        (
            grad_ln1_gain,
            grad_ln1_bias,
            grad_b_query,
            grad_b_value,
            grad_b_out,
            grad_ln2_gain,
            grad_ln2_bias,
            grad_b_up,
            grad_b_down,
        ),
        ("shard", "ctx"),
    )
    return (
        output,
        grad_input,
        small_sums[0],
        small_sums[1],
        shard_grads[0],
        small_sums[2],
        shard_grads[1],
        shard_grads[2],
        small_sums[3],
        shard_grads[3],
        small_sums[4],
        small_sums[5],
        small_sums[6],
        shard_grads[4],
        small_sums[7],
        shard_grads[5],
        small_sums[8],
    )


MESH = pl.DeviceIdType.MESH
F32 = jnp.float32
BF16 = jnp.bfloat16
NEG = -1e30
LIVE_LANE = 192


def nn(left, right):
    return jnp.dot(left, right, preferred_element_type=F32)


def nt(left, right):
    return lax.dot_general(left, right, (((1,), (1,)), ((), ())), preferred_element_type=F32)


def group(values, j):
    taken = values[:, :256] if j == 0 else pltpu.roll(values[:, 128:384], 192, 1)
    at = lax.broadcasted_iota(jnp.int32, taken.shape, 1)
    return jnp.where(at < 3 * HD, taken, 0.0)


def ungroup(first, second):
    turned = pltpu.roll(second, 64, 1)
    at = lax.broadcasted_iota(jnp.int32, turned.shape, 1)
    tail = jnp.concatenate([first[:, 128:], first[:, 128:]], axis=1)
    return jnp.concatenate([first[:, :128], jnp.where(at < 64, tail, turned)], axis=1)


def flip(values):
    return values.astype(F32).T.astype(BF16)


def layer_kernel(
    dims,
    frames,
    cot,
    lengths,
    v_gain1,
    v_bias1,
    v_b_out,
    v_gain2,
    v_bias2,
    v_b_down,
    v_b_up,
    v_b_query,
    v_b_value,
    w_query,
    w_key,
    w_value,
    w_up,
    w_down,
    w_out,
    out_h,
    gin_h,
    gf_h,
    go_h,
    gq_h,
    sums_h,
    ss,
    rs,
    ls,
    os,
    out_o,
    gin_o,
    gf_o,
    go_o,
    gq_o,
    sums_o,
    wqkv_own,
    bias_own,
    up_bias,
    a_all,
    a_t,
    wqkv,
    bias_all,
    wf,
    wo_sib,
    k_tr,
    v_tr,
    k_n,
    v_n,
    q_n,
    q_t,
    att_f,
    att_s,
    att_r,
    hid,
    z_all,
    z_t,
    g_n,
    g_t,
    act,
    gup,
    part_s,
    part_r,
    gz_s,
    gz_r,
    ghl_t,
    gatt_r,
    gatt_t,
    wg,
    wg_t,
    wg_x,
    wg_y,
    wg_zr,
    og_x,
    og_r,
    og_z,
    og_zr,
    dk_t,
    dv_t,
    dq_f,
    dlt,
    q_s,
    d_s,
    dkv_s,
    dkv_r,
    ga_r,
    qg,
    qg_r,
    qg_p,
    qg_z,
    qg_zr,
    sums,
    pairs,
    sum_p,
    sum_z,
    sum_c,
):
    S, C, R, D, GP, HG, FH = dims
    ga_s = a_all.at[pl.ds(0, C * R // 2), :]
    g_nat = a_all.at[pl.ds(C * R // 2, C * R // 2), :]
    OC = C // 2 * GP
    WF = OC + 2 * FH
    pieces = (slice(0, OC + FH), slice(OC + FH, WF))
    HF = R // 2
    CH = C // 2
    DB = D // (S * C)
    PB = C * DB
    s, z, c = lax.axis_index("shard"), lax.axis_index("ctx"), lax.axis_index("tp")
    o = 1 - c
    sib = (s, z, o)
    owed = []
    next_sem = [0]

    def sems(count):
        base = next_sem[0]
        next_sem[0] = base + count
        return base

    def remote(src, dst, index, device):
        return pltpu.make_async_remote_copy(
            src_ref=src,
            dst_ref=dst,
            send_sem=ss.at[index],
            recv_sem=rs.at[index],
            device_id=device,
            device_id_type=MESH,
        )

    def send(src, dst, index, device, when=None, like=None, owe=None):
        def go():
            remote(src, dst, index, device).start()

        if when is None:
            go()
        else:
            pl.when(when)(go)
        if owe is not False:
            owed.append((src if like is None else like, index, when if owe is None else owe))

    def settle(entries):
        for like, index, when in entries:

            def done(like=like, index=index):
                remote(like, like, index, sib).wait_send()

            if when is None:
                done()
            else:
                pl.when(when)(done)

    stored = []

    def store(src, dst):
        copy = pltpu.make_async_copy(src, dst, os.at[len(stored)])
        copy.start()
        stored.append(copy)

    def arrive(dst, index, when=None):
        def go():
            remote(dst, dst, index, sib).wait_recv()

        if when is None:
            go()
        else:
            pl.when(when)(go)

    def plane(k):
        return (lax.rem(s + k, S), z, c)

    near_x = s + 1 - 2 * lax.rem(s, 2)
    near_y = lax.rem(s + 2, 4)
    far = near_y + 1 - 2 * lax.rem(s, 2)
    to_x, to_y = (near_x, z, c), (near_y, z, c)

    def column(k):
        return (s, lax.rem(z + k, C), c)

    def s_from(k):
        return lax.rem(s + S - k, S)

    def z_from(k):
        return lax.rem(z + C - k, C)

    def rows_of(block):
        return pl.ds(pl.multiple_of(block * DB, 16), DB)

    def half_rows(block, half):
        return pl.ds(pl.multiple_of(block * R + half * HF, HF), HF)

    def blk(block):
        return pl.ds(pl.multiple_of(block * HF, HF), HF)

    k_bias = sems(1)
    k_q1 = sems(CH)
    k_q2 = sems(S)
    k_q3 = sems(1)
    k_a = sems(2 * C)
    k_as = sems(2 * C)
    k_f = sems(4 * C)
    k_fp = sems(8 * 2 * C)
    k_wo = sems(1)
    k_att = sems(C)
    k_n2 = sems(1)
    k_part = sems(1)
    k_gz = sems(1)
    k_out = sems(1)
    k_gatt = sems(C)
    k_wg = sems(6 * C)
    k_wgz = sems(C)
    k_ox = sems(1)
    k_og = sems(S)
    k_ogz = sems(C)
    k_dkv = sems(1)
    k_ga = sems(2 * C)
    k_qx = sems(1)
    k_qp = sems(S)
    k_qz = sems(CH)
    k_gin = sems(1)
    k_sp = sems(S)
    k_sz = sems(C)
    k_sc = sems(1)

    barrier = pltpu.get_barrier_semaphore()
    friends = [sib]
    friends += [plane(k) for k in range(1, S)]
    for k in range(1, C):
        friends += [(s, lax.rem(z + k, C), c), (s, lax.rem(z + k, C), o)]
    for friend in friends:
        pl.semaphore_signal(barrier, inc=1, device_id=friend, device_id_type=MESH)

    length = lengths[0]
    lane = lax.broadcasted_iota(jnp.int32, (HF, GP), 1)

    def head_lanes(count, h):
        at = lax.broadcasted_iota(jnp.int32, (count, GP), 1)
        return jnp.logical_and(at >= HD * h, at < HD * (h + 1))

    def only_head(values, h, keep_live=False):
        picked = head_lanes(values.shape[0], h)
        if keep_live:
            at = lax.broadcasted_iota(jnp.int32, values.shape, 1)
            picked = jnp.logical_or(picked, at == LIVE_LANE)
        return jnp.where(picked, values, jnp.zeros_like(values))

    ln1_gain, ln1_bias, b_out, ln2_gain, ln2_bias, b_down = (
        ref[...].reshape(1, D) for ref in (v_gain1, v_bias1, v_b_out, v_gain2, v_bias2, v_b_down)
    )
    for j in range(CH):
        for i, part in enumerate((w_key, w_value, w_query)):
            cols = slice(i * GP, (i + 1) * GP)
            wqkv_own[j, :, cols] = group(part[...].astype(F32), j).astype(BF16)
    mine_rows = rows_of(s * C + z)
    wf[mine_rows, OC : OC + FH] = w_up[...]
    wf[mine_rows, OC + FH :] = w_down[...]
    out_t = w_out[...].astype(F32)
    for j in range(CH):
        wf[mine_rows, j * GP : (j + 1) * GP] = group(out_t, j).astype(BF16)
    for j in range(CH):
        bias_own[j] = jnp.zeros((8, 3 * GP), F32)
        bias_own[j, 0:1, GP : 2 * GP] = group(v_b_value[...].reshape(1, CH * 3 * HD), j)
        bias_own[j, 0:1, 2 * GP :] = group(v_b_query[...].reshape(1, CH * 3 * HD), j)

    def norm(values):
        centred = values - jnp.mean(values, axis=-1, keepdims=True)
        inverse = lax.rsqrt(jnp.mean(centred * centred, axis=-1, keepdims=True) + EPSILON)
        return centred * inverse, inverse

    def live_of(first, count):
        at = z * R + first + lax.broadcasted_iota(jnp.int32, (count, 1), 0)
        return (at < length).astype(F32)

    sums[...] = jnp.zeros_like(sums)
    pl.semaphore_wait(barrier, len(friends))

    c_of_z = z // CH
    for j in range(CH):
        to_z = CH * c + j
        same = jnp.logical_and(to_z == z, c_of_z == c)
        for i in range(CH):
            ok = jnp.logical_and(z - CH * c_of_z == i, jnp.logical_not(same))
            here = wqkv.at[s, c_of_z, pl.ds(i * DB, DB), :]

            def go(i=i, here=here, j=j, to_z=to_z):
                pltpu.make_async_remote_copy(
                    src_ref=wqkv_own.at[j],
                    dst_ref=here,
                    send_sem=ls.at[j],
                    recv_sem=rs.at[k_q1 + i],
                    device_id=(s, to_z, c_of_z),
                    device_id_type=MESH,
                ).start()

            pl.when(ok)(go)

        def keep(j=j):
            wqkv[s, c, pl.ds(pl.multiple_of((z - CH * c) * DB, 16), DB), :] = wqkv_own[j]

        pl.when(same)(keep)
    send(bias_own, bias_all.at[c], k_bias, sib)
    bias_all[c] = bias_own[...]
    can_right, can_left = z + 1 < C, z >= 1

    def line_step(view, t, index, like):
        send(
            view(jnp.maximum(z - t, 0)),
            view(jnp.maximum(z - t, 0)),
            index + 2 * t,
            (s, jnp.minimum(z + 1, C - 1), c),
            goes_right[t],
            like,
        )
        send(
            view(jnp.minimum(z + t, C - 1)),
            view(jnp.minimum(z + t, C - 1)),
            index + 2 * t + 1,
            (s, jnp.maximum(z - 1, 0), c),
            goes_left[t],
            like,
        )

    goes_right = [jnp.logical_and(can_right, z - t >= 0) for t in range(C - 1)]
    goes_left = [jnp.logical_and(can_left, z + t < C) for t in range(C - 1)]
    like_f = [wf.at[pl.ds(0, DB), piece] for piece in pieces]
    like_a = a_all.at[pl.ds(0, HF), :]

    def f_step(t, p):
        view = lambda block: wf.at[rows_of(s * C + block), pieces[p]]
        line_step(view, t, k_f + 2 * C * p, like_f[p])

    def a_step(t):
        line_step(lambda block: a_all.at[half_rows(block, c), :], t, k_a, like_a)

    def from_left(t):
        return jnp.maximum(z - 1 - t, 0), z - 1 - t >= 0

    def from_right(t):
        return jnp.minimum(z + 1 + t, C - 1), z + 1 + t < C

    halves = []
    for piece in pieces:
        middle = (piece.start + piece.stop) // 2
        halves.append((slice(piece.start, middle), slice(middle, piece.stop)))
    like_fh = [wf.at[pl.ds(0, DB), half[0]] for half in halves]

    def row_of(shard, block):
        return rows_of(shard * C + block)

    labels_of = [
        ((2 * t + 2,) + from_left(t), (2 * t + 3,) + from_right(t)) for t in range(C - 1)
    ]
    own_label = ((0, z, None),)
    at_end = jnp.logical_or(z == 0, z == C - 1)
    near_end = jnp.minimum(z, C - 1 - z)
    inside = jnp.logical_not(at_end)
    wo_cols = slice(0, OC)

    def wo_pass(shard, block, ok):
        def go():
            at = row_of(shard, block)
            remote(wf.at[at, wo_cols], wo_sib.at[at, :], k_wo, sib).start()

        if ok is None:
            go()
        else:
            pl.when(ok)(go)


    def f_plane(labels, p):
        for label, block, ok in labels:
            index = k_fp + 8 * label + 4 * p
            at = wf.at[row_of(s, block), pieces[p]]
            send(at, at, index, to_x, ok, like_f[p])
            send(at, at, index + 1, to_y, ok, like_f[p])
            if p == 0:
                wo_pass(s, block, ok)

    def f_relay(labels, p, gate=None, owe=True):
        for label, block, ok in labels:
            index = k_fp + 8 * label + 4 * p
            now = ok if gate is None else jnp.logical_and(ok, gate)
            arrive(wf.at[row_of(near_x, block), pieces[p]], index, now)
            at = wf.at[row_of(near_x, block), halves[p][0]]
            send(at, at, index + 2, to_y, now, like_fh[p], ok if owe else False)
            arrive(wf.at[row_of(near_y, block), pieces[p]], index + 1, now)
            at = wf.at[row_of(near_y, block), halves[p][1]]
            send(at, at, index + 3, to_x, now, like_fh[p], ok if owe else False)
            if p == 0:
                wo_pass(near_x, block, now)
                wo_pass(near_y, block, now)

    def f_finish(labels, p):
        for label, block, ok in labels:
            index = k_fp + 8 * label + 4 * p
            for i in range(2):
                arrive(wf.at[row_of(far, block), halves[p][i]], index + 2 + i, ok)
            if p == 0:
                wo_pass(far, block, ok)

    def f_arrive(t, p):
        for side, (label, block, ok) in enumerate(labels_of[t]):
            arrive(wf.at[row_of(s, block), pieces[p]], k_f + 2 * C * p + 2 * t + side, ok)
        f_plane(labels_of[t], p)

    f_step(0, 0)
    f_step(0, 1)

    def first_norm(i, carry):
        at = pl.ds(pl.multiple_of(i * 64, 64), 64)
        to = pl.ds(pl.multiple_of(z * R + i * 64, 64), 64)
        normed, unused = norm(frames[at, :].astype(F32))
        a_all[to, :] = (normed * ln1_gain + ln1_bias).astype(BF16)
        g_n[at, :] = (cot[at, :].astype(F32) * live_of(i * 64, 64)).astype(BF16)
        return carry

    lax.fori_loop(0, R // 64, first_norm, 0)
    a_step(0)
    for i in range(CH):
        from_z = CH * c + i
        same = jnp.logical_and(from_z == z, c_of_z == c)
        arrive(wqkv.at[s, c, pl.ds(i * DB, DB), :], k_q1 + i, jnp.logical_not(same))
    for k in range(1, S):
        send(wqkv.at[s, c], wqkv.at[s, c], k_q2 + k, plane(k))
    f_plane(own_label, 0)
    f_plane(own_label, 1)
    key_at = lax.broadcasted_iota(jnp.int32, (GP - LIVE_LANE, C * R), 1)
    first_row = lax.broadcasted_iota(jnp.int32, (GP - LIVE_LANE, C * R), 0) == 0
    dead = jnp.where(jnp.logical_and(first_row, key_at >= length), NEG, 0.0)
    k_tr[LIVE_LANE:, :] = dead.astype(BF16)
    v_tr[LIVE_LANE:, :] = jnp.zeros((GP - LIVE_LANE, C * R), BF16)
    g_t[:, :HF] = flip(g_n[:HF, :])
    g_t[:, HF:] = flip(g_n[HF:, :])
    for k in range(1, S):
        arrive(wqkv.at[s_from(k), c], k_q2 + k)
    send(wqkv.at[:, c], wqkv.at[:, c], k_q3, sib)
    arrive(bias_all.at[o], k_bias)
    arrive(wqkv.at[:, o], k_q3)
    bias_z = bias_all[c_of_z, z - CH * c_of_z]

    def project(block, half):
        at = half_rows(block, half)
        rows = a_all[at, :]
        made = nn(rows, wqkv[...].reshape(D, 3 * GP)) + bias_z[0:1, :]
        keys = made[:, :GP].astype(BF16)
        values = made[:, GP : 2 * GP].astype(BF16)
        k_n[at, :] = keys
        v_n[at, :] = values
        k_tr[:LIVE_LANE, at] = flip(keys)[:LIVE_LANE, :]
        v_tr[:LIVE_LANE, at] = flip(values)[:LIVE_LANE, :]

        def own():
            queries = made[:, 2 * GP :].astype(BF16).astype(F32) * (HD**-0.5)
            queries = jnp.where(lane == LIVE_LANE, 1.0, queries).astype(BF16)
            q_n[blk(block), :] = queries
            q_t[:, blk(block)] = flip(queries)
            a_t[:, blk(block)] = flip(rows)

        pl.when(half == c)(own)

    def project_own(i, carry):
        project(z, lax.rem(c + i, 2))
        return carry

    a_given = []

    def remote_when(src, dst, index, device, when):
        def go():
            remote(src, dst, index, device).start()

        pl.when(when)(go)

    lax.fori_loop(0, 2, project_own, 0)
    f_arrive(0, 0)
    f_arrive(0, 1)
    f_relay(own_label, 0)
    f_relay(own_label, 1)
    for t in range(C - 1):
        if t == C - 2:
            for p in range(2):
                f_arrive(1, p)
                f_step(2, p)
        for side, (label, block, ok) in enumerate(labels_of[t]):
            arrive(a_all.at[half_rows(block, c), :], k_a + 2 * t + side, ok)
        if t == C - 3:
            f_step(1, 0)
            f_step(1, 1)
        if t + 1 < C - 1:
            a_step(t + 1)
        for side, (label, block, ok) in enumerate(labels_of[t]):
            at = a_all.at[half_rows(block, c), :]
            remote_when(at, at, k_as + 2 * t + side, sib, ok)
            a_given.append((like_a, k_as + 2 * t + side, ok))

        def come(i, carry, t=t):
            side = i // 2
            block = jnp.where(side == 0, from_left(t)[0], from_right(t)[0])
            ok = jnp.where(side == 0, z - 1 - t >= 0, z + 1 + t < C)

            def other_half():
                at = a_all.at[half_rows(block, o), :]
                remote(at, at, k_as + 2 * t + side, sib).wait_recv()

            def both():
                pl.when(lax.rem(i, 2) == 1)(other_half)
                project(block, lax.rem(c + i, 2))

            pl.when(ok)(both)
            return carry

        lax.fori_loop(0, 4, come, 0)
        if t == C - 3:
            f_relay(labels_of[0], 0)
            f_relay(labels_of[0], 1)
    for p in range(2):
        f_relay(labels_of[1], p, at_end)
    for p in range(2):
        f_finish(own_label, p)
        f_finish(labels_of[0], p)

    TQ = 128

    def attend(block):
        def step(i, carry):
            at = pl.ds(pl.multiple_of(block * HF + i * TQ, TQ), TQ)
            queries = q_n[at, :]
            total = jnp.zeros((TQ, GP), F32)
            log_sums = []
            for h in range(HG):
                scores = nn(only_head(queries, h, True), k_tr[...])
                top = jnp.max(scores, axis=-1, keepdims=True)
                weights = jnp.exp(scores - top)
                norm_sum = jnp.sum(weights, axis=-1, keepdims=True)
                got = nn(weights.astype(BF16), v_n[...]) * (1.0 / norm_sum)
                total = total + only_head(got, h)
                log_sums.append(top + jnp.log(norm_sum))
            att_f[at, :] = total
            for h in range(HG):
                att_f[at, LIVE_LANE + h : LIVE_LANE + h + 1] = log_sums[h]
            att_s[at, :] = total.astype(BF16)
            return carry

        lax.fori_loop(0, HF // TQ, step, 0)

    def attend_all(i, carry):
        inner = jnp.where(i == 0, 2, jnp.where(i == 1, 1, jnp.where(i == 2, 3, 0)))
        block = jnp.where(near_end == 0, lax.rem(i + 1, C), inner)
        block = jnp.where(2 * z < C, block, C - 1 - block)
        attend(block)

        def give():
            hop = lax.rem(block + C - z, C)
            device = (s, block, c)
            remote(att_s.at[blk(block), :], att_r.at[blk(z), :], k_att + hop, device).start()

        def poll_0():
            f_arrive(2, 0)

        def poll_1():
            f_relay(labels_of[1], 0, inside, False)

        def poll_2():
            f_relay(labels_of[1], 1, inside, False)
            f_relay(labels_of[2], 0)
            f_arrive(2, 1)

        pl.when(block != z)(give)
        pl.when(i == 0)(poll_0)
        pl.when(i == 1)(poll_1)
        pl.when(i == 2)(poll_2)
        return carry

    lax.fori_loop(0, C, attend_all, 0)
    att_r[blk(z), :] = att_s[blk(z), :]

    f_finish(labels_of[1], 0)
    f_finish(labels_of[2], 0)
    owed.append((wo_sib, k_wo, None))
    for k in range(1, C):
        arrive(att_r.at[blk(z_from(k)), :], k_att + k)
        remote(att_s.at[blk(z), :], att_r.at[blk(z), :], k_att + k, column(k)).wait_send()
    f_relay(labels_of[2], 1)
    arrive(wo_sib, k_wo)

    settle([entry for entry in owed if entry[0] is like_a])
    settle(a_given)
    owed[:] = [entry for entry in owed if entry[0] is not like_a]
    own_rows = pl.ds(pl.multiple_of(c * HF, HF), HF)
    hidden = frames[own_rows, :].astype(F32) + b_out
    for j in range(CH):
        hidden = hidden + nt(
            att_r[blk(CH * c + j), :], wf[:, j * GP : (j + 1) * GP]
        )
        hidden = hidden + nt(att_r[blk(CH * o + j), :], wo_sib[:, j * GP : (j + 1) * GP])
    hid[...] = hidden
    normed, unused = norm(hidden)
    z_all[own_rows, :] = (normed * ln2_gain + ln2_bias).astype(BF16)
    send(z_all.at[own_rows, :], z_all.at[own_rows, :], k_n2, sib)
    other_rows = pl.ds(pl.multiple_of(o * HF, HF), HF)
    z_t[:, own_rows] = flip(z_all[own_rows, :])
    arrive(z_all.at[other_rows, :], k_n2)
    z_t[:, other_rows] = flip(z_all[other_rows, :])

    f_finish(labels_of[1], 1)
    f_finish(labels_of[2], 1)
    TF, TG = 512, 512

    up_bias[...] = v_b_up[...].reshape(1, FH)

    def units(i, carry):
        cols = pl.ds(pl.multiple_of(i * TF, TF), TF)
        down = pl.ds(pl.multiple_of(OC + FH + i * TF, TF), TF)
        ups = pl.ds(pl.multiple_of(OC + i * TF, TF), TF)
        upper = nn(z_all[...], wf[:, ups]) + up_bias[:, cols]
        cumulative = 0.5 * (1.0 + lax.erf(upper * INV_ROOT_TWO))
        act[:, cols] = (upper * cumulative).astype(BF16)
        slope = cumulative + upper * jnp.exp(-0.5 * upper * upper) * INV_ROOT_TAU
        grad_units = (nn(g_n[...], wf[:, down]) * slope).astype(BF16)
        gup[:, cols] = grad_units
        return carry

    lax.fori_loop(0, FH // TF, units, 0)

    def unit_grads(i, carry):
        cols = pl.ds(pl.multiple_of(i * TG, TG), TG)
        down = pl.ds(pl.multiple_of(FH + i * TG, TG), TG)
        wg[:, cols] = nn(z_t[...], gup[:, cols]).astype(BF16)
        wg[:, down] = nn(g_t[...], act[:, cols]).astype(BF16)
        return carry

    lax.fori_loop(0, FH // TG, unit_grads, 0)

    part_order = ((3, 3), (2, 0), (1, 2), (0, 1))

    def part_z(j):
        chosen = jnp.where(near_end == 0, part_order[j][0], part_order[j][1])
        return jnp.where(2 * z < C, chosen, C - 1 - chosen)

    def part_rows(j):
        return pl.ds(pl.multiple_of(part_z(j) * DB, 16), DB)

    part_a, part_b = slice(0, FH), slice(FH, 2 * FH)
    like_g = wg.at[pl.ds(0, DB), :]
    like_gh = wg.at[pl.ds(0, DB), pl.ds(0, FH)]

    def wg_far(j):
        index = k_wg + 6 * j
        own_z = part_z(j)
        send(wg.at[row_of(far, own_z), part_a], wg_t.at[j, 0], index, to_x, like=like_gh)
        send(wg.at[row_of(far, own_z), part_b], wg_t.at[j, 1], index + 1, to_y, like=like_gh)

    def wg_near(j):
        index = k_wg + 6 * j
        own_z = part_z(j)
        near = wg.at[row_of(near_x, own_z), part_a]
        send(near, wg_x.at[part_rows(j), part_a], index + 2, to_x, like=like_gh)
        near = wg.at[row_of(near_y, own_z), part_b]
        send(near, wg_y.at[part_rows(j), part_b], index + 3, to_y, like=like_gh)

    def add_into(at, cols, others):
        def step(i, carry):
            here = pl.ds(pl.multiple_of(cols.start + i * 256, 256), 256)
            total = wg[at, here].astype(F32)
            for other, rows, start in others:
                there = pl.ds(pl.multiple_of(start + i * 256, 256), 256)
                total = total + other[rows, there].astype(F32)
            wg[at, here] = total.astype(BF16)
            return carry

        lax.fori_loop(0, (cols.stop - cols.start) // 256, step, 0)

    def wg_second(j):
        index = k_wg + 6 * j
        own_z = part_z(j)
        arrive(wg_t.at[j, 0], index)
        at = row_of(near_y, own_z)
        add_into(at, part_a, [(wg_t.at[j, 0], slice(None), 0)])
        near = wg.at[at, part_a]
        send(near, wg_y.at[part_rows(j), part_a], index + 4, to_y, like=like_gh)
        arrive(wg_t.at[j, 1], index + 1)
        at = row_of(near_x, own_z)
        add_into(at, part_b, [(wg_t.at[j, 1], slice(None), 0)])
        near = wg.at[at, part_b]
        send(near, wg_x.at[part_rows(j), part_b], index + 5, to_x, like=like_gh)

    def wg_third(j):
        index = k_wg + 6 * j
        arrive(wg_x.at[part_rows(j), part_a], index + 2)
        arrive(wg_y.at[part_rows(j), part_b], index + 3)
        arrive(wg_y.at[part_rows(j), part_a], index + 4)
        arrive(wg_x.at[part_rows(j), part_b], index + 5)
        at = row_of(s, part_z(j))
        add_into(
            at, slice(0, 2 * FH), [(wg_x, part_rows(j), 0), (wg_y, part_rows(j), 0)]
        )
        if j < C - 1:
            hop = lax.rem(part_z(j) + C - z, C)
            remote(wg.at[at, :], wg_zr.at[hop - 1], k_wgz + hop, (s, part_z(j), c)).start()

    wg_far(0)
    wg_near(0)
    wg_far(1)

    def z_grad(i, carry):
        at = pl.ds(pl.multiple_of(i * 256, 256), 256)
        gz_s[:, at] = nt(gup[other_rows, :], wf[at, OC : OC + FH]).astype(BF16)
        return carry

    lax.fori_loop(0, D // 256, z_grad, 0)
    send(gz_s, gz_r, k_gz, sib)

    gz_rows = jnp.concatenate(
        [nt(gup[own_rows, :], wf[i * 256 : (i + 1) * 256, OC : OC + FH]) for i in range(D // 256)], axis=1
    )
    arrive(gz_r, k_gz)
    grad_z = gz_rows + gz_r[...].astype(F32)
    live_own = live_of(c * HF, HF)
    normed, inverse = norm(hid[...])
    scaled = grad_z * ln2_gain
    inner = (
        scaled
        - jnp.mean(scaled, axis=-1, keepdims=True)
        - normed * jnp.mean(scaled * normed, axis=-1, keepdims=True)
    )
    g_own = g_n[own_rows, :].astype(F32)
    grad_hidden = g_own + inner * inverse
    gin_o[own_rows, :] = grad_hidden
    low = grad_hidden.astype(BF16)
    sums[3:4, :] = jnp.sum(grad_z * normed, axis=0, keepdims=True)
    sums[4:5, :] = jnp.sum(grad_z, axis=0, keepdims=True)
    sums[5:6, :] = jnp.sum(g_own, axis=0, keepdims=True)
    sums[2:3, :] = jnp.sum(low.astype(F32), axis=0, keepdims=True)
    for j in range(CH):
        att_s[blk(CH * c + j), :] = nn(
            low, wf[:, j * GP : (j + 1) * GP]
        ).astype(BF16)
        att_s[blk(CH * o + j), :] = nn(low, wo_sib[:, j * GP : (j + 1) * GP]).astype(BF16)
    for k in range(1, C):
        send(att_s.at[blk(lax.rem(z + k, C)), :], gatt_r.at[blk(z), :], k_gatt + k, column(k))
    gatt_r[blk(z), :] = att_s[blk(z), :]
    ghl_t[...] = flip(low)
    def down_part(i, carry):
        at = pl.ds(pl.multiple_of(i * 256, 256), 256)
        part_s[:, at] = nt(act[other_rows, :], wf[at, OC + FH :]).astype(BF16)
        return carry

    lax.fori_loop(0, D // 256, down_part, 0)
    send(part_s, part_r, k_part, sib)

    for j in range(CH):
        og_x[0, :, j * GP : (j + 1) * GP] = nn(ghl_t[...], att_r[blk(CH * o + j), :]).astype(BF16)
    remote(og_x.at[0], og_x.at[1], k_ox, sib).start()
    old = list(owed)
    owed.clear()
    dk_t[...] = jnp.zeros_like(dk_t)
    dv_t[...] = jnp.zeros_like(dv_t)
    TK = 512

    steps = C * R // TK

    def attend_back(polls):
        def block_step(b, carry):
            block = lax.rem(z + C - b, C)
            at = blk(block)

            def come():
                remote(gatt_r.at[at, :], gatt_r.at[at, :], k_gatt + b, sib).wait_recv()

            pl.when(b > 0)(come)
            gatt_t[...] = flip(gatt_r[at, :])
            product = gatt_r[at, :].astype(F32) * att_f[at, :]
            for h in range(HG):
                rows = slice(h * HF, (h + 1) * HF)
                dlt[rows, 0:1] = jnp.sum(only_head(product, h), axis=-1, keepdims=True)
                dlt[rows, 1:2] = att_f[at, LIVE_LANE + h : LIVE_LANE + h + 1]
                q_s[rows, :] = only_head(q_n[at, :], h, True)
                d_s[rows, :] = only_head(gatt_r[at, :], h)
            dq_f[...] = jnp.zeros_like(dq_f)

            def step(i, carry):
                keys = pl.ds(pl.multiple_of(i * TK, TK), TK)
                weights = jnp.exp(nn(q_s[...], k_tr[:, keys]) - dlt[:, 1:2])
                grads = nn(d_s[...], v_tr[:, keys])
                grad_scores = (weights * (grads - dlt[:, 0:1])).astype(BF16)
                weights = weights.astype(BF16)
                for h in range(HG):
                    head = slice(HD * h, HD * (h + 1))
                    rows = slice(h * HF, (h + 1) * HF)
                    dv_t[head, keys] += nn(gatt_t[head, :], weights[rows, :])
                    dk_t[head, keys] += nn(q_t[head, at], grad_scores[rows, :])
                dq_f[...] += nn(grad_scores, k_n[keys, :])
                for number, poll in polls:
                    pl.when(b * steps + i == number)(poll)
                return carry

            lax.fori_loop(0, steps, step, 0)
            for h in range(HG):
                rows = slice(h * HF, (h + 1) * HF)
                part = only_head(dq_f[rows, :], h)
                total = part if h == 0 else total + part
            g_nat[at, 2 * GP :] = (total * (HD**-0.5)).astype(BF16)
            return carry

        lax.fori_loop(0, C, block_step, 0)

    def og_reduce():
        for k in range(1, S):
            arrive(og_r.at[k - 1], k_og + k)
        own = pl.ds(pl.multiple_of(s * PB, 64), PB)
        total = og_x[0, own, :].astype(F32)
        for k in range(1, S):
            total = total + og_r[k - 1].astype(F32)
        og_z[...] = total.astype(BF16)
        for k in range(1, C):
            at = pl.ds(pl.multiple_of(lax.rem(z + k, C) * DB, 16), DB)
            send(og_z.at[at, :], og_zr.at[k - 1], k_ogz + k, column(k))

    def poll_a():
        wg_second(0)
        wg_near(1)

    def poll_b():
        wg_second(1)
        wg_far(2)
        wg_near(2)

    def poll_c():
        wg_second(2)
        wg_far(3)
        wg_near(3)

    down_rows = jnp.concatenate(
        [nt(act[own_rows, :], wf[i * 256 : (i + 1) * 256, OC + FH :]) for i in range(D // 256)],
        axis=1,
    )
    arrive(part_r, k_part)
    out_rows = live_own * (hid[...] + down_rows + part_r[...].astype(F32) + b_down)
    out_o[own_rows, :] = out_rows.astype(BF16)
    send(out_o.at[own_rows, :], out_o.at[own_rows, :], k_out, sib)
    for i in range(2):
        sums[pl.ds(6 + 2 * c + i, 1), :] = jnp.sum(
            gup[:, i * D : (i + 1) * D].astype(F32), axis=0, keepdims=True
        )
    arrive(og_x.at[1], k_ox)
    remote(og_x.at[0], og_x.at[1], k_ox, sib).wait_send()
    for j in range(CH):
        cols = slice(j * GP, (j + 1) * GP)
        own_part = nn(ghl_t[...], att_r[blk(CH * c + j), :])
        og_x[0, :, cols] = (own_part + og_x[1, :, cols].astype(F32)).astype(BF16)
    attend_back(
        (
            (0, poll_a),
            (3, poll_b),
            (6, lambda: wg_third(0)),
            (10, lambda: wg_third(1)),
            (11, poll_c),
        )
    )

    for i in range(C):
        cols = pl.ds(pl.multiple_of(i * R + o * HF, HF), HF)
        dkv_s[i, 0] = dk_t[:, cols].astype(BF16)
        dkv_s[i, 1] = dv_t[:, cols].astype(BF16)
    send(dkv_s, dkv_r, k_dkv, sib)
    wg_third(2)
    arrive(dkv_r, k_dkv)

    def finish(block):
        cols = pl.ds(pl.multiple_of(block * R + c * HF, HF), HF)
        at = blk(block)
        keys_t = dk_t[:, cols] + dkv_r[block, 0].astype(F32)
        values_t = dv_t[:, cols] + dkv_r[block, 1].astype(F32)
        none = jnp.zeros((GP - LIVE_LANE, HF), F32)
        g_nat[at, :GP] = jnp.concatenate([keys_t, none], axis=0).T.astype(BF16)
        g_nat[at, GP : 2 * GP] = jnp.concatenate([values_t, none], axis=0).T.astype(BF16)
        ga_s[at, :] = nt(g_nat[at, :], wqkv[...].reshape(D, 3 * GP)).astype(BF16)

    def finish_all(b, carry):
        finish(b)
        return carry

    lax.fori_loop(0, C, finish_all, 0)

    like_ga = ga_s.at[pl.ds(0, HF), :]

    def ga_send(t, side):
        target = jnp.where(side == 0, C - 1 - t, t)
        device = (s, jnp.clip(z + 1 - 2 * side, 0, C - 1), c)
        remote(ga_s.at[blk(target), :], ga_r.at[t, side], k_ga + 2 * t + side, device).start()

    def ga_ahead(t, side):
        return C - 1 - t > z if side == 0 else t < z

    for t in range(C - 1):
        for side in range(2):
            behind = z >= 1 if side == 0 else z + 1 < C
            first = jnp.logical_and(ga_ahead(t, side), jnp.logical_not(behind))
            pl.when(first)(lambda t=t, side=side: ga_send(t, side))
            owed.append((like_ga, k_ga + 2 * t + side, ga_ahead(t, side)))

    def ga_hop(u):
        for i in range(2):
            side = jnp.where(2 * z < C, i, 1 - i)
            t = jnp.where(side == 0, u - z, u - (C - 1 - z))
            target = jnp.where(side == 0, C - 1 - t, t)
            inner = jnp.logical_and(z >= 1, z + 1 < C)
            ahead = jnp.where(side == 0, target > z, target < z)
            ok = jnp.logical_and(jnp.logical_and(t >= 0, inner), ahead)

            def add(t=t, side=side, target=target):
                at = blk(target)
                arrive(ga_r.at[t, side], k_ga + 2 * t + side)
                ga_s[at, :] = (ga_s[at, :].astype(F32) + ga_r[t, side].astype(F32)).astype(BF16)
                ga_send(t, side)

            pl.when(ok)(add)

    wg_second(3)
    column_sum = jnp.sum(g_nat[...].astype(F32), axis=0, keepdims=True)
    sums[pl.ds(10 + z, 1), :] = column_sum
    pair_lane = lax.broadcasted_iota(jnp.int32, (PB, 128), 1)
    for i in range(S):
        got = nn(a_t[i * PB : (i + 1) * PB, :], g_nat[...])
        qg[i] = got.reshape(2, CH * DB, 3 * GP).astype(BF16)
        weights = wqkv[i].reshape(PB, 3 * GP).astype(F32)
        with_a = jnp.sum(got * weights, axis=-1, keepdims=True)
        alone = jnp.sum(weights * column_sum, axis=-1, keepdims=True)
        pairs[i * PB : (i + 1) * PB, :] = jnp.where(
            pair_lane == 0, with_a, jnp.where(pair_lane == 1, alone, 0.0)
        )
    send(qg.at[:, o], qg_r, k_qx, sib)
    turned = pairs[...].T
    sums[0:1, :] = (turned[0:1, :] - ln1_bias * turned[1:2, :]) / ln1_gain
    sums[1:2, :] = turned[1:2, :]
    sum_p[s] = sums[...]
    for k in range(1, S):
        send(sum_p.at[s], sum_p.at[s], k_sp + k, plane(k))
    for k in range(1, S):
        at = pl.ds(pl.multiple_of(lax.rem(s + k, S) * PB, 64), PB)
        send(og_x.at[0, at, :], og_r.at[k - 1], k_og + k, plane(k))
    arrive(qg_r, k_qx)
    for i in range(S):
        qg_r[i] = (qg_r[i].astype(F32) + qg[i, c].astype(F32)).astype(BF16)
    for k in range(1, S):
        send(qg_r.at[lax.rem(s + k, S)], qg_p.at[k - 1], k_qp + k, plane(k))
    settle(old)
    arrive(out_o.at[other_rows, :], k_out)
    store(out_o, out_h)
    for k in range(1, S):
        arrive(sum_p.at[s_from(k)], k_sp + k)
    total = sum_p[0]
    for k in range(1, S):
        total = total + sum_p[k]
    sum_z[z] = total
    for k in range(1, C):
        send(sum_z.at[z], sum_z.at[z], k_sz + k, column(k))
    wg_third(3)
    for hop in range(1, C):
        owed.append((like_g, k_wgz + hop, None))
    ga_hop(1)
    og_reduce()
    for u in range(2, C - 1):
        ga_hop(u)
    for k in range(1, S):
        arrive(qg_p.at[k - 1], k_qp + k)
    total = qg_r[s].astype(F32)
    for k in range(1, S):
        total = total + qg_p[k - 1].astype(F32)
    qg_z[...] = total.reshape(CH, DB, 3 * GP).astype(BF16)
    for i in range(CH):
        to_z = CH * c + i
        same = jnp.logical_and(to_z == z, c_of_z == c)
        for j in range(CH):
            ok = jnp.logical_and(z - CH * c_of_z == j, jnp.logical_not(same))

            def go(i=i, j=j, to_z=to_z):
                pltpu.make_async_remote_copy(
                    src_ref=qg_z.at[i],
                    dst_ref=qg_zr.at[j],
                    send_sem=ls.at[CH + i],
                    recv_sem=rs.at[k_qz + j],
                    device_id=(s, to_z, c_of_z),
                    device_id_type=MESH,
                ).start()

            pl.when(ok)(go)

        def keep(i=i):
            qg_zr[z - CH * c] = qg_z[i]

        pl.when(same)(keep)

    for k in range(1, C):
        arrive(sum_z.at[z_from(k)], k_sz + k)
    total = sum_z[0]
    for k in range(1, C):
        total = total + sum_z[k]
    sum_c[c] = total
    send(sum_c.at[c], sum_c.at[c], k_sc, sib)
    own_block = blk(z)
    hid[...] = ga_s[own_block, :].astype(F32)
    for t in range(C - 1):
        for side in range(2):
            target = C - 1 - t if side == 0 else t
            behind = z >= 1 if side == 0 else z + 1 < C

            def add(t=t, side=side):
                arrive(ga_r.at[t, side], k_ga + 2 * t + side)
                hid[...] += ga_r[t, side].astype(F32)

            pl.when(jnp.logical_and(target == z, behind))(add)
    grad_a = hid[...]
    normed, inverse = norm(frames[own_rows, :].astype(F32))
    scaled = grad_a * ln1_gain
    inner = (
        scaled
        - jnp.mean(scaled, axis=-1, keepdims=True)
        - normed * jnp.mean(scaled * normed, axis=-1, keepdims=True)
    )
    gin_o[own_rows, :] = gin_o[own_rows, :] + inner * inverse
    send(gin_o.at[own_rows, :], gin_o.at[own_rows, :], k_gin, sib)
    store(gin_o.at[own_rows, :], gin_h.at[own_rows, :])
    def last(own, got, index, to):
        for k in range(1, C):
            arrive(got.at[k - 1], index + k)
        total = own.astype(F32)
        for k in range(1, C):
            total = total + got[k - 1].astype(F32)
        to[...] = total

    last(wg[rows_of(s * C + z), :], wg_zr, k_wgz, gf_o)
    last(og_z[pl.ds(pl.multiple_of(z * DB, 16), DB), :], og_zr, k_ogz, go_o)
    store(gf_o, gf_h)
    store(go_o, go_h)
    for j in range(CH):
        same = jnp.logical_and(CH * c + j == z, c_of_z == c)
        arrive(qg_zr.at[j], k_qz + j, jnp.logical_not(same))
    gq_o[...] = qg_zr[...].astype(F32)
    store(gq_o, gq_h)
    arrive(sum_c.at[o], k_sc)
    sums_o[...] = sum_c[0] + sum_c[1]
    store(sums_o, sums_h)
    arrive(gin_o.at[other_rows, :], k_gin)
    store(gin_o.at[other_rows, :], gin_h.at[other_rows, :])

    settle(owed)
    for copy in stored:
        copy.wait()
    for j in range(CH):
        same = jnp.logical_and(CH * c + j == z, c_of_z == c)

        def done_weights(j=j):
            pltpu.make_async_remote_copy(
                src_ref=wqkv_own.at[j],
                dst_ref=wqkv_own.at[j],
                send_sem=ls.at[j],
                recv_sem=rs.at[k_q1],
                device_id=sib,
                device_id_type=MESH,
            ).wait_send()
            pltpu.make_async_remote_copy(
                src_ref=qg_z.at[j],
                dst_ref=qg_z.at[j],
                send_sem=ls.at[CH + j],
                recv_sem=rs.at[k_qz],
                device_id=sib,
                device_id_type=MESH,
            ).wait_send()

        pl.when(jnp.logical_not(same))(done_weights)
    assert next_sem[0] <= SEMS


def unpack_kernel(
    CH,
    output,
    grad_input,
    gf_h,
    go_h,
    gq_h,
    sums_h,
    output_o,
    grad_input_o,
    query_o,
    key_o,
    value_o,
    out_o,
    up_o,
    down_o,
    gain1_o,
    bias1_o,
    b_query_o,
    b_value_o,
    b_out_o,
    gain2_o,
    bias2_o,
    b_up_o,
    b_down_o,
    gf,
    go,
    gq,
    sums,
    sem,
):
    c = lax.axis_index("tp")
    FH = up_o.shape[1]
    D = sums.shape[1]
    GP = 256
    pairs = ((output, output_o), (grad_input, grad_input_o))
    pairs += ((gf_h, gf), (go_h, go), (gq_h, gq), (sums_h, sums))
    copies = [
        pltpu.make_async_copy(src, dst, sem.at[i]) for i, (src, dst) in enumerate(pairs)
    ]
    for copy in copies:
        copy.start()
    for copy in copies[2:]:
        copy.wait()
    for i, to in enumerate((key_o, value_o, query_o)):
        cols = slice(i * GP, (i + 1) * GP)
        to[...] = ungroup(gq[0, :, cols], gq[1, :, cols])
    out_o[...] = ungroup(go[:, :GP], go[:, GP : 2 * GP])
    up_o[...] = gf[:, :FH]
    down_o[...] = gf[:, FH:]
    for i, to in enumerate((gain1_o, bias1_o, b_out_o, gain2_o, bias2_o, b_down_o)):
        to[...] = sums[i, :]
    for i in range(FH // D):
        b_up_o[i * D : (i + 1) * D] = sums[6 + 2 * c + i, :]
    for to, start in ((b_value_o, GP), (b_query_o, 2 * GP)):
        row = [sums[pl.ds(10 + CH * c + j, 1), start : start + GP] for j in range(CH)]
        to[...] = ungroup(row[0], row[1])[0, :]
    for copy in copies[:2]:
        copy.wait()


SEMS = 180


def fits(frames, w_query, w_up):
    shards, ctx, cores = (lax.axis_size(name) for name in ("shard", "ctx", "tp"))
    slot_count, seg_rows, width = frames.shape
    heads = w_query.shape[1] * cores // HD
    return (
        slot_count == 1
        and cores == 2
        and ctx % 2 == 0
        and ctx == 4
        and shards == 4
        and heads == 3 * ctx
        and width % (16 * shards * ctx) == 0
        and width % 256 == 0
        and seg_rows % 512 == 0
        and w_up.shape[1] % 512 == 0
        and w_up.shape[1] == 2 * width
        and ctx * seg_rows <= 2048
        and width <= 768
        and w_up.shape[1] <= 1536
    )


def fast_layer(
    frames,
    lengths,
    cotangent,
    ln1_gain,
    ln1_bias,
    w_query,
    b_query,
    w_key,
    w_value,
    b_value,
    w_out,
    b_out,
    ln2_gain,
    ln2_bias,
    w_up,
    b_up,
    w_down,
    b_down,
):
    S, C = lax.axis_size("shard"), lax.axis_size("ctx")
    unused, R, D = frames.shape
    FH = w_up.shape[1]
    HG, CH = 3, C // 2
    G, GP = HG * HD, 256
    DB = D // (S * C)
    HF = R // 2
    PB = C * DB
    T = C * R

    WF = 2 * FH + CH * GP
    vmem = pl.BlockSpec(memory_space=pltpu.VMEM)
    V = pltpu.VMEM
    dims = (S, C, R, D, GP, HG, FH)
    scratch = [
        pltpu.SemaphoreType.DMA((SEMS,)),
        pltpu.SemaphoreType.DMA((SEMS,)),
        pltpu.SemaphoreType.DMA((2 * CH,)),
        pltpu.SemaphoreType.DMA((7,)),
        V((R, D), BF16),
        V((R, D), F32),
        V((DB, 2 * FH), F32),
        V((DB, CH * GP), F32),
        V((CH, DB, 3 * GP), F32),
        V((16, D), F32),
        V((CH, DB, 3 * GP), BF16),
        V((CH, 8, 3 * GP), F32),
        V((1, FH), F32),
        V((T, D), BF16),
        V((D, C * HF), BF16),
        V((S, 2, CH * DB, 3 * GP), BF16),
        V((2, CH, 8, 3 * GP), F32),
        V((D, WF), BF16),
        V((D, CH * GP), BF16),
        V((GP, T), BF16),
        V((GP, T), BF16),
        V((T, GP), BF16),
        V((T, GP), BF16),
        V((C * HF, GP), BF16),
        V((GP, C * HF), BF16),
        V((C * HF, GP), F32),
        V((C * HF, GP), BF16),
        V((C * HF, GP), BF16),
        V((HF, D), F32),
        V((R, D), BF16),
        V((D, R), BF16),
        V((R, D), BF16),
        V((D, R), BF16),
        V((R, FH), BF16),
        V((R, FH), BF16),
        V((HF, D), BF16),
        V((HF, D), BF16),
        V((HF, D), BF16),
        V((HF, D), BF16),
        V((D, HF), BF16),
        V((C * HF, GP), BF16),
        V((GP, HF), BF16),
        V((D, 2 * FH), BF16),
        V((C, 2, DB, FH), BF16),
        V((PB, 2 * FH), BF16),
        V((PB, 2 * FH), BF16),
        V((C - 1, DB, 2 * FH), BF16),
        V((2, D, CH * GP), BF16),
        V((S - 1, PB, CH * GP), BF16),
        V((PB, CH * GP), BF16),
        V((C - 1, DB, CH * GP), BF16),
        V((G, T), F32),
        V((G, T), F32),
        V((3 * HF, GP), F32),
        V((3 * HF, 8), F32),
        V((3 * HF, GP), BF16),
        V((3 * HF, GP), BF16),
        V((C, 2, G, HF), BF16),
        V((C, 2, G, HF), BF16),
        V((C - 1, 2, HF, D), BF16),
        V((S, 2, CH * DB, 3 * GP), BF16),
        V((S, CH * DB, 3 * GP), BF16),
        V((S - 1, CH * DB, 3 * GP), BF16),
        V((CH, DB, 3 * GP), BF16),
        V((CH, DB, 3 * GP), BF16),
        V((16, D), F32),
        V((D, 128), F32),
        V((S, 16, D), F32),
        V((C, 16, D), F32),
        V((2, 16, D), F32),
    ]
    outs = (
        jax.ShapeDtypeStruct((R, D), BF16),
        jax.ShapeDtypeStruct((R, D), F32),
        jax.ShapeDtypeStruct((DB, 2 * FH), F32),
        jax.ShapeDtypeStruct((DB, CH * GP), F32),
        jax.ShapeDtypeStruct((CH, DB, 3 * GP), F32),
        jax.ShapeDtypeStruct((16, D), F32),
    )
    output, grad_input, gf, go, gq, sums = pl.pallas_call(
        functools.partial(layer_kernel, dims),
        out_shape=outs,
        in_specs=[vmem, vmem, pl.BlockSpec(memory_space=pltpu.SMEM)] + [vmem] * 15,
        out_specs=[pl.BlockSpec(memory_space=pltpu.HBM)] * 6,
        scratch_shapes=scratch,
        compiler_params=pltpu.CompilerParams(
            collective_id=0, has_side_effects=True, vmem_limit_bytes=63 << 20
        ),
    )(
        frames[0],
        cotangent[0],
        lengths,
        ln1_gain,
        ln1_bias,
        b_out,
        ln2_gain,
        ln2_bias,
        b_down,
        b_up,
        b_query,
        b_value,
        w_query,
        w_key,
        w_value,
        w_up,
        w_down.T,
        w_out.T,
    )
    flat = [D, D, CH * G, CH * G, D, D, D, FH, D]
    results = pl.pallas_call(
        functools.partial(unpack_kernel, CH),
        out_shape=[
            jax.ShapeDtypeStruct((R, D), BF16),
            jax.ShapeDtypeStruct((R, D), F32),
            jax.ShapeDtypeStruct((DB, CH * G), F32),
            jax.ShapeDtypeStruct((DB, CH * G), F32),
            jax.ShapeDtypeStruct((DB, CH * G), F32),
            jax.ShapeDtypeStruct((DB, CH * G), F32),
            jax.ShapeDtypeStruct((DB, FH), F32),
            jax.ShapeDtypeStruct((DB, FH), F32),
        ]
        + [jax.ShapeDtypeStruct((length,), F32) for length in flat],
        in_specs=[pl.BlockSpec(memory_space=pltpu.HBM)] * 6,
        out_specs=[vmem] * 17,
        scratch_shapes=[
            V((DB, 2 * FH), F32),
            V((DB, CH * GP), F32),
            V((CH, DB, 3 * GP), F32),
            V((16, D), F32),
            pltpu.SemaphoreType.DMA((6,)),
        ],
        compiler_params=pltpu.CompilerParams(vmem_limit_bytes=63 << 20),
    )(output, grad_input, gf, go, gq, sums)
    output, grad_input, g_query, g_key, g_value, g_out, g_up, g_down = results[:8]
    g1, s1, bq, bv, bo, g2, s2, bu, bd = results[8:]
    return (
        output[None],
        grad_input[None],
        g1,
        s1,
        g_query,
        bq,
        g_key,
        g_value,
        bv,
        g_out.T,
        bo,
        g2,
        s2,
        g_up,
        bu,
        g_down.T,
        bd,
    )


def per_device(frames, lengths, cotangent, *params):
    if fits(frames, params[2], params[11]):
        return fast_layer(frames, lengths, cotangent, *params)
    return plain_layer(frames, lengths, cotangent, *params)


def solution(mesh):
    in_specs = (
        P("shard", "ctx", None),
        P("shard"),
        P("shard", "ctx", None),
        P(),
        P(),
        P(("shard", "ctx"), "tp"),
        P("tp"),
        P(("shard", "ctx"), "tp"),
        P(("shard", "ctx"), "tp"),
        P("tp"),
        P("tp", ("shard", "ctx")),
        P(),
        P(),
        P(),
        P(("shard", "ctx"), "tp"),
        P("tp"),
        P("tp", ("shard", "ctx")),
        P(),
    )
    out_specs = (
        P("shard", "ctx", None),
        P("shard", "ctx", None),
        P(),
        P(),
        P(("shard", "ctx"), "tp"),
        P("tp"),
        P(("shard", "ctx"), "tp"),
        P(("shard", "ctx"), "tp"),
        P("tp"),
        P("tp", ("shard", "ctx")),
        P(),
        P(),
        P(),
        P(("shard", "ctx"), "tp"),
        P("tp"),
        P("tp", ("shard", "ctx")),
        P(),
    )
    return jax.shard_map(
        per_device, mesh=mesh, in_specs=in_specs, out_specs=out_specs, check_vma=False
    )
```

```python
import functools
import math

import jax
import jax.numpy as jnp
from jax import lax
from jax.experimental import pallas as pl
from jax.experimental.pallas import tpu as pltpu
from jax.sharding import PartitionSpec as P

HD = 64


EPSILON = 1e-05
INV_ROOT_TWO = 0.7071067811865476
INV_ROOT_TAU = 0.3989422804014327


def norm_rows(values, gain, shift):
    centred = values - jnp.mean(values, axis=-1, keepdims=True)
    inverse = lax.rsqrt(jnp.mean(centred * centred, axis=-1, keepdims=True) + EPSILON)
    normed = centred * inverse
    return (normed * gain + shift, normed, inverse)


def norm_back(grad_rows, normed, inverse, gain):
    scaled = grad_rows * gain
    inner = (
        scaled
        - jnp.mean(scaled, axis=-1, keepdims=True)
        - normed * jnp.mean(scaled * normed, axis=-1, keepdims=True)
    )
    return (inner * inverse, jnp.sum(grad_rows * normed, axis=0), jnp.sum(grad_rows, axis=0))


def gelu_slope(values):
    return (
        0.5 * (1.0 + lax.erf(values * INV_ROOT_TWO))
        + values * jnp.exp(-0.5 * values * values) * INV_ROOT_TAU
    )


def pair_scores(queries, block_keys, score_scale):
    return (
        jnp.einsum("qhd,khd->hqk", queries, block_keys, preferred_element_type=jnp.float32)
        * score_scale
    )


def live_weights(scores, query_live, key_live, log_totals):
    both_live = query_live[None, :, None] & key_live[None, None, :]
    return jnp.where(both_live, jnp.exp(scores - log_totals[:, :, None]), 0.0)


def in_blocks(array, block_rows):
    return array.reshape((array.shape[0] // block_rows, block_rows) + array.shape[1:])


def slot_forward(queries, slot_keys, slot_values, query_live, key_live, key_block, score_scale):
    seg_rows, head_count, head_dim = queries.shape
    key_starts = jnp.arange(slot_keys.shape[0] // key_block, dtype=jnp.int32) * key_block
    blocks = (
        in_blocks(slot_keys, key_block),
        in_blocks(slot_values, key_block),
        in_blocks(key_live, key_block),
        key_starts,
    )
    start_state = (
        jnp.full((head_count, seg_rows), -jnp.inf, jnp.float32),
        jnp.zeros((head_count, seg_rows), jnp.float32),
    )

    def totals_step(carried, scan_item):
        block_keys, block_values, block_live, block_start = scan_item
        running_max, running_sum = carried
        scores = jnp.where(
            block_live[None, None, :], pair_scores(queries, block_keys, score_scale), -jnp.inf
        )
        new_max = jnp.maximum(running_max, jnp.max(scores, axis=-1))
        new_sum = running_sum * jnp.exp(running_max - new_max) + jnp.sum(
            jnp.exp(scores - new_max[:, :, None]), axis=-1
        )
        return ((new_max, new_sum), None)

    def whole_slot(ignored):
        final_state, unused = lax.scan(totals_step, start_state, blocks)
        log_totals = final_state[0] + jnp.log(final_state[1])

        def output_step(output_sum, scan_item):
            block_keys, block_values, block_live, block_start = scan_item
            weights_here = live_weights(
                pair_scores(queries, block_keys, score_scale), query_live, block_live, log_totals
            ).astype(jnp.bfloat16)
            return (
                output_sum
                + jnp.einsum(
                    "hqk,khd->qhd", weights_here, block_values, preferred_element_type=jnp.float32
                ),
                None,
            )

        attended, unused_too = lax.scan(
            output_step, jnp.zeros((seg_rows, head_count, head_dim), jnp.float32), blocks
        )
        return (log_totals, attended)

    return whole_slot(0)


def slot_back(
    queries,
    grad_att,
    log_totals,
    delta,
    slot_keys,
    slot_values,
    query_live,
    key_live,
    key_block,
    score_scale,
):
    seg_rows, head_count, head_dim = queries.shape
    key_starts = jnp.arange(slot_keys.shape[0] // key_block, dtype=jnp.int32) * key_block
    blocks = (
        in_blocks(slot_keys, key_block),
        in_blocks(slot_values, key_block),
        in_blocks(key_live, key_block),
        key_starts,
    )

    def grad_step(grad_query, scan_item):
        block_keys, block_values, block_live, block_start = scan_item
        partial_value = grad_query
        weights_full = live_weights(
            pair_scores(queries, block_keys, score_scale), query_live, block_live, log_totals
        )
        grad_probs = jnp.einsum(
            "qhd,khd->hqk", grad_att, block_values, preferred_element_type=jnp.float32
        )
        grad_scores = (weights_full * (grad_probs - delta[:, :, None])).astype(jnp.bfloat16)
        partial_value = (
            partial_value
            + jnp.einsum(
                "hqk,khd->qhd", grad_scores, block_keys, preferred_element_type=jnp.float32
            )
            * score_scale
        )
        grad_value = jnp.einsum(
            "hqk,qhd->khd",
            weights_full.astype(jnp.bfloat16),
            grad_att,
            preferred_element_type=jnp.float32,
        )
        grad_key = (
            jnp.einsum("hqk,qhd->khd", grad_scores, queries, preferred_element_type=jnp.float32)
            * score_scale
        )
        return (partial_value, (grad_key, grad_value))

    def whole_slot(ignored):
        grad_query, key_parts = lax.scan(
            grad_step, jnp.zeros((seg_rows, head_count, head_dim), jnp.float32), blocks
        )
        return (
            grad_query,
            key_parts[0].reshape(slot_keys.shape),
            key_parts[1].reshape(slot_keys.shape),
        )

    return whole_slot(0)


def plain_layer(
    frames,
    lengths,
    cotangent,
    ln1_gain,
    ln1_bias,
    w_query,
    b_query,
    w_key,
    w_value,
    b_value,
    w_out,
    b_out,
    ln2_gain,
    ln2_bias,
    w_up,
    b_up,
    w_down,
    b_down,
):
    slot_count, seg_rows, model_width = frames.shape
    row_count = slot_count * seg_rows
    head_cols = w_query.shape[1]
    head_count = head_cols // HD
    seq_length = seg_rows * lax.axis_size("ctx")
    seg_start = lax.axis_index("ctx") * seg_rows
    score_scale = HD ** (-0.5)
    key_block = math.gcd(seq_length, 512)
    positions = seg_start + jnp.arange(seg_rows, dtype=jnp.int32)
    query_live = positions[None, :] < lengths[:, None]
    key_live = jnp.arange(seq_length, dtype=jnp.int32)[None, :] < lengths[:, None]
    live_rows = query_live.astype(jnp.float32).reshape(row_count, 1)
    weight_query, weight_key, weight_value, weight_out = (
        lax.all_gather(w_query, ("shard", "ctx"), axis=0, tiled=True),
        lax.all_gather(w_key, ("shard", "ctx"), axis=0, tiled=True),
        lax.all_gather(w_value, ("shard", "ctx"), axis=0, tiled=True),
        lax.all_gather(w_out, ("shard", "ctx"), axis=1, tiled=True),
    )
    frames_flat = frames.astype(jnp.float32).reshape(row_count, model_width)
    first, normed_one, inverse_one = norm_rows(frames_flat, ln1_gain, ln1_bias)
    first_low = first.astype(jnp.bfloat16)
    queries = (
        jnp.dot(first_low, weight_query, preferred_element_type=jnp.float32) + b_query
    ).astype(jnp.bfloat16)
    keys_local = jnp.dot(first_low, weight_key, preferred_element_type=jnp.float32).astype(
        jnp.bfloat16
    )
    values_local = (
        jnp.dot(first_low, weight_value, preferred_element_type=jnp.float32) + b_value
    ).astype(jnp.bfloat16)
    keys_all, values_all = (
        lax.all_gather(
            keys_local.reshape(slot_count, seg_rows, head_cols), "ctx", axis=1, tiled=True
        ),
        lax.all_gather(
            values_local.reshape(slot_count, seg_rows, head_cols), "ctx", axis=1, tiled=True
        ),
    )
    query_heads = queries.reshape(slot_count, seg_rows, head_count, HD)
    key_heads = keys_all.reshape(slot_count, seq_length, head_count, HD)
    value_heads = values_all.reshape(slot_count, seq_length, head_count, HD)
    slot = 0
    log_totals, attended_slot = slot_forward(
        query_heads[slot],
        key_heads[slot],
        value_heads[slot],
        query_live[slot],
        key_live[slot],
        key_block,
        score_scale,
    )
    totals_list = [log_totals]
    attended_list = [attended_slot]
    attended = jnp.stack(attended_list).reshape(row_count, head_cols)
    attended_low = attended.astype(jnp.bfloat16)
    attn_sum = lax.psum(
        jnp.dot(attended_low, weight_out, preferred_element_type=jnp.float32).astype(jnp.bfloat16),
        "tp",
    ).astype(jnp.float32)
    hidden = frames_flat + attn_sum + b_out
    weight_up, weight_down = (
        lax.all_gather(w_up, ("shard", "ctx"), axis=0, tiled=True),
        lax.all_gather(w_down, ("shard", "ctx"), axis=1, tiled=True),
    )
    second, normed_two, inverse_two = norm_rows(hidden, ln2_gain, ln2_bias)
    second_low = second.astype(jnp.bfloat16)
    upper = jnp.dot(second_low, weight_up, preferred_element_type=jnp.float32) + b_up
    activated = jax.nn.gelu(upper, approximate=False).astype(jnp.bfloat16)
    mlp_sum = lax.psum(
        jnp.dot(activated, weight_down, preferred_element_type=jnp.float32).astype(jnp.bfloat16),
        "tp",
    ).astype(jnp.float32)
    output = (
        (live_rows * (hidden + mlp_sum + b_down))
        .astype(jnp.bfloat16)
        .reshape(slot_count, seg_rows, model_width)
    )
    grad_out = live_rows * cotangent.astype(jnp.float32).reshape(row_count, model_width)
    grad_out_low = grad_out.astype(jnp.bfloat16)
    grad_b_down = jnp.sum(grad_out, axis=0)
    grad_w_down = jnp.einsum(
        "rf,rd->fd", activated, grad_out_low, preferred_element_type=jnp.float32
    )
    grad_act = jnp.einsum(
        "rd,fd->rf", grad_out_low, weight_down, preferred_element_type=jnp.float32
    )
    grad_upper = (grad_act * gelu_slope(upper)).astype(jnp.bfloat16)
    grad_b_up = jnp.sum(grad_upper.astype(jnp.float32), axis=0)
    grad_w_up = jnp.einsum("rd,rf->df", second_low, grad_upper, preferred_element_type=jnp.float32)
    grad_second = lax.psum(
        jnp.einsum("rf,df->rd", grad_upper, weight_up, preferred_element_type=jnp.float32).astype(
            jnp.bfloat16
        ),
        "tp",
    ).astype(jnp.float32)
    grad_norm_two, grad_ln2_gain, grad_ln2_bias = norm_back(
        grad_second, normed_two, inverse_two, ln2_gain
    )
    grad_hidden = grad_out + grad_norm_two
    grad_hidden_low = grad_hidden.astype(jnp.bfloat16)
    grad_b_out = jnp.sum(grad_hidden_low.astype(jnp.float32), axis=0)
    grad_w_out = jnp.einsum(
        "rc,rd->cd", attended_low, grad_hidden_low, preferred_element_type=jnp.float32
    )
    grad_att = jnp.einsum(
        "rd,cd->rc", grad_hidden_low, weight_out, preferred_element_type=jnp.float32
    ).astype(jnp.bfloat16)
    delta = jnp.sum(
        (grad_att.astype(jnp.float32) * attended).reshape(row_count, head_count, HD), axis=-1
    )
    delta_heads = delta.reshape(slot_count, seg_rows, head_count)
    grad_att_heads = grad_att.reshape(slot_count, seg_rows, head_count, HD)
    slot = 0
    grad_query_slot, key_part, value_part = slot_back(
        query_heads[slot],
        grad_att_heads[slot],
        totals_list[slot],
        delta_heads[slot].T,
        key_heads[slot],
        value_heads[slot],
        query_live[slot],
        key_live[slot],
        key_block,
        score_scale,
    )
    grad_query_list = [grad_query_slot]
    key_part_list = [key_part.reshape(seq_length, head_cols)]
    value_part_list = [value_part.reshape(seq_length, head_cols)]
    grad_keys, grad_values = (
        lax.psum_scatter(
            jnp.stack(key_part_list).astype(jnp.bfloat16), "ctx", scatter_dimension=1, tiled=True
        ).astype(jnp.float32),
        lax.psum_scatter(
            jnp.stack(value_part_list).astype(jnp.bfloat16), "ctx", scatter_dimension=1, tiled=True
        ).astype(jnp.float32),
    )
    grad_query_low = jnp.stack(grad_query_list).reshape(row_count, head_cols).astype(jnp.bfloat16)
    grad_key_low = grad_keys.reshape(row_count, head_cols).astype(jnp.bfloat16)
    grad_value_low = grad_values.reshape(row_count, head_cols).astype(jnp.bfloat16)
    grad_b_query = jnp.sum(grad_query_low.astype(jnp.float32), axis=0)
    grad_b_value = jnp.sum(grad_value_low.astype(jnp.float32), axis=0)
    grad_w_query = jnp.einsum(
        "rd,rc->dc", first_low, grad_query_low, preferred_element_type=jnp.float32
    )
    grad_w_key = jnp.einsum(
        "rd,rc->dc", first_low, grad_key_low, preferred_element_type=jnp.float32
    )
    grad_w_value = jnp.einsum(
        "rd,rc->dc", first_low, grad_value_low, preferred_element_type=jnp.float32
    )
    first_terms = jnp.einsum(
        "rc,dc->rd", grad_query_low, weight_query, preferred_element_type=jnp.float32
    )
    first_terms = first_terms + jnp.einsum(
        "rc,dc->rd", grad_key_low, weight_key, preferred_element_type=jnp.float32
    )
    first_terms = first_terms + jnp.einsum(
        "rc,dc->rd", grad_value_low, weight_value, preferred_element_type=jnp.float32
    )
    grad_first = lax.psum(first_terms.astype(jnp.bfloat16), "tp").astype(jnp.float32)
    grad_norm_one, grad_ln1_gain, grad_ln1_bias = norm_back(
        grad_first, normed_one, inverse_one, ln1_gain
    )
    grad_input = (grad_hidden + grad_norm_one).reshape(slot_count, seg_rows, model_width)
    shard_grads = (
        lax.psum_scatter(grad_w_query, ("shard", "ctx"), scatter_dimension=0, tiled=True),
        lax.psum_scatter(grad_w_key, ("shard", "ctx"), scatter_dimension=0, tiled=True),
        lax.psum_scatter(grad_w_value, ("shard", "ctx"), scatter_dimension=0, tiled=True),
        lax.psum_scatter(grad_w_out, ("shard", "ctx"), scatter_dimension=1, tiled=True),
        lax.psum_scatter(grad_w_up, ("shard", "ctx"), scatter_dimension=0, tiled=True),
        lax.psum_scatter(grad_w_down, ("shard", "ctx"), scatter_dimension=1, tiled=True),
    )
    small_sums = lax.psum(
        (
            grad_ln1_gain,
            grad_ln1_bias,
            grad_b_query,
            grad_b_value,
            grad_b_out,
            grad_ln2_gain,
            grad_ln2_bias,
            grad_b_up,
            grad_b_down,
        ),
        ("shard", "ctx"),
    )
    return (
        output,
        grad_input,
        small_sums[0],
        small_sums[1],
        shard_grads[0],
        small_sums[2],
        shard_grads[1],
        shard_grads[2],
        small_sums[3],
        shard_grads[3],
        small_sums[4],
        small_sums[5],
        small_sums[6],
        shard_grads[4],
        small_sums[7],
        shard_grads[5],
        small_sums[8],
    )


MESH = pl.DeviceIdType.MESH
F32 = jnp.float32
BF16 = jnp.bfloat16
NEG = -1e30
LIVE_LANE = 192


def nn(left, right):
    return jnp.dot(left, right, preferred_element_type=F32)


def nt(left, right):
    return lax.dot_general(left, right, (((1,), (1,)), ((), ())), preferred_element_type=F32)


def group(values, j):
    taken = values[:, :256] if j == 0 else pltpu.roll(values[:, 128:384], 192, 1)
    at = lax.broadcasted_iota(jnp.int32, taken.shape, 1)
    return jnp.where(at < 3 * HD, taken, 0.0)


def ungroup(first, second):
    turned = pltpu.roll(second, 64, 1)
    at = lax.broadcasted_iota(jnp.int32, turned.shape, 1)
    tail = jnp.concatenate([first[:, 128:], first[:, 128:]], axis=1)
    return jnp.concatenate([first[:, :128], jnp.where(at < 64, tail, turned)], axis=1)


def flip(values):
    return values.astype(F32).T.astype(BF16)


def layer_kernel(
    dims,
    frames,
    cot,
    lengths,
    v_gain1,
    v_bias1,
    v_b_out,
    v_gain2,
    v_bias2,
    v_b_down,
    v_b_up,
    v_b_query,
    v_b_value,
    w_query,
    w_key,
    w_value,
    w_up,
    w_down,
    w_out,
    out_h,
    gin_h,
    gf_h,
    go_h,
    gq_h,
    sums_h,
    ss,
    rs,
    ls,
    os,
    out_o,
    gin_o,
    gf_o,
    go_o,
    gq_o,
    sums_o,
    wqkv_own,
    bias_own,
    up_bias,
    a_all,
    a_t,
    wqkv,
    bias_all,
    wf,
    wo_sib,
    k_tr,
    v_tr,
    k_n,
    v_n,
    q_n,
    q_t,
    att_f,
    att_s,
    att_r,
    hid,
    z_all,
    z_t,
    g_n,
    g_t,
    act,
    gup,
    part_s,
    part_r,
    gz_s,
    gz_r,
    ghl_t,
    gatt_r,
    gatt_t,
    wg,
    wg_t,
    wg_x,
    wg_y,
    wg_zr,
    og_x,
    og_r,
    og_z,
    og_zr,
    dk_t,
    dv_t,
    dq_f,
    dlt,
    q_s,
    d_s,
    dkv_s,
    dkv_r,
    ga_r,
    qg,
    qg_r,
    qg_p,
    qg_z,
    qg_zr,
    sums,
    pairs,
    sum_p,
    sum_z,
    sum_c,
):
    S, C, R, D, GP, HG, FH = dims
    ga_s = a_all.at[pl.ds(0, C * R // 2), :]
    g_nat = a_all.at[pl.ds(C * R // 2, C * R // 2), :]
    OC = C // 2 * GP
    WF = OC + 2 * FH
    pieces = (slice(0, OC + FH), slice(OC + FH, WF))
    HF = R // 2
    CH = C // 2
    DB = D // (S * C)
    PB = C * DB
    s, z, c = lax.axis_index("shard"), lax.axis_index("ctx"), lax.axis_index("tp")
    o = 1 - c
    sib = (s, z, o)
    owed = []
    next_sem = [0]

    def sems(count):
        base = next_sem[0]
        next_sem[0] = base + count
        return base

    def remote(src, dst, index, device, sent=None):
        return pltpu.make_async_remote_copy(
            src_ref=src,
            dst_ref=dst,
            send_sem=ss.at[index if sent is None else sent],
            recv_sem=rs.at[index],
            device_id=device,
            device_id_type=MESH,
        )

    def send(src, dst, index, device, when=None, like=None, owe=None, sent=None):
        def go():
            remote(src, dst, index, device, sent).start()

        if when is None:
            go()
        else:
            pl.when(when)(go)
        if owe is not False:
            owed.append((src if like is None else like, index, when if owe is None else owe))

    def settle(entries):
        for like, index, when in entries:

            def done(like=like, index=index):
                remote(like, like, index, sib).wait_send()

            if when is None:
                done()
            else:
                pl.when(when)(done)

    stored = []

    def store(src, dst):
        copy = pltpu.make_async_copy(src, dst, os.at[len(stored)])
        copy.start()
        stored.append(copy)

    def arrive(dst, index, when=None):
        def go():
            remote(dst, dst, index, sib, 0).wait_recv()

        if when is None:
            go()
        else:
            pl.when(when)(go)

    def plane(k):
        return (lax.rem(s + k, S), z, c)

    near_x = s + 1 - 2 * lax.rem(s, 2)
    near_y = lax.rem(s + 2, 4)
    far = near_y + 1 - 2 * lax.rem(s, 2)
    to_x, to_y = (near_x, z, c), (near_y, z, c)

    def column(k):
        return (s, lax.rem(z + k, C), c)

    def s_from(k):
        return lax.rem(s + S - k, S)

    def z_from(k):
        return lax.rem(z + C - k, C)

    def rows_of(block):
        return pl.ds(pl.multiple_of(block * DB, 16), DB)

    def half_rows(block, half):
        return pl.ds(pl.multiple_of(block * R + half * HF, HF), HF)

    def blk(block):
        return pl.ds(pl.multiple_of(block * HF, HF), HF)

    k_bias = sems(1)
    k_q1 = sems(CH)
    k_q2 = sems(S - 1) - 1
    k_q3 = sems(1)
    k_a = sems(2 * (C - 1))
    k_as = sems(2 * (C - 1))
    k_f = sems(4 * (C - 1))
    k_fs = sems(1)
    k_gs = sems(1)
    k_wo = sems(1)
    k_att = sems(C - 1) - 1
    k_n2 = sems(1)
    k_part = sems(1)
    k_gz = sems(1)
    k_out = sems(1)
    k_gatt = sems(C - 1) - 1
    k_wgz = sems(C - 1) - 1
    k_ox = sems(1)
    k_og = sems(S - 1) - 1
    k_ogz = sems(C - 1) - 1
    k_dkv = sems(1)
    k_ga = sems(2 * (C - 1))
    k_qx = sems(1)
    k_qp = sems(S - 1) - 1
    k_qz = sems(CH)
    k_gin = sems(1)
    k_sp = sems(S - 1) - 1
    k_sz = sems(C - 1) - 1
    k_sc = sems(1)
    k_fp = sems(8 * (2 * C - 1))
    k_wg = sems(6 * C)

    barrier = pltpu.get_barrier_semaphore()
    friends = [sib]
    friends += [plane(k) for k in range(1, S)]
    for k in range(1, C):
        friends += [(s, lax.rem(z + k, C), c), (s, lax.rem(z + k, C), o)]
    for friend in friends:
        pl.semaphore_signal(barrier, inc=1, device_id=friend, device_id_type=MESH)

    length = lengths[0]
    lane = lax.broadcasted_iota(jnp.int32, (HF, GP), 1)

    def head_lanes(count, h):
        at = lax.broadcasted_iota(jnp.int32, (count, GP), 1)
        return jnp.logical_and(at >= HD * h, at < HD * (h + 1))

    def only_head(values, h, keep_live=False):
        picked = head_lanes(values.shape[0], h)
        if keep_live:
            at = lax.broadcasted_iota(jnp.int32, values.shape, 1)
            picked = jnp.logical_or(picked, at == LIVE_LANE)
        return jnp.where(picked, values, jnp.zeros_like(values))

    ln1_gain, ln1_bias, b_out, ln2_gain, ln2_bias, b_down = (
        ref[...].reshape(1, D) for ref in (v_gain1, v_bias1, v_b_out, v_gain2, v_bias2, v_b_down)
    )
    for j in range(CH):
        for i, part in enumerate((w_key, w_value, w_query)):
            cols = slice(i * GP, (i + 1) * GP)
            wqkv_own[j, :, cols] = group(part[...].astype(F32), j).astype(BF16)
    mine_rows = rows_of(s * C + z)
    wf[mine_rows, OC : OC + FH] = w_up[...]
    wf[mine_rows, OC + FH :] = w_down[...]
    out_t = w_out[...].astype(F32)
    for j in range(CH):
        wf[mine_rows, j * GP : (j + 1) * GP] = group(out_t, j).astype(BF16)
    for j in range(CH):
        bias_own[j] = jnp.zeros((8, 3 * GP), F32)
        bias_own[j, 0:1, GP : 2 * GP] = group(v_b_value[...].reshape(1, CH * 3 * HD), j)
        bias_own[j, 0:1, 2 * GP :] = group(v_b_query[...].reshape(1, CH * 3 * HD), j)

    def norm(values):
        centred = values - jnp.mean(values, axis=-1, keepdims=True)
        inverse = lax.rsqrt(jnp.mean(centred * centred, axis=-1, keepdims=True) + EPSILON)
        return centred * inverse, inverse

    def live_of(first, count):
        at = z * R + first + lax.broadcasted_iota(jnp.int32, (count, 1), 0)
        return (at < length).astype(F32)

    sums[...] = jnp.zeros_like(sums)
    pl.semaphore_wait(barrier, len(friends))

    c_of_z = z // CH
    for j in range(CH):
        to_z = CH * c + j
        same = jnp.logical_and(to_z == z, c_of_z == c)
        for i in range(CH):
            ok = jnp.logical_and(z - CH * c_of_z == i, jnp.logical_not(same))
            here = wqkv.at[s, c_of_z, pl.ds(i * DB, DB), :]

            def go(i=i, here=here, j=j, to_z=to_z):
                pltpu.make_async_remote_copy(
                    src_ref=wqkv_own.at[j],
                    dst_ref=here,
                    send_sem=ls.at[j],
                    recv_sem=rs.at[k_q1 + i],
                    device_id=(s, to_z, c_of_z),
                    device_id_type=MESH,
                ).start()

            pl.when(ok)(go)

        def keep(j=j):
            wqkv[s, c, pl.ds(pl.multiple_of((z - CH * c) * DB, 16), DB), :] = wqkv_own[j]

        pl.when(same)(keep)
    send(bias_own, bias_all.at[c], k_bias, sib)
    bias_all[c] = bias_own[...]
    can_right, can_left = z + 1 < C, z >= 1

    def line_step(view, t, index, like):
        send(
            view(jnp.maximum(z - t, 0)),
            view(jnp.maximum(z - t, 0)),
            index + 2 * t,
            (s, jnp.minimum(z + 1, C - 1), c),
            goes_right[t],
            like,
        )
        send(
            view(jnp.minimum(z + t, C - 1)),
            view(jnp.minimum(z + t, C - 1)),
            index + 2 * t + 1,
            (s, jnp.maximum(z - 1, 0), c),
            goes_left[t],
            like,
        )

    goes_right = [jnp.logical_and(can_right, z - t >= 0) for t in range(C - 1)]
    goes_left = [jnp.logical_and(can_left, z + t < C) for t in range(C - 1)]
    like_f = [wf.at[pl.ds(0, DB), piece] for piece in pieces]
    like_a = a_all.at[pl.ds(0, HF), :]

    def f_step(t, p):
        view = lambda block: wf.at[rows_of(s * C + block), pieces[p]]
        line_step(view, t, k_f + 2 * (C - 1) * p, like_f[p])

    def a_step(t):
        line_step(lambda block: a_all.at[half_rows(block, c), :], t, k_a, like_a)

    def from_left(t):
        return jnp.maximum(z - 1 - t, 0), z - 1 - t >= 0

    def from_right(t):
        return jnp.minimum(z + 1 + t, C - 1), z + 1 + t < C

    halves = []
    for piece in pieces:
        middle = (piece.start + piece.stop) // 2
        halves.append((slice(piece.start, middle), slice(middle, piece.stop)))

    def row_of(shard, block):
        return rows_of(shard * C + block)

    labels_of = [
        ((2 * t + 1,) + from_left(t), (2 * t + 2,) + from_right(t)) for t in range(C - 1)
    ]
    own_label = ((0, z, None),)
    at_end = jnp.logical_or(z == 0, z == C - 1)
    near_end = jnp.minimum(z, C - 1 - z)
    inside = jnp.logical_not(at_end)
    wo_cols = slice(0, OC)

    def wo_pass(shard, block, ok):
        def go():
            at = row_of(shard, block)
            remote(wf.at[at, wo_cols], wo_sib.at[at, :], k_wo, sib).start()

        if ok is None:
            go()
        else:
            pl.when(ok)(go)


    def f_plane(labels, p):
        for label, block, ok in labels:
            index = k_fp + 8 * label + 4 * p
            at = wf.at[row_of(s, block), pieces[p]]
            send(at, at, index, to_x, ok, None, False, k_fs)
            send(at, at, index + 1, to_y, ok, None, False, k_fs)
            if p == 0:
                wo_pass(s, block, ok)

    def f_relay(labels, p, gate=None):
        for label, block, ok in labels:
            index = k_fp + 8 * label + 4 * p
            now = ok if gate is None else jnp.logical_and(ok, gate)
            arrive(wf.at[row_of(near_x, block), pieces[p]], index, now)
            at = wf.at[row_of(near_x, block), halves[p][0]]
            send(at, at, index + 2, to_y, now, None, False, k_fs)
            arrive(wf.at[row_of(near_y, block), pieces[p]], index + 1, now)
            at = wf.at[row_of(near_y, block), halves[p][1]]
            send(at, at, index + 3, to_x, now, None, False, k_fs)
            if p == 0:
                wo_pass(near_x, block, now)
                wo_pass(near_y, block, now)

    def f_finish(labels, p):
        for label, block, ok in labels:
            index = k_fp + 8 * label + 4 * p
            for i in range(2):
                arrive(wf.at[row_of(far, block), halves[p][i]], index + 2 + i, ok)
            if p == 0:
                wo_pass(far, block, ok)

    def f_arrive(t, p):
        for side, (label, block, ok) in enumerate(labels_of[t]):
            arrive(wf.at[row_of(s, block), pieces[p]], k_f + 2 * (C - 1) * p + 2 * t + side, ok)
        f_plane(labels_of[t], p)

    f_step(0, 0)
    f_step(0, 1)

    def first_norm(i, carry):
        at = pl.ds(pl.multiple_of(i * 64, 64), 64)
        to = pl.ds(pl.multiple_of(z * R + i * 64, 64), 64)
        normed, unused = norm(frames[at, :].astype(F32))
        a_all[to, :] = (normed * ln1_gain + ln1_bias).astype(BF16)
        g_n[at, :] = (cot[at, :].astype(F32) * live_of(i * 64, 64)).astype(BF16)
        return carry

    lax.fori_loop(0, R // 64, first_norm, 0)
    a_step(0)
    for i in range(CH):
        from_z = CH * c + i
        same = jnp.logical_and(from_z == z, c_of_z == c)
        arrive(wqkv.at[s, c, pl.ds(i * DB, DB), :], k_q1 + i, jnp.logical_not(same))
    for k in range(1, S):
        send(wqkv.at[s, c], wqkv.at[s, c], k_q2 + k, plane(k))
    f_plane(own_label, 0)
    f_plane(own_label, 1)
    key_at = lax.broadcasted_iota(jnp.int32, (GP - LIVE_LANE, C * R), 1)
    first_row = lax.broadcasted_iota(jnp.int32, (GP - LIVE_LANE, C * R), 0) == 0
    dead = jnp.where(jnp.logical_and(first_row, key_at >= length), NEG, 0.0)
    k_tr[LIVE_LANE:, :] = dead.astype(BF16)
    v_tr[LIVE_LANE:, :] = jnp.zeros((GP - LIVE_LANE, C * R), BF16)
    g_t[:, :HF] = flip(g_n[:HF, :])
    g_t[:, HF:] = flip(g_n[HF:, :])
    for k in range(1, S):
        arrive(wqkv.at[s_from(k), c], k_q2 + k)
    send(wqkv.at[:, c], wqkv.at[:, c], k_q3, sib)
    arrive(bias_all.at[o], k_bias)
    arrive(wqkv.at[:, o], k_q3)
    bias_z = bias_all[c_of_z, z - CH * c_of_z]

    def project(block, half):
        at = half_rows(block, half)
        rows = a_all[at, :]
        made = nn(rows, wqkv[...].reshape(D, 3 * GP)) + bias_z[0:1, :]
        keys = made[:, :GP].astype(BF16)
        values = made[:, GP : 2 * GP].astype(BF16)
        k_n[at, :] = keys
        v_n[at, :] = values
        k_tr[:LIVE_LANE, at] = flip(keys)[:LIVE_LANE, :]
        v_tr[:LIVE_LANE, at] = flip(values)[:LIVE_LANE, :]

        def own():
            queries = made[:, 2 * GP :].astype(BF16).astype(F32) * (HD**-0.5)
            queries = jnp.where(lane == LIVE_LANE, 1.0, queries).astype(BF16)
            q_n[blk(block), :] = queries
            q_t[:, blk(block)] = flip(queries)
            a_t[:, blk(block)] = flip(rows)

        pl.when(half == c)(own)

    def project_own(i, carry):
        project(z, lax.rem(c + i, 2))
        return carry

    a_given = []

    def remote_when(src, dst, index, device, when):
        def go():
            remote(src, dst, index, device).start()

        pl.when(when)(go)

    lax.fori_loop(0, 2, project_own, 0)
    f_arrive(0, 0)
    f_arrive(0, 1)
    f_relay(own_label, 0)
    f_relay(own_label, 1)
    for t in range(C - 1):
        if t == C - 2:
            for p in range(2):
                f_arrive(1, p)
                f_step(2, p)
        for side, (label, block, ok) in enumerate(labels_of[t]):
            arrive(a_all.at[half_rows(block, c), :], k_a + 2 * t + side, ok)
        if t == C - 3:
            f_step(1, 0)
            f_step(1, 1)
        if t + 1 < C - 1:
            a_step(t + 1)
        for side, (label, block, ok) in enumerate(labels_of[t]):
            at = a_all.at[half_rows(block, c), :]
            remote_when(at, at, k_as + 2 * t + side, sib, ok)
            a_given.append((like_a, k_as + 2 * t + side, ok))

        def come(i, carry, t=t):
            side = i // 2
            block = jnp.where(side == 0, from_left(t)[0], from_right(t)[0])
            ok = jnp.where(side == 0, z - 1 - t >= 0, z + 1 + t < C)

            def other_half():
                at = a_all.at[half_rows(block, o), :]
                remote(at, at, k_as + 2 * t + side, sib).wait_recv()

            def both():
                pl.when(lax.rem(i, 2) == 1)(other_half)
                project(block, lax.rem(c + i, 2))

            pl.when(ok)(both)
            return carry

        lax.fori_loop(0, 4, come, 0)
        if t == C - 3:
            f_relay(labels_of[0], 0)
            f_relay(labels_of[0], 1)
    for p in range(2):
        f_relay(labels_of[1], p, at_end)
    for p in range(2):
        f_finish(own_label, p)
        f_finish(labels_of[0], p)

    TQ = 128

    def attend(block):
        def step(i, carry):
            at = pl.ds(pl.multiple_of(block * HF + i * TQ, TQ), TQ)
            queries = q_n[at, :]
            total = jnp.zeros((TQ, GP), F32)
            log_sums = []
            for h in range(HG):
                scores = nn(only_head(queries, h, True), k_tr[...])
                top = jnp.max(scores, axis=-1, keepdims=True)
                weights = jnp.exp(scores - top)
                norm_sum = jnp.sum(weights, axis=-1, keepdims=True)
                got = nn(weights.astype(BF16), v_n[...]) * (1.0 / norm_sum)
                total = total + only_head(got, h)
                log_sums.append(top + jnp.log(norm_sum))
            att_f[at, :] = total
            for h in range(HG):
                att_f[at, LIVE_LANE + h : LIVE_LANE + h + 1] = log_sums[h]
            att_s[at, :] = total.astype(BF16)
            return carry

        lax.fori_loop(0, HF // TQ, step, 0)

    def attend_all(i, carry):
        inner = jnp.where(i == 0, 2, jnp.where(i == 1, 1, jnp.where(i == 2, 3, 0)))
        block = jnp.where(near_end == 0, lax.rem(i + 1, C), inner)
        block = jnp.where(2 * z < C, block, C - 1 - block)
        attend(block)

        def give():
            hop = lax.rem(block + C - z, C)
            device = (s, block, c)
            remote(att_s.at[blk(block), :], att_r.at[blk(z), :], k_att + hop, device).start()

        def poll_0():
            f_arrive(2, 0)

        def poll_1():
            f_relay(labels_of[1], 0, inside)

        def poll_2():
            f_relay(labels_of[1], 1, inside)
            f_relay(labels_of[2], 0)
            f_arrive(2, 1)

        pl.when(block != z)(give)
        pl.when(i == 0)(poll_0)
        pl.when(i == 1)(poll_1)
        pl.when(i == 2)(poll_2)
        return carry

    lax.fori_loop(0, C, attend_all, 0)
    att_r[blk(z), :] = att_s[blk(z), :]

    f_finish(labels_of[1], 0)
    f_finish(labels_of[2], 0)
    owed.append((wo_sib, k_wo, None))
    owed.append((wf.at[pl.ds(0, 3 * C * DB), :], k_fs, None))
    for k in range(1, C):
        arrive(att_r.at[blk(z_from(k)), :], k_att + k)
        remote(att_s.at[blk(z), :], att_r.at[blk(z), :], k_att + k, column(k)).wait_send()
    f_relay(labels_of[2], 1)
    arrive(wo_sib, k_wo)

    settle([entry for entry in owed if entry[0] is like_a])
    settle(a_given)
    owed[:] = [entry for entry in owed if entry[0] is not like_a]
    own_rows = pl.ds(pl.multiple_of(c * HF, HF), HF)
    hidden = frames[own_rows, :].astype(F32) + b_out
    for j in range(CH):
        hidden = hidden + nt(
            att_r[blk(CH * c + j), :], wf[:, j * GP : (j + 1) * GP]
        )
        hidden = hidden + nt(att_r[blk(CH * o + j), :], wo_sib[:, j * GP : (j + 1) * GP])
    hid[...] = hidden
    normed, unused = norm(hidden)
    z_all[own_rows, :] = (normed * ln2_gain + ln2_bias).astype(BF16)
    send(z_all.at[own_rows, :], z_all.at[own_rows, :], k_n2, sib)
    other_rows = pl.ds(pl.multiple_of(o * HF, HF), HF)
    z_t[:, own_rows] = flip(z_all[own_rows, :])
    arrive(z_all.at[other_rows, :], k_n2)
    z_t[:, other_rows] = flip(z_all[other_rows, :])

    f_finish(labels_of[1], 1)
    f_finish(labels_of[2], 1)
    TF, TG = 512, 512

    up_bias[...] = v_b_up[...].reshape(1, FH)

    def units(i, carry):
        cols = pl.ds(pl.multiple_of(i * TF, TF), TF)
        down = pl.ds(pl.multiple_of(OC + FH + i * TF, TF), TF)
        ups = pl.ds(pl.multiple_of(OC + i * TF, TF), TF)
        upper = nn(z_all[...], wf[:, ups]) + up_bias[:, cols]
        cumulative = 0.5 * (1.0 + lax.erf(upper * INV_ROOT_TWO))
        act[:, cols] = (upper * cumulative).astype(BF16)
        slope = cumulative + upper * jnp.exp(-0.5 * upper * upper) * INV_ROOT_TAU
        grad_units = (nn(g_n[...], wf[:, down]) * slope).astype(BF16)
        gup[:, cols] = grad_units
        return carry

    lax.fori_loop(0, FH // TF, units, 0)

    def unit_grads(i, carry):
        cols = pl.ds(pl.multiple_of(i * TG, TG), TG)
        down = pl.ds(pl.multiple_of(FH + i * TG, TG), TG)
        wg[:, cols] = nn(z_t[...], gup[:, cols]).astype(BF16)
        wg[:, down] = nn(g_t[...], act[:, cols]).astype(BF16)
        return carry

    lax.fori_loop(0, FH // TG, unit_grads, 0)

    part_order = ((3, 3), (2, 0), (1, 2), (0, 1))

    def part_z(j):
        chosen = jnp.where(near_end == 0, part_order[j][0], part_order[j][1])
        return jnp.where(2 * z < C, chosen, C - 1 - chosen)

    def part_rows(j):
        return pl.ds(pl.multiple_of(part_z(j) * DB, 16), DB)

    part_a, part_b = slice(0, FH), slice(FH, 2 * FH)

    def wg_far(j):
        index = k_wg + 6 * j
        own_z = part_z(j)
        send(wg.at[row_of(far, own_z), part_a], wg_t.at[j, 0], index, to_x, owe=False, sent=k_gs)
        send(wg.at[row_of(far, own_z), part_b], wg_t.at[j, 1], index + 1, to_y, owe=False, sent=k_gs)

    def wg_near(j):
        index = k_wg + 6 * j
        own_z = part_z(j)
        near = wg.at[row_of(near_x, own_z), part_a]
        send(near, wg_x.at[part_rows(j), part_a], index + 2, to_x, owe=False, sent=k_gs)
        near = wg.at[row_of(near_y, own_z), part_b]
        send(near, wg_y.at[part_rows(j), part_b], index + 3, to_y, owe=False, sent=k_gs)

    def add_into(at, cols, others):
        def step(i, carry):
            here = pl.ds(pl.multiple_of(cols.start + i * 256, 256), 256)
            total = wg[at, here].astype(F32)
            for other, rows, start in others:
                there = pl.ds(pl.multiple_of(start + i * 256, 256), 256)
                total = total + other[rows, there].astype(F32)
            wg[at, here] = total.astype(BF16)
            return carry

        lax.fori_loop(0, (cols.stop - cols.start) // 256, step, 0)

    def wg_second(j):
        index = k_wg + 6 * j
        own_z = part_z(j)
        arrive(wg_t.at[j, 0], index)
        at = row_of(near_y, own_z)
        add_into(at, part_a, [(wg_t.at[j, 0], slice(None), 0)])
        near = wg.at[at, part_a]
        send(near, wg_y.at[part_rows(j), part_a], index + 4, to_y, owe=False, sent=k_gs)
        arrive(wg_t.at[j, 1], index + 1)
        at = row_of(near_x, own_z)
        add_into(at, part_b, [(wg_t.at[j, 1], slice(None), 0)])
        near = wg.at[at, part_b]
        send(near, wg_x.at[part_rows(j), part_b], index + 5, to_x, owe=False, sent=k_gs)

    def wg_third(j):
        index = k_wg + 6 * j
        arrive(wg_x.at[part_rows(j), part_a], index + 2)
        arrive(wg_y.at[part_rows(j), part_b], index + 3)
        arrive(wg_y.at[part_rows(j), part_a], index + 4)
        arrive(wg_x.at[part_rows(j), part_b], index + 5)
        at = row_of(s, part_z(j))
        add_into(
            at, slice(0, 2 * FH), [(wg_x, part_rows(j), 0), (wg_y, part_rows(j), 0)]
        )
        if j < C - 1:
            hop = lax.rem(part_z(j) + C - z, C)
            device = (s, part_z(j), c)
            remote(wg.at[at, :], wg_zr.at[hop - 1], k_wgz + hop, device, k_gs).start()

    wg_far(0)
    wg_near(0)
    wg_far(1)

    def z_grad(i, carry):
        at = pl.ds(pl.multiple_of(i * 256, 256), 256)
        gz_s[:, at] = nt(gup[other_rows, :], wf[at, OC : OC + FH]).astype(BF16)
        return carry

    lax.fori_loop(0, D // 256, z_grad, 0)
    send(gz_s, gz_r, k_gz, sib)

    gz_rows = jnp.concatenate(
        [nt(gup[own_rows, :], wf[i * 256 : (i + 1) * 256, OC : OC + FH]) for i in range(D // 256)], axis=1
    )
    arrive(gz_r, k_gz)
    grad_z = gz_rows + gz_r[...].astype(F32)
    live_own = live_of(c * HF, HF)
    normed, inverse = norm(hid[...])
    scaled = grad_z * ln2_gain
    inner = (
        scaled
        - jnp.mean(scaled, axis=-1, keepdims=True)
        - normed * jnp.mean(scaled * normed, axis=-1, keepdims=True)
    )
    g_own = g_n[own_rows, :].astype(F32)
    grad_hidden = g_own + inner * inverse
    gin_o[own_rows, :] = grad_hidden
    low = grad_hidden.astype(BF16)
    sums[3:4, :] = jnp.sum(grad_z * normed, axis=0, keepdims=True)
    sums[4:5, :] = jnp.sum(grad_z, axis=0, keepdims=True)
    sums[5:6, :] = jnp.sum(g_own, axis=0, keepdims=True)
    sums[2:3, :] = jnp.sum(low.astype(F32), axis=0, keepdims=True)
    for j in range(CH):
        att_s[blk(CH * c + j), :] = nn(
            low, wf[:, j * GP : (j + 1) * GP]
        ).astype(BF16)
        att_s[blk(CH * o + j), :] = nn(low, wo_sib[:, j * GP : (j + 1) * GP]).astype(BF16)
    for k in range(1, C):
        send(att_s.at[blk(lax.rem(z + k, C)), :], gatt_r.at[blk(z), :], k_gatt + k, column(k))
    gatt_r[blk(z), :] = att_s[blk(z), :]
    ghl_t[...] = flip(low)
    def down_part(i, carry):
        at = pl.ds(pl.multiple_of(i * 256, 256), 256)
        part_s[:, at] = nt(act[other_rows, :], wf[at, OC + FH :]).astype(BF16)
        return carry

    lax.fori_loop(0, D // 256, down_part, 0)
    send(part_s, part_r, k_part, sib)

    for j in range(CH):
        og_x[0, :, j * GP : (j + 1) * GP] = nn(ghl_t[...], att_r[blk(CH * o + j), :]).astype(BF16)
    remote(og_x.at[0], og_x.at[1], k_ox, sib).start()
    old = list(owed)
    owed.clear()
    dk_t[...] = jnp.zeros_like(dk_t)
    dv_t[...] = jnp.zeros_like(dv_t)
    TK = 512

    steps = C * R // TK

    def attend_back(polls):
        def block_step(b, carry):
            block = lax.rem(z + C - b, C)
            at = blk(block)

            def come():
                remote(gatt_r.at[at, :], gatt_r.at[at, :], k_gatt + b, sib).wait_recv()

            pl.when(b > 0)(come)
            gatt_t[...] = flip(gatt_r[at, :])
            product = gatt_r[at, :].astype(F32) * att_f[at, :]
            for h in range(HG):
                rows = slice(h * HF, (h + 1) * HF)
                dlt[rows, 0:1] = jnp.sum(only_head(product, h), axis=-1, keepdims=True)
                dlt[rows, 1:2] = att_f[at, LIVE_LANE + h : LIVE_LANE + h + 1]
                q_s[rows, :] = only_head(q_n[at, :], h, True)
                d_s[rows, :] = only_head(gatt_r[at, :], h)
            dq_f[...] = jnp.zeros_like(dq_f)

            def step(i, carry):
                keys = pl.ds(pl.multiple_of(i * TK, TK), TK)
                weights = jnp.exp(nn(q_s[...], k_tr[:, keys]) - dlt[:, 1:2])
                grads = nn(d_s[...], v_tr[:, keys])
                grad_scores = (weights * (grads - dlt[:, 0:1])).astype(BF16)
                weights = weights.astype(BF16)
                for h in range(HG):
                    head = slice(HD * h, HD * (h + 1))
                    rows = slice(h * HF, (h + 1) * HF)
                    dv_t[head, keys] += nn(gatt_t[head, :], weights[rows, :])
                    dk_t[head, keys] += nn(q_t[head, at], grad_scores[rows, :])
                dq_f[...] += nn(grad_scores, k_n[keys, :])
                for number, poll in polls:
                    pl.when(b * steps + i == number)(poll)
                return carry

            lax.fori_loop(0, steps, step, 0)
            for h in range(HG):
                rows = slice(h * HF, (h + 1) * HF)
                part = only_head(dq_f[rows, :], h)
                total = part if h == 0 else total + part
            g_nat[at, 2 * GP :] = (total * (HD**-0.5)).astype(BF16)
            return carry

        lax.fori_loop(0, C, block_step, 0)

    def og_reduce():
        for k in range(1, S):
            arrive(og_r.at[k - 1], k_og + k)
        own = pl.ds(pl.multiple_of(s * PB, 64), PB)
        total = og_x[0, own, :].astype(F32)
        for k in range(1, S):
            total = total + og_r[k - 1].astype(F32)
        og_z[...] = total.astype(BF16)
        for k in range(1, C):
            at = pl.ds(pl.multiple_of(lax.rem(z + k, C) * DB, 16), DB)
            send(og_z.at[at, :], og_zr.at[k - 1], k_ogz + k, column(k))

    def poll_a():
        wg_second(0)
        wg_near(1)

    def poll_b():
        wg_second(1)
        wg_far(2)
        wg_near(2)

    def poll_c():
        wg_second(2)
        wg_far(3)
        wg_near(3)

    down_rows = jnp.concatenate(
        [nt(act[own_rows, :], wf[i * 256 : (i + 1) * 256, OC + FH :]) for i in range(D // 256)],
        axis=1,
    )
    arrive(part_r, k_part)
    out_rows = live_own * (hid[...] + down_rows + part_r[...].astype(F32) + b_down)
    out_o[own_rows, :] = out_rows.astype(BF16)
    send(out_o.at[own_rows, :], out_o.at[own_rows, :], k_out, sib)
    for i in range(2):
        sums[pl.ds(6 + 2 * c + i, 1), :] = jnp.sum(
            gup[:, i * D : (i + 1) * D].astype(F32), axis=0, keepdims=True
        )
    arrive(og_x.at[1], k_ox)
    remote(og_x.at[0], og_x.at[1], k_ox, sib).wait_send()
    for j in range(CH):
        cols = slice(j * GP, (j + 1) * GP)
        own_part = nn(ghl_t[...], att_r[blk(CH * c + j), :])
        og_x[0, :, cols] = (own_part + og_x[1, :, cols].astype(F32)).astype(BF16)
    attend_back(
        (
            (0, poll_a),
            (3, poll_b),
            (6, lambda: wg_third(0)),
            (10, lambda: wg_third(1)),
            (11, poll_c),
        )
    )

    for i in range(C):
        cols = pl.ds(pl.multiple_of(i * R + o * HF, HF), HF)
        dkv_s[i, 0] = dk_t[:, cols].astype(BF16)
        dkv_s[i, 1] = dv_t[:, cols].astype(BF16)
    send(dkv_s, dkv_r, k_dkv, sib)
    wg_third(2)
    arrive(dkv_r, k_dkv)

    def finish(block):
        cols = pl.ds(pl.multiple_of(block * R + c * HF, HF), HF)
        at = blk(block)
        keys_t = dk_t[:, cols] + dkv_r[block, 0].astype(F32)
        values_t = dv_t[:, cols] + dkv_r[block, 1].astype(F32)
        none = jnp.zeros((GP - LIVE_LANE, HF), F32)
        g_nat[at, :GP] = jnp.concatenate([keys_t, none], axis=0).T.astype(BF16)
        g_nat[at, GP : 2 * GP] = jnp.concatenate([values_t, none], axis=0).T.astype(BF16)
        ga_s[at, :] = nt(g_nat[at, :], wqkv[...].reshape(D, 3 * GP)).astype(BF16)

    def finish_all(b, carry):
        finish(b)
        return carry

    lax.fori_loop(0, C, finish_all, 0)

    like_ga = ga_s.at[pl.ds(0, HF), :]

    def ga_send(t, side):
        target = jnp.where(side == 0, C - 1 - t, t)
        device = (s, jnp.clip(z + 1 - 2 * side, 0, C - 1), c)
        remote(ga_s.at[blk(target), :], ga_r.at[t, side], k_ga + 2 * t + side, device).start()

    def ga_ahead(t, side):
        return C - 1 - t > z if side == 0 else t < z

    for t in range(C - 1):
        for side in range(2):
            behind = z >= 1 if side == 0 else z + 1 < C
            first = jnp.logical_and(ga_ahead(t, side), jnp.logical_not(behind))
            pl.when(first)(lambda t=t, side=side: ga_send(t, side))
            owed.append((like_ga, k_ga + 2 * t + side, ga_ahead(t, side)))

    def ga_hop(u):
        for i in range(2):
            side = jnp.where(2 * z < C, i, 1 - i)
            t = jnp.where(side == 0, u - z, u - (C - 1 - z))
            target = jnp.where(side == 0, C - 1 - t, t)
            inner = jnp.logical_and(z >= 1, z + 1 < C)
            ahead = jnp.where(side == 0, target > z, target < z)
            ok = jnp.logical_and(jnp.logical_and(t >= 0, inner), ahead)

            def add(t=t, side=side, target=target):
                at = blk(target)
                arrive(ga_r.at[t, side], k_ga + 2 * t + side)
                ga_s[at, :] = (ga_s[at, :].astype(F32) + ga_r[t, side].astype(F32)).astype(BF16)
                ga_send(t, side)

            pl.when(ok)(add)

    wg_second(3)
    column_sum = jnp.sum(g_nat[...].astype(F32), axis=0, keepdims=True)
    sums[pl.ds(10 + z, 1), :] = column_sum
    pair_lane = lax.broadcasted_iota(jnp.int32, (PB, 128), 1)
    for i in range(S):
        got = nn(a_t[i * PB : (i + 1) * PB, :], g_nat[...])
        qg[i] = got.reshape(2, CH * DB, 3 * GP).astype(BF16)
        weights = wqkv[i].reshape(PB, 3 * GP).astype(F32)
        with_a = jnp.sum(got * weights, axis=-1, keepdims=True)
        alone = jnp.sum(weights * column_sum, axis=-1, keepdims=True)
        pairs[i * PB : (i + 1) * PB, :] = jnp.where(
            pair_lane == 0, with_a, jnp.where(pair_lane == 1, alone, 0.0)
        )
    send(qg.at[:, o], qg_r, k_qx, sib)
    turned = pairs[...].T
    sums[0:1, :] = (turned[0:1, :] - ln1_bias * turned[1:2, :]) / ln1_gain
    sums[1:2, :] = turned[1:2, :]
    sum_p[s] = sums[...]
    for k in range(1, S):
        send(sum_p.at[s], sum_p.at[s], k_sp + k, plane(k))
    for k in range(1, S):
        at = pl.ds(pl.multiple_of(lax.rem(s + k, S) * PB, 64), PB)
        send(og_x.at[0, at, :], og_r.at[k - 1], k_og + k, plane(k))
    arrive(qg_r, k_qx)
    for i in range(S):
        qg_r[i] = (qg_r[i].astype(F32) + qg[i, c].astype(F32)).astype(BF16)
    for k in range(1, S):
        send(qg_r.at[lax.rem(s + k, S)], qg_p.at[k - 1], k_qp + k, plane(k))
    settle(old)
    arrive(out_o.at[other_rows, :], k_out)
    store(out_o, out_h)
    for k in range(1, S):
        arrive(sum_p.at[s_from(k)], k_sp + k)
    total = sum_p[0]
    for k in range(1, S):
        total = total + sum_p[k]
    sum_z[z] = total
    for k in range(1, C):
        send(sum_z.at[z], sum_z.at[z], k_sz + k, column(k))
    wg_third(3)
    owed.append((wg.at[pl.ds(0, (4 * C - 1) * DB), :], k_gs, None))
    ga_hop(1)
    og_reduce()
    for u in range(2, C - 1):
        ga_hop(u)
    for k in range(1, S):
        arrive(qg_p.at[k - 1], k_qp + k)
    total = qg_r[s].astype(F32)
    for k in range(1, S):
        total = total + qg_p[k - 1].astype(F32)
    qg_z[...] = total.reshape(CH, DB, 3 * GP).astype(BF16)
    for i in range(CH):
        to_z = CH * c + i
        same = jnp.logical_and(to_z == z, c_of_z == c)
        for j in range(CH):
            ok = jnp.logical_and(z - CH * c_of_z == j, jnp.logical_not(same))

            def go(i=i, j=j, to_z=to_z):
                pltpu.make_async_remote_copy(
                    src_ref=qg_z.at[i],
                    dst_ref=qg_zr.at[j],
                    send_sem=ls.at[CH + i],
                    recv_sem=rs.at[k_qz + j],
                    device_id=(s, to_z, c_of_z),
                    device_id_type=MESH,
                ).start()

            pl.when(ok)(go)

        def keep(i=i):
            qg_zr[z - CH * c] = qg_z[i]

        pl.when(same)(keep)

    for k in range(1, C):
        arrive(sum_z.at[z_from(k)], k_sz + k)
    total = sum_z[0]
    for k in range(1, C):
        total = total + sum_z[k]
    sum_c[c] = total
    send(sum_c.at[c], sum_c.at[c], k_sc, sib)
    own_block = blk(z)
    hid[...] = ga_s[own_block, :].astype(F32)
    for t in range(C - 1):
        for side in range(2):
            target = C - 1 - t if side == 0 else t
            behind = z >= 1 if side == 0 else z + 1 < C

            def add(t=t, side=side):
                arrive(ga_r.at[t, side], k_ga + 2 * t + side)
                hid[...] += ga_r[t, side].astype(F32)

            pl.when(jnp.logical_and(target == z, behind))(add)
    grad_a = hid[...]
    normed, inverse = norm(frames[own_rows, :].astype(F32))
    scaled = grad_a * ln1_gain
    inner = (
        scaled
        - jnp.mean(scaled, axis=-1, keepdims=True)
        - normed * jnp.mean(scaled * normed, axis=-1, keepdims=True)
    )
    gin_o[own_rows, :] = gin_o[own_rows, :] + inner * inverse
    send(gin_o.at[own_rows, :], gin_o.at[own_rows, :], k_gin, sib)
    store(gin_o.at[own_rows, :], gin_h.at[own_rows, :])
    def last(own, got, index, to):
        for k in range(1, C):
            arrive(got.at[k - 1], index + k)
        total = own.astype(F32)
        for k in range(1, C):
            total = total + got[k - 1].astype(F32)
        to[...] = total

    last(wg[rows_of(s * C + z), :], wg_zr, k_wgz, gf_o)
    last(og_z[pl.ds(pl.multiple_of(z * DB, 16), DB), :], og_zr, k_ogz, go_o)
    store(gf_o, gf_h)
    store(go_o, go_h)
    for j in range(CH):
        same = jnp.logical_and(CH * c + j == z, c_of_z == c)
        arrive(qg_zr.at[j], k_qz + j, jnp.logical_not(same))
    gq_o[...] = qg_zr[...].astype(F32)
    store(gq_o, gq_h)
    arrive(sum_c.at[o], k_sc)
    sums_o[...] = sum_c[0] + sum_c[1]
    store(sums_o, sums_h)
    arrive(gin_o.at[other_rows, :], k_gin)
    store(gin_o.at[other_rows, :], gin_h.at[other_rows, :])

    settle(owed)
    for copy in stored:
        copy.wait()
    for j in range(CH):
        same = jnp.logical_and(CH * c + j == z, c_of_z == c)

        def done_weights(j=j):
            pltpu.make_async_remote_copy(
                src_ref=wqkv_own.at[j],
                dst_ref=wqkv_own.at[j],
                send_sem=ls.at[j],
                recv_sem=rs.at[k_q1],
                device_id=sib,
                device_id_type=MESH,
            ).wait_send()
            pltpu.make_async_remote_copy(
                src_ref=qg_z.at[j],
                dst_ref=qg_z.at[j],
                send_sem=ls.at[CH + j],
                recv_sem=rs.at[k_qz],
                device_id=sib,
                device_id_type=MESH,
            ).wait_send()

        pl.when(jnp.logical_not(same))(done_weights)
    assert (next_sem[0], k_fp) == (SEMS, SENDS)


def unpack_kernel(
    CH,
    output,
    grad_input,
    gf_h,
    go_h,
    gq_h,
    sums_h,
    output_o,
    grad_input_o,
    query_o,
    key_o,
    value_o,
    out_o,
    up_o,
    down_o,
    gain1_o,
    bias1_o,
    b_query_o,
    b_value_o,
    b_out_o,
    gain2_o,
    bias2_o,
    b_up_o,
    b_down_o,
    gf,
    go,
    gq,
    sums,
    sem,
):
    c = lax.axis_index("tp")
    FH = up_o.shape[1]
    D = sums.shape[1]
    GP = 256
    pairs = ((output, output_o), (grad_input, grad_input_o))
    pairs += ((gf_h, gf), (go_h, go), (gq_h, gq), (sums_h, sums))
    copies = [
        pltpu.make_async_copy(src, dst, sem.at[i]) for i, (src, dst) in enumerate(pairs)
    ]
    for copy in copies:
        copy.start()
    for copy in copies[2:]:
        copy.wait()
    for i, to in enumerate((key_o, value_o, query_o)):
        cols = slice(i * GP, (i + 1) * GP)
        to[...] = ungroup(gq[0, :, cols], gq[1, :, cols])
    out_o[...] = ungroup(go[:, :GP], go[:, GP : 2 * GP])
    up_o[...] = gf[:, :FH]
    down_o[...] = gf[:, FH:]
    for i, to in enumerate((gain1_o, bias1_o, b_out_o, gain2_o, bias2_o, b_down_o)):
        to[...] = sums[i, :]
    for i in range(FH // D):
        b_up_o[i * D : (i + 1) * D] = sums[6 + 2 * c + i, :]
    for to, start in ((b_value_o, GP), (b_query_o, 2 * GP)):
        row = [sums[pl.ds(10 + CH * c + j, 1), start : start + GP] for j in range(CH)]
        to[...] = ungroup(row[0], row[1])[0, :]
    for copy in copies[:2]:
        copy.wait()


SEMS, SENDS = 155, 75


def fits(frames, w_query, w_up):
    shards, ctx, cores = (lax.axis_size(name) for name in ("shard", "ctx", "tp"))
    slot_count, seg_rows, width = frames.shape
    heads = w_query.shape[1] * cores // HD
    return (
        slot_count == 1
        and cores == 2
        and ctx % 2 == 0
        and ctx == 4
        and shards == 4
        and heads == 3 * ctx
        and width % (16 * shards * ctx) == 0
        and width % 256 == 0
        and seg_rows % 512 == 0
        and w_up.shape[1] % 512 == 0
        and w_up.shape[1] == 2 * width
        and ctx * seg_rows <= 2048
        and width <= 768
        and w_up.shape[1] <= 1536
    )


def fast_layer(
    frames,
    lengths,
    cotangent,
    ln1_gain,
    ln1_bias,
    w_query,
    b_query,
    w_key,
    w_value,
    b_value,
    w_out,
    b_out,
    ln2_gain,
    ln2_bias,
    w_up,
    b_up,
    w_down,
    b_down,
):
    S, C = lax.axis_size("shard"), lax.axis_size("ctx")
    unused, R, D = frames.shape
    FH = w_up.shape[1]
    HG, CH = 3, C // 2
    G, GP = HG * HD, 256
    DB = D // (S * C)
    HF = R // 2
    PB = C * DB
    T = C * R

    WF = 2 * FH + CH * GP
    vmem = pl.BlockSpec(memory_space=pltpu.VMEM)
    V = pltpu.VMEM
    dims = (S, C, R, D, GP, HG, FH)
    scratch = [
        pltpu.SemaphoreType.DMA((SENDS,)),
        pltpu.SemaphoreType.DMA((SEMS,)),
        pltpu.SemaphoreType.DMA((2 * CH,)),
        pltpu.SemaphoreType.DMA((7,)),
        V((R, D), BF16),
        V((R, D), F32),
        V((DB, 2 * FH), F32),
        V((DB, CH * GP), F32),
        V((CH, DB, 3 * GP), F32),
        V((16, D), F32),
        V((CH, DB, 3 * GP), BF16),
        V((CH, 8, 3 * GP), F32),
        V((1, FH), F32),
        V((T, D), BF16),
        V((D, C * HF), BF16),
        V((S, 2, CH * DB, 3 * GP), BF16),
        V((2, CH, 8, 3 * GP), F32),
        V((D, WF), BF16),
        V((D, CH * GP), BF16),
        V((GP, T), BF16),
        V((GP, T), BF16),
        V((T, GP), BF16),
        V((T, GP), BF16),
        V((C * HF, GP), BF16),
        V((GP, C * HF), BF16),
        V((C * HF, GP), F32),
        V((C * HF, GP), BF16),
        V((C * HF, GP), BF16),
        V((HF, D), F32),
        V((R, D), BF16),
        V((D, R), BF16),
        V((R, D), BF16),
        V((D, R), BF16),
        V((R, FH), BF16),
        V((R, FH), BF16),
        V((HF, D), BF16),
        V((HF, D), BF16),
        V((HF, D), BF16),
        V((HF, D), BF16),
        V((D, HF), BF16),
        V((C * HF, GP), BF16),
        V((GP, HF), BF16),
        V((D, 2 * FH), BF16),
        V((C, 2, DB, FH), BF16),
        V((PB, 2 * FH), BF16),
        V((PB, 2 * FH), BF16),
        V((C - 1, DB, 2 * FH), BF16),
        V((2, D, CH * GP), BF16),
        V((S - 1, PB, CH * GP), BF16),
        V((PB, CH * GP), BF16),
        V((C - 1, DB, CH * GP), BF16),
        V((G, T), F32),
        V((G, T), F32),
        V((3 * HF, GP), F32),
        V((3 * HF, 8), F32),
        V((3 * HF, GP), BF16),
        V((3 * HF, GP), BF16),
        V((C, 2, G, HF), BF16),
        V((C, 2, G, HF), BF16),
        V((C - 1, 2, HF, D), BF16),
        V((S, 2, CH * DB, 3 * GP), BF16),
        V((S, CH * DB, 3 * GP), BF16),
        V((S - 1, CH * DB, 3 * GP), BF16),
        V((CH, DB, 3 * GP), BF16),
        V((CH, DB, 3 * GP), BF16),
        V((16, D), F32),
        V((D, 128), F32),
        V((S, 16, D), F32),
        V((C, 16, D), F32),
        V((2, 16, D), F32),
    ]
    outs = (
        jax.ShapeDtypeStruct((R, D), BF16),
        jax.ShapeDtypeStruct((R, D), F32),
        jax.ShapeDtypeStruct((DB, 2 * FH), F32),
        jax.ShapeDtypeStruct((DB, CH * GP), F32),
        jax.ShapeDtypeStruct((CH, DB, 3 * GP), F32),
        jax.ShapeDtypeStruct((16, D), F32),
    )
    output, grad_input, gf, go, gq, sums = pl.pallas_call(
        functools.partial(layer_kernel, dims),
        out_shape=outs,
        in_specs=[vmem, vmem, pl.BlockSpec(memory_space=pltpu.SMEM)] + [vmem] * 15,
        out_specs=[pl.BlockSpec(memory_space=pltpu.HBM)] * 6,
        scratch_shapes=scratch,
        compiler_params=pltpu.CompilerParams(
            collective_id=0, has_side_effects=True, vmem_limit_bytes=63 << 20
        ),
    )(
        frames[0],
        cotangent[0],
        lengths,
        ln1_gain,
        ln1_bias,
        b_out,
        ln2_gain,
        ln2_bias,
        b_down,
        b_up,
        b_query,
        b_value,
        w_query,
        w_key,
        w_value,
        w_up,
        w_down.T,
        w_out.T,
    )
    flat = [D, D, CH * G, CH * G, D, D, D, FH, D]
    results = pl.pallas_call(
        functools.partial(unpack_kernel, CH),
        out_shape=[
            jax.ShapeDtypeStruct((R, D), BF16),
            jax.ShapeDtypeStruct((R, D), F32),
            jax.ShapeDtypeStruct((DB, CH * G), F32),
            jax.ShapeDtypeStruct((DB, CH * G), F32),
            jax.ShapeDtypeStruct((DB, CH * G), F32),
            jax.ShapeDtypeStruct((DB, CH * G), F32),
            jax.ShapeDtypeStruct((DB, FH), F32),
            jax.ShapeDtypeStruct((DB, FH), F32),
        ]
        + [jax.ShapeDtypeStruct((length,), F32) for length in flat],
        in_specs=[pl.BlockSpec(memory_space=pltpu.HBM)] * 6,
        out_specs=[vmem] * 17,
        scratch_shapes=[
            V((DB, 2 * FH), F32),
            V((DB, CH * GP), F32),
            V((CH, DB, 3 * GP), F32),
            V((16, D), F32),
            pltpu.SemaphoreType.DMA((6,)),
        ],
        compiler_params=pltpu.CompilerParams(vmem_limit_bytes=63 << 20),
    )(output, grad_input, gf, go, gq, sums)
    output, grad_input, g_query, g_key, g_value, g_out, g_up, g_down = results[:8]
    g1, s1, bq, bv, bo, g2, s2, bu, bd = results[8:]
    return (
        output[None],
        grad_input[None],
        g1,
        s1,
        g_query,
        bq,
        g_key,
        g_value,
        bv,
        g_out.T,
        bo,
        g2,
        s2,
        g_up,
        bu,
        g_down.T,
        bd,
    )


def per_device(frames, lengths, cotangent, *params):
    if fits(frames, params[2], params[11]):
        return fast_layer(frames, lengths, cotangent, *params)
    return plain_layer(frames, lengths, cotangent, *params)


def solution(mesh):
    in_specs = (
        P("shard", "ctx", None),
        P("shard"),
        P("shard", "ctx", None),
        P(),
        P(),
        P(("shard", "ctx"), "tp"),
        P("tp"),
        P(("shard", "ctx"), "tp"),
        P(("shard", "ctx"), "tp"),
        P("tp"),
        P("tp", ("shard", "ctx")),
        P(),
        P(),
        P(),
        P(("shard", "ctx"), "tp"),
        P("tp"),
        P("tp", ("shard", "ctx")),
        P(),
    )
    out_specs = (
        P("shard", "ctx", None),
        P("shard", "ctx", None),
        P(),
        P(),
        P(("shard", "ctx"), "tp"),
        P("tp"),
        P(("shard", "ctx"), "tp"),
        P(("shard", "ctx"), "tp"),
        P("tp"),
        P("tp", ("shard", "ctx")),
        P(),
        P(),
        P(),
        P(("shard", "ctx"), "tp"),
        P("tp"),
        P("tp", ("shard", "ctx")),
        P(),
    )
    return jax.shard_map(
        per_device, mesh=mesh, in_specs=in_specs, out_specs=out_specs, check_vma=False
    )
```

```python
import functools
import math

import jax
import jax.numpy as jnp
from jax import lax
from jax.experimental import pallas as pl
from jax.experimental.pallas import tpu as pltpu
from jax.sharding import PartitionSpec as P

HD = 64


EPSILON = 1e-05
INV_ROOT_TWO = 0.7071067811865476
INV_ROOT_TAU = 0.3989422804014327


def norm_rows(values, gain, shift):
    centred = values - jnp.mean(values, axis=-1, keepdims=True)
    inverse = lax.rsqrt(jnp.mean(centred * centred, axis=-1, keepdims=True) + EPSILON)
    normed = centred * inverse
    return (normed * gain + shift, normed, inverse)


def norm_back(grad_rows, normed, inverse, gain):
    scaled = grad_rows * gain
    inner = (
        scaled
        - jnp.mean(scaled, axis=-1, keepdims=True)
        - normed * jnp.mean(scaled * normed, axis=-1, keepdims=True)
    )
    return (inner * inverse, jnp.sum(grad_rows * normed, axis=0), jnp.sum(grad_rows, axis=0))


def gelu_slope(values):
    return (
        0.5 * (1.0 + lax.erf(values * INV_ROOT_TWO))
        + values * jnp.exp(-0.5 * values * values) * INV_ROOT_TAU
    )


def pair_scores(queries, block_keys, score_scale):
    return (
        jnp.einsum("qhd,khd->hqk", queries, block_keys, preferred_element_type=jnp.float32)
        * score_scale
    )


def live_weights(scores, query_live, key_live, log_totals):
    both_live = query_live[None, :, None] & key_live[None, None, :]
    return jnp.where(both_live, jnp.exp(scores - log_totals[:, :, None]), 0.0)


def in_blocks(array, block_rows):
    return array.reshape((array.shape[0] // block_rows, block_rows) + array.shape[1:])


def slot_forward(queries, slot_keys, slot_values, query_live, key_live, key_block, score_scale):
    seg_rows, head_count, head_dim = queries.shape
    key_starts = jnp.arange(slot_keys.shape[0] // key_block, dtype=jnp.int32) * key_block
    blocks = (
        in_blocks(slot_keys, key_block),
        in_blocks(slot_values, key_block),
        in_blocks(key_live, key_block),
        key_starts,
    )
    start_state = (
        jnp.full((head_count, seg_rows), -jnp.inf, jnp.float32),
        jnp.zeros((head_count, seg_rows), jnp.float32),
    )

    def totals_step(carried, scan_item):
        block_keys, block_values, block_live, block_start = scan_item
        running_max, running_sum = carried
        scores = jnp.where(
            block_live[None, None, :], pair_scores(queries, block_keys, score_scale), -jnp.inf
        )
        new_max = jnp.maximum(running_max, jnp.max(scores, axis=-1))
        new_sum = running_sum * jnp.exp(running_max - new_max) + jnp.sum(
            jnp.exp(scores - new_max[:, :, None]), axis=-1
        )
        return ((new_max, new_sum), None)

    def whole_slot(ignored):
        final_state, unused = lax.scan(totals_step, start_state, blocks)
        log_totals = final_state[0] + jnp.log(final_state[1])

        def output_step(output_sum, scan_item):
            block_keys, block_values, block_live, block_start = scan_item
            weights_here = live_weights(
                pair_scores(queries, block_keys, score_scale), query_live, block_live, log_totals
            ).astype(jnp.bfloat16)
            return (
                output_sum
                + jnp.einsum(
                    "hqk,khd->qhd", weights_here, block_values, preferred_element_type=jnp.float32
                ),
                None,
            )

        attended, unused_too = lax.scan(
            output_step, jnp.zeros((seg_rows, head_count, head_dim), jnp.float32), blocks
        )
        return (log_totals, attended)

    return whole_slot(0)


def slot_back(
    queries,
    grad_att,
    log_totals,
    delta,
    slot_keys,
    slot_values,
    query_live,
    key_live,
    key_block,
    score_scale,
):
    seg_rows, head_count, head_dim = queries.shape
    key_starts = jnp.arange(slot_keys.shape[0] // key_block, dtype=jnp.int32) * key_block
    blocks = (
        in_blocks(slot_keys, key_block),
        in_blocks(slot_values, key_block),
        in_blocks(key_live, key_block),
        key_starts,
    )

    def grad_step(grad_query, scan_item):
        block_keys, block_values, block_live, block_start = scan_item
        partial_value = grad_query
        weights_full = live_weights(
            pair_scores(queries, block_keys, score_scale), query_live, block_live, log_totals
        )
        grad_probs = jnp.einsum(
            "qhd,khd->hqk", grad_att, block_values, preferred_element_type=jnp.float32
        )
        grad_scores = (weights_full * (grad_probs - delta[:, :, None])).astype(jnp.bfloat16)
        partial_value = (
            partial_value
            + jnp.einsum(
                "hqk,khd->qhd", grad_scores, block_keys, preferred_element_type=jnp.float32
            )
            * score_scale
        )
        grad_value = jnp.einsum(
            "hqk,qhd->khd",
            weights_full.astype(jnp.bfloat16),
            grad_att,
            preferred_element_type=jnp.float32,
        )
        grad_key = (
            jnp.einsum("hqk,qhd->khd", grad_scores, queries, preferred_element_type=jnp.float32)
            * score_scale
        )
        return (partial_value, (grad_key, grad_value))

    def whole_slot(ignored):
        grad_query, key_parts = lax.scan(
            grad_step, jnp.zeros((seg_rows, head_count, head_dim), jnp.float32), blocks
        )
        return (
            grad_query,
            key_parts[0].reshape(slot_keys.shape),
            key_parts[1].reshape(slot_keys.shape),
        )

    return whole_slot(0)


def plain_layer(
    frames,
    lengths,
    cotangent,
    ln1_gain,
    ln1_bias,
    w_query,
    b_query,
    w_key,
    w_value,
    b_value,
    w_out,
    b_out,
    ln2_gain,
    ln2_bias,
    w_up,
    b_up,
    w_down,
    b_down,
):
    slot_count, seg_rows, model_width = frames.shape
    row_count = slot_count * seg_rows
    head_cols = w_query.shape[1]
    head_count = head_cols // HD
    seq_length = seg_rows * lax.axis_size("ctx")
    seg_start = lax.axis_index("ctx") * seg_rows
    score_scale = HD ** (-0.5)
    key_block = math.gcd(seq_length, 512)
    positions = seg_start + jnp.arange(seg_rows, dtype=jnp.int32)
    query_live = positions[None, :] < lengths[:, None]
    key_live = jnp.arange(seq_length, dtype=jnp.int32)[None, :] < lengths[:, None]
    live_rows = query_live.astype(jnp.float32).reshape(row_count, 1)
    weight_query, weight_key, weight_value, weight_out = (
        lax.all_gather(w_query, ("shard", "ctx"), axis=0, tiled=True),
        lax.all_gather(w_key, ("shard", "ctx"), axis=0, tiled=True),
        lax.all_gather(w_value, ("shard", "ctx"), axis=0, tiled=True),
        lax.all_gather(w_out, ("shard", "ctx"), axis=1, tiled=True),
    )
    frames_flat = frames.astype(jnp.float32).reshape(row_count, model_width)
    first, normed_one, inverse_one = norm_rows(frames_flat, ln1_gain, ln1_bias)
    first_low = first.astype(jnp.bfloat16)
    queries = (
        jnp.dot(first_low, weight_query, preferred_element_type=jnp.float32) + b_query
    ).astype(jnp.bfloat16)
    keys_local = jnp.dot(first_low, weight_key, preferred_element_type=jnp.float32).astype(
        jnp.bfloat16
    )
    values_local = (
        jnp.dot(first_low, weight_value, preferred_element_type=jnp.float32) + b_value
    ).astype(jnp.bfloat16)
    keys_all, values_all = (
        lax.all_gather(
            keys_local.reshape(slot_count, seg_rows, head_cols), "ctx", axis=1, tiled=True
        ),
        lax.all_gather(
            values_local.reshape(slot_count, seg_rows, head_cols), "ctx", axis=1, tiled=True
        ),
    )
    query_heads = queries.reshape(slot_count, seg_rows, head_count, HD)
    key_heads = keys_all.reshape(slot_count, seq_length, head_count, HD)
    value_heads = values_all.reshape(slot_count, seq_length, head_count, HD)
    slot = 0
    log_totals, attended_slot = slot_forward(
        query_heads[slot],
        key_heads[slot],
        value_heads[slot],
        query_live[slot],
        key_live[slot],
        key_block,
        score_scale,
    )
    totals_list = [log_totals]
    attended_list = [attended_slot]
    attended = jnp.stack(attended_list).reshape(row_count, head_cols)
    attended_low = attended.astype(jnp.bfloat16)
    attn_sum = lax.psum(
        jnp.dot(attended_low, weight_out, preferred_element_type=jnp.float32).astype(jnp.bfloat16),
        "tp",
    ).astype(jnp.float32)
    hidden = frames_flat + attn_sum + b_out
    weight_up, weight_down = (
        lax.all_gather(w_up, ("shard", "ctx"), axis=0, tiled=True),
        lax.all_gather(w_down, ("shard", "ctx"), axis=1, tiled=True),
    )
    second, normed_two, inverse_two = norm_rows(hidden, ln2_gain, ln2_bias)
    second_low = second.astype(jnp.bfloat16)
    upper = jnp.dot(second_low, weight_up, preferred_element_type=jnp.float32) + b_up
    activated = jax.nn.gelu(upper, approximate=False).astype(jnp.bfloat16)
    mlp_sum = lax.psum(
        jnp.dot(activated, weight_down, preferred_element_type=jnp.float32).astype(jnp.bfloat16),
        "tp",
    ).astype(jnp.float32)
    output = (
        (live_rows * (hidden + mlp_sum + b_down))
        .astype(jnp.bfloat16)
        .reshape(slot_count, seg_rows, model_width)
    )
    grad_out = live_rows * cotangent.astype(jnp.float32).reshape(row_count, model_width)
    grad_out_low = grad_out.astype(jnp.bfloat16)
    grad_b_down = jnp.sum(grad_out, axis=0)
    grad_w_down = jnp.einsum(
        "rf,rd->fd", activated, grad_out_low, preferred_element_type=jnp.float32
    )
    grad_act = jnp.einsum(
        "rd,fd->rf", grad_out_low, weight_down, preferred_element_type=jnp.float32
    )
    grad_upper = (grad_act * gelu_slope(upper)).astype(jnp.bfloat16)
    grad_b_up = jnp.sum(grad_upper.astype(jnp.float32), axis=0)
    grad_w_up = jnp.einsum("rd,rf->df", second_low, grad_upper, preferred_element_type=jnp.float32)
    grad_second = lax.psum(
        jnp.einsum("rf,df->rd", grad_upper, weight_up, preferred_element_type=jnp.float32).astype(
            jnp.bfloat16
        ),
        "tp",
    ).astype(jnp.float32)
    grad_norm_two, grad_ln2_gain, grad_ln2_bias = norm_back(
        grad_second, normed_two, inverse_two, ln2_gain
    )
    grad_hidden = grad_out + grad_norm_two
    grad_hidden_low = grad_hidden.astype(jnp.bfloat16)
    grad_b_out = jnp.sum(grad_hidden_low.astype(jnp.float32), axis=0)
    grad_w_out = jnp.einsum(
        "rc,rd->cd", attended_low, grad_hidden_low, preferred_element_type=jnp.float32
    )
    grad_att = jnp.einsum(
        "rd,cd->rc", grad_hidden_low, weight_out, preferred_element_type=jnp.float32
    ).astype(jnp.bfloat16)
    delta = jnp.sum(
        (grad_att.astype(jnp.float32) * attended).reshape(row_count, head_count, HD), axis=-1
    )
    delta_heads = delta.reshape(slot_count, seg_rows, head_count)
    grad_att_heads = grad_att.reshape(slot_count, seg_rows, head_count, HD)
    slot = 0
    grad_query_slot, key_part, value_part = slot_back(
        query_heads[slot],
        grad_att_heads[slot],
        totals_list[slot],
        delta_heads[slot].T,
        key_heads[slot],
        value_heads[slot],
        query_live[slot],
        key_live[slot],
        key_block,
        score_scale,
    )
    grad_query_list = [grad_query_slot]
    key_part_list = [key_part.reshape(seq_length, head_cols)]
    value_part_list = [value_part.reshape(seq_length, head_cols)]
    grad_keys, grad_values = (
        lax.psum_scatter(
            jnp.stack(key_part_list).astype(jnp.bfloat16), "ctx", scatter_dimension=1, tiled=True
        ).astype(jnp.float32),
        lax.psum_scatter(
            jnp.stack(value_part_list).astype(jnp.bfloat16), "ctx", scatter_dimension=1, tiled=True
        ).astype(jnp.float32),
    )
    grad_query_low = jnp.stack(grad_query_list).reshape(row_count, head_cols).astype(jnp.bfloat16)
    grad_key_low = grad_keys.reshape(row_count, head_cols).astype(jnp.bfloat16)
    grad_value_low = grad_values.reshape(row_count, head_cols).astype(jnp.bfloat16)
    grad_b_query = jnp.sum(grad_query_low.astype(jnp.float32), axis=0)
    grad_b_value = jnp.sum(grad_value_low.astype(jnp.float32), axis=0)
    grad_w_query = jnp.einsum(
        "rd,rc->dc", first_low, grad_query_low, preferred_element_type=jnp.float32
    )
    grad_w_key = jnp.einsum(
        "rd,rc->dc", first_low, grad_key_low, preferred_element_type=jnp.float32
    )
    grad_w_value = jnp.einsum(
        "rd,rc->dc", first_low, grad_value_low, preferred_element_type=jnp.float32
    )
    first_terms = jnp.einsum(
        "rc,dc->rd", grad_query_low, weight_query, preferred_element_type=jnp.float32
    )
    first_terms = first_terms + jnp.einsum(
        "rc,dc->rd", grad_key_low, weight_key, preferred_element_type=jnp.float32
    )
    first_terms = first_terms + jnp.einsum(
        "rc,dc->rd", grad_value_low, weight_value, preferred_element_type=jnp.float32
    )
    grad_first = lax.psum(first_terms.astype(jnp.bfloat16), "tp").astype(jnp.float32)
    grad_norm_one, grad_ln1_gain, grad_ln1_bias = norm_back(
        grad_first, normed_one, inverse_one, ln1_gain
    )
    grad_input = (grad_hidden + grad_norm_one).reshape(slot_count, seg_rows, model_width)
    shard_grads = (
        lax.psum_scatter(grad_w_query, ("shard", "ctx"), scatter_dimension=0, tiled=True),
        lax.psum_scatter(grad_w_key, ("shard", "ctx"), scatter_dimension=0, tiled=True),
        lax.psum_scatter(grad_w_value, ("shard", "ctx"), scatter_dimension=0, tiled=True),
        lax.psum_scatter(grad_w_out, ("shard", "ctx"), scatter_dimension=1, tiled=True),
        lax.psum_scatter(grad_w_up, ("shard", "ctx"), scatter_dimension=0, tiled=True),
        lax.psum_scatter(grad_w_down, ("shard", "ctx"), scatter_dimension=1, tiled=True),
    )
    small_sums = lax.psum(
        (
            grad_ln1_gain,
            grad_ln1_bias,
            grad_b_query,
            grad_b_value,
            grad_b_out,
            grad_ln2_gain,
            grad_ln2_bias,
            grad_b_up,
            grad_b_down,
        ),
        ("shard", "ctx"),
    )
    return (
        output,
        grad_input,
        small_sums[0],
        small_sums[1],
        shard_grads[0],
        small_sums[2],
        shard_grads[1],
        shard_grads[2],
        small_sums[3],
        shard_grads[3],
        small_sums[4],
        small_sums[5],
        small_sums[6],
        shard_grads[4],
        small_sums[7],
        shard_grads[5],
        small_sums[8],
    )


MESH = pl.DeviceIdType.MESH
F32 = jnp.float32
BF16 = jnp.bfloat16
NEG = -1e30
LIVE_LANE = 192


def nn(left, right):
    return jnp.dot(left, right, preferred_element_type=F32)


def nt(left, right):
    return lax.dot_general(left, right, (((1,), (1,)), ((), ())), preferred_element_type=F32)


def group(values, j):
    taken = values[:, :256] if j == 0 else pltpu.roll(values[:, 128:384], 192, 1)
    at = lax.broadcasted_iota(jnp.int32, taken.shape, 1)
    return jnp.where(at < 3 * HD, taken, 0.0)


def ungroup(first, second):
    turned = pltpu.roll(second, 64, 1)
    at = lax.broadcasted_iota(jnp.int32, turned.shape, 1)
    tail = jnp.concatenate([first[:, 128:], first[:, 128:]], axis=1)
    return jnp.concatenate([first[:, :128], jnp.where(at < 64, tail, turned)], axis=1)


def flip(values):
    return values.astype(F32).T.astype(BF16)


def layer_kernel(
    dims,
    frames,
    cot,
    lengths,
    v_gain1,
    v_bias1,
    v_b_out,
    v_gain2,
    v_bias2,
    v_b_down,
    v_b_up,
    v_b_query,
    v_b_value,
    w_query,
    w_key,
    w_value,
    w_up,
    w_down,
    w_out,
    out_h,
    gin_h,
    gf_h,
    go_h,
    gq_h,
    sums_h,
    ss,
    rs,
    ls,
    os,
    out_o,
    gin_o,
    gf_o,
    go_o,
    gq_o,
    sums_o,
    wqkv_own,
    bias_own,
    up_bias,
    a_all,
    a_t,
    wqkv,
    bias_all,
    wf,
    wo_sib,
    k_tr,
    v_tr,
    k_n,
    v_n,
    q_n,
    q_t,
    att_f,
    att_s,
    att_r,
    hid,
    z_all,
    z_t,
    g_n,
    g_t,
    act,
    gup,
    part_s,
    part_r,
    gz_s,
    gz_r,
    ghl_t,
    gatt_r,
    gatt_t,
    wg,
    wg_t,
    wg_x,
    wg_y,
    wg_zr,
    og_x,
    og_r,
    og_z,
    og_zr,
    dk_t,
    dv_t,
    dq_f,
    dlt,
    q_s,
    d_s,
    dkv_s,
    dkv_r,
    ga_r,
    qg,
    qg_r,
    qg_p,
    qg_z,
    qg_zr,
    sums,
    pairs,
    sum_p,
    sum_z,
    sum_c,
):
    S, C, R, D, GP, HG, FH = dims
    ga_s = a_all.at[pl.ds(0, C * R // 2), :]
    g_nat = a_all.at[pl.ds(C * R // 2, C * R // 2), :]
    OC = C // 2 * GP
    WF = OC + 2 * FH
    pieces = (slice(0, OC + FH), slice(OC + FH, WF))
    HF = R // 2
    CH = C // 2
    DB = D // (S * C)
    PB = C * DB
    s, z, c = lax.axis_index("shard"), lax.axis_index("ctx"), lax.axis_index("tp")
    o = 1 - c
    sib = (s, z, o)
    owed = []
    next_sem = [0]

    def sems(count):
        base = next_sem[0]
        next_sem[0] = base + count
        return base

    def remote(src, dst, index, device, sent=None):
        return pltpu.make_async_remote_copy(
            src_ref=src,
            dst_ref=dst,
            send_sem=ss.at[index if sent is None else sent],
            recv_sem=rs.at[index],
            device_id=device,
            device_id_type=MESH,
        )

    def send(src, dst, index, device, when=None, like=None, owe=None, sent=None):
        def go():
            remote(src, dst, index, device, sent).start()

        if when is None:
            go()
        else:
            pl.when(when)(go)
        if owe is not False:
            owed.append((src if like is None else like, index, when if owe is None else owe))

    def settle(entries):
        for like, index, when in entries:

            def done(like=like, index=index):
                remote(like, like, index, sib).wait_send()

            if when is None:
                done()
            else:
                pl.when(when)(done)

    stored = []

    def store(src, dst):
        copy = pltpu.make_async_copy(src, dst, os.at[len(stored)])
        copy.start()
        stored.append(copy)

    def arrive(dst, index, when=None):
        def go():
            remote(dst, dst, index, sib, 0).wait_recv()

        if when is None:
            go()
        else:
            pl.when(when)(go)

    def plane(k):
        return (lax.rem(s + k, S), z, c)

    near_x = s + 1 - 2 * lax.rem(s, 2)
    near_y = lax.rem(s + 2, 4)
    far = near_y + 1 - 2 * lax.rem(s, 2)
    to_x, to_y = (near_x, z, c), (near_y, z, c)

    def column(k):
        return (s, lax.rem(z + k, C), c)

    def s_from(k):
        return lax.rem(s + S - k, S)

    def z_from(k):
        return lax.rem(z + C - k, C)

    def rows_of(block):
        return pl.ds(pl.multiple_of(block * DB, 16), DB)

    def half_rows(block, half):
        return pl.ds(pl.multiple_of(block * R + half * HF, HF), HF)

    def blk(block):
        return pl.ds(pl.multiple_of(block * HF, HF), HF)

    k_bias = sems(1)
    k_q1 = sems(CH)
    k_q2 = sems(S - 1) - 1
    k_q3 = sems(1)
    k_a = sems(2 * (C - 1))
    k_as = sems(2 * (C - 1))
    k_f = sems(4 * (C - 1))
    k_fs = sems(1)
    k_gs = sems(1)
    k_wo = sems(1)
    k_att = sems(C - 1) - 1
    k_n2 = sems(1)
    k_part = sems(1)
    k_gz = sems(1)
    k_out = sems(1)
    k_gatt = sems(C - 1) - 1
    k_wgz = sems(C - 1) - 1
    k_ox = sems(1)
    k_og = sems(S - 1) - 1
    k_ogz = sems(C - 1) - 1
    k_dkv = sems(1)
    k_ga = sems(2 * (C - 1))
    k_qx = sems(1)
    k_qp = sems(S - 1) - 1
    k_qz = sems(CH)
    k_gin = sems(1)
    k_sp = sems(S - 1) - 1
    k_sz = sems(C - 1) - 1
    k_sc = sems(1)
    k_fp = sems(8 * (2 * C - 1))
    k_wg = sems(6 * C)

    barrier = pltpu.get_barrier_semaphore()
    friends = [sib]
    friends += [plane(k) for k in range(1, S)]
    for k in range(1, C):
        friends += [(s, lax.rem(z + k, C), c), (s, lax.rem(z + k, C), o)]
    for friend in friends:
        pl.semaphore_signal(barrier, inc=1, device_id=friend, device_id_type=MESH)

    length = lengths[0]
    lane = lax.broadcasted_iota(jnp.int32, (HF, GP), 1)

    def head_lanes(count, h):
        at = lax.broadcasted_iota(jnp.int32, (count, GP), 1)
        return jnp.logical_and(at >= HD * h, at < HD * (h + 1))

    def only_head(values, h, keep_live=False):
        picked = head_lanes(values.shape[0], h)
        if keep_live:
            at = lax.broadcasted_iota(jnp.int32, values.shape, 1)
            picked = jnp.logical_or(picked, at == LIVE_LANE)
        return jnp.where(picked, values, jnp.zeros_like(values))

    ln1_gain, ln1_bias, b_out, ln2_gain, ln2_bias, b_down = (
        ref[...].reshape(1, D) for ref in (v_gain1, v_bias1, v_b_out, v_gain2, v_bias2, v_b_down)
    )
    for j in range(CH):
        for i, part in enumerate((w_key, w_value, w_query)):
            cols = slice(i * GP, (i + 1) * GP)
            wqkv_own[j, :, cols] = group(part[...].astype(F32), j).astype(BF16)
    mine_rows = rows_of(s * C + z)
    wf[mine_rows, OC : OC + FH] = w_up[...]
    wf[mine_rows, OC + FH :] = w_down[...]
    out_t = w_out[...].astype(F32)
    for j in range(CH):
        wf[mine_rows, j * GP : (j + 1) * GP] = group(out_t, j).astype(BF16)
    for j in range(CH):
        bias_own[j] = jnp.zeros((8, 3 * GP), F32)
        bias_own[j, 0:1, GP : 2 * GP] = group(v_b_value[...].reshape(1, CH * 3 * HD), j)
        bias_own[j, 0:1, 2 * GP :] = group(v_b_query[...].reshape(1, CH * 3 * HD), j)

    def norm(values):
        centred = values - jnp.mean(values, axis=-1, keepdims=True)
        inverse = lax.rsqrt(jnp.mean(centred * centred, axis=-1, keepdims=True) + EPSILON)
        return centred * inverse, inverse

    def live_of(first, count):
        at = z * R + first + lax.broadcasted_iota(jnp.int32, (count, 1), 0)
        return (at < length).astype(F32)

    sums[...] = jnp.zeros_like(sums)
    pl.semaphore_wait(barrier, len(friends))

    c_of_z = z // CH
    for j in range(CH):
        to_z = CH * c + j
        same = jnp.logical_and(to_z == z, c_of_z == c)
        for i in range(CH):
            ok = jnp.logical_and(z - CH * c_of_z == i, jnp.logical_not(same))
            here = wqkv.at[s, c_of_z, pl.ds(i * DB, DB), :]

            def go(i=i, here=here, j=j, to_z=to_z):
                pltpu.make_async_remote_copy(
                    src_ref=wqkv_own.at[j],
                    dst_ref=here,
                    send_sem=ls.at[j],
                    recv_sem=rs.at[k_q1 + i],
                    device_id=(s, to_z, c_of_z),
                    device_id_type=MESH,
                ).start()

            pl.when(ok)(go)

        def keep(j=j):
            wqkv[s, c, pl.ds(pl.multiple_of((z - CH * c) * DB, 16), DB), :] = wqkv_own[j]

        pl.when(same)(keep)
    send(bias_own, bias_all.at[c], k_bias, sib)
    bias_all[c] = bias_own[...]
    can_right, can_left = z + 1 < C, z >= 1

    def line_step(view, t, index, like):
        send(
            view(jnp.maximum(z - t, 0)),
            view(jnp.maximum(z - t, 0)),
            index + 2 * t,
            (s, jnp.minimum(z + 1, C - 1), c),
            goes_right[t],
            like,
        )
        send(
            view(jnp.minimum(z + t, C - 1)),
            view(jnp.minimum(z + t, C - 1)),
            index + 2 * t + 1,
            (s, jnp.maximum(z - 1, 0), c),
            goes_left[t],
            like,
        )

    goes_right = [jnp.logical_and(can_right, z - t >= 0) for t in range(C - 1)]
    goes_left = [jnp.logical_and(can_left, z + t < C) for t in range(C - 1)]
    like_f = [wf.at[pl.ds(0, DB), piece] for piece in pieces]
    like_a = a_all.at[pl.ds(0, HF), :]

    def f_step(t, p):
        view = lambda block: wf.at[rows_of(s * C + block), pieces[p]]
        line_step(view, t, k_f + 2 * (C - 1) * p, like_f[p])

    def a_step(t):
        line_step(lambda block: a_all.at[half_rows(block, c), :], t, k_a, like_a)

    def from_left(t):
        return jnp.maximum(z - 1 - t, 0), z - 1 - t >= 0

    def from_right(t):
        return jnp.minimum(z + 1 + t, C - 1), z + 1 + t < C

    halves = []
    for piece in pieces:
        middle = (piece.start + piece.stop) // 2
        halves.append((slice(piece.start, middle), slice(middle, piece.stop)))

    def row_of(shard, block):
        return rows_of(shard * C + block)

    labels_of = [
        ((2 * t + 1,) + from_left(t), (2 * t + 2,) + from_right(t)) for t in range(C - 1)
    ]
    own_label = ((0, z, None),)
    at_end = jnp.logical_or(z == 0, z == C - 1)
    near_end = jnp.minimum(z, C - 1 - z)
    inside = jnp.logical_not(at_end)
    wo_cols = slice(0, OC)

    def wo_pass(shard, block, ok):
        def go():
            at = row_of(shard, block)
            remote(wf.at[at, wo_cols], wo_sib.at[at, :], k_wo, sib).start()

        if ok is None:
            go()
        else:
            pl.when(ok)(go)


    def f_plane(labels, p):
        for label, block, ok in labels:
            index = k_fp + 8 * label + 4 * p
            at = wf.at[row_of(s, block), pieces[p]]
            send(at, at, index, to_x, ok, None, False, k_fs)
            send(at, at, index + 1, to_y, ok, None, False, k_fs)
            if p == 0:
                wo_pass(s, block, ok)

    def f_relay(labels, p, gate=None):
        for label, block, ok in labels:
            index = k_fp + 8 * label + 4 * p
            now = ok if gate is None else jnp.logical_and(ok, gate)
            arrive(wf.at[row_of(near_x, block), pieces[p]], index, now)
            at = wf.at[row_of(near_x, block), halves[p][0]]
            send(at, at, index + 2, to_y, now, None, False, k_fs)
            arrive(wf.at[row_of(near_y, block), pieces[p]], index + 1, now)
            at = wf.at[row_of(near_y, block), halves[p][1]]
            send(at, at, index + 3, to_x, now, None, False, k_fs)
            if p == 0:
                wo_pass(near_x, block, now)
                wo_pass(near_y, block, now)

    def f_finish(labels, p):
        for label, block, ok in labels:
            index = k_fp + 8 * label + 4 * p
            for i in range(2):
                arrive(wf.at[row_of(far, block), halves[p][i]], index + 2 + i, ok)
            if p == 0:
                wo_pass(far, block, ok)

    def f_arrive(t, p):
        for side, (label, block, ok) in enumerate(labels_of[t]):
            arrive(wf.at[row_of(s, block), pieces[p]], k_f + 2 * (C - 1) * p + 2 * t + side, ok)
        f_plane(labels_of[t], p)

    f_step(0, 0)
    f_step(0, 1)

    def first_norm(i, carry):
        at = pl.ds(pl.multiple_of(i * 64, 64), 64)
        to = pl.ds(pl.multiple_of(z * R + i * 64, 64), 64)
        normed, unused = norm(frames[at, :].astype(F32))
        a_all[to, :] = (normed * ln1_gain + ln1_bias).astype(BF16)
        g_n[at, :] = (cot[at, :].astype(F32) * live_of(i * 64, 64)).astype(BF16)
        return carry

    lax.fori_loop(0, R // 64, first_norm, 0)
    a_step(0)
    for i in range(CH):
        from_z = CH * c + i
        same = jnp.logical_and(from_z == z, c_of_z == c)
        arrive(wqkv.at[s, c, pl.ds(i * DB, DB), :], k_q1 + i, jnp.logical_not(same))
    for k in range(1, S):
        send(wqkv.at[s, c], wqkv.at[s, c], k_q2 + k, plane(k))
    f_plane(own_label, 0)
    f_plane(own_label, 1)
    key_at = lax.broadcasted_iota(jnp.int32, (GP - LIVE_LANE, C * R), 1)
    first_row = lax.broadcasted_iota(jnp.int32, (GP - LIVE_LANE, C * R), 0) == 0
    dead = jnp.where(jnp.logical_and(first_row, key_at >= length), NEG, 0.0)
    k_tr[LIVE_LANE:, :] = dead.astype(BF16)
    v_tr[LIVE_LANE:, :] = jnp.zeros((GP - LIVE_LANE, C * R), BF16)
    g_t[:, :HF] = flip(g_n[:HF, :])
    g_t[:, HF:] = flip(g_n[HF:, :])
    for k in range(1, S):
        arrive(wqkv.at[s_from(k), c], k_q2 + k)
    send(wqkv.at[:, c], wqkv.at[:, c], k_q3, sib)
    arrive(bias_all.at[o], k_bias)
    arrive(wqkv.at[:, o], k_q3)
    bias_z = bias_all[c_of_z, z - CH * c_of_z]

    def project(block, half):
        at = half_rows(block, half)
        rows = a_all[at, :]
        made = nn(rows, wqkv[...].reshape(D, 3 * GP)) + bias_z[0:1, :]
        keys = made[:, :GP].astype(BF16)
        values = made[:, GP : 2 * GP].astype(BF16)
        k_n[at, :] = keys
        v_n[at, :] = values
        k_tr[:LIVE_LANE, at] = flip(keys)[:LIVE_LANE, :]
        v_tr[:LIVE_LANE, at] = flip(values)[:LIVE_LANE, :]

        def own():
            queries = made[:, 2 * GP :].astype(BF16).astype(F32) * (HD**-0.5)
            queries = jnp.where(lane == LIVE_LANE, 1.0, queries).astype(BF16)
            q_n[blk(block), :] = queries
            q_t[:, blk(block)] = flip(queries)
            a_t[:, blk(block)] = flip(rows)

        pl.when(half == c)(own)

    def project_own(i, carry):
        project(z, lax.rem(c + i, 2))
        return carry

    a_given = []

    def remote_when(src, dst, index, device, when):
        def go():
            remote(src, dst, index, device).start()

        pl.when(when)(go)

    lax.fori_loop(0, 2, project_own, 0)
    f_arrive(0, 0)
    f_arrive(0, 1)
    f_relay(own_label, 0)
    f_relay(own_label, 1)
    for t in range(C - 1):
        if t == C - 2:
            for p in range(2):
                f_arrive(1, p)
                f_step(2, p)
        for side, (label, block, ok) in enumerate(labels_of[t]):
            arrive(a_all.at[half_rows(block, c), :], k_a + 2 * t + side, ok)
        if t == C - 3:
            f_step(1, 0)
            f_step(1, 1)
        if t + 1 < C - 1:
            a_step(t + 1)
        for side, (label, block, ok) in enumerate(labels_of[t]):
            at = a_all.at[half_rows(block, c), :]
            remote_when(at, at, k_as + 2 * t + side, sib, ok)
            a_given.append((like_a, k_as + 2 * t + side, ok))

        def come(i, carry, t=t):
            side = i // 2
            block = jnp.where(side == 0, from_left(t)[0], from_right(t)[0])
            ok = jnp.where(side == 0, z - 1 - t >= 0, z + 1 + t < C)

            def other_half():
                at = a_all.at[half_rows(block, o), :]
                remote(at, at, k_as + 2 * t + side, sib).wait_recv()

            def both():
                pl.when(lax.rem(i, 2) == 1)(other_half)
                project(block, lax.rem(c + i, 2))

            pl.when(ok)(both)
            return carry

        lax.fori_loop(0, 4, come, 0)
        if t == C - 3:
            f_relay(labels_of[0], 0)
            f_relay(labels_of[0], 1)
    for p in range(2):
        f_relay(labels_of[1], p, at_end)
    for p in range(2):
        f_finish(own_label, p)
        f_finish(labels_of[0], p)

    TQ = 128

    def attend(block):
        def step(i, carry):
            at = pl.ds(pl.multiple_of(block * HF + i * TQ, TQ), TQ)
            queries = q_n[at, :]
            total = jnp.zeros((TQ, GP), F32)
            log_sums = []
            for h in range(HG):
                scores = nn(only_head(queries, h, True), k_tr[...])
                top = jnp.max(scores, axis=-1, keepdims=True)
                weights = jnp.exp(scores - top)
                norm_sum = jnp.sum(weights, axis=-1, keepdims=True)
                got = nn(weights.astype(BF16), v_n[...]) * (1.0 / norm_sum)
                total = total + only_head(got, h)
                log_sums.append(top + jnp.log(norm_sum))
            att_f[at, :] = total
            for h in range(HG):
                att_f[at, LIVE_LANE + h : LIVE_LANE + h + 1] = log_sums[h]
            att_s[at, :] = total.astype(BF16)
            return carry

        lax.fori_loop(0, HF // TQ, step, 0)

    def attend_all(i, carry):
        inner = jnp.where(i == 0, 2, jnp.where(i == 1, 1, jnp.where(i == 2, 3, 0)))
        block = jnp.where(near_end == 0, lax.rem(i + 1, C), inner)
        block = jnp.where(2 * z < C, block, C - 1 - block)
        attend(block)

        def give():
            hop = lax.rem(block + C - z, C)
            device = (s, block, c)
            remote(att_s.at[blk(block), :], att_r.at[blk(z), :], k_att + hop, device).start()

        def poll_0():
            f_arrive(2, 0)

        def poll_1():
            f_relay(labels_of[1], 0, inside)

        def poll_2():
            f_relay(labels_of[1], 1, inside)
            f_relay(labels_of[2], 0)
            f_arrive(2, 1)

        pl.when(block != z)(give)
        pl.when(i == 0)(poll_0)
        pl.when(i == 1)(poll_1)
        pl.when(i == 2)(poll_2)
        return carry

    lax.fori_loop(0, C, attend_all, 0)
    att_r[blk(z), :] = att_s[blk(z), :]

    f_finish(labels_of[1], 0)
    f_finish(labels_of[2], 0)
    owed.append((wo_sib, k_wo, None))
    owed.append((wf.at[pl.ds(0, 3 * C * DB), :], k_fs, None))
    for k in range(1, C):
        arrive(att_r.at[blk(z_from(k)), :], k_att + k)
        remote(att_s.at[blk(z), :], att_r.at[blk(z), :], k_att + k, column(k)).wait_send()
    f_relay(labels_of[2], 1)
    arrive(wo_sib, k_wo)

    settle([entry for entry in owed if entry[0] is like_a])
    settle(a_given)
    owed[:] = [entry for entry in owed if entry[0] is not like_a]
    own_rows = pl.ds(pl.multiple_of(c * HF, HF), HF)
    hidden = frames[own_rows, :].astype(F32) + b_out
    for j in range(CH):
        hidden = hidden + nt(
            att_r[blk(CH * c + j), :], wf[:, j * GP : (j + 1) * GP]
        )
        hidden = hidden + nt(att_r[blk(CH * o + j), :], wo_sib[:, j * GP : (j + 1) * GP])
    hid[...] = hidden
    normed, unused = norm(hidden)
    z_all[own_rows, :] = (normed * ln2_gain + ln2_bias).astype(BF16)
    send(z_all.at[own_rows, :], z_all.at[own_rows, :], k_n2, sib)
    other_rows = pl.ds(pl.multiple_of(o * HF, HF), HF)
    z_t[:, own_rows] = flip(z_all[own_rows, :])
    arrive(z_all.at[other_rows, :], k_n2)
    z_t[:, other_rows] = flip(z_all[other_rows, :])

    f_finish(labels_of[1], 1)
    f_finish(labels_of[2], 1)
    TF, TG = 512, 512

    up_bias[...] = v_b_up[...].reshape(1, FH)

    def units(i, carry):
        cols = pl.ds(pl.multiple_of(i * TF, TF), TF)
        down = pl.ds(pl.multiple_of(OC + FH + i * TF, TF), TF)
        ups = pl.ds(pl.multiple_of(OC + i * TF, TF), TF)
        upper = nn(z_all[...], wf[:, ups]) + up_bias[:, cols]
        cumulative = 0.5 * (1.0 + lax.erf(upper * INV_ROOT_TWO))
        act[:, cols] = (upper * cumulative).astype(BF16)
        slope = cumulative + upper * jnp.exp(-0.5 * upper * upper) * INV_ROOT_TAU
        grad_units = (nn(g_n[...], wf[:, down]) * slope).astype(BF16)
        gup[:, cols] = grad_units
        return carry

    lax.fori_loop(0, FH // TF, units, 0)

    def unit_grads(i, carry):
        cols = pl.ds(pl.multiple_of(i * TG, TG), TG)
        down = pl.ds(pl.multiple_of(FH + i * TG, TG), TG)
        wg[:, cols] = nn(z_t[...], gup[:, cols]).astype(BF16)
        wg[:, down] = nn(g_t[...], act[:, cols]).astype(BF16)
        return carry

    lax.fori_loop(0, FH // TG, unit_grads, 0)

    part_order = ((3, 3), (2, 0), (1, 2), (0, 1))

    def part_z(j):
        chosen = jnp.where(near_end == 0, part_order[j][0], part_order[j][1])
        return jnp.where(2 * z < C, chosen, C - 1 - chosen)

    def part_rows(j):
        return pl.ds(pl.multiple_of(part_z(j) * DB, 16), DB)

    part_a, part_b = slice(0, FH), slice(FH, 2 * FH)

    def wg_far(j):
        index = k_wg + 6 * j
        own_z = part_z(j)
        send(wg.at[row_of(far, own_z), part_a], wg_t.at[j, 0], index, to_x, owe=False, sent=k_gs)
        send(wg.at[row_of(far, own_z), part_b], wg_t.at[j, 1], index + 1, to_y, owe=False, sent=k_gs)

    def wg_near(j):
        index = k_wg + 6 * j
        own_z = part_z(j)
        near = wg.at[row_of(near_x, own_z), part_a]
        send(near, wg_x.at[part_rows(j), part_a], index + 2, to_x, owe=False, sent=k_gs)
        near = wg.at[row_of(near_y, own_z), part_b]
        send(near, wg_y.at[part_rows(j), part_b], index + 3, to_y, owe=False, sent=k_gs)

    def add_into(at, cols, others):
        def step(i, carry):
            here = pl.ds(pl.multiple_of(cols.start + i * 256, 256), 256)
            total = wg[at, here].astype(F32)
            for other, rows, start in others:
                there = pl.ds(pl.multiple_of(start + i * 256, 256), 256)
                total = total + other[rows, there].astype(F32)
            wg[at, here] = total.astype(BF16)
            return carry

        lax.fori_loop(0, (cols.stop - cols.start) // 256, step, 0)

    def wg_second(j):
        index = k_wg + 6 * j
        own_z = part_z(j)
        arrive(wg_t.at[j, 0], index)
        at = row_of(near_y, own_z)
        add_into(at, part_a, [(wg_t.at[j, 0], slice(None), 0)])
        near = wg.at[at, part_a]
        send(near, wg_y.at[part_rows(j), part_a], index + 4, to_y, owe=False, sent=k_gs)
        arrive(wg_t.at[j, 1], index + 1)
        at = row_of(near_x, own_z)
        add_into(at, part_b, [(wg_t.at[j, 1], slice(None), 0)])
        near = wg.at[at, part_b]
        send(near, wg_x.at[part_rows(j), part_b], index + 5, to_x, owe=False, sent=k_gs)

    def wg_third(j):
        index = k_wg + 6 * j
        arrive(wg_x.at[part_rows(j), part_a], index + 2)
        arrive(wg_y.at[part_rows(j), part_b], index + 3)
        arrive(wg_y.at[part_rows(j), part_a], index + 4)
        arrive(wg_x.at[part_rows(j), part_b], index + 5)
        at = row_of(s, part_z(j))
        add_into(
            at, slice(0, 2 * FH), [(wg_x, part_rows(j), 0), (wg_y, part_rows(j), 0)]
        )
        if j < C - 1:
            hop = lax.rem(part_z(j) + C - z, C)
            device = (s, part_z(j), c)
            remote(wg.at[at, :], wg_zr.at[hop - 1], k_wgz + hop, device, k_gs).start()

    wg_far(0)
    wg_near(0)
    wg_far(1)

    def z_grad(i, carry):
        at = pl.ds(pl.multiple_of(i * 256, 256), 256)
        gz_s[:, at] = nt(gup[other_rows, :], wf[at, OC : OC + FH]).astype(BF16)
        return carry

    lax.fori_loop(0, D // 256, z_grad, 0)
    send(gz_s, gz_r, k_gz, sib)

    gz_rows = jnp.concatenate(
        [nt(gup[own_rows, :], wf[i * 256 : (i + 1) * 256, OC : OC + FH]) for i in range(D // 256)], axis=1
    )
    arrive(gz_r, k_gz)
    grad_z = gz_rows + gz_r[...].astype(F32)
    live_own = live_of(c * HF, HF)
    normed, inverse = norm(hid[...])
    scaled = grad_z * ln2_gain
    inner = (
        scaled
        - jnp.mean(scaled, axis=-1, keepdims=True)
        - normed * jnp.mean(scaled * normed, axis=-1, keepdims=True)
    )
    g_own = g_n[own_rows, :].astype(F32)
    grad_hidden = g_own + inner * inverse
    gin_o[own_rows, :] = grad_hidden
    low = grad_hidden.astype(BF16)
    sums[3:4, :] = jnp.sum(grad_z * normed, axis=0, keepdims=True)
    sums[4:5, :] = jnp.sum(grad_z, axis=0, keepdims=True)
    sums[5:6, :] = jnp.sum(g_own, axis=0, keepdims=True)
    sums[2:3, :] = jnp.sum(low.astype(F32), axis=0, keepdims=True)
    for j in range(CH):
        att_s[blk(CH * c + j), :] = nn(
            low, wf[:, j * GP : (j + 1) * GP]
        ).astype(BF16)
        att_s[blk(CH * o + j), :] = nn(low, wo_sib[:, j * GP : (j + 1) * GP]).astype(BF16)
    for k in range(1, C):
        send(att_s.at[blk(lax.rem(z + k, C)), :], gatt_r.at[blk(z), :], k_gatt + k, column(k))
    gatt_r[blk(z), :] = att_s[blk(z), :]
    ghl_t[...] = flip(low)
    def down_part(i, carry):
        at = pl.ds(pl.multiple_of(i * 256, 256), 256)
        part_s[:, at] = nt(act[other_rows, :], wf[at, OC + FH :]).astype(BF16)
        return carry

    lax.fori_loop(0, D // 256, down_part, 0)
    send(part_s, part_r, k_part, sib)

    for j in range(CH):
        og_x[0, :, j * GP : (j + 1) * GP] = nn(ghl_t[...], att_r[blk(CH * o + j), :]).astype(BF16)
    remote(og_x.at[0], og_x.at[1], k_ox, sib).start()
    old = list(owed)
    owed.clear()
    dk_t[...] = jnp.zeros_like(dk_t)
    dv_t[...] = jnp.zeros_like(dv_t)
    TK = 512

    steps = C * R // TK

    def attend_back(polls):
        def block_step(b, carry):
            block = lax.rem(z + C - b, C)
            at = blk(block)

            def come():
                remote(gatt_r.at[at, :], gatt_r.at[at, :], k_gatt + b, sib).wait_recv()

            pl.when(b > 0)(come)
            gatt_t[...] = flip(gatt_r[at, :])
            product = gatt_r[at, :].astype(F32) * att_f[at, :]
            for h in range(HG):
                rows = slice(h * HF, (h + 1) * HF)
                dlt[rows, 0:1] = jnp.sum(only_head(product, h), axis=-1, keepdims=True)
                dlt[rows, 1:2] = att_f[at, LIVE_LANE + h : LIVE_LANE + h + 1]
                q_s[rows, :] = only_head(q_n[at, :], h, True)
                d_s[rows, :] = only_head(gatt_r[at, :], h)
            dq_f[...] = jnp.zeros_like(dq_f)

            def step(i, carry):
                keys = pl.ds(pl.multiple_of(i * TK, TK), TK)
                weights = jnp.exp(nn(q_s[...], k_tr[:, keys]) - dlt[:, 1:2])
                grads = nn(d_s[...], v_tr[:, keys])
                grad_scores = (weights * (grads - dlt[:, 0:1])).astype(BF16)
                weights = weights.astype(BF16)
                for h in range(HG):
                    head = slice(HD * h, HD * (h + 1))
                    rows = slice(h * HF, (h + 1) * HF)
                    dv_t[head, keys] += nn(gatt_t[head, :], weights[rows, :])
                    dk_t[head, keys] += nn(q_t[head, at], grad_scores[rows, :])
                dq_f[...] += nn(grad_scores, k_n[keys, :])
                for number, poll in polls:
                    pl.when(b * steps + i == number)(poll)
                return carry

            lax.fori_loop(0, steps, step, 0)
            for h in range(HG):
                rows = slice(h * HF, (h + 1) * HF)
                part = only_head(dq_f[rows, :], h)
                total = part if h == 0 else total + part
            g_nat[at, 2 * GP :] = (total * (HD**-0.5)).astype(BF16)
            return carry

        lax.fori_loop(0, C, block_step, 0)

    def og_reduce():
        for k in range(1, S):
            arrive(og_r.at[k - 1], k_og + k)
        own = pl.ds(pl.multiple_of(s * PB, 64), PB)
        total = og_x[0, own, :].astype(F32)
        for k in range(1, S):
            total = total + og_r[k - 1].astype(F32)
        og_z[...] = total.astype(BF16)
        for k in range(1, C):
            at = pl.ds(pl.multiple_of(lax.rem(z + k, C) * DB, 16), DB)
            send(og_z.at[at, :], og_zr.at[k - 1], k_ogz + k, column(k))

    def poll_a():
        wg_second(0)
        wg_near(1)

    def poll_b():
        wg_second(1)
        wg_far(2)
        wg_near(2)

    def poll_c():
        wg_second(2)
        wg_far(3)
        wg_near(3)

    down_rows = jnp.concatenate(
        [nt(act[own_rows, :], wf[i * 256 : (i + 1) * 256, OC + FH :]) for i in range(D // 256)],
        axis=1,
    )
    arrive(part_r, k_part)
    out_rows = live_own * (hid[...] + down_rows + part_r[...].astype(F32) + b_down)
    out_o[own_rows, :] = out_rows.astype(BF16)
    send(out_o.at[own_rows, :], out_o.at[own_rows, :], k_out, sib)
    for i in range(2):
        sums[pl.ds(6 + 2 * c + i, 1), :] = jnp.sum(
            gup[:, i * D : (i + 1) * D].astype(F32), axis=0, keepdims=True
        )
    arrive(og_x.at[1], k_ox)
    remote(og_x.at[0], og_x.at[1], k_ox, sib).wait_send()
    for j in range(CH):
        cols = slice(j * GP, (j + 1) * GP)
        own_part = nn(ghl_t[...], att_r[blk(CH * c + j), :])
        og_x[0, :, cols] = (own_part + og_x[1, :, cols].astype(F32)).astype(BF16)
    attend_back(
        (
            (0, poll_a),
            (3, poll_b),
            (6, lambda: wg_third(0)),
            (10, lambda: wg_third(1)),
            (11, poll_c),
        )
    )

    for i in range(C):
        cols = pl.ds(pl.multiple_of(i * R + o * HF, HF), HF)
        dkv_s[i, 0] = dk_t[:, cols].astype(BF16)
        dkv_s[i, 1] = dv_t[:, cols].astype(BF16)
    send(dkv_s, dkv_r, k_dkv, sib)
    wg_third(2)
    arrive(dkv_r, k_dkv)

    def finish(block):
        cols = pl.ds(pl.multiple_of(block * R + c * HF, HF), HF)
        at = blk(block)
        keys_t = dk_t[:, cols] + dkv_r[block, 0].astype(F32)
        values_t = dv_t[:, cols] + dkv_r[block, 1].astype(F32)
        none = jnp.zeros((GP - LIVE_LANE, HF), F32)
        g_nat[at, :GP] = jnp.concatenate([keys_t, none], axis=0).T.astype(BF16)
        g_nat[at, GP : 2 * GP] = jnp.concatenate([values_t, none], axis=0).T.astype(BF16)
        ga_s[at, :] = nt(g_nat[at, :], wqkv[...].reshape(D, 3 * GP)).astype(BF16)

    def finish_all(b, carry):
        finish(b)
        return carry

    lax.fori_loop(0, C, finish_all, 0)

    like_ga = ga_s.at[pl.ds(0, HF), :]

    def ga_send(t, side):
        target = jnp.where(side == 0, C - 1 - t, t)
        device = (s, jnp.clip(z + 1 - 2 * side, 0, C - 1), c)
        remote(ga_s.at[blk(target), :], ga_r.at[t, side], k_ga + 2 * t + side, device).start()

    def ga_ahead(t, side):
        return C - 1 - t > z if side == 0 else t < z

    for t in range(C - 1):
        for side in range(2):
            behind = z >= 1 if side == 0 else z + 1 < C
            first = jnp.logical_and(ga_ahead(t, side), jnp.logical_not(behind))
            pl.when(first)(lambda t=t, side=side: ga_send(t, side))
            owed.append((like_ga, k_ga + 2 * t + side, ga_ahead(t, side)))

    def ga_hop(u):
        for i in range(2):
            side = jnp.where(2 * z < C, i, 1 - i)
            t = jnp.where(side == 0, u - z, u - (C - 1 - z))
            target = jnp.where(side == 0, C - 1 - t, t)
            inner = jnp.logical_and(z >= 1, z + 1 < C)
            ahead = jnp.where(side == 0, target > z, target < z)
            ok = jnp.logical_and(jnp.logical_and(t >= 0, inner), ahead)

            def add(t=t, side=side, target=target):
                at = blk(target)
                arrive(ga_r.at[t, side], k_ga + 2 * t + side)
                ga_s[at, :] = (ga_s[at, :].astype(F32) + ga_r[t, side].astype(F32)).astype(BF16)
                ga_send(t, side)

            pl.when(ok)(add)

    wg_second(3)
    column_sum = jnp.sum(g_nat[...].astype(F32), axis=0, keepdims=True)
    sums[pl.ds(10 + z, 1), :] = column_sum
    pair_lane = lax.broadcasted_iota(jnp.int32, (PB, 128), 1)
    for i in range(S):
        got = nn(a_t[i * PB : (i + 1) * PB, :], g_nat[...])
        qg[i] = got.reshape(2, CH * DB, 3 * GP).astype(BF16)
        weights = wqkv[i].reshape(PB, 3 * GP).astype(F32)
        with_a = jnp.sum(got * weights, axis=-1, keepdims=True)
        alone = jnp.sum(weights * column_sum, axis=-1, keepdims=True)
        pairs[i * PB : (i + 1) * PB, :] = jnp.where(
            pair_lane == 0, with_a, jnp.where(pair_lane == 1, alone, 0.0)
        )
    send(qg.at[:, o], qg_r, k_qx, sib)
    turned = pairs[...].T
    sums[0:1, :] = (turned[0:1, :] - ln1_bias * turned[1:2, :]) / ln1_gain
    sums[1:2, :] = turned[1:2, :]
    sum_p[s] = sums[...]
    for k in range(1, S):
        send(sum_p.at[s], sum_p.at[s], k_sp + k, plane(k))
    arrive(qg_r, k_qx)
    for i in range(S):
        qg_r[i] = (qg_r[i].astype(F32) + qg[i, c].astype(F32)).astype(BF16)
    for k in range(1, S):
        send(qg_r.at[lax.rem(s + k, S)], qg_p.at[k - 1], k_qp + k, plane(k))
    for k in range(1, S):
        at = pl.ds(pl.multiple_of(lax.rem(s + k, S) * PB, 64), PB)
        send(og_x.at[0, at, :], og_r.at[k - 1], k_og + k, plane(k))
    settle(old)
    arrive(out_o.at[other_rows, :], k_out)
    store(out_o, out_h)
    for k in range(1, S):
        arrive(sum_p.at[s_from(k)], k_sp + k)
    total = sum_p[0]
    for k in range(1, S):
        total = total + sum_p[k]
    sum_z[z] = total
    for k in range(1, C):
        send(sum_z.at[z], sum_z.at[z], k_sz + k, column(k))
    wg_third(3)
    owed.append((wg.at[pl.ds(0, (4 * C - 1) * DB), :], k_gs, None))
    ga_hop(1)
    og_reduce()
    for u in range(2, C - 1):
        ga_hop(u)
    for k in range(1, S):
        arrive(qg_p.at[k - 1], k_qp + k)
    total = qg_r[s].astype(F32)
    for k in range(1, S):
        total = total + qg_p[k - 1].astype(F32)
    qg_z[...] = total.reshape(CH, DB, 3 * GP).astype(BF16)
    for i in range(CH):
        to_z = CH * c + i
        same = jnp.logical_and(to_z == z, c_of_z == c)
        for j in range(CH):
            ok = jnp.logical_and(z - CH * c_of_z == j, jnp.logical_not(same))

            def go(i=i, j=j, to_z=to_z):
                pltpu.make_async_remote_copy(
                    src_ref=qg_z.at[i],
                    dst_ref=qg_zr.at[j],
                    send_sem=ls.at[CH + i],
                    recv_sem=rs.at[k_qz + j],
                    device_id=(s, to_z, c_of_z),
                    device_id_type=MESH,
                ).start()

            pl.when(ok)(go)

        def keep(i=i):
            qg_zr[z - CH * c] = qg_z[i]

        pl.when(same)(keep)

    for k in range(1, C):
        arrive(sum_z.at[z_from(k)], k_sz + k)
    total = sum_z[0]
    for k in range(1, C):
        total = total + sum_z[k]
    sum_c[c] = total
    send(sum_c.at[c], sum_c.at[c], k_sc, sib)
    own_block = blk(z)
    hid[...] = ga_s[own_block, :].astype(F32)
    for t in range(C - 1):
        for side in range(2):
            target = C - 1 - t if side == 0 else t
            behind = z >= 1 if side == 0 else z + 1 < C

            def add(t=t, side=side):
                arrive(ga_r.at[t, side], k_ga + 2 * t + side)
                hid[...] += ga_r[t, side].astype(F32)

            pl.when(jnp.logical_and(target == z, behind))(add)
    grad_a = hid[...]
    normed, inverse = norm(frames[own_rows, :].astype(F32))
    scaled = grad_a * ln1_gain
    inner = (
        scaled
        - jnp.mean(scaled, axis=-1, keepdims=True)
        - normed * jnp.mean(scaled * normed, axis=-1, keepdims=True)
    )
    gin_o[own_rows, :] = gin_o[own_rows, :] + inner * inverse
    send(gin_o.at[own_rows, :], gin_o.at[own_rows, :], k_gin, sib)
    store(gin_o.at[own_rows, :], gin_h.at[own_rows, :])
    def last(own, got, index, to):
        for k in range(1, C):
            arrive(got.at[k - 1], index + k)
        total = own.astype(F32)
        for k in range(1, C):
            total = total + got[k - 1].astype(F32)
        to[...] = total

    last(wg[rows_of(s * C + z), :], wg_zr, k_wgz, gf_o)
    last(og_z[pl.ds(pl.multiple_of(z * DB, 16), DB), :], og_zr, k_ogz, go_o)
    store(gf_o, gf_h)
    store(go_o, go_h)
    for j in range(CH):
        same = jnp.logical_and(CH * c + j == z, c_of_z == c)
        arrive(qg_zr.at[j], k_qz + j, jnp.logical_not(same))
    gq_o[...] = qg_zr[...].astype(F32)
    store(gq_o, gq_h)
    arrive(sum_c.at[o], k_sc)
    sums_o[...] = sum_c[0] + sum_c[1]
    store(sums_o, sums_h)
    arrive(gin_o.at[other_rows, :], k_gin)
    store(gin_o.at[other_rows, :], gin_h.at[other_rows, :])

    settle(owed)
    for copy in stored:
        copy.wait()
    for j in range(CH):
        same = jnp.logical_and(CH * c + j == z, c_of_z == c)

        def done_weights(j=j):
            pltpu.make_async_remote_copy(
                src_ref=wqkv_own.at[j],
                dst_ref=wqkv_own.at[j],
                send_sem=ls.at[j],
                recv_sem=rs.at[k_q1],
                device_id=sib,
                device_id_type=MESH,
            ).wait_send()
            pltpu.make_async_remote_copy(
                src_ref=qg_z.at[j],
                dst_ref=qg_z.at[j],
                send_sem=ls.at[CH + j],
                recv_sem=rs.at[k_qz],
                device_id=sib,
                device_id_type=MESH,
            ).wait_send()

        pl.when(jnp.logical_not(same))(done_weights)
    assert (next_sem[0], k_fp) == (SEMS, SENDS)


def unpack_kernel(
    CH,
    output,
    grad_input,
    gf_h,
    go_h,
    gq_h,
    sums_h,
    output_o,
    grad_input_o,
    query_o,
    key_o,
    value_o,
    out_o,
    up_o,
    down_o,
    gain1_o,
    bias1_o,
    b_query_o,
    b_value_o,
    b_out_o,
    gain2_o,
    bias2_o,
    b_up_o,
    b_down_o,
    gf,
    go,
    gq,
    sums,
    sem,
):
    c = lax.axis_index("tp")
    FH = up_o.shape[1]
    D = sums.shape[1]
    GP = 256
    pairs = ((output, output_o), (grad_input, grad_input_o))
    pairs += ((gf_h, gf), (go_h, go), (gq_h, gq), (sums_h, sums))
    copies = [
        pltpu.make_async_copy(src, dst, sem.at[i]) for i, (src, dst) in enumerate(pairs)
    ]
    for copy in copies:
        copy.start()
    for copy in copies[2:]:
        copy.wait()
    for i, to in enumerate((key_o, value_o, query_o)):
        cols = slice(i * GP, (i + 1) * GP)
        to[...] = ungroup(gq[0, :, cols], gq[1, :, cols])
    out_o[...] = ungroup(go[:, :GP], go[:, GP : 2 * GP])
    up_o[...] = gf[:, :FH]
    down_o[...] = gf[:, FH:]
    for i, to in enumerate((gain1_o, bias1_o, b_out_o, gain2_o, bias2_o, b_down_o)):
        to[...] = sums[i, :]
    for i in range(FH // D):
        b_up_o[i * D : (i + 1) * D] = sums[6 + 2 * c + i, :]
    for to, start in ((b_value_o, GP), (b_query_o, 2 * GP)):
        row = [sums[pl.ds(10 + CH * c + j, 1), start : start + GP] for j in range(CH)]
        to[...] = ungroup(row[0], row[1])[0, :]
    for copy in copies[:2]:
        copy.wait()


SEMS, SENDS = 155, 75


def fits(frames, w_query, w_up):
    shards, ctx, cores = (lax.axis_size(name) for name in ("shard", "ctx", "tp"))
    slot_count, seg_rows, width = frames.shape
    heads = w_query.shape[1] * cores // HD
    return (
        slot_count == 1
        and cores == 2
        and ctx % 2 == 0
        and ctx == 4
        and shards == 4
        and heads == 3 * ctx
        and width % (16 * shards * ctx) == 0
        and width % 256 == 0
        and seg_rows % 512 == 0
        and w_up.shape[1] % 512 == 0
        and w_up.shape[1] == 2 * width
        and ctx * seg_rows <= 2048
        and width <= 768
        and w_up.shape[1] <= 1536
    )


def fast_layer(
    frames,
    lengths,
    cotangent,
    ln1_gain,
    ln1_bias,
    w_query,
    b_query,
    w_key,
    w_value,
    b_value,
    w_out,
    b_out,
    ln2_gain,
    ln2_bias,
    w_up,
    b_up,
    w_down,
    b_down,
):
    S, C = lax.axis_size("shard"), lax.axis_size("ctx")
    unused, R, D = frames.shape
    FH = w_up.shape[1]
    HG, CH = 3, C // 2
    G, GP = HG * HD, 256
    DB = D // (S * C)
    HF = R // 2
    PB = C * DB
    T = C * R

    WF = 2 * FH + CH * GP
    vmem = pl.BlockSpec(memory_space=pltpu.VMEM)
    V = pltpu.VMEM
    dims = (S, C, R, D, GP, HG, FH)
    scratch = [
        pltpu.SemaphoreType.DMA((SENDS,)),
        pltpu.SemaphoreType.DMA((SEMS,)),
        pltpu.SemaphoreType.DMA((2 * CH,)),
        pltpu.SemaphoreType.DMA((7,)),
        V((R, D), BF16),
        V((R, D), F32),
        V((DB, 2 * FH), F32),
        V((DB, CH * GP), F32),
        V((CH, DB, 3 * GP), F32),
        V((16, D), F32),
        V((CH, DB, 3 * GP), BF16),
        V((CH, 8, 3 * GP), F32),
        V((1, FH), F32),
        V((T, D), BF16),
        V((D, C * HF), BF16),
        V((S, 2, CH * DB, 3 * GP), BF16),
        V((2, CH, 8, 3 * GP), F32),
        V((D, WF), BF16),
        V((D, CH * GP), BF16),
        V((GP, T), BF16),
        V((GP, T), BF16),
        V((T, GP), BF16),
        V((T, GP), BF16),
        V((C * HF, GP), BF16),
        V((GP, C * HF), BF16),
        V((C * HF, GP), F32),
        V((C * HF, GP), BF16),
        V((C * HF, GP), BF16),
        V((HF, D), F32),
        V((R, D), BF16),
        V((D, R), BF16),
        V((R, D), BF16),
        V((D, R), BF16),
        V((R, FH), BF16),
        V((R, FH), BF16),
        V((HF, D), BF16),
        V((HF, D), BF16),
        V((HF, D), BF16),
        V((HF, D), BF16),
        V((D, HF), BF16),
        V((C * HF, GP), BF16),
        V((GP, HF), BF16),
        V((D, 2 * FH), BF16),
        V((C, 2, DB, FH), BF16),
        V((PB, 2 * FH), BF16),
        V((PB, 2 * FH), BF16),
        V((C - 1, DB, 2 * FH), BF16),
        V((2, D, CH * GP), BF16),
        V((S - 1, PB, CH * GP), BF16),
        V((PB, CH * GP), BF16),
        V((C - 1, DB, CH * GP), BF16),
        V((G, T), F32),
        V((G, T), F32),
        V((3 * HF, GP), F32),
        V((3 * HF, 8), F32),
        V((3 * HF, GP), BF16),
        V((3 * HF, GP), BF16),
        V((C, 2, G, HF), BF16),
        V((C, 2, G, HF), BF16),
        V((C - 1, 2, HF, D), BF16),
        V((S, 2, CH * DB, 3 * GP), BF16),
        V((S, CH * DB, 3 * GP), BF16),
        V((S - 1, CH * DB, 3 * GP), BF16),
        V((CH, DB, 3 * GP), BF16),
        V((CH, DB, 3 * GP), BF16),
        V((16, D), F32),
        V((D, 128), F32),
        V((S, 16, D), F32),
        V((C, 16, D), F32),
        V((2, 16, D), F32),
    ]
    outs = (
        jax.ShapeDtypeStruct((R, D), BF16),
        jax.ShapeDtypeStruct((R, D), F32),
        jax.ShapeDtypeStruct((DB, 2 * FH), F32),
        jax.ShapeDtypeStruct((DB, CH * GP), F32),
        jax.ShapeDtypeStruct((CH, DB, 3 * GP), F32),
        jax.ShapeDtypeStruct((16, D), F32),
    )
    output, grad_input, gf, go, gq, sums = pl.pallas_call(
        functools.partial(layer_kernel, dims),
        out_shape=outs,
        in_specs=[vmem, vmem, pl.BlockSpec(memory_space=pltpu.SMEM)] + [vmem] * 15,
        out_specs=[pl.BlockSpec(memory_space=pltpu.HBM)] * 6,
        scratch_shapes=scratch,
        compiler_params=pltpu.CompilerParams(
            collective_id=0, has_side_effects=True, vmem_limit_bytes=63 << 20
        ),
    )(
        frames[0],
        cotangent[0],
        lengths,
        ln1_gain,
        ln1_bias,
        b_out,
        ln2_gain,
        ln2_bias,
        b_down,
        b_up,
        b_query,
        b_value,
        w_query,
        w_key,
        w_value,
        w_up,
        w_down.T,
        w_out.T,
    )
    flat = [D, D, CH * G, CH * G, D, D, D, FH, D]
    results = pl.pallas_call(
        functools.partial(unpack_kernel, CH),
        out_shape=[
            jax.ShapeDtypeStruct((R, D), BF16),
            jax.ShapeDtypeStruct((R, D), F32),
            jax.ShapeDtypeStruct((DB, CH * G), F32),
            jax.ShapeDtypeStruct((DB, CH * G), F32),
            jax.ShapeDtypeStruct((DB, CH * G), F32),
            jax.ShapeDtypeStruct((DB, CH * G), F32),
            jax.ShapeDtypeStruct((DB, FH), F32),
            jax.ShapeDtypeStruct((DB, FH), F32),
        ]
        + [jax.ShapeDtypeStruct((length,), F32) for length in flat],
        in_specs=[pl.BlockSpec(memory_space=pltpu.HBM)] * 6,
        out_specs=[vmem] * 17,
        scratch_shapes=[
            V((DB, 2 * FH), F32),
            V((DB, CH * GP), F32),
            V((CH, DB, 3 * GP), F32),
            V((16, D), F32),
            pltpu.SemaphoreType.DMA((6,)),
        ],
        compiler_params=pltpu.CompilerParams(vmem_limit_bytes=63 << 20),
    )(output, grad_input, gf, go, gq, sums)
    output, grad_input, g_query, g_key, g_value, g_out, g_up, g_down = results[:8]
    g1, s1, bq, bv, bo, g2, s2, bu, bd = results[8:]
    return (
        output[None],
        grad_input[None],
        g1,
        s1,
        g_query,
        bq,
        g_key,
        g_value,
        bv,
        g_out.T,
        bo,
        g2,
        s2,
        g_up,
        bu,
        g_down.T,
        bd,
    )


def per_device(frames, lengths, cotangent, *params):
    if fits(frames, params[2], params[11]):
        return fast_layer(frames, lengths, cotangent, *params)
    return plain_layer(frames, lengths, cotangent, *params)


def solution(mesh):
    in_specs = (
        P("shard", "ctx", None),
        P("shard"),
        P("shard", "ctx", None),
        P(),
        P(),
        P(("shard", "ctx"), "tp"),
        P("tp"),
        P(("shard", "ctx"), "tp"),
        P(("shard", "ctx"), "tp"),
        P("tp"),
        P("tp", ("shard", "ctx")),
        P(),
        P(),
        P(),
        P(("shard", "ctx"), "tp"),
        P("tp"),
        P("tp", ("shard", "ctx")),
        P(),
    )
    out_specs = (
        P("shard", "ctx", None),
        P("shard", "ctx", None),
        P(),
        P(),
        P(("shard", "ctx"), "tp"),
        P("tp"),
        P(("shard", "ctx"), "tp"),
        P(("shard", "ctx"), "tp"),
        P("tp"),
        P("tp", ("shard", "ctx")),
        P(),
        P(),
        P(),
        P(("shard", "ctx"), "tp"),
        P("tp"),
        P("tp", ("shard", "ctx")),
        P(),
    )
    return jax.shard_map(
        per_device, mesh=mesh, in_specs=in_specs, out_specs=out_specs, check_vma=False
    )
```
